32 devices in a mesh: seq: 8 (over z, x), ctx: 4 (over y, core).
Axes of the slice: x: 2, y: 2, z: 4, core: 2. Of those that a mesh axis runs over, the one named last changes fastest.
Arguments:
- hidden_in: bfloat16 [2, 8, 256, 2048], P(None, 'seq', 'ctx'), may hold values from -6 to 6
- token_marks: int32 [2, 8, 256, 3], P(None, 'seq', 'ctx'), may hold values from 0 to 255, as said below
- out_grad: bfloat16 [2, 8, 256, 2048], P(None, 'seq', 'ctx'), may hold values from -6 to 6
- qkv_weight: bfloat16 [2048, 6144], P(('seq', 'ctx')), may hold values from -0.125 to 0.125
- proj_weight: bfloat16 [2048, 2048], P(('seq', 'ctx')), may hold values from -1 to 1
- gate_weight: bfloat16 [2048, 5461], P(('seq', 'ctx')), may hold values from -0.125 to 0.125
- up_weight: bfloat16 [2048, 5461], P(('seq', 'ctx')), may hold values from -0.125 to 0.125
- down_weight: bfloat16 [2048, 5461], P(('seq', 'ctx')), may hold values from -0.15625 to 0.15625
- first_gain: bfloat16 [2048], P(('seq', 'ctx')), may hold values from 0.25 to 1.75
- first_shift: bfloat16 [2048], P(('seq', 'ctx')), may hold values from -1.75 to 1.75
- second_gain: bfloat16 [2048], P(('seq', 'ctx')), may hold values from 0.25 to 1.75
- second_shift: bfloat16 [2048], P(('seq', 'ctx')), may hold values from -1.75 to 1.75
Outputs:
- layer_out: bfloat16 [2, 8, 256, 2048], P(None, 'seq', 'ctx')
- input_grad: bfloat16 [2, 8, 256, 2048], P(None, 'seq', 'ctx')
- qkv_grad: float32 [2048, 6144], P(('seq', 'ctx'))
- proj_grad: float32 [2048, 2048], P(('seq', 'ctx'))
- gate_grad: float32 [2048, 5461], P(('seq', 'ctx'))
- up_grad: float32 [2048, 5461], P(('seq', 'ctx'))
- down_grad: float32 [2048, 5461], P(('seq', 'ctx'))
- first_gain_grad: float32 [2048], P(('seq', 'ctx'))
- first_shift_grad: float32 [2048], P(('seq', 'ctx'))
- second_gain_grad: float32 [2048], P(('seq', 'ctx'))
- second_shift_grad: float32 [2048], P(('seq', 'ctx'))
The draws below stay inside these ranges and needn't reach their ends.
Inputs may be any that keep to these rules, and one draw needn't show every extreme that they name: `token_marks`: within each row, segments are runs of positions and one starts at position 0. Column 0 is the first position of the token's segment; column 1 is the end of that segment's bidirectional prefix, from the segment's first position to one before the segment's end; column 2 is the token's position within its segment. Packed row 0 of micro-batch 0 is a single segment.
All inputs are finite; a program needn't handle non-finite values.
Results may differ from the reference program's by a relative error of at most 0.015.
Values may be sent and summed in bfloat16 or wider, within the bound.
A program may use at most 448 MiB of HBM per device.

```python
import math
import jax
import jax.numpy as jnp
from jax import lax

D = 2048
HEADS = 16
HEAD_DIM = 128
FF = 5461
MICRO = 2
ROWS = 8
ROW_LEN = 256


def draw_token_marks(key, part):
    row_total = MICRO * ROWS
    first_key, second_key = jax.random.split(key)
    coins = jax.random.randint(first_key, (row_total, ROW_LEN), 0, ROW_LEN)
    place = jnp.arange(ROW_LEN, dtype=jnp.int32)[None, :]
    row_index = jnp.arange(row_total, dtype=jnp.int32)[:, None]
    starts = (coins < 3) & (row_index != 0) | (place == 0)
    start_of = lax.cummax(jnp.where(starts, place, 0), axis=1)
    upcoming = lax.cummin(jnp.where(starts, place, ROW_LEN), axis=1, reverse=True)
    next_start = jnp.concatenate([upcoming[:, 1:], jnp.full((row_total, 1), ROW_LEN, jnp.int32)], axis=1)
    span = next_start - start_of
    picks = jax.random.randint(second_key, (row_total, ROW_LEN), 0, 2 ** 20)
    at_start = jnp.take_along_axis(picks, start_of, axis=1)
    prefix = at_start * span // 2 ** 20
    marks = jnp.stack([start_of, start_of + prefix, place - start_of], axis=-1)
    return marks.reshape(MICRO, ROWS, ROW_LEN, 3).astype(jnp.int32)


def levels(key, shape, cuts, least, top_value):
    def one(position, parts):
        heights = jax.random.uniform(jax.random.fold_in(jax.random.fold_in(key, 6), position), (parts,), jnp.float32, least / len(cuts), top_value / len(cuts))
        return jnp.repeat(jnp.exp(heights), shape[position] // parts).reshape((-1,) + (1,) * (len(shape) - position - 1))

    gain = one(*cuts[0])
    for cut in cuts[1:]:
        gain = gain * one(*cut)
    return gain


def noise(own_key, dims, scale, reach, pieces=(), kind=jnp.bfloat16):
    drawn = scale * jax.random.normal(own_key, dims, jnp.float32)
    if pieces:
        drawn = drawn * levels(own_key, dims, pieces, -0.22, 0.18)
    return jnp.clip(drawn, -reach, reach).astype(kind)


def setup_inputs(seed: int = 0) -> dict:
    streams_of = jax.random.split(jax.random.key(seed), 13)
    hidden_in = noise(streams_of[0], (MICRO, ROWS, ROW_LEN, D), 1.0, 6.0, ((1, 8), (2, 4)))
    token_marks = draw_token_marks(jax.random.fold_in(streams_of[12], 71), 0)
    out_grad = noise(streams_of[2], (MICRO, ROWS, ROW_LEN, D), 1.0, 6.0, ((1, 8), (2, 4)))
    qkv_weight = noise(streams_of[3], (D, 3 * D), D ** -0.5, 0.125, ((0, 32),))
    proj_weight = noise(streams_of[4], (D, D), (D // 64) ** -0.5, 1.0, ((0, 32),))
    gate_weight = noise(streams_of[5], (D, FF), D ** -0.5, 0.125, ((0, 32),))
    up_weight = noise(streams_of[6], (D, FF), D ** -0.5, 0.125, ((0, 32),))
    down_weight = noise(streams_of[7], (D, FF), (FF // 4) ** -0.5, 0.15625, ((0, 32),))
    first_gain = jnp.clip(1.0 + 0.15 * jax.random.normal(streams_of[8], (D,), jnp.float32), 0.25, 1.75).astype(jnp.bfloat16)
    first_shift = noise(streams_of[9], (D,), 0.3, 1.75, ((0, 32),))
    second_gain = jnp.clip(1.0 + 0.15 * jax.random.normal(streams_of[10], (D,), jnp.float32), 0.25, 1.75).astype(jnp.bfloat16)
    second_shift = noise(streams_of[11], (D,), 0.3, 1.75, ((0, 32),))
    return dict(hidden_in=hidden_in, token_marks=token_marks, out_grad=out_grad, qkv_weight=qkv_weight, proj_weight=proj_weight, gate_weight=gate_weight, up_weight=up_weight, down_weight=down_weight, first_gain=first_gain, first_shift=first_shift, second_gain=second_gain, second_shift=second_shift)


@jax.custom_vjp
def low(v):
    return lax.optimization_barrier(v.astype(jnp.bfloat16)).astype(jnp.float32)

@jax.custom_vjp
def low_back(v):
    return v

def low_keep(v):
    return (low(v), None)

def low_pass(kept, grad):
    return (grad,)

def back_keep(v):
    return (v, None)

def back_low(kept, grad):
    return (low(grad),)
low.defvjp(low_keep, low_pass)
low_back.defvjp(back_keep, back_low)
deep_alpha = 48.0 ** 0.25
norm_eps = 1e-05
masked_score = -1e+30
top_precision = lax.Precision.HIGHEST

def matmul(left_side, right_side):
    return jnp.dot(left_side, right_side, preferred_element_type=jnp.float32, precision=top_precision)

def layer_norm(values, gain_vec, shift_vec):
    center = values - lax.optimization_barrier(jnp.mean(values, axis=-1, keepdims=True))
    spread = lax.optimization_barrier(jnp.mean(center * center, axis=-1, keepdims=True))
    return center * lax.rsqrt(spread + norm_eps) * gain_vec + shift_vec

def rotary_tables(positions):
    exponent = jnp.arange(HEAD_DIM // 2, dtype=jnp.float32) * (2.0 / HEAD_DIM)
    angles = positions.astype(jnp.float32)[:, None] * jnp.exp(-math.log(10000.0) * exponent)[None, :]
    return (jnp.cos(angles), jnp.sin(angles))

def rotate(matrix, cosine, sine):
    row_count = matrix.shape[0]
    split_view = matrix.reshape(row_count, HEADS, HEAD_DIM)
    half_dim = HEAD_DIM // 2
    front_half = split_view[..., :half_dim]
    back_half = split_view[..., half_dim:]
    cos_rows = cosine[:, None, :]
    sin_rows = sine[:, None, :]
    turned = jnp.concatenate([front_half * cos_rows - back_half * sin_rows, back_half * cos_rows + front_half * sin_rows], axis=-1)
    return turned.reshape(row_count, D)

def forward_row(x_row, marks_row, qkv_weight, proj_weight, gate_weight, up_weight, down_weight, first_gain, first_shift, second_gain, second_shift):
    length = x_row.shape[0]
    mixed = low_back(matmul(x_row, qkv_weight))
    cosine, sine = rotary_tables(marks_row[:, 2])
    queries = low(rotate(mixed[:, :D], cosine, sine))
    key_rows = low(rotate(mixed[:, D:2 * D], cosine, sine))
    value_rows = low(mixed[:, 2 * D:])
    place = jnp.arange(length, dtype=jnp.int32)
    same_segment = marks_row[:, 0][:, None] == marks_row[:, 0][None, :]
    earlier = place[None, :] <= place[:, None]
    opened = (place < marks_row[:, 1])[None, :]
    allowed = same_segment & (earlier | opened)
    query_heads = queries.reshape(length, HEADS, HEAD_DIM)
    key_heads = key_rows.reshape(length, HEADS, HEAD_DIM)
    value_heads = value_rows.reshape(length, HEADS, HEAD_DIM)
    scores = low_back(jnp.einsum('qhd,khd->hqk', query_heads, key_heads, precision=top_precision) * (1.0 / math.sqrt(HEAD_DIM)))
    scores = jnp.where(allowed[None], scores, masked_score)
    probs = low(jax.nn.softmax(scores, axis=-1))
    context = jnp.einsum('hqk,khd->qhd', probs, value_heads, precision=top_precision).reshape(length, D)
    context = low(low_back(context))
    branch = low_back(matmul(context, proj_weight))
    normed = low(layer_norm(deep_alpha * x_row + branch, first_gain, first_shift))
    gate_val = low_back(matmul(normed, gate_weight))
    up_val = low_back(matmul(normed, up_weight))
    active = low(jax.nn.gelu(gate_val, approximate=False) * up_val)
    down_val = low_back(matmul(active, down_weight.T))
    return layer_norm(deep_alpha * normed + down_val, second_gain, second_shift)

def reference(hidden_in, token_marks, out_grad, qkv_weight, proj_weight, gate_weight, up_weight, down_weight, first_gain, first_shift, second_gain, second_shift):
    params = tuple((weight_arg.astype(jnp.float32) for weight_arg in (qkv_weight, proj_weight, gate_weight, up_weight, down_weight, first_gain, first_shift, second_gain, second_shift)))
    x_all = hidden_in.astype(jnp.float32).reshape(MICRO * ROWS, ROW_LEN, D)
    marks_all = token_marks.reshape(MICRO * ROWS, ROW_LEN, 3)
    cot_all = out_grad.astype(jnp.float32).reshape(MICRO * ROWS, ROW_LEN, D)

    def one_row(carry, row_data):
        x_row, marks_row, cot_row = row_data

        def local_forward(x_value, *weights):
            return forward_row(x_value, marks_row, *weights)
        out_row, back_fn = jax.vjp(local_forward, x_row, *params)
        grads = back_fn(cot_row)
        carry = tuple((running + arrived for running, arrived in zip(carry, grads[1:])))
        return (carry, (out_row.astype(jnp.bfloat16), grads[0].astype(jnp.bfloat16)))
    start = tuple((jnp.zeros(weight_arg.shape, jnp.float32) for weight_arg in params))
    totals, (outs_all, dins_all) = lax.scan(one_row, start, (x_all, marks_all, cot_all))
    return (outs_all.reshape(MICRO, ROWS, ROW_LEN, D), dins_all.reshape(MICRO, ROWS, ROW_LEN, D), totals[0], totals[1], totals[2], totals[3], totals[4], totals[5], totals[6], totals[7], totals[8])
```

```python
import math

import jax
import jax.numpy as jnp
import numpy as np
from jax import lax
from jax.sharding import Mesh
from jax.sharding import PartitionSpec as P

HEAD_DIM = 128
LANES = 128

deep_alpha = 48.0**0.25
norm_eps = 1e-05
masked_score = -1e30

ALL = ("zo", "zi", "x", "y", "c")
HEAD_AXES = ("x", "y", "c")
UNIT_AXES = ("zi", "c")
HEAD_COPIES = ("zo", "zi")
UNIT_COPIES = ("zo", "x", "y")


def contract_last(left_side, right_side):
    return lax.dot_general(
        left_side, right_side, (((1,), (1,)), ((), ())), preferred_element_type=jnp.float32
    )


def contract_first(left_side, right_side):
    return lax.dot_general(
        left_side, right_side, (((0,), (0,)), ((), ())), preferred_element_type=jnp.float32
    )


def dot(left_side, right_side):
    return jnp.dot(left_side, right_side, preferred_element_type=jnp.float32)


def low(values):
    return values.astype(jnp.bfloat16)


def norm_parts(values):
    center = values - jnp.mean(values, axis=-1, keepdims=True)
    spread = jnp.mean(center * center, axis=-1, keepdims=True)
    inverse = lax.rsqrt(spread + norm_eps)
    return center * inverse, inverse


def norm_back(cotangent, hat, inverse, gain_vec):
    scaled = cotangent * gain_vec
    return (
        scaled
        - jnp.mean(scaled, axis=-1, keepdims=True)
        - hat * jnp.mean(scaled * hat, axis=-1, keepdims=True)
    ) * inverse


def rotary_tables(positions):
    half = HEAD_DIM // 2
    exponent = jnp.arange(half, dtype=jnp.float32) * (2.0 / HEAD_DIM)
    angles = positions.astype(jnp.float32)[..., None] * jnp.exp(-math.log(10000.0) * exponent)
    return (jnp.cos(angles), jnp.sin(angles))


def rotate(values, cosine, sine):
    half = HEAD_DIM // 2
    front, back = values[..., :half], values[..., half:]
    return jnp.concatenate(
        [front * cosine - back * sine, back * cosine + front * sine], axis=-1
    )


def gather(values, axes):
    return lax.all_gather(values, axes, axis=0, tiled=True)


def scatter_sum(values, axes):
    return lax.psum_scatter(values, axes, scatter_dimension=0, tiled=True)


def gelu_parts(value):
    phi = 0.5 * lax.erfc(-value * math.sqrt(0.5))
    density = jnp.exp(-0.5 * value * value) * (1.0 / math.sqrt(2.0 * math.pi))
    return value * phi, phi + value * density


def body(
    hidden_in,
    token_marks,
    out_grad,
    qkv_weight,
    proj_weight,
    gate_weight,
    up_weight,
    down_weight,
    first_gain,
    first_shift,
    second_gain,
    second_shift,
):
    micro_count, _, pos_count, width = hidden_in.shape
    rows_own = qkv_weight.shape[0]
    units = gate_weight.shape[1]
    head_ways = math.prod(lax.axis_size(name) for name in HEAD_AXES)
    unit_ways = math.prod(lax.axis_size(name) for name in UNIT_AXES)
    device_count = math.prod(lax.axis_size(name) for name in ALL)
    chunk_count = lax.axis_size("y") * lax.axis_size("c")
    row_length = pos_count * chunk_count
    x_size = lax.axis_size("x")
    own = micro_count * pos_count
    head_width = width // head_ways
    heads_here = head_width // HEAD_DIM
    unit_width = -(-units // (unit_ways * LANES)) * LANES
    unit_pad = unit_width * unit_ways - units

    small = jnp.stack([first_gain, first_shift, second_gain, second_shift])[None]
    small_all = gather(small, ALL).transpose(1, 0, 2).reshape(4, width).astype(jnp.float32)
    gain_one, shift_one, gain_two, shift_two = (small_all[i][None] for i in range(4))
    marks = gather(token_marks.reshape(1, micro_count, pos_count, 3), HEAD_AXES)

    qkv_parts = (
        qkv_weight.reshape(rows_own, 3, head_ways, head_width)
        .transpose(2, 0, 1, 3)
        .reshape(head_ways * rows_own, 3 * head_width)
    )
    qkv_here = gather(
        lax.all_to_all(qkv_parts, HEAD_AXES, split_axis=0, concat_axis=0, tiled=True), HEAD_COPIES
    )
    proj_full = gather(proj_weight, ALL)

    sizes = [lax.axis_size(name) for name in ALL]

    ffn = jnp.stack([gate_weight, up_weight, down_weight])
    ffn = jnp.pad(ffn, ((0, 0), (0, 0), (0, unit_pad)))
    ffn = (
        ffn.reshape(3, rows_own, unit_ways, unit_width)
        .transpose(2, 0, 1, 3)
        .reshape(unit_ways * 3, rows_own, unit_width)
    )
    ffn = lax.all_to_all(ffn, UNIT_AXES, split_axis=0, concat_axis=0, tiled=True)

    def unit_full(index):
        part = ffn.reshape(unit_ways, 3, rows_own, unit_width)[:, index]
        whole = gather(part, UNIT_COPIES)
        zo, zi, x, y, c = sizes
        return (
            whole.reshape(zo, x, y, zi, c, rows_own, unit_width)
            .transpose(0, 3, 1, 2, 4, 5, 6)
            .reshape(width, unit_width)
        )

    gate_here, up_here, down_here = (unit_full(index) for index in range(3))

    x_own = hidden_in.reshape(own, width)
    x_all = gather(x_own, HEAD_AXES)
    mixed = dot(x_all, qkv_here)

    def to_rows(values):
        inner = values.shape[1:]
        values = values.reshape((x_size, chunk_count, micro_count, pos_count) + inner)
        return jnp.swapaxes(values, 1, 2).reshape((x_size * micro_count, row_length) + inner)

    def from_rows(values):
        inner = values.shape[2:]
        values = values.reshape((x_size, micro_count, chunk_count, pos_count) + inner)
        return jnp.swapaxes(values, 1, 2).reshape((head_ways * own,) + inner)

    row_marks = to_rows(marks.reshape(head_ways * own, 3))
    cosine, sine = rotary_tables(row_marks[..., 2])
    cosine, sine = cosine[:, :, None, :], sine[:, :, None, :]
    mixed = to_rows(mixed).reshape(x_size * micro_count, row_length, 3, heads_here, HEAD_DIM)
    queries = low(rotate(mixed[:, :, 0], cosine, sine))
    key_rows = low(rotate(mixed[:, :, 1], cosine, sine))
    value_rows = low(mixed[:, :, 2])
    place = jnp.arange(row_length, dtype=jnp.int32)
    allowed = (row_marks[:, :, None, 0] == row_marks[:, None, :, 0]) & (
        (place[None, None, :] <= place[None, :, None])
        | (place[None, :] < row_marks[:, :, 1])[:, None, :]
    )
    score_scale = 1.0 / math.sqrt(HEAD_DIM)

    def pair(spec, left_side, right_side):
        return jnp.einsum(spec, left_side, right_side, preferred_element_type=jnp.float32)

    scores = pair("rqhd,rkhd->rhqk", queries, key_rows) * score_scale
    scores = jnp.where(allowed[:, None], scores, masked_score)
    exp_scores = jnp.exp(scores - jnp.max(scores, axis=-1, keepdims=True))
    probs = exp_scores / jnp.sum(exp_scores, axis=-1, keepdims=True)
    probs_low = low(probs)
    context = low(pair("rhqk,rkhd->rqhd", probs_low, value_rows))

    def heads_to_tokens(values):
        values = values.reshape(head_ways, own, head_width)
        values = lax.all_to_all(values, HEAD_AXES, split_axis=0, concat_axis=0, tiled=True)
        return values.transpose(1, 0, 2).reshape(own, width)

    def tokens_to_heads(values):
        values = values.reshape(own, head_ways, head_width).transpose(1, 0, 2)
        values = lax.all_to_all(values, HEAD_AXES, split_axis=0, concat_axis=0, tiled=True)
        return values.reshape(head_ways * own, head_width)

    context_own = heads_to_tokens(from_rows(context))
    first_sum = deep_alpha * x_own.astype(jnp.float32) + dot(context_own, proj_full)
    hat_one, inverse_one = norm_parts(first_sum)
    normed = low(hat_one * gain_one + shift_one)

    normed_all = gather(normed, UNIT_AXES)
    gate_val = dot(normed_all, gate_here)
    up_val = dot(normed_all, up_here)
    gelu_val, gelu_slope = gelu_parts(gate_val)
    active = low(gelu_val * up_val)
    down_val = scatter_sum(low(contract_last(active, down_here)), UNIT_AXES)
    second_sum = deep_alpha * normed.astype(jnp.float32) + down_val.astype(jnp.float32)
    hat_two, inverse_two = norm_parts(second_sum)
    layer_rows = low(hat_two * gain_two + shift_two)

    grad_own = out_grad.reshape(own, width).astype(jnp.float32)
    gain_two_grad = jnp.sum(grad_own * hat_two, axis=0)
    shift_two_grad = jnp.sum(grad_own, axis=0)
    d_second = norm_back(grad_own, hat_two, inverse_two, gain_two)
    down_low = gather(low(d_second), UNIT_AXES)
    d_active = dot(down_low, down_here)
    gate_low = low(d_active * up_val * gelu_slope)
    up_low = low(d_active * gelu_val)
    d_normed_part = low(contract_last(gate_low, gate_here) + contract_last(up_low, up_here))
    d_normed = deep_alpha * d_second + scatter_sum(d_normed_part, UNIT_AXES).astype(jnp.float32)

    def unit_grad(left_side, right_side):
        zo, zi, x, y, c = sizes
        part = low(contract_first(left_side, right_side))
        part = (
            part.reshape(zo, zi, x, y, c, rows_own, unit_width)
            .transpose(0, 2, 3, 1, 4, 5, 6)
            .reshape(width, unit_width)
        )
        part = scatter_sum(part, UNIT_COPIES).reshape(unit_ways, rows_own, unit_width)
        part = lax.all_to_all(part, UNIT_AXES, split_axis=0, concat_axis=0, tiled=True)
        part = part.transpose(1, 0, 2).reshape(rows_own, unit_ways * unit_width)
        return part[:, :units].astype(jnp.float32)

    down_grad = unit_grad(down_low, active)
    gate_grad = unit_grad(normed_all, gate_low)
    up_grad = unit_grad(normed_all, up_low)

    gain_one_grad = jnp.sum(d_normed * hat_one, axis=0)
    shift_one_grad = jnp.sum(d_normed, axis=0)
    d_first = norm_back(d_normed, hat_one, inverse_one, gain_one)
    branch_low = low(d_first)
    small_grads = jnp.stack([gain_one_grad, shift_one_grad, gain_two_grad, shift_two_grad])
    small_grads = small_grads.reshape(4, device_count, rows_own).transpose(1, 0, 2)
    small_grads = scatter_sum(small_grads, ALL)[0]

    proj_grad = scatter_sum(low(contract_first(context_own, branch_low)), ALL).astype(jnp.float32)
    d_context = to_rows(tokens_to_heads(low(contract_last(branch_low, proj_full))))
    d_context = d_context.reshape(x_size * micro_count, row_length, heads_here, HEAD_DIM)
    d_probs = pair("rqhd,rkhd->rhqk", d_context, value_rows)
    d_scores = low(probs * (d_probs - jnp.sum(probs * d_probs, axis=-1, keepdims=True)))
    d_query = pair("rhqk,rkhd->rqhd", d_scores, key_rows) * score_scale
    d_keys = pair("rhqk,rqhd->rkhd", d_scores, queries) * score_scale
    d_values = pair("rhqk,rqhd->rkhd", probs_low, d_context)
    d_mixed = low(
        jnp.stack(
            [rotate(d_query, cosine, -sine), rotate(d_keys, cosine, -sine), d_values], axis=2
        )
    )
    d_mixed = from_rows(d_mixed.reshape(x_size * micro_count, row_length, 3 * head_width))
    d_input = scatter_sum(low(contract_last(d_mixed, qkv_here)), HEAD_AXES).astype(jnp.float32)
    d_input = deep_alpha * d_first + d_input

    qkv_part = scatter_sum(low(contract_first(x_all, d_mixed)), HEAD_COPIES)
    qkv_part = lax.all_to_all(
        qkv_part.reshape(head_ways, rows_own, 3 * head_width),
        HEAD_AXES,
        split_axis=0,
        concat_axis=0,
        tiled=True,
    )
    qkv_grad = (
        qkv_part.reshape(head_ways, rows_own, 3, head_width)
        .transpose(1, 2, 0, 3)
        .reshape(rows_own, 3 * width)
        .astype(jnp.float32)
    )
    return (
        layer_rows.reshape(micro_count, 1, pos_count, width),
        low(d_input).reshape(micro_count, 1, pos_count, width),
        qkv_grad,
        proj_grad,
        gate_grad,
        up_grad,
        down_grad,
        small_grads[0],
        small_grads[1],
        small_grads[2],
        small_grads[3],
    )


def solution(mesh):
    seq_size, ctx_size = mesh.shape["seq"], mesh.shape["ctx"]
    cores, x_size = 2, 2
    zi_size = math.gcd(4, seq_size // x_size)
    zo_size = seq_size // (x_size * zi_size)
    devices = np.asarray(mesh.devices).reshape(
        zo_size, zi_size, x_size, ctx_size // cores, cores
    )
    inner = Mesh(devices, ALL)
    tokens = P(None, ("zo", "zi", "x"), ("y", "c"), None)
    matrix = P(ALL, None)
    vector = P(ALL)
    return jax.shard_map(
        body,
        mesh=inner,
        in_specs=(tokens,) * 3 + (matrix,) * 5 + (vector,) * 4,
        out_specs=(tokens,) * 2 + (matrix,) * 5 + (vector,) * 4,
        check_vma=False,
    )
```

```python
import math

import jax
import jax.numpy as jnp
import numpy as np
from jax import lax
from jax.experimental import pallas as pl
from jax.experimental.pallas import tpu as pltpu
from jax.sharding import Mesh
from jax.sharding import PartitionSpec as P

HEAD_DIM = 128
LANES = 128

deep_alpha = 48.0**0.25
norm_eps = 1e-05
masked_score = -1e30

ALL = ("zo", "zi", "x", "y", "c")
HEAD_AXES = ("x", "y", "c")
UNIT_AXES = ("zi", "c")
HEAD_COPIES = ("zo", "zi")
UNIT_COPIES = ("zo", "x", "y")


def contract_last(left_side, right_side):
    return lax.dot_general(
        left_side, right_side, (((1,), (1,)), ((), ())), preferred_element_type=jnp.float32
    )


def contract_first(left_side, right_side):
    return lax.dot_general(
        left_side, right_side, (((0,), (0,)), ((), ())), preferred_element_type=jnp.float32
    )


def dot(left_side, right_side):
    return jnp.dot(left_side, right_side, preferred_element_type=jnp.float32)


def low(values):
    return values.astype(jnp.bfloat16)


def norm_parts(values):
    center = values - jnp.mean(values, axis=-1, keepdims=True)
    spread = jnp.mean(center * center, axis=-1, keepdims=True)
    inverse = lax.rsqrt(spread + norm_eps)
    return center * inverse, inverse


def norm_back(cotangent, hat, inverse, gain_vec):
    scaled = cotangent * gain_vec
    return (
        scaled
        - jnp.mean(scaled, axis=-1, keepdims=True)
        - hat * jnp.mean(scaled * hat, axis=-1, keepdims=True)
    ) * inverse


def rotary_tables(positions):
    half = HEAD_DIM // 2
    exponent = jnp.arange(half, dtype=jnp.float32) * (2.0 / HEAD_DIM)
    angles = positions.astype(jnp.float32)[..., None] * jnp.exp(-math.log(10000.0) * exponent)
    return (jnp.cos(angles), jnp.sin(angles))


def rotate(values, cosine, sine):
    half = HEAD_DIM // 2
    front, back = values[..., :half], values[..., half:]
    return jnp.concatenate(
        [front * cosine - back * sine, back * cosine + front * sine], axis=-1
    )


def gather(values, axes):
    return lax.all_gather(values, axes, axis=0, tiled=True)


def scatter_sum(values, axes):
    return lax.psum_scatter(values, axes, scatter_dimension=0, tiled=True)


def gelu_parts(value):
    phi = 0.5 * lax.erfc(-value * math.sqrt(0.5))
    density = jnp.exp(-0.5 * value * value) * (1.0 / math.sqrt(2.0 * math.pi))
    return value * phi, phi + value * density


MESH = pl.DeviceIdType.MESH


class Wire:
    def __init__(self, send_sems, recv_sems):
        self.send_sems, self.recv_sems = send_sems, recv_sems
        self.keys, self.sent = {}, []

    def number(self, key):
        return self.keys.setdefault(key, len(self.keys))

    def copy(self, key, source, target, device):
        index = self.number(key)
        return pltpu.make_async_remote_copy(
            src_ref=source,
            dst_ref=target,
            send_sem=self.send_sems.at[index],
            recv_sem=self.recv_sems.at[index],
            device_id=device,
            device_id_type=MESH,
        )

    def send(self, key, source, target, device, when=None):
        copy = self.copy(key, source, target, device)
        if when is None:
            copy.start()
        else:
            pl.when(when)(copy.start)
        self.sent.append((copy, when))

    def arrive(self, key, target, device, when=None):
        copy = self.copy(key, target, target, device)
        if when is None:
            copy.wait_recv()
        else:
            pl.when(when)(copy.wait_recv)

    def drain(self):
        for copy, when in self.sent:
            if when is None:
                copy.wait_send()
            else:
                pl.when(when)(copy.wait_send)


def flip(value, bit):
    return 1 - value if bit else value


def enter(devices):
    barrier = pltpu.get_barrier_semaphore()
    for device in devices:
        pl.semaphore_signal(barrier, inc=1, device_id=device, device_id_type=MESH)
    pl.semaphore_wait(barrier, len(devices))


class Place:
    def __init__(self):
        self.zo, self.zi, self.x, self.y, self.c = (lax.axis_index(name) for name in ALL)
        self.rank = self.x * 4 + self.y * 2 + self.c
        self.unit = self.zi * 2 + self.c

    def plane(self, delta):
        dx, dy, dc = delta >> 2 & 1, delta >> 1 & 1, delta & 1
        x, y, c = flip(self.x, dx), flip(self.y, dy), flip(self.c, dc)
        return (self.zo, self.zi, x, y, c), x * 4 + y * 2 + c

    def column(self, step):
        other = lax.rem(self.unit + step + 8, 8)
        return (self.zo, other // 2, self.x, self.y, lax.rem(other, 2)), other

    def line(self, z):
        return (self.zo, z, self.x, self.y, self.c)

    def neighbours(self):
        plane = [self.plane(delta)[0] for delta in range(1, 8)]
        column = []
        for dz in range(1, 4):
            z = lax.rem(self.zi + dz, 4)
            column += [(self.zo, z, self.x, self.y, core) for core in (0, 1)]
        return plane + column


def gather_kernel(qkv_in, ffn_in, x_in, qkv_out, ffn_out, x_out, send_sems, recv_sems, own_sems):
    at = Place()
    wire = Wire(send_sems, recv_sems)
    enter(at.neighbours())
    x_side, y_side, core_side = at.plane(4)[0], at.plane(2)[0], at.plane(1)[0]
    half = x_in.shape[0] // 2

    own = [
        pltpu.make_async_copy(x_in, x_out.at[at.rank], own_sems.at[0]),
        pltpu.make_async_copy(qkv_in.at[at.rank], qkv_out.at[at.zi, at.rank], own_sems.at[1]),
        pltpu.make_async_copy(
            ffn_in.at[at.unit], ffn_out.at[:, at.zi, at.x, at.y, at.c], own_sems.at[2]
        ),
    ]
    for copy in own:
        copy.start()

    for step in (1, 7, 2, 6, 3, 5, 4):
        device, other = at.column(step)
        slot = ffn_out.at[:, at.zi, at.x, at.y, at.c]
        wire.send(("f", step), ffn_in.at[other], slot, device)
    for delta in range(1, 8):
        device, other = at.plane(delta)
        wire.send(("q", delta), qkv_in.at[other], qkv_out.at[at.zi, at.rank], device)
    wire.send("xx", x_in, x_out.at[at.rank], x_side)
    wire.send("xy", x_in, x_out.at[at.rank], y_side)
    wire.send("xc0", x_in, x_out.at[at.rank], core_side)
    for copy in own:
        copy.wait()

    def qkv_slot(z, delta):
        return qkv_out.at[jnp.clip(z, 0, 3), at.plane(delta)[1]]

    up, down = at.line(jnp.minimum(at.zi + 1, 3)), at.line(jnp.maximum(at.zi - 1, 0))

    def qkv_hop(hop, delta):
        below, above = qkv_slot(at.zi - hop, delta), qkv_slot(at.zi + hop, delta)
        if hop == 0:
            if delta:
                wire.arrive(("q", delta), below, at.plane(delta)[0])
        else:
            wire.arrive(("up", hop - 1, delta), below, down, at.zi >= hop)
            wire.arrive(("down", hop - 1, delta), above, up, at.zi <= 3 - hop)
        if hop < 3:
            wire.send(("up", hop, delta), below, below, up, (at.zi >= hop) & (at.zi < 3))
            wire.send(("down", hop, delta), above, above, down, (at.zi <= 3 - hop) & (at.zi > 0))

    def ffn_slot(step, x, y):
        source = lax.rem(at.unit - step + 8, 8)
        return ffn_out.at[:, source // 2, x, y, lax.rem(source, 2)]

    def ffn_first(step):
        slot = ffn_slot(step, at.x, at.y)
        if step:
            wire.arrive(("f", step), slot, at.column(-step)[0])
        wire.send(("fx", step), slot, slot, x_side)
        wire.send(("fy", step), slot, slot, y_side)

    def ffn_second(step, turn):
        from_x, from_y = ffn_slot(step, 1 - at.x, at.y), ffn_slot(step, at.x, 1 - at.y)
        wire.arrive(("fx", step), from_x, x_side)
        wire.arrive(("fy", step), from_y, y_side)
        if turn % 2:
            wire.send(("fd", step), from_x, from_x, y_side)
        else:
            wire.send(("fd", step), from_y, from_y, x_side)

    from_x, from_y, from_xy = (at.plane(delta)[1] for delta in (4, 2, 6))
    low_half, high_half = pl.ds(0, half), pl.ds(half, half)
    ffn_first(0)
    wire.arrive("xx", x_out.at[from_x], x_side)
    wire.send("xd0", x_out.at[from_x, low_half], x_out.at[from_x, low_half], y_side)
    wire.send("xc1", x_out.at[from_x], x_out.at[from_x], core_side)
    wire.arrive("xy", x_out.at[from_y], y_side)
    wire.send("xd1", x_out.at[from_y, high_half], x_out.at[from_y, high_half], x_side)
    wire.send("xc2", x_out.at[from_y], x_out.at[from_y], core_side)
    for delta in range(8):
        qkv_hop(0, delta)
    wire.arrive("xd0", x_out.at[from_xy, low_half], y_side)
    wire.arrive("xd1", x_out.at[from_xy, high_half], x_side)
    wire.send("xc3", x_out.at[from_xy], x_out.at[from_xy], core_side)

    steps = (1, 7, 2, 6, 3, 5, 4)
    ffn_second(0, 0)
    for turn, step in enumerate(steps):
        ffn_first(step)
        qkv_hop(1, turn)
        if turn >= 2:
            ffn_second(steps[turn - 2], turn - 2 + 1)
    qkv_hop(1, 7)
    for delta in range(8):
        qkv_hop(2, delta)
        if delta < 2:
            ffn_second(steps[5 + delta], 5 + delta + 1)
    for delta in range(8):
        qkv_hop(3, delta)
    for index, delta in enumerate((1, 5, 3, 7)):
        other = at.plane(delta)[1]
        wire.arrive("xc%d" % index, x_out.at[other], core_side)
    for step in range(8):
        wire.arrive(("fd", step), ffn_slot(step, 1 - at.x, 1 - at.y), x_side)
    wire.drain()


def reduce_kernel(
    qkv_in,
    ffn_in,
    qkv_out,
    ffn_out,
    first_in,
    second_in,
    second_sum,
    total,
    up_in,
    down_in,
    up_sum,
    down_sum,
    qkv_total,
    send_sems,
    recv_sems,
    own_sems,
):
    at = Place()
    wire = Wire(send_sems, recv_sems)
    enter(at.neighbours())
    x_side, y_side = at.plane(4)[0], at.plane(2)[0]
    steps = (4, 3, 5, 2, 6, 1, 7, 0)

    def add(*terms):
        whole = terms[0].astype(jnp.float32)
        for term in terms[1:]:
            whole = whole + term.astype(jnp.float32)
        return whole.astype(jnp.bfloat16)

    def owner(step):
        other = at.column(step)[1]
        return other // 2, lax.rem(other, 2)

    for turn, step in enumerate(steps):
        z, c = owner(step)
        if turn % 2:
            wire.send(("a", step), ffn_in.at[:, z, 1 - at.x, :, c], first_in.at[step], x_side)
        else:
            wire.send(("a", step), ffn_in.at[:, z, :, 1 - at.y, c], first_in.at[step], y_side)

    def ffn_second(step, turn):
        z, c = owner(step)
        if turn % 2:
            wire.arrive(("a", step), first_in.at[step], x_side)
            mine = ffn_in[:, z, at.x, 1 - at.y, c]
            second_sum[step] = add(mine, first_in[step, :, 1 - at.y])
            wire.send(("b", step), second_sum.at[step], second_in.at[step], y_side)
        else:
            wire.arrive(("a", step), first_in.at[step], y_side)
            mine = ffn_in[:, z, 1 - at.x, at.y, c]
            second_sum[step] = add(mine, first_in[step, :, 1 - at.x])
            wire.send(("b", step), second_sum.at[step], second_in.at[step], x_side)

    def ffn_last(step, turn):
        z, c = owner(step)
        near = at.y if turn % 2 else at.x
        wire.arrive(("b", step), second_in.at[step], x_side)
        total[step] = add(ffn_in[:, z, at.x, at.y, c], first_in[step, :, near], second_in[step])
        if step:
            wire.send(("c", step), total.at[step], ffn_out.at[at.unit], at.column(step)[0])
        else:
            pltpu.make_async_copy(total.at[0], ffn_out.at[at.unit], own_sems.at[0]).start()

    pieces = 4
    wide = 8 // pieces
    up, down = at.line(jnp.minimum(at.zi + 1, 3)), at.line(jnp.maximum(at.zi - 1, 0))

    def qkv_pass(goal, piece):
        part = pl.ds(piece * wide, wide)

        if goal > 0:

            @pl.when(at.zi < goal)
            def _():
                @pl.when(at.zi == 0)
                def _():
                    up_sum[goal, part] = qkv_in[goal, part]

                @pl.when(at.zi > 0)
                def _():
                    wire.arrive(("u", goal, piece), up_in.at[goal, part], down)
                    up_sum[goal, part] = add(qkv_in[goal, part], up_in[goal, part])

            wire.send(
                ("u", goal, piece),
                up_sum.at[goal, part],
                up_in.at[goal, part],
                up,
                at.zi < goal,
            )
        back = 3 - goal
        if back < 3:

            @pl.when(at.zi > back)
            def _():
                @pl.when(at.zi == 3)
                def _():
                    down_sum[back, part] = qkv_in[back, part]

                @pl.when(at.zi < 3)
                def _():
                    wire.arrive(("d", back, piece), down_in.at[back, part], up)
                    down_sum[back, part] = add(qkv_in[back, part], down_in[back, part])

            wire.send(
                ("d", back, piece),
                down_sum.at[back, part],
                down_in.at[back, part],
                down,
                at.zi > back,
            )

    def qkv_last(piece):
        part = pl.ds(piece * wide, wide)
        for goal in range(4):

            @pl.when(at.zi == goal)
            def _():
                terms = [qkv_in[goal, part]]
                if goal > 0:
                    wire.arrive(("u", goal, piece), up_in.at[goal, part], down)
                    terms.append(up_in[goal, part])
                if goal < 3:
                    wire.arrive(("d", goal, piece), down_in.at[goal, part], up)
                    terms.append(down_in[goal, part])
                qkv_total[part] = add(*terms)

    turn = 0
    order = [(goal, piece) for goal in (3, 2, 1) for piece in range(pieces)]
    for index, (goal, piece) in enumerate(order):
        qkv_pass(goal, piece)
        if index < 8:
            ffn_second(steps[index], index)
        if index >= 3 and index - 3 < 8:
            ffn_last(steps[index - 3], index - 3)
    for index in range(len(order) - 3, 8):
        ffn_last(steps[index], index)
    for piece in range(pieces):
        qkv_last(piece)
    own_qkv = pltpu.make_async_copy(
        qkv_total.at[at.rank], qkv_out.at[at.rank], own_sems.at[1]
    )
    own_qkv.start()
    for delta in range(1, 8):
        device, other = at.plane(delta)
        wire.send(("q", delta), qkv_total.at[other], qkv_out.at[at.rank], device)
    own_qkv.wait()
    pltpu.make_async_copy(total.at[0], ffn_out.at[at.unit], own_sems.at[0]).wait()
    for delta in range(1, 8):
        device, other = at.plane(delta)
        wire.arrive(("q", delta), qkv_out.at[other], device)
    for step in steps:
        if step:
            device, other = at.column(-step)
            wire.arrive(("c", step), ffn_out.at[other], device)
    wire.drain()


ANY = pl.BlockSpec(memory_space=pl.ANY)
VMEM = pl.BlockSpec(memory_space=pltpu.VMEM)


def comm_params(number):
    return pltpu.CompilerParams(
        collective_id=number, has_side_effects=True, vmem_limit_bytes=63 * 2**20
    )


def gather_weights(qkv_parts, ffn_parts, x_own):
    _, rows_own, qkv_width = qkv_parts.shape
    unit_width = ffn_parts.shape[-1]
    own, width = x_own.shape
    low_type = jnp.bfloat16
    return pl.pallas_call(
        gather_kernel,
        out_shape=(
            jax.ShapeDtypeStruct((4, 8, rows_own, qkv_width), low_type),
            jax.ShapeDtypeStruct((3, 4, 2, 2, 2, rows_own, unit_width), low_type),
            jax.ShapeDtypeStruct((8, own, width), low_type),
        ),
        in_specs=[VMEM] * 3,
        out_specs=(ANY,) * 3,
        scratch_shapes=[
            pltpu.SemaphoreType.DMA((100,)),
            pltpu.SemaphoreType.DMA((100,)),
            pltpu.SemaphoreType.DMA((3,)),
        ],
        compiler_params=comm_params(1),
        cost_estimate=pl.CostEstimate(
            flops=0, bytes_accessed=400_000_000, transcendentals=0
        ),
        name="gather_weights",
    )(qkv_parts, ffn_parts, x_own)


def reduce_grads(qkv_part, ffn_part):
    _, _, rows_own, qkv_width = qkv_part.shape
    unit_width = ffn_part.shape[-1]
    low_type = jnp.bfloat16
    block = (rows_own, unit_width)
    line = (4, 8, rows_own, qkv_width)
    return pl.pallas_call(
        reduce_kernel,
        out_shape=(
            jax.ShapeDtypeStruct((8, rows_own, qkv_width), low_type),
            jax.ShapeDtypeStruct((8, 3) + block, low_type),
        ),
        in_specs=[VMEM] * 2,
        out_specs=(ANY,) * 2,
        scratch_shapes=[
            pltpu.VMEM((8, 3, 2) + block, low_type),
            pltpu.VMEM((8, 3) + block, low_type),
            pltpu.VMEM((8, 3) + block, low_type),
            pltpu.VMEM((8, 3) + block, low_type),
            pltpu.VMEM(line, low_type),
            pltpu.VMEM(line, low_type),
            pltpu.VMEM(line, low_type),
            pltpu.VMEM(line, low_type),
            pltpu.VMEM(line[1:], low_type),
            pltpu.SemaphoreType.DMA((64,)),
            pltpu.SemaphoreType.DMA((64,)),
            pltpu.SemaphoreType.DMA((2,)),
        ],
        compiler_params=comm_params(2),
        cost_estimate=pl.CostEstimate(
            flops=0, bytes_accessed=400_000_000, transcendentals=0
        ),
        name="reduce_grads",
    )(qkv_part, ffn_part)


def body(
    hidden_in,
    token_marks,
    out_grad,
    qkv_weight,
    proj_weight,
    gate_weight,
    up_weight,
    down_weight,
    first_gain,
    first_shift,
    second_gain,
    second_shift,
):
    micro_count, _, pos_count, width = hidden_in.shape
    rows_own = qkv_weight.shape[0]
    units = gate_weight.shape[1]
    head_ways = math.prod(lax.axis_size(name) for name in HEAD_AXES)
    unit_ways = math.prod(lax.axis_size(name) for name in UNIT_AXES)
    chunk_count = lax.axis_size("y") * lax.axis_size("c")
    row_length = pos_count * chunk_count
    x_size = lax.axis_size("x")
    own = micro_count * pos_count
    head_width = width // head_ways
    heads_here = head_width // HEAD_DIM
    unit_width = -(-units // (unit_ways * LANES)) * LANES
    unit_pad = unit_width * unit_ways - units

    small = jnp.stack([first_gain, first_shift, second_gain, second_shift])[None]
    small_all = gather(small, ALL).transpose(1, 0, 2).reshape(4, width).astype(jnp.float32)
    gain_one, shift_one, gain_two, shift_two = (small_all[i][None] for i in range(4))
    marks = gather(token_marks.reshape(1, micro_count, pos_count, 3), HEAD_AXES)

    qkv_parts = (
        qkv_weight.reshape(rows_own, 3, head_ways, head_width)
        .transpose(2, 0, 1, 3)
        .reshape(head_ways, rows_own, 3 * head_width)
    )
    proj_full = gather(proj_weight, ALL)

    sizes = [lax.axis_size(name) for name in ALL]

    ffn = jnp.stack([gate_weight, up_weight, down_weight])
    ffn = jnp.pad(ffn, ((0, 0), (0, 0), (0, unit_pad)))
    ffn = ffn.reshape(3, rows_own, unit_ways, unit_width).transpose(2, 0, 1, 3)

    x_own = hidden_in.reshape(own, width)
    qkv_here, ffn, x_all = gather_weights(qkv_parts, ffn, x_own)
    qkv_here = qkv_here.reshape(-1, 3 * head_width)
    ffn = ffn.reshape(3, -1, unit_width)
    x_all = x_all.reshape(-1, width)
    if sizes[0] > 1:
        qkv_here = gather(qkv_here, "zo")
        ffn = lax.all_gather(ffn, "zo", axis=1, tiled=True)
    gate_here, up_here, down_here = ffn[0], ffn[1], ffn[2]

    mixed = dot(x_all, qkv_here)

    def to_rows(values):
        inner = values.shape[1:]
        values = values.reshape((x_size, chunk_count, micro_count, pos_count) + inner)
        return jnp.swapaxes(values, 1, 2).reshape((x_size * micro_count, row_length) + inner)

    def from_rows(values):
        inner = values.shape[2:]
        values = values.reshape((x_size, micro_count, chunk_count, pos_count) + inner)
        return jnp.swapaxes(values, 1, 2).reshape((head_ways * own,) + inner)

    row_marks = to_rows(marks.reshape(head_ways * own, 3))
    cosine, sine = rotary_tables(row_marks[..., 2])
    cosine, sine = cosine[:, :, None, :], sine[:, :, None, :]
    mixed = to_rows(mixed).reshape(x_size * micro_count, row_length, 3, heads_here, HEAD_DIM)
    queries = low(rotate(mixed[:, :, 0], cosine, sine))
    key_rows = low(rotate(mixed[:, :, 1], cosine, sine))
    value_rows = low(mixed[:, :, 2])
    place = jnp.arange(row_length, dtype=jnp.int32)
    allowed = (row_marks[:, :, None, 0] == row_marks[:, None, :, 0]) & (
        (place[None, None, :] <= place[None, :, None])
        | (place[None, :] < row_marks[:, :, 1])[:, None, :]
    )
    score_scale = 1.0 / math.sqrt(HEAD_DIM)

    def pair(spec, left_side, right_side):
        return jnp.einsum(spec, left_side, right_side, preferred_element_type=jnp.float32)

    scores = pair("rqhd,rkhd->rhqk", queries, key_rows) * score_scale
    scores = jnp.where(allowed[:, None], scores, masked_score)
    exp_scores = jnp.exp(scores - jnp.max(scores, axis=-1, keepdims=True))
    probs = exp_scores / jnp.sum(exp_scores, axis=-1, keepdims=True)
    probs_low = low(probs)
    context = low(pair("rhqk,rkhd->rqhd", probs_low, value_rows))

    def heads_to_tokens(values):
        values = values.reshape(head_ways, own, head_width)
        values = lax.all_to_all(values, HEAD_AXES, split_axis=0, concat_axis=0, tiled=True)
        return values.transpose(1, 0, 2).reshape(own, width)

    def tokens_to_heads(values):
        values = values.reshape(own, head_ways, head_width).transpose(1, 0, 2)
        values = lax.all_to_all(values, HEAD_AXES, split_axis=0, concat_axis=0, tiled=True)
        return values.reshape(head_ways * own, head_width)

    context_own = heads_to_tokens(from_rows(context))
    first_sum = deep_alpha * x_own.astype(jnp.float32) + dot(context_own, proj_full)
    hat_one, inverse_one = norm_parts(first_sum)
    normed = low(hat_one * gain_one + shift_one)

    normed_all = gather(normed, UNIT_AXES)
    gate_val = dot(normed_all, gate_here)
    up_val = dot(normed_all, up_here)
    gelu_val, gelu_slope = gelu_parts(gate_val)
    active = low(gelu_val * up_val)
    down_val = scatter_sum(low(contract_last(active, down_here)), UNIT_AXES)
    second_sum = deep_alpha * normed.astype(jnp.float32) + down_val.astype(jnp.float32)
    hat_two, inverse_two = norm_parts(second_sum)
    layer_rows = low(hat_two * gain_two + shift_two)

    grad_own = out_grad.reshape(own, width).astype(jnp.float32)
    gain_two_grad = jnp.sum(grad_own * hat_two, axis=0)
    shift_two_grad = jnp.sum(grad_own, axis=0)
    d_second = norm_back(grad_own, hat_two, inverse_two, gain_two)
    down_low = gather(low(d_second), UNIT_AXES)
    d_active = dot(down_low, down_here)
    gate_low = low(d_active * up_val * gelu_slope)
    up_low = low(d_active * gelu_val)
    d_normed_part = low(contract_last(gate_low, gate_here) + contract_last(up_low, up_here))
    d_normed = deep_alpha * d_second + scatter_sum(d_normed_part, UNIT_AXES).astype(jnp.float32)

    ffn_part = jnp.stack(
        [
            low(contract_first(normed_all, gate_low)),
            low(contract_first(normed_all, up_low)),
            low(contract_first(down_low, active)),
        ]
    )

    gain_one_grad = jnp.sum(d_normed * hat_one, axis=0)
    shift_one_grad = jnp.sum(d_normed, axis=0)
    d_first = norm_back(d_normed, hat_one, inverse_one, gain_one)
    branch_low = low(d_first)
    small_grads = jnp.stack([gain_one_grad, shift_one_grad, gain_two_grad, shift_two_grad])
    place_own = lax.axis_index(ALL) * rows_own
    small_grads = gather(small_grads[None], ALL)
    small_grads = lax.dynamic_slice_in_dim(small_grads, place_own, rows_own, axis=2)
    small_grads = jnp.sum(small_grads, axis=0)

    proj_grad = scatter_sum(low(contract_first(context_own, branch_low)), ALL).astype(jnp.float32)
    d_context = to_rows(tokens_to_heads(low(contract_last(branch_low, proj_full))))
    d_context = d_context.reshape(x_size * micro_count, row_length, heads_here, HEAD_DIM)
    d_probs = pair("rqhd,rkhd->rhqk", d_context, value_rows)
    d_scores = low(probs * (d_probs - jnp.sum(probs * d_probs, axis=-1, keepdims=True)))
    d_query = pair("rhqk,rkhd->rqhd", d_scores, key_rows) * score_scale
    d_keys = pair("rhqk,rqhd->rkhd", d_scores, queries) * score_scale
    d_values = pair("rhqk,rqhd->rkhd", probs_low, d_context)
    d_mixed = low(
        jnp.stack(
            [rotate(d_query, cosine, -sine), rotate(d_keys, cosine, -sine), d_values], axis=2
        )
    )
    d_mixed = from_rows(d_mixed.reshape(x_size * micro_count, row_length, 3 * head_width))
    d_input = scatter_sum(low(contract_last(d_mixed, qkv_here)), HEAD_AXES).astype(jnp.float32)
    d_input = deep_alpha * d_first + d_input

    qkv_part = low(contract_first(x_all, d_mixed))
    if sizes[0] > 1:
        qkv_part = scatter_sum(qkv_part, "zo")
        ffn_part = lax.psum_scatter(ffn_part, "zo", scatter_dimension=1, tiled=True)
    qkv_part, ffn_part = reduce_grads(
        qkv_part.reshape(4, 8, rows_own, 3 * head_width),
        ffn_part.reshape(3, 4, 2, 2, 2, rows_own, unit_width),
    )
    qkv_grad = (
        qkv_part.reshape(head_ways, rows_own, 3, head_width)
        .transpose(1, 2, 0, 3)
        .reshape(rows_own, 3 * width)
        .astype(jnp.float32)
    )
    ffn_part = ffn_part.transpose(1, 2, 0, 3).reshape(3, rows_own, unit_ways * unit_width)
    gate_grad, up_grad, down_grad = (
        ffn_part[index, :, :units].astype(jnp.float32) for index in range(3)
    )
    return (
        layer_rows.reshape(micro_count, 1, pos_count, width),
        low(d_input).reshape(micro_count, 1, pos_count, width),
        qkv_grad,
        proj_grad,
        gate_grad,
        up_grad,
        down_grad,
        small_grads[0],
        small_grads[1],
        small_grads[2],
        small_grads[3],
    )


def solution(mesh):
    seq_size, ctx_size = mesh.shape["seq"], mesh.shape["ctx"]
    cores, x_size = 2, 2
    zi_size = math.gcd(4, seq_size // x_size)
    zo_size = seq_size // (x_size * zi_size)
    devices = np.asarray(mesh.devices).reshape(
        zo_size, zi_size, x_size, ctx_size // cores, cores
    )
    inner = Mesh(devices, ALL)
    tokens = P(None, ("zo", "zi", "x"), ("y", "c"), None)
    matrix = P(ALL, None)
    vector = P(ALL)
    return jax.shard_map(
        body,
        mesh=inner,
        in_specs=(tokens,) * 3 + (matrix,) * 5 + (vector,) * 4,
        out_specs=(tokens,) * 2 + (matrix,) * 5 + (vector,) * 4,
        check_vma=False,
    )
```

```python
import math

import jax
import jax.numpy as jnp
import numpy as np
from jax import lax
from jax.experimental import pallas as pl
from jax.experimental.pallas import tpu as pltpu
from jax.sharding import Mesh
from jax.sharding import PartitionSpec as P

HEAD_DIM = 128
LANES = 128

deep_alpha = 48.0**0.25
norm_eps = 1e-05
masked_score = -1e30

ALL = ("zo", "zi", "x", "y", "c")
HEAD_AXES = ("x", "y", "c")
UNIT_AXES = ("zi", "c")
HEAD_COPIES = ("zo", "zi")
UNIT_COPIES = ("zo", "x", "y")


def contract_last(left_side, right_side):
    return lax.dot_general(
        left_side, right_side, (((1,), (1,)), ((), ())), preferred_element_type=jnp.float32
    )


def contract_first(left_side, right_side):
    return lax.dot_general(
        left_side, right_side, (((0,), (0,)), ((), ())), preferred_element_type=jnp.float32
    )


def dot(left_side, right_side):
    return jnp.dot(left_side, right_side, preferred_element_type=jnp.float32)


def low(values):
    return values.astype(jnp.bfloat16)


def norm_parts(values):
    center = values - jnp.mean(values, axis=-1, keepdims=True)
    spread = jnp.mean(center * center, axis=-1, keepdims=True)
    inverse = lax.rsqrt(spread + norm_eps)
    return center * inverse, inverse


def norm_back(cotangent, hat, inverse, gain_vec):
    scaled = cotangent * gain_vec
    return (
        scaled
        - jnp.mean(scaled, axis=-1, keepdims=True)
        - hat * jnp.mean(scaled * hat, axis=-1, keepdims=True)
    ) * inverse


def rotary_tables(positions):
    half = HEAD_DIM // 2
    exponent = jnp.arange(half, dtype=jnp.float32) * (2.0 / HEAD_DIM)
    angles = positions.astype(jnp.float32)[..., None] * jnp.exp(-math.log(10000.0) * exponent)
    return (jnp.cos(angles), jnp.sin(angles))


def rotate(values, cosine, sine):
    half = HEAD_DIM // 2
    front, back = values[..., :half], values[..., half:]
    return jnp.concatenate(
        [front * cosine - back * sine, back * cosine + front * sine], axis=-1
    )


def gather(values, axes):
    return lax.all_gather(values, axes, axis=0, tiled=True)


def scatter_sum(values, axes):
    return lax.psum_scatter(values, axes, scatter_dimension=0, tiled=True)


def gelu_parts(value):
    phi = 0.5 * lax.erfc(-value * math.sqrt(0.5))
    density = jnp.exp(-0.5 * value * value) * (1.0 / math.sqrt(2.0 * math.pi))
    return value * phi, phi + value * density


MESH = pl.DeviceIdType.MESH


class Wire:
    def __init__(self, send_sems, recv_sems):
        self.send_sems, self.recv_sems = send_sems, recv_sems
        self.keys, self.sent = {}, []

    def number(self, key, span=1):
        if key not in self.keys:
            self.keys[key] = sum(size for _, size in self.keys.values()), span
        return self.keys[key][0]

    def copy(self, key, source, target, device, slot=0, span=1, recv=None):
        send = self.number(key, span)
        receive = send if recv is None else self.number(recv)
        return pltpu.make_async_remote_copy(
            src_ref=source,
            dst_ref=target,
            send_sem=self.send_sems.at[send],
            recv_sem=self.recv_sems.at[receive + slot],
            device_id=device,
            device_id_type=MESH,
        )

    def send(self, key, source, target, device, when=None, recv=None):
        copy = self.copy(key, source, target, device, recv=recv)
        if when is None:
            copy.start()
        else:
            pl.when(when)(copy.start)
        self.sent.append((copy, when))

    def send_to_slot(self, key, source, target, device, slot, span, when):
        copy = self.copy(key, source, target, device, slot, span)
        pl.when(when)(copy.start)
        self.sent.append((copy, when))

    def arrive(self, key, target, device, when=None):
        copy = self.copy(key, target, target, device)
        if when is None:
            copy.wait_recv()
        else:
            pl.when(when)(copy.wait_recv)

    def arrive_slot(self, key, target, device, slot, span, when):
        pl.when(when)(self.copy(key, target, target, device, slot, span).wait_recv)

    def drain(self):
        for copy, when in self.sent:
            if when is None:
                copy.wait_send()
            else:
                pl.when(when)(copy.wait_send)


def flip(value, bit):
    return 1 - value if bit else value


def enter(devices):
    barrier = pltpu.get_barrier_semaphore()
    for device in devices:
        pl.semaphore_signal(barrier, inc=1, device_id=device, device_id_type=MESH)
    pl.semaphore_wait(barrier, len(devices))


class Place:
    def __init__(self):
        self.zo, self.zi, self.x, self.y, self.c = (lax.axis_index(name) for name in ALL)
        self.rank = self.x * 4 + self.y * 2 + self.c
        self.unit = self.zi * 2 + self.c

    def plane(self, delta):
        dx, dy, dc = delta >> 2 & 1, delta >> 1 & 1, delta & 1
        x, y, c = flip(self.x, dx), flip(self.y, dy), flip(self.c, dc)
        return (self.zo, self.zi, x, y, c), x * 4 + y * 2 + c

    def column(self, step):
        other = lax.rem(self.unit + step + 8, 8)
        return (self.zo, other // 2, self.x, self.y, lax.rem(other, 2)), other

    def line(self, z):
        return (self.zo, z, self.x, self.y, self.c)

    def neighbours(self):
        plane = [self.plane(delta)[0] for delta in range(1, 8)]
        column = []
        for dz in range(1, 4):
            z = lax.rem(self.zi + dz, 4)
            column += [(self.zo, z, self.x, self.y, core) for core in (0, 1)]
        return plane + column


def gather_kernel(
    qkv_in,
    ffn_in,
    proj_in,
    x_in,
    small_in,
    qkv_out,
    ffn_out,
    proj_out,
    x_out,
    small_out,
    send_sems,
    recv_sems,
    own_sems,
):
    at = Place()
    wire = Wire(send_sems, recv_sems)
    enter(at.neighbours())
    x_side, y_side, core_side = at.plane(4)[0], at.plane(2)[0], at.plane(1)[0]
    half = x_in.shape[0] // 2

    own = [
        pltpu.make_async_copy(x_in, x_out.at[at.rank], own_sems.at[0]),
        pltpu.make_async_copy(qkv_in.at[at.rank], qkv_out.at[at.zi, at.rank], own_sems.at[1]),
        pltpu.make_async_copy(
            ffn_in.at[at.unit], ffn_out.at[:, at.zi, at.x, at.y, at.c], own_sems.at[2]
        ),
        pltpu.make_async_copy(small_in, small_out.at[at.zi, at.rank], own_sems.at[3]),
    ]
    for copy in own:
        copy.start()

    chunk = at.y * 2 + at.c
    holder = at.zi * 2 + at.x
    proj_home = at.rank // 2
    proj_first = at.rank == holder
    proj_own = pltpu.make_async_copy(proj_in, proj_out.at[chunk], own_sems.at[4])
    pl.when(proj_first)(proj_own.start)

    def small_first():
        for delta in range(1, 8):
            device, _ = at.plane(delta)
            slot = small_out.at[at.zi, at.rank]
            wire.send(("s", delta), small_in, slot, device)

    small_first()

    for step in (1, 7, 2, 6, 3, 5, 4):
        device, other = at.column(step)
        slot = ffn_out.at[:, at.zi, at.x, at.y, at.c]
        wire.send(("f", step), ffn_in.at[other], slot, device)
    for delta in range(1, 8):
        device, other = at.plane(delta)
        wire.send(("q", delta), qkv_in.at[other], qkv_out.at[at.zi, at.rank], device)
    holder_device = (at.zo, at.zi, holder // 4, lax.rem(holder // 2, 2), lax.rem(holder, 2))
    wire.send_to_slot("p", proj_in, proj_out.at[chunk], holder_device, chunk, 4, at.rank != holder)
    wire.send("xx", x_in, x_out.at[at.rank], x_side)
    wire.send("xy", x_in, x_out.at[at.rank], y_side)
    wire.send("xc0", x_in, x_out.at[at.rank], core_side)
    for copy in own:
        copy.wait()
    pl.when(proj_first)(proj_own.wait)

    def small_second():
        for delta in range(1, 8):
            device, other = at.plane(delta)
            wire.arrive(("s", delta), small_out.at[at.zi, other], device)
        for dz in range(1, 4):
            device = at.line(lax.rem(at.zi + dz, 4))
            wire.send(("t", dz), small_out.at[at.zi], small_out.at[at.zi], device)

    def small_last():
        for dz in range(1, 4):
            z = lax.rem(at.zi - dz + 4, 4)
            wire.arrive(("t", dz), small_out.at[z], at.line(z))

    def proj_start():
        for slot in range(4):
            source = (at.zo, at.zi, lax.rem(at.rank, 2), slot // 2, slot % 2)
            mine = (at.zi == proj_home) & ((chunk != slot) | (at.rank != holder))
            wire.arrive_slot("p", proj_out.at[slot], source, slot, 4, mine)
        wire.send("pu0", proj_out, proj_out, up, (at.zi == proj_home) & (at.zi < 3))
        wire.send("pd0", proj_out, proj_out, down, (at.zi == proj_home) & (at.zi > 0))

    def proj_relay():
        above, below = at.zi > proj_home, at.zi < proj_home
        wire.arrive("pu0", proj_out, down, above)
        wire.arrive("pd0", proj_out, up, below)
        wire.send("pu1", proj_out, proj_out, up, above & (at.zi < 3), recv="pu0")
        wire.send("pd1", proj_out, proj_out, down, below & (at.zi > 0), recv="pd0")

    def qkv_slot(z, delta):
        return qkv_out.at[jnp.clip(z, 0, 3), at.plane(delta)[1]]

    up, down = at.line(jnp.minimum(at.zi + 1, 3)), at.line(jnp.maximum(at.zi - 1, 0))

    def qkv_hop(hop, delta):
        below, above = qkv_slot(at.zi - hop, delta), qkv_slot(at.zi + hop, delta)
        if hop == 0:
            if delta:
                wire.arrive(("q", delta), below, at.plane(delta)[0])
        else:
            wire.arrive(("up", hop - 1, delta), below, down, at.zi >= hop)
            wire.arrive(("down", hop - 1, delta), above, up, at.zi <= 3 - hop)
        if hop < 3:
            wire.send(("up", hop, delta), below, below, up, (at.zi >= hop) & (at.zi < 3))
            wire.send(("down", hop, delta), above, above, down, (at.zi <= 3 - hop) & (at.zi > 0))

    def ffn_slot(step, x, y):
        source = lax.rem(at.unit - step + 8, 8)
        return ffn_out.at[:, source // 2, x, y, lax.rem(source, 2)]

    def ffn_first(step):
        slot = ffn_slot(step, at.x, at.y)
        if step:
            wire.arrive(("f", step), slot, at.column(-step)[0])
        wire.send(("fx", step), slot, slot, x_side)
        wire.send(("fy", step), slot, slot, y_side)

    def ffn_second(step, turn):
        from_x, from_y = ffn_slot(step, 1 - at.x, at.y), ffn_slot(step, at.x, 1 - at.y)
        wire.arrive(("fx", step), from_x, x_side)
        wire.arrive(("fy", step), from_y, y_side)
        if turn % 2:
            wire.send(("fd", step), from_x, from_x, y_side)
        else:
            wire.send(("fd", step), from_y, from_y, x_side)

    from_x, from_y, from_xy = (at.plane(delta)[1] for delta in (4, 2, 6))
    low_half, high_half = pl.ds(0, half), pl.ds(half, half)
    ffn_first(0)
    wire.arrive("xx", x_out.at[from_x], x_side)
    wire.send("xd0", x_out.at[from_x, low_half], x_out.at[from_x, low_half], y_side)
    wire.send("xc1", x_out.at[from_x], x_out.at[from_x], core_side)
    wire.arrive("xy", x_out.at[from_y], y_side)
    wire.send("xd1", x_out.at[from_y, high_half], x_out.at[from_y, high_half], x_side)
    wire.send("xc2", x_out.at[from_y], x_out.at[from_y], core_side)
    small_second()
    for delta in range(8):
        qkv_hop(0, delta)
    proj_start()
    wire.arrive("xd0", x_out.at[from_xy, low_half], y_side)
    wire.arrive("xd1", x_out.at[from_xy, high_half], x_side)
    wire.send("xc3", x_out.at[from_xy], x_out.at[from_xy], core_side)

    steps = (1, 7, 2, 6, 3, 5, 4)
    ffn_second(0, 0)
    for turn, step in enumerate(steps):
        ffn_first(step)
        qkv_hop(1, turn)
        if turn >= 2:
            ffn_second(steps[turn - 2], turn - 2 + 1)
    qkv_hop(1, 7)
    proj_relay()
    for delta in range(8):
        qkv_hop(2, delta)
        if delta < 2:
            ffn_second(steps[5 + delta], 5 + delta + 1)
    for delta in range(8):
        qkv_hop(3, delta)
    for index, delta in enumerate((1, 5, 3, 7)):
        other = at.plane(delta)[1]
        wire.arrive("xc%d" % index, x_out.at[other], core_side)
    for step in range(8):
        wire.arrive(("fd", step), ffn_slot(step, 1 - at.x, 1 - at.y), x_side)
    small_last()
    wire.drain()


def reduce_kernel(
    qkv_in,
    ffn_in,
    proj_in,
    small_in,
    qkv_out,
    ffn_out,
    proj_out,
    small_out,
    proj_below,
    proj_above,
    proj_sum,
    small_plane,
    small_mid,
    small_line,
    first_in,
    second_in,
    second_sum,
    total,
    up_in,
    down_in,
    up_sum,
    down_sum,
    qkv_total,
    send_sems,
    recv_sems,
    own_sems,
):
    at = Place()
    wire = Wire(send_sems, recv_sems)
    enter(at.neighbours())
    x_side, y_side = at.plane(4)[0], at.plane(2)[0]
    steps = (4, 3, 5, 2, 6, 1, 7, 0)

    def add(*terms):
        whole = terms[0].astype(jnp.float32)
        for term in terms[1:]:
            whole = whole + term.astype(jnp.float32)
        return whole.astype(jnp.bfloat16)

    def owner(step):
        other = at.column(step)[1]
        return other // 2, lax.rem(other, 2)

    for delta in range(1, 8):
        device, other = at.plane(delta)
        wire.send(("s", delta), small_in.at[other], small_plane.at[at.rank], device)

    def small_second():
        whole = small_in[at.rank]
        for delta in range(1, 8):
            device, other = at.plane(delta)
            wire.arrive(("s", delta), small_plane.at[other], device)
            whole = whole + small_plane[other]
        small_mid[...] = whole
        for dz in range(1, 4):
            z = lax.rem(at.zi + dz, 4)
            wire.send(("t", dz), small_mid.at[z], small_line.at[at.zi], at.line(z))

    def small_last():
        whole = small_mid[at.zi]
        for dz in range(1, 4):
            z = lax.rem(at.zi - dz + 4, 4)
            wire.arrive(("t", dz), small_line.at[z], at.line(z))
            whole = whole + small_line[z]
        small_out[...] = whole

    for turn, step in enumerate(steps):
        z, c = owner(step)
        if turn % 2:
            wire.send(("a", step), ffn_in.at[:, z, 1 - at.x, :, c], first_in.at[step], x_side)
        else:
            wire.send(("a", step), ffn_in.at[:, z, :, 1 - at.y, c], first_in.at[step], y_side)

    def ffn_second(step, turn):
        z, c = owner(step)
        if turn % 2:
            wire.arrive(("a", step), first_in.at[step], x_side)
            mine = ffn_in[:, z, at.x, 1 - at.y, c]
            second_sum[step] = add(mine, first_in[step, :, 1 - at.y])
            wire.send(("b", step), second_sum.at[step], second_in.at[step], y_side)
        else:
            wire.arrive(("a", step), first_in.at[step], y_side)
            mine = ffn_in[:, z, 1 - at.x, at.y, c]
            second_sum[step] = add(mine, first_in[step, :, 1 - at.x])
            wire.send(("b", step), second_sum.at[step], second_in.at[step], x_side)

    def ffn_last(step, turn):
        z, c = owner(step)
        near = at.y if turn % 2 else at.x
        wire.arrive(("b", step), second_in.at[step], x_side)
        total[step] = add(ffn_in[:, z, at.x, at.y, c], first_in[step, :, near], second_in[step])
        if step:
            wire.send(("c", step), total.at[step], ffn_out.at[at.unit], at.column(step)[0])
        else:
            pltpu.make_async_copy(total.at[0], ffn_out.at[at.unit], own_sems.at[0]).start()

    pieces = 4
    wide = 8 // pieces
    up, down = at.line(jnp.minimum(at.zi + 1, 3)), at.line(jnp.maximum(at.zi - 1, 0))

    def qkv_pass(goal, piece):
        part = pl.ds(piece * wide, wide)

        if goal > 0:

            @pl.when(at.zi < goal)
            def _():
                @pl.when(at.zi == 0)
                def _():
                    up_sum[goal, part] = qkv_in[goal, part]

                @pl.when(at.zi > 0)
                def _():
                    wire.arrive(("u", goal, piece), up_in.at[goal, part], down)
                    up_sum[goal, part] = add(qkv_in[goal, part], up_in[goal, part])

            wire.send(
                ("u", goal, piece),
                up_sum.at[goal, part],
                up_in.at[goal, part],
                up,
                at.zi < goal,
            )
        back = 3 - goal
        if back < 3:

            @pl.when(at.zi > back)
            def _():
                @pl.when(at.zi == 3)
                def _():
                    down_sum[back, part] = qkv_in[back, part]

                @pl.when(at.zi < 3)
                def _():
                    wire.arrive(("d", back, piece), down_in.at[back, part], up)
                    down_sum[back, part] = add(qkv_in[back, part], down_in[back, part])

            wire.send(
                ("d", back, piece),
                down_sum.at[back, part],
                down_in.at[back, part],
                down,
                at.zi > back,
            )

    proj_home = at.rank // 2

    def each_rows(step, count, function):
        @pl.loop(0, count // step)
        def _(index):
            function(pl.ds(pl.multiple_of(index * step, step), step))

    def proj_add(out, *terms):
        for slot in range(4):

            def rows(part):
                out[slot, part] = add(*(term[slot, part] for term in terms))

            each_rows(16, proj_in.shape[1], rows)

    def proj_pass():
        ends = (at.zi == 0) | (at.zi == 3)
        below, above = at.zi < proj_home, at.zi > proj_home
        wire.send("pu0", proj_in, proj_below, up, below & ends)
        wire.send("pd0", proj_in, proj_above, down, above & ends)

    def proj_climb():
        below, above = at.zi < proj_home, at.zi > proj_home

        def climb():
            wire.arrive("pu0", proj_below, down)
            proj_add(proj_sum, proj_in, proj_below)

        def descend():
            wire.arrive("pd0", proj_above, up)
            proj_add(proj_sum, proj_in, proj_above)

        pl.when(below & (at.zi > 0))(climb)
        pl.when(above & (at.zi < 3))(descend)
        wire.send("pu1", proj_sum, proj_below, up, below & (at.zi > 0), recv="pu0")
        wire.send("pd1", proj_sum, proj_above, down, above & (at.zi < 3), recv="pd0")

    holder = at.zi * 2 + at.x
    chunk = at.y * 2 + at.c
    holder_device = (at.zo, at.zi, holder // 4, lax.rem(holder // 2, 2), lax.rem(holder, 2))

    def proj_last():
        home = at.zi == proj_home

        def first():
            wire.arrive("pu0", proj_below, down)
            proj_add(proj_sum, proj_in, proj_below)

        def only():
            wire.arrive("pd0", proj_above, up)
            proj_add(proj_sum, proj_in, proj_above)

        def both():
            wire.arrive("pd0", proj_above, up)
            proj_add(proj_sum, proj_sum, proj_above)

        pl.when(home & (at.zi > 0))(first)
        pl.when(home & (at.zi == 0))(only)
        pl.when(home & (at.zi > 0) & (at.zi < 3))(both)
        for slot in range(4):
            target = (at.zo, at.zi, lax.rem(at.rank, 2), slot // 2, slot % 2)
            other = (chunk != slot) | (at.rank != holder)
            wire.send(("o", slot), proj_sum.at[slot], proj_out, target, home & other, recv="o")
        own = pltpu.make_async_copy(proj_sum.at[chunk], proj_out, own_sems.at[2])
        pl.when(home & (at.rank == holder))(own.start)
        pl.when(home & (at.rank == holder))(own.wait)

    def qkv_last(piece):
        part = pl.ds(piece * wide, wide)
        for goal in range(4):

            @pl.when(at.zi == goal)
            def _():
                terms = [qkv_in[goal, part]]
                if goal > 0:
                    wire.arrive(("u", goal, piece), up_in.at[goal, part], down)
                    terms.append(up_in[goal, part])
                if goal < 3:
                    wire.arrive(("d", goal, piece), down_in.at[goal, part], up)
                    terms.append(down_in[goal, part])
                qkv_total[part] = add(*terms)

    proj_pass()
    order = [(goal, piece) for goal in (3, 2, 1) for piece in range(pieces)]
    for index, (goal, piece) in enumerate(order):
        qkv_pass(goal, piece)
        if index == 4:
            proj_climb()
        if index < 8:
            ffn_second(steps[index], index)
        if index >= 3 and index - 3 < 8:
            ffn_last(steps[index - 3], index - 3)
    for index in range(len(order) - 3, 8):
        ffn_last(steps[index], index)
    small_second()
    proj_last()
    for piece in range(pieces):
        qkv_last(piece)
    own_qkv = pltpu.make_async_copy(
        qkv_total.at[at.rank], qkv_out.at[at.rank], own_sems.at[1]
    )
    own_qkv.start()
    for delta in range(1, 8):
        device, other = at.plane(delta)
        wire.send(("q", delta), qkv_total.at[other], qkv_out.at[at.rank], device)
    own_qkv.wait()
    pltpu.make_async_copy(total.at[0], ffn_out.at[at.unit], own_sems.at[0]).wait()
    for delta in range(1, 8):
        device, other = at.plane(delta)
        wire.arrive(("q", delta), qkv_out.at[other], device)
    for step in steps:
        if step:
            device, other = at.column(-step)
            wire.arrive(("c", step), ffn_out.at[other], device)
    small_last()
    wire.arrive("o", proj_out, holder_device, at.rank != holder)
    wire.drain()


ANY = pl.BlockSpec(memory_space=pl.ANY)
VMEM = pl.BlockSpec(memory_space=pltpu.VMEM)


def comm_params(number):
    return pltpu.CompilerParams(
        collective_id=number, has_side_effects=True, vmem_limit_bytes=63 * 2**20
    )


def gather_weights(qkv_parts, ffn_parts, proj_own, x_own, small):
    _, rows_own, qkv_width = qkv_parts.shape
    unit_width = ffn_parts.shape[-1]
    own, width = x_own.shape
    low_type = jnp.bfloat16
    return pl.pallas_call(
        gather_kernel,
        out_shape=(
            jax.ShapeDtypeStruct((4, 8, rows_own, qkv_width), low_type),
            jax.ShapeDtypeStruct((3, 4, 2, 2, 2, rows_own, unit_width), low_type),
            jax.ShapeDtypeStruct((4, rows_own, width), low_type),
            jax.ShapeDtypeStruct((8, own, width), low_type),
            jax.ShapeDtypeStruct((4, 8) + small.shape, small.dtype),
        ),
        in_specs=[VMEM] * 5,
        out_specs=(ANY,) * 5,
        scratch_shapes=[
            pltpu.SemaphoreType.DMA((128,)),
            pltpu.SemaphoreType.DMA((128,)),
            pltpu.SemaphoreType.DMA((5,)),
        ],
        compiler_params=comm_params(1),
        cost_estimate=pl.CostEstimate(
            flops=0, bytes_accessed=400_000_000, transcendentals=0
        ),
        name="gather_weights",
    )(qkv_parts, ffn_parts, proj_own, x_own, small)


def reduce_grads(qkv_part, ffn_part, proj_part, small_part):
    _, _, rows_own, qkv_width = qkv_part.shape
    unit_width = ffn_part.shape[-1]
    width = proj_part.shape[-1]
    low_type = jnp.bfloat16
    block = (rows_own, unit_width)
    line = (4, 8, rows_own, qkv_width)
    small_shape = small_part.shape[1:]
    return pl.pallas_call(
        reduce_kernel,
        out_shape=(
            jax.ShapeDtypeStruct((8, rows_own, qkv_width), low_type),
            jax.ShapeDtypeStruct((8, 3) + block, low_type),
            jax.ShapeDtypeStruct((rows_own, width), low_type),
            jax.ShapeDtypeStruct(small_shape[1:], small_part.dtype),
        ),
        in_specs=[VMEM] * 4,
        out_specs=(ANY,) * 3 + (VMEM,),
        scratch_shapes=[
            pltpu.VMEM((4, rows_own, width), low_type),
            pltpu.VMEM((4, rows_own, width), low_type),
            pltpu.VMEM((4, rows_own, width), low_type),
            pltpu.VMEM(small_part.shape, small_part.dtype),
            pltpu.VMEM(small_shape, small_part.dtype),
            pltpu.VMEM(small_shape, small_part.dtype),
            pltpu.VMEM((8, 3, 2) + block, low_type),
            pltpu.VMEM((8, 3) + block, low_type),
            pltpu.VMEM((8, 3) + block, low_type),
            pltpu.VMEM((8, 3) + block, low_type),
            pltpu.VMEM(line, low_type),
            pltpu.VMEM(line, low_type),
            pltpu.VMEM(line, low_type),
            pltpu.VMEM(line, low_type),
            pltpu.VMEM(line[1:], low_type),
            pltpu.SemaphoreType.DMA((96,)),
            pltpu.SemaphoreType.DMA((96,)),
            pltpu.SemaphoreType.DMA((3,)),
        ],
        compiler_params=comm_params(2),
        cost_estimate=pl.CostEstimate(
            flops=0, bytes_accessed=400_000_000, transcendentals=0
        ),
        name="reduce_grads",
    )(qkv_part, ffn_part, proj_part, small_part)


def add_rows(out, *terms):
    step = 16

    @pl.loop(0, out.shape[0] // step)
    def _(index):
        part = pl.ds(pl.multiple_of(index * step, step), step)
        whole = terms[0][part].astype(jnp.float32)
        for term in terms[1:]:
            whole = whole + term[part].astype(jnp.float32)
        out[part] = whole.astype(out.dtype)


def plane_scatter_kernel(part, out, core_in, core_sum, side_in, side_sum, last_in, ss, rs):
    at = Place()
    wire = Wire(ss, rs)
    x_side, y_side, core_side = at.plane(4)[0], at.plane(2)[0], at.plane(1)[0]
    enter([x_side, y_side, core_side])
    half = out.shape[1] // 2
    halves = (pl.ds(0, half), pl.ds(half, half))
    order = ((1, 1), (1, 0), (0, 1), (0, 0))

    def place(dx, dy):
        return flip(at.x, dx), flip(at.y, dy)

    for dx, dy in order:
        x, y = place(dx, dy)
        other = x * 4 + y * 2 + 1 - at.c
        wire.send(("c", dx, dy), part.at[other], core_in.at[dx * 2 + dy], core_side)
    for dx, dy in order:
        x, y = place(dx, dy)
        mine = x * 4 + y * 2 + at.c
        slot = dx * 2 + dy
        wire.arrive(("c", dx, dy), core_in.at[slot], core_side)
        add_rows(core_sum.at[slot], part.at[mine], core_in.at[slot])
        if dx:
            source = core_sum.at[slot, :, halves[0]]
            wire.send(("a", dy), source, side_in.at[0, dy], x_side)
        if dy:
            source = core_sum.at[slot, :, halves[1]]
            wire.send(("b", dx), source, side_in.at[1, dx], y_side)
    wire.arrive(("a", 1), side_in.at[0, 1], x_side)
    add_rows(side_sum.at[0], core_sum.at[1, :, halves[0]], side_in.at[0, 1])
    wire.send("y", side_sum.at[0], last_in.at[0], y_side)
    wire.arrive(("b", 1), side_in.at[1, 1], y_side)
    add_rows(side_sum.at[1], core_sum.at[2, :, halves[1]], side_in.at[1, 1])
    wire.send("x", side_sum.at[1], last_in.at[1], x_side)
    wire.arrive(("a", 0), side_in.at[0, 0], x_side)
    wire.arrive(("b", 0), side_in.at[1, 0], y_side)
    wire.arrive("y", last_in.at[0], y_side)
    add_rows(
        out.at[:, halves[0]], core_sum.at[0, :, halves[0]], side_in.at[0, 0], last_in.at[0]
    )
    wire.arrive("x", last_in.at[1], x_side)
    add_rows(
        out.at[:, halves[1]], core_sum.at[0, :, halves[1]], side_in.at[1, 0], last_in.at[1]
    )
    wire.drain()


def plane_scatter(part, number):
    _, own, width = part.shape
    low_type = part.dtype
    return pl.pallas_call(
        plane_scatter_kernel,
        out_shape=jax.ShapeDtypeStruct((own, width), jnp.float32),
        in_specs=[VMEM],
        out_specs=VMEM,
        scratch_shapes=[
            pltpu.VMEM((4, own, width), low_type),
            pltpu.VMEM((4, own, width), low_type),
            pltpu.VMEM((2, 2, own, width // 2), low_type),
            pltpu.VMEM((2, own, width // 2), low_type),
            pltpu.VMEM((2, own, width // 2), low_type),
            pltpu.SemaphoreType.DMA((16,)),
            pltpu.SemaphoreType.DMA((16,)),
        ],
        compiler_params=comm_params(number),
        name="plane_scatter_%d" % number,
    )(part)


def plane_gather_kernel(own_in, out, ss, rs, own_sem):
    at = Place()
    wire = Wire(ss, rs)
    x_side, y_side, core_side = at.plane(4)[0], at.plane(2)[0], at.plane(1)[0]
    enter([x_side, y_side, core_side])
    half = own_in.shape[0] // 2
    mine = out.at[at.rank]
    wire.send("x", own_in, mine, x_side)
    wire.send("y", own_in, mine, y_side)
    wire.send("c0", own_in, mine, core_side)
    own = pltpu.make_async_copy(own_in, mine, own_sem)
    own.start()
    from_x, from_y, from_xy = (at.plane(delta)[1] for delta in (4, 2, 6))
    low_half, high_half = pl.ds(0, half), pl.ds(half, half)
    wire.arrive("x", out.at[from_x], x_side)
    wire.send("d0", out.at[from_x, low_half], out.at[from_x, low_half], y_side)
    wire.send("c1", out.at[from_x], out.at[from_x], core_side)
    wire.arrive("y", out.at[from_y], y_side)
    wire.send("d1", out.at[from_y, high_half], out.at[from_y, high_half], x_side)
    wire.send("c2", out.at[from_y], out.at[from_y], core_side)
    wire.arrive("d0", out.at[from_xy, low_half], y_side)
    wire.arrive("d1", out.at[from_xy, high_half], x_side)
    wire.send("c3", out.at[from_xy], out.at[from_xy], core_side)
    own.wait()
    for index, delta in enumerate((1, 5, 3, 7)):
        wire.arrive("c%d" % index, out.at[at.plane(delta)[1]], core_side)
    wire.drain()


def plane_gather(own_block, number):
    return pl.pallas_call(
        plane_gather_kernel,
        out_shape=jax.ShapeDtypeStruct((8,) + own_block.shape, own_block.dtype),
        in_specs=[VMEM],
        out_specs=VMEM,
        scratch_shapes=[
            pltpu.SemaphoreType.DMA((16,)),
            pltpu.SemaphoreType.DMA((16,)),
            pltpu.SemaphoreType.DMA,
        ],
        compiler_params=comm_params(number),
        name="plane_gather_%d" % number,
    )(own_block)


def group_body(
    hidden_in,
    token_marks,
    out_grad,
    qkv_weight,
    proj_weight,
    gate_weight,
    up_weight,
    down_weight,
    first_gain,
    first_shift,
    second_gain,
    second_shift,
):
    micro_count, _, pos_count, width = hidden_in.shape
    rows_own = qkv_weight.shape[0]
    units = gate_weight.shape[1]
    head_ways = math.prod(lax.axis_size(name) for name in HEAD_AXES)
    unit_ways = math.prod(lax.axis_size(name) for name in UNIT_AXES)
    chunk_count = lax.axis_size("y") * lax.axis_size("c")
    row_length = pos_count * chunk_count
    x_size = lax.axis_size("x")
    marks_own = token_marks.astype(jnp.float32)
    own = micro_count * pos_count
    head_width = width // head_ways
    heads_here = head_width // HEAD_DIM
    unit_width = -(-units // (unit_ways * LANES)) * LANES
    unit_pad = unit_width * unit_ways - units
    x_own = hidden_in.reshape(own, width)

    params = jnp.stack([first_gain, first_shift, second_gain, second_shift])
    small = jnp.concatenate([params.astype(jnp.float32).ravel(), marks_own.ravel()])
    small = jnp.pad(small, (0, -small.size % (8 * LANES))).reshape(-1, LANES)

    qkv_parts = (
        qkv_weight.reshape(rows_own, 3, head_ways, head_width)
        .transpose(2, 0, 1, 3)
        .reshape(head_ways, rows_own, 3 * head_width)
    )
    ffn = jnp.stack([gate_weight, up_weight, down_weight])
    ffn = jnp.pad(ffn, ((0, 0), (0, 0), (0, unit_pad)))
    ffn = ffn.reshape(3, rows_own, unit_ways, unit_width).transpose(2, 0, 1, 3)

    qkv_here, ffn, proj_here, x_all, small = gather_weights(
        qkv_parts, ffn, proj_weight, x_own, small
    )
    qkv_here = qkv_here.reshape(-1, 3 * head_width)
    ffn = ffn.reshape(3, -1, unit_width)
    x_all = x_all.reshape(-1, width)
    proj_here = proj_here.reshape(head_width, width)
    gate_here, up_here, down_here = ffn[0], ffn[1], ffn[2]
    small = small.reshape(unit_ways * 4, -1)
    params = small[:, : 4 * rows_own].reshape(-1, 4, rows_own).transpose(1, 0, 2)
    gain_one, shift_one, gain_two, shift_two = params.reshape(4, 1, width)
    marks = small.reshape(4, head_ways, -1)[lax.axis_index("zi")]
    marks = marks[:, 4 * rows_own : 4 * rows_own + own * 3].astype(jnp.int32)

    mixed = dot(x_all, qkv_here)

    def to_rows(values):
        inner = values.shape[1:]
        values = values.reshape((x_size, chunk_count, micro_count, pos_count) + inner)
        return jnp.swapaxes(values, 1, 2).reshape((x_size * micro_count, row_length) + inner)

    def from_rows(values):
        inner = values.shape[2:]
        values = values.reshape((x_size, micro_count, chunk_count, pos_count) + inner)
        return jnp.swapaxes(values, 1, 2).reshape((head_ways * own,) + inner)

    row_marks = to_rows(marks.reshape(head_ways * own, 3))
    cosine, sine = rotary_tables(row_marks[..., 2])
    cosine, sine = cosine[:, :, None, :], sine[:, :, None, :]
    mixed = to_rows(mixed).reshape(x_size * micro_count, row_length, 3, heads_here, HEAD_DIM)
    queries = low(rotate(mixed[:, :, 0], cosine, sine))
    key_rows = low(rotate(mixed[:, :, 1], cosine, sine))
    value_rows = low(mixed[:, :, 2])
    place = jnp.arange(row_length, dtype=jnp.int32)
    allowed = (row_marks[:, :, None, 0] == row_marks[:, None, :, 0]) & (
        (place[None, None, :] <= place[None, :, None])
        | (place[None, :] < row_marks[:, :, 1])[:, None, :]
    )
    score_scale = 1.0 / math.sqrt(HEAD_DIM)

    def pair(spec, left_side, right_side):
        return jnp.einsum(spec, left_side, right_side, preferred_element_type=jnp.float32)

    scores = pair("rqhd,rkhd->rhqk", queries, key_rows) * score_scale
    scores = jnp.where(allowed[:, None], scores, masked_score)
    exp_scores = jnp.exp(scores - jnp.max(scores, axis=-1, keepdims=True))
    probs = exp_scores / jnp.sum(exp_scores, axis=-1, keepdims=True)
    probs_low = low(probs)
    context = low(pair("rhqk,rkhd->rqhd", probs_low, value_rows))

    context = from_rows(context).reshape(-1, head_width)
    branch = plane_scatter(low(dot(context, proj_here)).reshape(head_ways, own, width), 4)
    first_sum = deep_alpha * x_own.astype(jnp.float32) + branch
    hat_one, inverse_one = norm_parts(first_sum)
    normed = low(hat_one * gain_one + shift_one)

    normed_all = gather(normed, UNIT_AXES)
    gate_val = dot(normed_all, gate_here)
    up_val = dot(normed_all, up_here)
    gelu_val, gelu_slope = gelu_parts(gate_val)
    active = low(gelu_val * up_val)
    down_val = scatter_sum(low(contract_last(active, down_here)), UNIT_AXES)
    second_sum = deep_alpha * normed.astype(jnp.float32) + down_val.astype(jnp.float32)
    hat_two, inverse_two = norm_parts(second_sum)
    layer_rows = low(hat_two * gain_two + shift_two)

    grad_own = out_grad.reshape(own, width).astype(jnp.float32)
    gain_two_grad = jnp.sum(grad_own * hat_two, axis=0)
    shift_two_grad = jnp.sum(grad_own, axis=0)
    d_second = norm_back(grad_own, hat_two, inverse_two, gain_two)
    down_low = gather(low(d_second), UNIT_AXES)
    d_active = dot(down_low, down_here)
    gate_low = low(d_active * up_val * gelu_slope)
    up_low = low(d_active * gelu_val)
    d_normed_part = low(contract_last(gate_low, gate_here) + contract_last(up_low, up_here))
    d_normed = deep_alpha * d_second + scatter_sum(d_normed_part, UNIT_AXES).astype(jnp.float32)

    ffn_part = jnp.stack(
        [
            low(contract_first(normed_all, gate_low)),
            low(contract_first(normed_all, up_low)),
            low(contract_first(down_low, active)),
        ]
    )

    gain_one_grad = jnp.sum(d_normed * hat_one, axis=0)
    shift_one_grad = jnp.sum(d_normed, axis=0)
    d_first = norm_back(d_normed, hat_one, inverse_one, gain_one)
    branch_low = low(d_first)
    small_grads = jnp.stack([gain_one_grad, shift_one_grad, gain_two_grad, shift_two_grad])
    small_grads = small_grads.reshape(4, 4, head_ways, rows_own).transpose(2, 1, 0, 3)
    small_grads = small_grads.reshape(head_ways, 4, 4 * rows_own // LANES, LANES)
    small_grads = jnp.pad(small_grads, ((0, 0), (0, 0), (0, -small_grads.shape[2] % 8), (0, 0)))

    branch_all = plane_gather(branch_low, 5).reshape(-1, width)
    proj_part = low(contract_first(context, branch_all)).reshape(4, rows_own, width)
    d_context = to_rows(low(contract_last(branch_all, proj_here)))
    d_context = d_context.reshape(x_size * micro_count, row_length, heads_here, HEAD_DIM)
    d_probs = pair("rqhd,rkhd->rhqk", d_context, value_rows)
    d_scores = low(probs * (d_probs - jnp.sum(probs * d_probs, axis=-1, keepdims=True)))
    d_query = pair("rhqk,rkhd->rqhd", d_scores, key_rows) * score_scale
    d_keys = pair("rhqk,rqhd->rkhd", d_scores, queries) * score_scale
    d_values = pair("rhqk,rqhd->rkhd", probs_low, d_context)
    d_mixed = low(
        jnp.stack(
            [rotate(d_query, cosine, -sine), rotate(d_keys, cosine, -sine), d_values], axis=2
        )
    )
    d_mixed = from_rows(d_mixed.reshape(x_size * micro_count, row_length, 3 * head_width))
    d_input = low(contract_last(d_mixed, qkv_here)).reshape(head_ways, own, width)
    d_input = plane_scatter(d_input, 6)
    d_input = deep_alpha * d_first + d_input

    qkv_part = low(contract_first(x_all, d_mixed))
    qkv_part, ffn_part, proj_part, small_grads = reduce_grads(
        qkv_part.reshape(4, 8, rows_own, 3 * head_width),
        ffn_part.reshape(3, 4, 2, 2, 2, rows_own, unit_width),
        proj_part,
        small_grads,
    )
    small_grads = small_grads.ravel()[: 4 * rows_own].reshape(4, rows_own)
    qkv_grad = (
        qkv_part.reshape(head_ways, rows_own, 3, head_width)
        .transpose(1, 2, 0, 3)
        .reshape(rows_own, 3 * width)
        .astype(jnp.float32)
    )
    ffn_part = ffn_part.transpose(1, 2, 0, 3).reshape(3, rows_own, unit_ways * unit_width)
    gate_grad, up_grad, down_grad = (
        ffn_part[index, :, :units].astype(jnp.float32) for index in range(3)
    )
    return (
        layer_rows.reshape(micro_count, 1, pos_count, width),
        low(d_input).reshape(micro_count, 1, pos_count, width),
        qkv_grad,
        proj_part.astype(jnp.float32),
        gate_grad,
        up_grad,
        down_grad,
        small_grads[0],
        small_grads[1],
        small_grads[2],
        small_grads[3],
    )


def body(hidden_in, token_marks, out_grad, *weights):
    joined = lax.axis_size("zo")
    if joined == 1:
        return group_body(hidden_in, token_marks, out_grad, *weights)
    rows = weights[0].shape[0]
    width = hidden_in.shape[-1]
    groups = width // (joined * rows)
    group_place = lax.axis_index(ALL[1:])

    def inward(values):
        shape = values.shape
        values = values.reshape(shape[:-1] + (joined, groups, rows))
        return jnp.swapaxes(values, -3, -2).reshape(shape)

    def outward(values):
        shape = values.shape
        values = values.reshape(shape[:-1] + (groups, joined, rows))
        return jnp.swapaxes(values, -3, -2).reshape(shape)

    proj = gather(weights[1], ALL)
    proj = inward(lax.dynamic_slice_in_dim(proj, group_place * joined * rows, joined * rows))
    weights = [gather(weight, "zo") for weight in weights]
    weights[1] = proj
    outs = list(group_body(inward(hidden_in), token_marks, inward(out_grad), *weights))
    outs[:2] = outward(outs[0]), outward(outs[1])
    proj_grad = jnp.zeros((width, width), jnp.float32)
    proj_grad = lax.dynamic_update_slice_in_dim(
        proj_grad, outward(outs[3]), group_place * joined * rows, 0
    )
    outs[2:] = [scatter_sum(grad, "zo") for grad in outs[2:]]
    outs[3] = scatter_sum(proj_grad, ALL)
    return tuple(outs)


def solution(mesh):
    seq_size, ctx_size = mesh.shape["seq"], mesh.shape["ctx"]
    cores, x_size = 2, 2
    zi_size = math.gcd(4, seq_size // x_size)
    zo_size = seq_size // (x_size * zi_size)
    devices = np.asarray(mesh.devices).reshape(
        zo_size, zi_size, x_size, ctx_size // cores, cores
    )
    inner = Mesh(devices, ALL)
    tokens = P(None, ("zo", "zi", "x"), ("y", "c"), None)
    matrix = P(ALL, None)
    vector = P(ALL)
    return jax.shard_map(
        body,
        mesh=inner,
        in_specs=(tokens,) * 3 + (matrix,) * 5 + (vector,) * 4,
        out_specs=(tokens,) * 2 + (matrix,) * 5 + (vector,) * 4,
        check_vma=False,
    )
```

```python
import math

import jax
import jax.numpy as jnp
import numpy as np
from jax import lax
from jax.experimental import pallas as pl
from jax.experimental.pallas import tpu as pltpu
from jax.sharding import Mesh
from jax.sharding import PartitionSpec as P

HEAD_DIM = 128
LANES = 128

deep_alpha = 48.0**0.25
norm_eps = 1e-05
masked_score = -1e30

ALL = ("zo", "zi", "x", "y", "c")
HEAD_AXES = ("x", "y", "c")
UNIT_AXES = ("zi", "c")
HEAD_COPIES = ("zo", "zi")
UNIT_COPIES = ("zo", "x", "y")


def contract_last(left_side, right_side):
    return lax.dot_general(
        left_side, right_side, (((1,), (1,)), ((), ())), preferred_element_type=jnp.float32
    )


def contract_first(left_side, right_side):
    return lax.dot_general(
        left_side, right_side, (((0,), (0,)), ((), ())), preferred_element_type=jnp.float32
    )


def dot(left_side, right_side):
    return jnp.dot(left_side, right_side, preferred_element_type=jnp.float32)


def low(values):
    return values.astype(jnp.bfloat16)


def norm_parts(values):
    center = values - jnp.mean(values, axis=-1, keepdims=True)
    spread = jnp.mean(center * center, axis=-1, keepdims=True)
    inverse = lax.rsqrt(spread + norm_eps)
    return center * inverse, inverse


def norm_back(cotangent, hat, inverse, gain_vec):
    scaled = cotangent * gain_vec
    return (
        scaled
        - jnp.mean(scaled, axis=-1, keepdims=True)
        - hat * jnp.mean(scaled * hat, axis=-1, keepdims=True)
    ) * inverse


def rotary_tables(positions):
    half = HEAD_DIM // 2
    exponent = jnp.arange(half, dtype=jnp.float32) * (2.0 / HEAD_DIM)
    angles = positions.astype(jnp.float32)[..., None] * jnp.exp(-math.log(10000.0) * exponent)
    return (jnp.cos(angles), jnp.sin(angles))


def rotate(values, cosine, sine):
    half = HEAD_DIM // 2
    front, back = values[..., :half], values[..., half:]
    return jnp.concatenate(
        [front * cosine - back * sine, back * cosine + front * sine], axis=-1
    )


def gather(values, axes):
    return lax.all_gather(values, axes, axis=0, tiled=True)


def scatter_sum(values, axes):
    return lax.psum_scatter(values, axes, scatter_dimension=0, tiled=True)


def gelu_parts(value):
    phi = 0.5 * lax.erfc(-value * math.sqrt(0.5))
    density = jnp.exp(-0.5 * value * value) * (1.0 / math.sqrt(2.0 * math.pi))
    return value * phi, phi + value * density


MESH = pl.DeviceIdType.MESH


class Wire:
    def __init__(self, send_sems, recv_sems):
        self.send_sems, self.recv_sems = send_sems, recv_sems
        self.keys, self.sent = {}, []

    def number(self, key, span=1):
        if key not in self.keys:
            self.keys[key] = sum(size for _, size in self.keys.values()), span
        return self.keys[key][0]

    def copy(self, key, source, target, device, slot=0, span=1, recv=None):
        send = self.number(key, span)
        receive = send if recv is None else self.number(recv)
        return pltpu.make_async_remote_copy(
            src_ref=source,
            dst_ref=target,
            send_sem=self.send_sems.at[send],
            recv_sem=self.recv_sems.at[receive + slot],
            device_id=device,
            device_id_type=MESH,
        )

    def send(self, key, source, target, device, when=None, recv=None):
        copy = self.copy(key, source, target, device, recv=recv)
        if when is None:
            copy.start()
        else:
            pl.when(when)(copy.start)
        self.sent.append((copy, when))

    def send_to_slot(self, key, source, target, device, slot, span, when):
        copy = self.copy(key, source, target, device, slot, span)
        pl.when(when)(copy.start)
        self.sent.append((copy, when))

    def arrive(self, key, target, device, when=None):
        copy = self.copy(key, target, target, device)
        if when is None:
            copy.wait_recv()
        else:
            pl.when(when)(copy.wait_recv)

    def arrive_slot(self, key, target, device, slot, span, when):
        pl.when(when)(self.copy(key, target, target, device, slot, span).wait_recv)

    def drain(self):
        for copy, when in self.sent:
            if when is None:
                copy.wait_send()
            else:
                pl.when(when)(copy.wait_send)


def flip(value, bit):
    return 1 - value if bit else value


def enter(devices):
    barrier = pltpu.get_barrier_semaphore()
    for device in devices:
        pl.semaphore_signal(barrier, inc=1, device_id=device, device_id_type=MESH)
    pl.semaphore_wait(barrier, len(devices))


class Place:
    def __init__(self):
        self.zo, self.zi, self.x, self.y, self.c = (lax.axis_index(name) for name in ALL)
        self.rank = self.x * 4 + self.y * 2 + self.c
        self.unit = self.zi * 2 + self.c

    def plane(self, delta):
        dx, dy, dc = delta >> 2 & 1, delta >> 1 & 1, delta & 1
        x, y, c = flip(self.x, dx), flip(self.y, dy), flip(self.c, dc)
        return (self.zo, self.zi, x, y, c), x * 4 + y * 2 + c

    def column(self, step):
        other = lax.rem(self.unit + step + 8, 8)
        return (self.zo, other // 2, self.x, self.y, lax.rem(other, 2)), other

    def ends(self):
        return self.line(jnp.minimum(self.zi + 1, 3)), self.line(jnp.maximum(self.zi - 1, 0))

    def line(self, z):
        return (self.zo, z, self.x, self.y, self.c)

    def neighbours(self):
        plane = [self.plane(delta)[0] for delta in range(1, 8)]
        column = []
        for dz in range(1, 4):
            z = lax.rem(self.zi + dz, 4)
            column += [(self.zo, z, self.x, self.y, core) for core in (0, 1)]
        return plane + column


def gather_kernel(
    qkv_in,
    ffn_in,
    proj_in,
    x_in,
    small_in,
    qkv_out,
    ffn_out,
    proj_out,
    x_out,
    small_out,
    send_sems,
    recv_sems,
    own_sems,
):
    at = Place()
    wire = Wire(send_sems, recv_sems)
    enter(at.neighbours())
    x_side, y_side, core_side = at.plane(4)[0], at.plane(2)[0], at.plane(1)[0]
    half = x_in.shape[0] // 2

    own = [
        pltpu.make_async_copy(x_in, x_out.at[at.rank], own_sems.at[0]),
        pltpu.make_async_copy(qkv_in.at[at.rank], qkv_out.at[at.zi, at.rank], own_sems.at[1]),
        pltpu.make_async_copy(
            ffn_in.at[at.unit], ffn_out.at[:, at.zi, at.x, at.y, at.c], own_sems.at[2]
        ),
        pltpu.make_async_copy(small_in, small_out.at[at.zi, at.rank], own_sems.at[3]),
    ]
    for copy in own:
        copy.start()

    chunk = at.y * 2 + at.c
    holder = at.zi * 2 + at.x
    proj_home = at.rank // 2
    proj_first = at.rank == holder
    proj_own = pltpu.make_async_copy(proj_in, proj_out.at[chunk], own_sems.at[4])
    pl.when(proj_first)(proj_own.start)

    def small_first():
        for delta in range(1, 8):
            device, _ = at.plane(delta)
            slot = small_out.at[at.zi, at.rank]
            wire.send(("s", delta), small_in, slot, device)

    small_first()

    for step in (1, 7, 2, 6, 3, 5, 4):
        device, other = at.column(step)
        slot = ffn_out.at[:, at.zi, at.x, at.y, at.c]
        wire.send(("f", step), ffn_in.at[other], slot, device)
    for delta in range(1, 8):
        device, other = at.plane(delta)
        wire.send(("q", delta), qkv_in.at[other], qkv_out.at[at.zi, at.rank], device)
    holder_device = (at.zo, at.zi, holder // 4, lax.rem(holder // 2, 2), lax.rem(holder, 2))
    wire.send_to_slot("p", proj_in, proj_out.at[chunk], holder_device, chunk, 4, at.rank != holder)
    wire.send("xx", x_in, x_out.at[at.rank], x_side)
    wire.send("xy", x_in, x_out.at[at.rank], y_side)
    wire.send("xc0", x_in, x_out.at[at.rank], core_side)
    for copy in own:
        copy.wait()
    pl.when(proj_first)(proj_own.wait)

    def small_second():
        for delta in range(1, 8):
            device, other = at.plane(delta)
            wire.arrive(("s", delta), small_out.at[at.zi, other], device)
        for dz in range(1, 4):
            device = at.line(lax.rem(at.zi + dz, 4))
            wire.send(("t", dz), small_out.at[at.zi], small_out.at[at.zi], device)

    def small_last():
        for dz in range(1, 4):
            z = lax.rem(at.zi - dz + 4, 4)
            wire.arrive(("t", dz), small_out.at[z], at.line(z))

    def proj_start():
        for slot in range(4):
            source = (at.zo, at.zi, lax.rem(at.rank, 2), slot // 2, slot % 2)
            mine = (at.zi == proj_home) & ((chunk != slot) | (at.rank != holder))
            wire.arrive_slot("p", proj_out.at[slot], source, slot, 4, mine)
        wire.send("pu0", proj_out, proj_out, up, (at.zi == proj_home) & (at.zi < 3))
        wire.send("pd0", proj_out, proj_out, down, (at.zi == proj_home) & (at.zi > 0))

    def proj_relay():
        above, below = at.zi > proj_home, at.zi < proj_home
        wire.arrive("pu0", proj_out, down, above)
        wire.arrive("pd0", proj_out, up, below)
        wire.send("pu1", proj_out, proj_out, up, above & (at.zi < 3), recv="pu0")
        wire.send("pd1", proj_out, proj_out, down, below & (at.zi > 0), recv="pd0")

    def qkv_slot(z, delta):
        return qkv_out.at[jnp.clip(z, 0, 3), at.plane(delta)[1]]

    up, down = at.line(jnp.minimum(at.zi + 1, 3)), at.line(jnp.maximum(at.zi - 1, 0))

    def qkv_hop(hop, delta):
        below, above = qkv_slot(at.zi - hop, delta), qkv_slot(at.zi + hop, delta)
        if hop == 0:
            if delta:
                wire.arrive(("q", delta), below, at.plane(delta)[0])
        else:
            wire.arrive(("up", hop - 1, delta), below, down, at.zi >= hop)
            wire.arrive(("down", hop - 1, delta), above, up, at.zi <= 3 - hop)
        if hop < 3:
            wire.send(("up", hop, delta), below, below, up, (at.zi >= hop) & (at.zi < 3))
            wire.send(("down", hop, delta), above, above, down, (at.zi <= 3 - hop) & (at.zi > 0))

    def ffn_slot(step, x, y):
        source = lax.rem(at.unit - step + 8, 8)
        return ffn_out.at[:, source // 2, x, y, lax.rem(source, 2)]

    def ffn_first(step):
        slot = ffn_slot(step, at.x, at.y)
        if step:
            wire.arrive(("f", step), slot, at.column(-step)[0])
        wire.send(("fx", step), slot, slot, x_side)
        wire.send(("fy", step), slot, slot, y_side)

    def ffn_second(step, turn):
        from_x, from_y = ffn_slot(step, 1 - at.x, at.y), ffn_slot(step, at.x, 1 - at.y)
        wire.arrive(("fx", step), from_x, x_side)
        wire.arrive(("fy", step), from_y, y_side)
        if turn % 2:
            wire.send(("fd", step), from_x, from_x, y_side)
        else:
            wire.send(("fd", step), from_y, from_y, x_side)

    from_x, from_y, from_xy = (at.plane(delta)[1] for delta in (4, 2, 6))
    low_half, high_half = pl.ds(0, half), pl.ds(half, half)
    ffn_first(0)
    wire.arrive("xx", x_out.at[from_x], x_side)
    wire.send("xd0", x_out.at[from_x, low_half], x_out.at[from_x, low_half], y_side)
    wire.send("xc1", x_out.at[from_x], x_out.at[from_x], core_side)
    wire.arrive("xy", x_out.at[from_y], y_side)
    wire.send("xd1", x_out.at[from_y, high_half], x_out.at[from_y, high_half], x_side)
    wire.send("xc2", x_out.at[from_y], x_out.at[from_y], core_side)
    small_second()
    for delta in range(8):
        qkv_hop(0, delta)
    proj_start()
    wire.arrive("xd0", x_out.at[from_xy, low_half], y_side)
    wire.arrive("xd1", x_out.at[from_xy, high_half], x_side)
    wire.send("xc3", x_out.at[from_xy], x_out.at[from_xy], core_side)

    steps = (1, 7, 2, 6, 3, 5, 4)
    ffn_second(0, 0)
    for turn, step in enumerate(steps):
        ffn_first(step)
        qkv_hop(1, turn)
        if turn >= 2:
            ffn_second(steps[turn - 2], turn - 2 + 1)
    qkv_hop(1, 7)
    proj_relay()
    for delta in range(8):
        qkv_hop(2, delta)
        if delta < 2:
            ffn_second(steps[5 + delta], 5 + delta + 1)
    for delta in range(8):
        qkv_hop(3, delta)
    for index, delta in enumerate((1, 5, 3, 7)):
        other = at.plane(delta)[1]
        wire.arrive("xc%d" % index, x_out.at[other], core_side)
    for step in range(8):
        wire.arrive(("fd", step), ffn_slot(step, 1 - at.x, 1 - at.y), x_side)
    small_last()
    wire.drain()


ANY = pl.BlockSpec(memory_space=pl.ANY)
VMEM = pl.BlockSpec(memory_space=pltpu.VMEM)


def comm_params(number):
    return pltpu.CompilerParams(
        collective_id=number, has_side_effects=True, vmem_limit_bytes=63 * 2**20
    )


def gather_weights(qkv_parts, ffn_parts, proj_own, x_own, small):
    _, rows_own, qkv_width = qkv_parts.shape
    unit_width = ffn_parts.shape[-1]
    own, width = x_own.shape
    low_type = jnp.bfloat16
    return pl.pallas_call(
        gather_kernel,
        out_shape=(
            jax.ShapeDtypeStruct((4, 8, rows_own, qkv_width), low_type),
            jax.ShapeDtypeStruct((3, 4, 2, 2, 2, rows_own, unit_width), low_type),
            jax.ShapeDtypeStruct((4, rows_own, width), low_type),
            jax.ShapeDtypeStruct((8, own, width), low_type),
            jax.ShapeDtypeStruct((4, 8) + small.shape, small.dtype),
        ),
        in_specs=[VMEM] * 5,
        out_specs=(ANY,) * 5,
        scratch_shapes=[
            pltpu.SemaphoreType.DMA((128,)),
            pltpu.SemaphoreType.DMA((128,)),
            pltpu.SemaphoreType.DMA((5,)),
        ],
        compiler_params=comm_params(1),
        cost_estimate=pl.CostEstimate(
            flops=0, bytes_accessed=400_000_000, transcendentals=0
        ),
        name="gather_weights",
    )(qkv_parts, ffn_parts, proj_own, x_own, small)


def add_rows(out, *terms):
    step = 32

    @pl.loop(0, out.shape[0] // step)
    def _(index):
        part = pl.ds(pl.multiple_of(index * step, step), step)
        whole = terms[0][part].astype(jnp.float32)
        for term in terms[1:]:
            whole = whole + term[part].astype(jnp.float32)
        out[part] = whole.astype(out.dtype)


def column_scatter_flow(at, wire, part, out, core_in, core_sum, up_in, down_in, up_sum, down_sum):
    core_side = at.plane(1)[0]
    up, down = at.ends()
    for goal in (3, 0, 2, 1):
        source = part.at[goal * 2 + 1 - at.c]
        wire.send(("rc", goal), source, core_in.at[goal], core_side)
    yield
    for goal in (3, 0, 2, 1):
        wire.arrive(("rc", goal), core_in.at[goal], core_side)
        add_rows(core_sum.at[goal], part.at[goal * 2 + at.c], core_in.at[goal])
        source = core_sum.at[goal]
        if goal > 0:
            wire.send(("ru", goal), source, up_in.at[goal], up, at.zi == 0)
        if goal < 3:
            wire.send(("rd", goal), source, down_in.at[goal], down, at.zi == 3)

    def climb(goal):
        wire.arrive(("ru", goal), up_in.at[goal], down)
        add_rows(up_sum.at[goal], core_sum.at[goal], up_in.at[goal])

    def descend(goal):
        wire.arrive(("rd", goal), down_in.at[goal], up)
        add_rows(down_sum.at[goal], core_sum.at[goal], down_in.at[goal])

    for goal in (3, 2):
        yield
        back = 3 - goal
        passing = (at.zi > 0) & (at.zi < goal)
        pl.when(passing)(lambda: climb(goal))
        key = "ru", goal
        wire.send(("ru2", goal), up_sum.at[goal], up_in.at[goal], up, passing, recv=key)
        passing = (at.zi < 3) & (at.zi > back)
        pl.when(passing)(lambda: descend(back))
        key = "rd", back
        wire.send(("rd2", back), down_sum.at[back], down_in.at[back], down, passing, recv=key)
    yield
    add_rows(out, core_sum.at[at.zi])

    def last(key, source, device):
        wire.arrive(key, source, device)
        add_rows(out, out, source)

    for goal in range(4):
        if goal > 0:
            pl.when(at.zi == goal)(lambda: last(("ru", goal), up_in.at[goal], down))
        if goal < 3:
            pl.when(at.zi == goal)(lambda: last(("rd", goal), down_in.at[goal], up))


def column_scratch(own, width):
    return [pltpu.VMEM((4, own, width), jnp.bfloat16)] * 6


def plane_scatter_flow(at, wire, part, out, core_in, core_sum, side_in, side_sum, last_in):
    x_side, y_side, core_side = at.plane(4)[0], at.plane(2)[0], at.plane(1)[0]
    half = out.shape[1] // 2
    halves = (pl.ds(0, half), pl.ds(half, half))
    order = ((1, 1), (1, 0), (0, 1), (0, 0))

    def place(dx, dy):
        return flip(at.x, dx), flip(at.y, dy)

    for dx, dy in order:
        x, y = place(dx, dy)
        other = x * 4 + y * 2 + 1 - at.c
        wire.send(("c", dx, dy), part.at[other], core_in.at[dx * 2 + dy], core_side)
    yield
    for dx, dy in order:
        x, y = place(dx, dy)
        mine = x * 4 + y * 2 + at.c
        slot = dx * 2 + dy
        wire.arrive(("c", dx, dy), core_in.at[slot], core_side)
        add_rows(core_sum.at[slot], part.at[mine], core_in.at[slot])
        if dx:
            source = core_sum.at[slot, :, halves[0]]
            wire.send(("sa", dy), source, side_in.at[0, dy], x_side)
        if dy:
            source = core_sum.at[slot, :, halves[1]]
            wire.send(("sb", dx), source, side_in.at[1, dx], y_side)
    yield
    wire.arrive(("sa", 1), side_in.at[0, 1], x_side)
    add_rows(side_sum.at[0], core_sum.at[1, :, halves[0]], side_in.at[0, 1])
    wire.send("sy", side_sum.at[0], last_in.at[0], y_side)
    wire.arrive(("sb", 1), side_in.at[1, 1], y_side)
    add_rows(side_sum.at[1], core_sum.at[2, :, halves[1]], side_in.at[1, 1])
    wire.send("sx", side_sum.at[1], last_in.at[1], x_side)
    yield
    wire.arrive(("sa", 0), side_in.at[0, 0], x_side)
    wire.arrive(("sb", 0), side_in.at[1, 0], y_side)
    wire.arrive("sy", last_in.at[0], y_side)
    terms = core_sum.at[0, :, halves[0]], side_in.at[0, 0], last_in.at[0]
    add_rows(out.at[:, halves[0]], *terms)
    wire.arrive("sx", last_in.at[1], x_side)
    terms = core_sum.at[0, :, halves[1]], side_in.at[1, 0], last_in.at[1]
    add_rows(out.at[:, halves[1]], *terms)


def plane_scratch(own, width):
    return [
        pltpu.VMEM((4, own, width), jnp.bfloat16),
        pltpu.VMEM((4, own, width), jnp.bfloat16),
        pltpu.VMEM((2, 2, own, width // 2), jnp.bfloat16),
        pltpu.VMEM((2, own, width // 2), jnp.bfloat16),
        pltpu.VMEM((2, own, width // 2), jnp.bfloat16),
    ]


def plane_gather_flow(at, wire, own_in, out, own_sem):
    x_side, y_side, core_side = at.plane(4)[0], at.plane(2)[0], at.plane(1)[0]
    half = own_in.shape[0] // 2
    mine = out.at[at.rank]
    wire.send("gx", own_in, mine, x_side)
    wire.send("gy", own_in, mine, y_side)
    wire.send("gc0", own_in, mine, core_side)
    own = pltpu.make_async_copy(own_in, mine, own_sem)
    own.start()
    yield
    from_x, from_y, from_xy = (at.plane(delta)[1] for delta in (4, 2, 6))
    low_half, high_half = pl.ds(0, half), pl.ds(half, half)
    wire.arrive("gx", out.at[from_x], x_side)
    wire.send("gd0", out.at[from_x, low_half], out.at[from_x, low_half], y_side)
    wire.send("gc1", out.at[from_x], out.at[from_x], core_side)
    wire.arrive("gy", out.at[from_y], y_side)
    wire.send("gd1", out.at[from_y, high_half], out.at[from_y, high_half], x_side)
    wire.send("gc2", out.at[from_y], out.at[from_y], core_side)
    yield
    wire.arrive("gd0", out.at[from_xy, low_half], y_side)
    wire.arrive("gd1", out.at[from_xy, high_half], x_side)
    wire.send("gc3", out.at[from_xy], out.at[from_xy], core_side)
    own.wait()
    for index, delta in enumerate((1, 5, 3, 7)):
        wire.arrive("gc%d" % index, out.at[at.plane(delta)[1]], core_side)


def close_units_kernel(
    gate_in,
    raise_in,
    lower_in,
    part,
    d_second,
    hat,
    inverse,
    gain,
    ffn_out,
    branch_out,
    d_first,
    norm_out,
    first_in,
    second_sum,
    second_in,
    total,
    d_normed,
    branch_low,
    core_in,
    core_sum,
    up_in,
    down_in,
    up_sum,
    down_sum,
    send_sems,
    recv_sems,
    own_sems,
):
    at = Place()
    wire = Wire(send_sems, recv_sems)
    enter(at.neighbours())
    x_side, y_side = at.plane(4)[0], at.plane(2)[0]
    steps = (4, 3, 5, 2, 6, 1, 7, 0)
    sources = gate_in, raise_in, lower_in

    def owner(step):
        other = at.column(step)[1]
        return other // 2, lax.rem(other, 2)

    def ffn_first(turn):
        step = steps[turn]
        z, c = owner(step)
        for index, source in enumerate(sources):
            if turn % 2:
                block, device = source.at[z, 1 - at.x, :, c], x_side
            else:
                block, device = source.at[z, :, 1 - at.y, c], y_side
            wire.send(("a", step, index), block, first_in.at[step, index], device)

    def ffn_second(turn):
        step = steps[turn]
        z, c = owner(step)
        for index, source in enumerate(sources):
            if turn % 2:
                wire.arrive(("a", step, index), first_in.at[step, index], x_side)
                terms = source.at[z, at.x, 1 - at.y, c], first_in.at[step, index, 1 - at.y]
            else:
                wire.arrive(("a", step, index), first_in.at[step, index], y_side)
                terms = source.at[z, 1 - at.x, at.y, c], first_in.at[step, index, 1 - at.x]
            add_rows(second_sum.at[step, index], *terms)
        wire.send(
            ("b", step), second_sum.at[step], second_in.at[step], y_side if turn % 2 else x_side
        )

    own_total = pltpu.make_async_copy(total.at[0], ffn_out.at[at.unit], own_sems.at[0])

    def ffn_last(turn):
        step = steps[turn]
        z, c = owner(step)
        near = at.y if turn % 2 else at.x
        wire.arrive(("b", step), second_in.at[step], x_side)
        for index, source in enumerate(sources):
            add_rows(
                total.at[step, index],
                source.at[z, at.x, at.y, c],
                first_in.at[step, index, near],
                second_in.at[step, index],
            )
        if step:
            wire.send(("f", step), total.at[step], ffn_out.at[at.unit], at.column(step)[0])
        else:
            own_total.start()

    def norm_rows():
        count = 16
        norm_out[...] = jnp.zeros_like(norm_out)

        @pl.loop(0, hat.shape[0] // count)
        def _(index):
            rows = pl.ds(pl.multiple_of(index * count, count), count)
            cotangent = deep_alpha * d_second[rows] + d_normed[rows]
            near = hat[rows]
            result = norm_back(cotangent, near, inverse[rows], gain[...])
            d_first[rows] = result
            branch_low[rows] = result.astype(jnp.bfloat16)
            along = cotangent * near
            norm_out[0] += along[:8] + along[8:]
            norm_out[1] += cotangent[:8] + cotangent[8:]

    scatter = column_scatter_flow(
        at, wire, part, d_normed, core_in, core_sum, up_in, down_in, up_sum, down_sum
    )
    next(scatter)
    for turn in range(5):
        ffn_first(turn)
    next(scatter)
    next(scatter)
    ffn_second(0)
    ffn_second(1)
    next(scatter)
    ffn_second(2)
    ffn_last(0)
    for _ in scatter:
        pass
    norm_rows()
    spread = plane_gather_flow(at, wire, branch_low, branch_out, own_sems.at[1])
    next(spread)
    for turn in range(5, 8):
        ffn_first(turn)
    ffn_last(1)
    ffn_second(3)
    ffn_second(4)
    next(spread)
    ffn_last(2)
    ffn_last(3)
    ffn_second(5)
    ffn_last(4)
    next(spread, None)
    ffn_second(6)
    ffn_second(7)
    for _ in spread:
        pass
    for turn in range(5, 8):
        ffn_last(turn)
    own_total.wait()
    for step in steps:
        if step:
            device, other = at.column(-step)
            wire.arrive(("f", step), ffn_out.at[other], device)
    wire.drain()


def close_units(grads, part, d_second, hat, inverse, gain):
    rows_own, unit_width = grads[0].shape[-2:]
    _, own, width = part.shape
    low_type = jnp.bfloat16
    block = (rows_own, unit_width)
    return pl.pallas_call(
        close_units_kernel,
        out_shape=(
            jax.ShapeDtypeStruct((8, 3) + block, low_type),
            jax.ShapeDtypeStruct((8, own, width), low_type),
            jax.ShapeDtypeStruct((own, width), jnp.float32),
            jax.ShapeDtypeStruct((2, 8, width), jnp.float32),
        ),
        in_specs=[VMEM] * 8,
        out_specs=(ANY, ANY, VMEM, VMEM),
        scratch_shapes=[
            pltpu.VMEM((8, 3, 2) + block, low_type),
            pltpu.VMEM((8, 3) + block, low_type),
            pltpu.VMEM((8, 3) + block, low_type),
            pltpu.VMEM((8, 3) + block, low_type),
            pltpu.VMEM((own, width), jnp.float32),
            pltpu.VMEM((own, width), low_type),
        ]
        + column_scratch(own, width)
        + [
            pltpu.SemaphoreType.DMA((80,)),
            pltpu.SemaphoreType.DMA((80,)),
            pltpu.SemaphoreType.DMA((2,)),
        ],
        compiler_params=comm_params(3),
        name="close_units",
    )(*grads, part, d_second, hat, inverse, gain)


def close_heads_kernel(
    qkv_in,
    proj_in,
    small_in,
    part,
    qkv_out,
    proj_out,
    small_out,
    d_input,
    proj_below,
    proj_above,
    proj_sum,
    small_plane,
    small_mid,
    small_line,
    up_in,
    down_in,
    up_sum,
    down_sum,
    qkv_total,
    core_in,
    core_sum,
    side_in,
    side_sum,
    last_in,
    send_sems,
    recv_sems,
    own_sems,
):
    at = Place()
    wire = Wire(send_sems, recv_sems)
    enter(at.neighbours())
    scatter = plane_scatter_flow(
        at, wire, part, d_input, core_in, core_sum, side_in, side_sum, last_in
    )
    next(scatter)

    def add(*terms):
        whole = terms[0].astype(jnp.float32)
        for term in terms[1:]:
            whole = whole + term.astype(jnp.float32)
        return whole.astype(jnp.bfloat16)

    for delta in range(1, 8):
        device, other = at.plane(delta)
        wire.send(("s", delta), small_in.at[other], small_plane.at[at.rank], device)

    def small_second():
        whole = small_in[at.rank]
        for delta in range(1, 8):
            device, other = at.plane(delta)
            wire.arrive(("s", delta), small_plane.at[other], device)
            whole = whole + small_plane[other]
        small_mid[...] = whole
        for dz in range(1, 4):
            z = lax.rem(at.zi + dz, 4)
            wire.send(("t", dz), small_mid.at[z], small_line.at[at.zi], at.line(z))

    def small_last():
        whole = small_mid[at.zi]
        for dz in range(1, 4):
            z = lax.rem(at.zi - dz + 4, 4)
            wire.arrive(("t", dz), small_line.at[z], at.line(z))
            whole = whole + small_line[z]
        small_out[...] = whole

    pieces = 4
    wide = 8 // pieces
    up, down = at.line(jnp.minimum(at.zi + 1, 3)), at.line(jnp.maximum(at.zi - 1, 0))

    def qkv_pass(goal, piece):
        part = pl.ds(piece * wide, wide)

        if goal > 0:

            @pl.when(at.zi < goal)
            def _():
                @pl.when(at.zi == 0)
                def _():
                    up_sum[goal, part] = qkv_in[goal, part]

                @pl.when(at.zi > 0)
                def _():
                    wire.arrive(("u", goal, piece), up_in.at[goal, part], down)
                    up_sum[goal, part] = add(qkv_in[goal, part], up_in[goal, part])

            wire.send(
                ("u", goal, piece),
                up_sum.at[goal, part],
                up_in.at[goal, part],
                up,
                at.zi < goal,
            )
        back = 3 - goal
        if back < 3:

            @pl.when(at.zi > back)
            def _():
                @pl.when(at.zi == 3)
                def _():
                    down_sum[back, part] = qkv_in[back, part]

                @pl.when(at.zi < 3)
                def _():
                    wire.arrive(("d", back, piece), down_in.at[back, part], up)
                    down_sum[back, part] = add(qkv_in[back, part], down_in[back, part])

            wire.send(
                ("d", back, piece),
                down_sum.at[back, part],
                down_in.at[back, part],
                down,
                at.zi > back,
            )

    proj_home = at.rank // 2

    def each_rows(step, count, function):
        @pl.loop(0, count // step)
        def _(index):
            function(pl.ds(pl.multiple_of(index * step, step), step))

    def proj_add(out, *terms):
        for slot in range(4):

            def rows(part):
                out[slot, part] = add(*(term[slot, part] for term in terms))

            each_rows(16, proj_in.shape[1], rows)

    def proj_pass():
        ends = (at.zi == 0) | (at.zi == 3)
        below, above = at.zi < proj_home, at.zi > proj_home
        wire.send("pu0", proj_in, proj_below, up, below & ends)
        wire.send("pd0", proj_in, proj_above, down, above & ends)

    def proj_climb():
        below, above = at.zi < proj_home, at.zi > proj_home

        def climb():
            wire.arrive("pu0", proj_below, down)
            proj_add(proj_sum, proj_in, proj_below)

        def descend():
            wire.arrive("pd0", proj_above, up)
            proj_add(proj_sum, proj_in, proj_above)

        pl.when(below & (at.zi > 0))(climb)
        pl.when(above & (at.zi < 3))(descend)
        wire.send("pu1", proj_sum, proj_below, up, below & (at.zi > 0), recv="pu0")
        wire.send("pd1", proj_sum, proj_above, down, above & (at.zi < 3), recv="pd0")

    holder = at.zi * 2 + at.x
    chunk = at.y * 2 + at.c
    holder_device = (at.zo, at.zi, holder // 4, lax.rem(holder // 2, 2), lax.rem(holder, 2))

    def proj_last():
        home = at.zi == proj_home

        def first():
            wire.arrive("pu0", proj_below, down)
            proj_add(proj_sum, proj_in, proj_below)

        def only():
            wire.arrive("pd0", proj_above, up)
            proj_add(proj_sum, proj_in, proj_above)

        def both():
            wire.arrive("pd0", proj_above, up)
            proj_add(proj_sum, proj_sum, proj_above)

        pl.when(home & (at.zi > 0))(first)
        pl.when(home & (at.zi == 0))(only)
        pl.when(home & (at.zi > 0) & (at.zi < 3))(both)
        for slot in range(4):
            target = (at.zo, at.zi, lax.rem(at.rank, 2), slot // 2, slot % 2)
            other = (chunk != slot) | (at.rank != holder)
            wire.send(("o", slot), proj_sum.at[slot], proj_out, target, home & other, recv="o")
        own = pltpu.make_async_copy(proj_sum.at[chunk], proj_out, own_sems.at[2])
        pl.when(home & (at.rank == holder))(own.start)
        pl.when(home & (at.rank == holder))(own.wait)

    def qkv_last(piece):
        part = pl.ds(piece * wide, wide)
        for goal in range(4):

            @pl.when(at.zi == goal)
            def _():
                terms = [qkv_in[goal, part]]
                if goal > 0:
                    wire.arrive(("u", goal, piece), up_in.at[goal, part], down)
                    terms.append(up_in[goal, part])
                if goal < 3:
                    wire.arrive(("d", goal, piece), down_in.at[goal, part], up)
                    terms.append(down_in[goal, part])
                qkv_total[part] = add(*terms)

    for piece in range(pieces):
        qkv_pass(3, piece)
    proj_pass()
    next(scatter)
    small_second()
    for piece in range(pieces):
        qkv_pass(2, piece)
    next(scatter)
    for _ in scatter:
        pass
    proj_climb()
    for piece in range(pieces):
        qkv_pass(1, piece)
    proj_last()
    for piece in range(pieces):
        qkv_last(piece)
    own_qkv = pltpu.make_async_copy(
        qkv_total.at[at.rank], qkv_out.at[at.rank], own_sems.at[1]
    )
    own_qkv.start()
    for delta in range(1, 8):
        device, other = at.plane(delta)
        wire.send(("q", delta), qkv_total.at[other], qkv_out.at[at.rank], device)
    own_qkv.wait()
    for delta in range(1, 8):
        device, other = at.plane(delta)
        wire.arrive(("q", delta), qkv_out.at[other], device)
    small_last()
    wire.arrive("o", proj_out, holder_device, at.rank != holder)
    wire.drain()


def close_heads(qkv_part, proj_part, small_part, part):
    _, _, rows_own, qkv_width = qkv_part.shape
    _, own, width = part.shape
    low_type = jnp.bfloat16
    line = (4, 8, rows_own, qkv_width)
    small_shape = small_part.shape[1:]
    return pl.pallas_call(
        close_heads_kernel,
        out_shape=(
            jax.ShapeDtypeStruct((8, rows_own, qkv_width), low_type),
            jax.ShapeDtypeStruct((rows_own, width), low_type),
            jax.ShapeDtypeStruct(small_shape[1:], small_part.dtype),
            jax.ShapeDtypeStruct((own, width), jnp.float32),
        ),
        in_specs=[VMEM] * 4,
        out_specs=(ANY, ANY, VMEM, VMEM),
        scratch_shapes=[
            pltpu.VMEM((4, rows_own, width), low_type),
            pltpu.VMEM((4, rows_own, width), low_type),
            pltpu.VMEM((4, rows_own, width), low_type),
            pltpu.VMEM(small_part.shape, small_part.dtype),
            pltpu.VMEM(small_shape, small_part.dtype),
            pltpu.VMEM(small_shape, small_part.dtype),
            pltpu.VMEM(line, low_type),
            pltpu.VMEM(line, low_type),
            pltpu.VMEM(line, low_type),
            pltpu.VMEM(line, low_type),
            pltpu.VMEM(line[1:], low_type),
        ]
        + plane_scratch(own, width)
        + [
            pltpu.SemaphoreType.DMA((80,)),
            pltpu.SemaphoreType.DMA((80,)),
            pltpu.SemaphoreType.DMA((3,)),
        ],
        compiler_params=comm_params(2),
        name="close_heads",
    )(qkv_part, proj_part, small_part, part)


def plane_scatter_kernel(part, out, *rest):
    at = Place()
    wire = Wire(*rest[-2:])
    enter([at.plane(delta)[0] for delta in (4, 2, 1)])
    for _ in plane_scatter_flow(at, wire, part, out, *rest[:-2]):
        pass
    wire.drain()


def plane_scatter(part, number):
    _, own, width = part.shape
    return pl.pallas_call(
        plane_scatter_kernel,
        out_shape=jax.ShapeDtypeStruct((own, width), jnp.float32),
        in_specs=[VMEM],
        out_specs=VMEM,
        scratch_shapes=plane_scratch(own, width)
        + [pltpu.SemaphoreType.DMA((16,)), pltpu.SemaphoreType.DMA((16,))],
        compiler_params=comm_params(number),
        name="plane_scatter_%d" % number,
    )(part)


def group_body(
    hidden_in,
    token_marks,
    out_grad,
    qkv_weight,
    proj_weight,
    gate_weight,
    up_weight,
    down_weight,
    first_gain,
    first_shift,
    second_gain,
    second_shift,
):
    micro_count, _, pos_count, width = hidden_in.shape
    rows_own = qkv_weight.shape[0]
    units = gate_weight.shape[1]
    head_ways = math.prod(lax.axis_size(name) for name in HEAD_AXES)
    unit_ways = math.prod(lax.axis_size(name) for name in UNIT_AXES)
    chunk_count = lax.axis_size("y") * lax.axis_size("c")
    row_length = pos_count * chunk_count
    x_size = lax.axis_size("x")
    marks_own = token_marks.astype(jnp.float32)
    own = micro_count * pos_count
    head_width = width // head_ways
    heads_here = head_width // HEAD_DIM
    unit_width = -(-units // (unit_ways * LANES)) * LANES
    unit_pad = unit_width * unit_ways - units
    x_own = hidden_in.reshape(own, width)

    params = jnp.stack([first_gain, first_shift, second_gain, second_shift])
    small = jnp.concatenate([params.astype(jnp.float32).ravel(), marks_own.ravel()])
    small = jnp.pad(small, (0, -small.size % (8 * LANES))).reshape(-1, LANES)

    qkv_parts = (
        qkv_weight.reshape(rows_own, 3, head_ways, head_width)
        .transpose(2, 0, 1, 3)
        .reshape(head_ways, rows_own, 3 * head_width)
    )
    ffn = jnp.stack([gate_weight, up_weight, down_weight])
    ffn = jnp.pad(ffn, ((0, 0), (0, 0), (0, unit_pad)))
    ffn = ffn.reshape(3, rows_own, unit_ways, unit_width).transpose(2, 0, 1, 3)

    qkv_here, ffn, proj_here, x_all, small = gather_weights(
        qkv_parts, ffn, proj_weight, x_own, small
    )
    qkv_here = qkv_here.reshape(-1, 3 * head_width)
    ffn = ffn.reshape(3, -1, unit_width)
    x_all = x_all.reshape(-1, width)
    proj_here = proj_here.reshape(head_width, width)
    gate_here, up_here, down_here = ffn[0], ffn[1], ffn[2]
    small = small.reshape(unit_ways * 4, -1)
    params = small[:, : 4 * rows_own].reshape(-1, 4, rows_own).transpose(1, 0, 2)
    gain_one, shift_one, gain_two, shift_two = params.reshape(4, 1, width)
    marks = small.reshape(4, head_ways, -1)[lax.axis_index("zi")]
    marks = marks[:, 4 * rows_own : 4 * rows_own + own * 3].astype(jnp.int32)

    mixed = dot(x_all, qkv_here)

    def to_rows(values):
        inner = values.shape[1:]
        values = values.reshape((x_size, chunk_count, micro_count, pos_count) + inner)
        return jnp.swapaxes(values, 1, 2).reshape((x_size * micro_count, row_length) + inner)

    def from_rows(values):
        inner = values.shape[2:]
        values = values.reshape((x_size, micro_count, chunk_count, pos_count) + inner)
        return jnp.swapaxes(values, 1, 2).reshape((head_ways * own,) + inner)

    row_marks = to_rows(marks.reshape(head_ways * own, 3))
    cosine, sine = rotary_tables(row_marks[..., 2])
    cosine, sine = cosine[:, :, None, :], sine[:, :, None, :]
    mixed = to_rows(mixed).reshape(x_size * micro_count, row_length, 3, heads_here, HEAD_DIM)
    queries = low(rotate(mixed[:, :, 0], cosine, sine))
    key_rows = low(rotate(mixed[:, :, 1], cosine, sine))
    value_rows = low(mixed[:, :, 2])
    place = jnp.arange(row_length, dtype=jnp.int32)
    allowed = (row_marks[:, :, None, 0] == row_marks[:, None, :, 0]) & (
        (place[None, None, :] <= place[None, :, None])
        | (place[None, :] < row_marks[:, :, 1])[:, None, :]
    )
    score_scale = 1.0 / math.sqrt(HEAD_DIM)

    def pair(spec, left_side, right_side):
        return jnp.einsum(spec, left_side, right_side, preferred_element_type=jnp.float32)

    scores = pair("rqhd,rkhd->rhqk", queries, key_rows) * score_scale
    scores = jnp.where(allowed[:, None], scores, masked_score)
    exp_scores = jnp.exp(scores - jnp.max(scores, axis=-1, keepdims=True))
    probs = exp_scores / jnp.sum(exp_scores, axis=-1, keepdims=True)
    probs_low = low(probs)
    context = low(pair("rhqk,rkhd->rqhd", probs_low, value_rows))

    context = from_rows(context).reshape(-1, head_width)
    branch = plane_scatter(low(dot(context, proj_here)).reshape(head_ways, own, width), 4)
    first_sum = deep_alpha * x_own.astype(jnp.float32) + branch
    hat_one, inverse_one = norm_parts(first_sum)
    normed = low(hat_one * gain_one + shift_one)

    normed_all = gather(normed, UNIT_AXES)
    gate_val = dot(normed_all, gate_here)
    up_val = dot(normed_all, up_here)
    gelu_val, gelu_slope = gelu_parts(gate_val)
    active = low(gelu_val * up_val)
    down_val = scatter_sum(low(contract_last(active, down_here)), UNIT_AXES)
    second_sum = deep_alpha * normed.astype(jnp.float32) + down_val.astype(jnp.float32)
    hat_two, inverse_two = norm_parts(second_sum)
    layer_rows = low(hat_two * gain_two + shift_two)

    grad_own = out_grad.reshape(own, width).astype(jnp.float32)
    gain_two_grad = jnp.sum(grad_own * hat_two, axis=0)
    shift_two_grad = jnp.sum(grad_own, axis=0)
    d_second = norm_back(grad_own, hat_two, inverse_two, gain_two)
    down_low = gather(low(d_second), UNIT_AXES)
    d_active = dot(down_low, down_here)
    gate_low = low(d_active * up_val * gelu_slope)
    up_low = low(d_active * gelu_val)
    d_normed_part = low(contract_last(gate_low, gate_here) + contract_last(up_low, up_here))

    def unit_grad(left_side, right_side):
        part = low(contract_first(left_side, right_side))
        return part.reshape(4, 2, 2, 2, rows_own, unit_width)

    ffn_grads = (
        unit_grad(normed_all, gate_low),
        unit_grad(normed_all, up_low),
        unit_grad(down_low, active),
    )
    ffn_part, branch_all, d_first, norm_grads = close_units(
        ffn_grads,
        d_normed_part.reshape(unit_ways, own, width),
        d_second,
        hat_one,
        inverse_one,
        gain_one,
    )
    gain_one_grad, shift_one_grad = jnp.sum(norm_grads, axis=1)
    branch_all = branch_all.reshape(-1, width)
    small_grads = jnp.stack([gain_one_grad, shift_one_grad, gain_two_grad, shift_two_grad])
    small_grads = small_grads.reshape(4, 4, head_ways, rows_own).transpose(2, 1, 0, 3)
    small_grads = small_grads.reshape(head_ways, 4, 4 * rows_own // LANES, LANES)
    small_grads = jnp.pad(small_grads, ((0, 0), (0, 0), (0, -small_grads.shape[2] % 8), (0, 0)))

    proj_part = low(contract_first(context, branch_all)).reshape(4, rows_own, width)
    d_context = to_rows(low(contract_last(branch_all, proj_here)))
    d_context = d_context.reshape(x_size * micro_count, row_length, heads_here, HEAD_DIM)
    d_probs = pair("rqhd,rkhd->rhqk", d_context, value_rows)
    d_scores = low(probs * (d_probs - jnp.sum(probs * d_probs, axis=-1, keepdims=True)))
    d_query = pair("rhqk,rkhd->rqhd", d_scores, key_rows) * score_scale
    d_keys = pair("rhqk,rqhd->rkhd", d_scores, queries) * score_scale
    d_values = pair("rhqk,rqhd->rkhd", probs_low, d_context)
    d_mixed = low(
        jnp.stack(
            [rotate(d_query, cosine, -sine), rotate(d_keys, cosine, -sine), d_values], axis=2
        )
    )
    d_mixed = from_rows(d_mixed.reshape(x_size * micro_count, row_length, 3 * head_width))
    d_input = low(contract_last(d_mixed, qkv_here)).reshape(head_ways, own, width)
    qkv_part = low(contract_first(x_all, d_mixed))
    qkv_part, proj_part, small_grads, d_input = close_heads(
        qkv_part.reshape(4, 8, rows_own, 3 * head_width), proj_part, small_grads, d_input
    )
    d_input = deep_alpha * d_first + d_input
    small_grads = small_grads.ravel()[: 4 * rows_own].reshape(4, rows_own)
    qkv_grad = (
        qkv_part.reshape(head_ways, rows_own, 3, head_width)
        .transpose(1, 2, 0, 3)
        .reshape(rows_own, 3 * width)
        .astype(jnp.float32)
    )
    ffn_part = ffn_part.transpose(1, 2, 0, 3).reshape(3, rows_own, unit_ways * unit_width)
    gate_grad, up_grad, down_grad = (
        ffn_part[index, :, :units].astype(jnp.float32) for index in range(3)
    )
    return (
        layer_rows.reshape(micro_count, 1, pos_count, width),
        low(d_input).reshape(micro_count, 1, pos_count, width),
        qkv_grad,
        proj_part.astype(jnp.float32),
        gate_grad,
        up_grad,
        down_grad,
        small_grads[0],
        small_grads[1],
        small_grads[2],
        small_grads[3],
    )


def body(hidden_in, token_marks, out_grad, *weights):
    joined = lax.axis_size("zo")
    if joined == 1:
        return group_body(hidden_in, token_marks, out_grad, *weights)
    rows = weights[0].shape[0]
    width = hidden_in.shape[-1]
    groups = width // (joined * rows)
    group_place = lax.axis_index(ALL[1:])

    def inward(values):
        shape = values.shape
        values = values.reshape(shape[:-1] + (joined, groups, rows))
        return jnp.swapaxes(values, -3, -2).reshape(shape)

    def outward(values):
        shape = values.shape
        values = values.reshape(shape[:-1] + (groups, joined, rows))
        return jnp.swapaxes(values, -3, -2).reshape(shape)

    proj = gather(weights[1], ALL)
    proj = inward(lax.dynamic_slice_in_dim(proj, group_place * joined * rows, joined * rows))
    weights = [gather(weight, "zo") for weight in weights]
    weights[1] = proj
    outs = list(group_body(inward(hidden_in), token_marks, inward(out_grad), *weights))
    outs[:2] = outward(outs[0]), outward(outs[1])
    proj_grad = jnp.zeros((width, width), jnp.float32)
    proj_grad = lax.dynamic_update_slice_in_dim(
        proj_grad, outward(outs[3]), group_place * joined * rows, 0
    )
    outs[2:] = [scatter_sum(grad, "zo") for grad in outs[2:]]
    outs[3] = scatter_sum(proj_grad, ALL)
    return tuple(outs)


def solution(mesh):
    seq_size, ctx_size = mesh.shape["seq"], mesh.shape["ctx"]
    cores, x_size = 2, 2
    zi_size = math.gcd(4, seq_size // x_size)
    zo_size = seq_size // (x_size * zi_size)
    devices = np.asarray(mesh.devices).reshape(
        zo_size, zi_size, x_size, ctx_size // cores, cores
    )
    inner = Mesh(devices, ALL)
    tokens = P(None, ("zo", "zi", "x"), ("y", "c"), None)
    matrix = P(ALL, None)
    vector = P(ALL)
    return jax.shard_map(
        body,
        mesh=inner,
        in_specs=(tokens,) * 3 + (matrix,) * 5 + (vector,) * 4,
        out_specs=(tokens,) * 2 + (matrix,) * 5 + (vector,) * 4,
        check_vma=False,
    )
```

```python
import math

import jax
import jax.numpy as jnp
import numpy as np
from jax import lax
from jax.experimental import pallas as pl
from jax.experimental.pallas import tpu as pltpu
from jax.sharding import Mesh
from jax.sharding import PartitionSpec as P

HEAD_DIM = 128
LANES = 128

deep_alpha = 48.0**0.25
norm_eps = 1e-05
masked_score = -1e30

ALL = ("zo", "zi", "x", "y", "c")
HEAD_AXES = ("x", "y", "c")
UNIT_AXES = ("zi", "c")
HEAD_COPIES = ("zo", "zi")
UNIT_COPIES = ("zo", "x", "y")


def contract_last(left_side, right_side):
    return lax.dot_general(
        left_side, right_side, (((1,), (1,)), ((), ())), preferred_element_type=jnp.float32
    )


def contract_first(left_side, right_side):
    return lax.dot_general(
        left_side, right_side, (((0,), (0,)), ((), ())), preferred_element_type=jnp.float32
    )


def dot(left_side, right_side):
    return jnp.dot(left_side, right_side, preferred_element_type=jnp.float32)


def low(values):
    return values.astype(jnp.bfloat16)


def norm_parts(values):
    center = values - jnp.mean(values, axis=-1, keepdims=True)
    spread = jnp.mean(center * center, axis=-1, keepdims=True)
    inverse = lax.rsqrt(spread + norm_eps)
    return center * inverse, inverse


def norm_back(cotangent, hat, inverse, gain_vec):
    scaled = cotangent * gain_vec
    return (
        scaled
        - jnp.mean(scaled, axis=-1, keepdims=True)
        - hat * jnp.mean(scaled * hat, axis=-1, keepdims=True)
    ) * inverse


def rotary_tables(positions):
    half = HEAD_DIM // 2
    exponent = jnp.arange(half, dtype=jnp.float32) * (2.0 / HEAD_DIM)
    angles = positions.astype(jnp.float32)[..., None] * jnp.exp(-math.log(10000.0) * exponent)
    return (jnp.cos(angles), jnp.sin(angles))


def rotate(values, cosine, sine):
    half = HEAD_DIM // 2
    front, back = values[..., :half], values[..., half:]
    return jnp.concatenate(
        [front * cosine - back * sine, back * cosine + front * sine], axis=-1
    )


def gather(values, axes):
    return lax.all_gather(values, axes, axis=0, tiled=True)


def scatter_sum(values, axes):
    return lax.psum_scatter(values, axes, scatter_dimension=0, tiled=True)


def gelu_parts(value):
    phi = 0.5 * lax.erfc(-value * math.sqrt(0.5))
    density = jnp.exp(-0.5 * value * value) * (1.0 / math.sqrt(2.0 * math.pi))
    return value * phi, phi + value * density


MESH = pl.DeviceIdType.MESH


class Wire:
    def __init__(self, send_sems, recv_sems):
        self.send_sems, self.recv_sems = send_sems, recv_sems
        self.keys, self.sent = {}, []

    def number(self, key, span=1):
        if key not in self.keys:
            self.keys[key] = sum(size for _, size in self.keys.values()), span
        return self.keys[key][0]

    def copy(self, key, source, target, device, slot=0, span=1, recv=None):
        send = self.number(key, span)
        receive = send if recv is None else self.number(recv)
        return pltpu.make_async_remote_copy(
            src_ref=source,
            dst_ref=target,
            send_sem=self.send_sems.at[send],
            recv_sem=self.recv_sems.at[receive + slot],
            device_id=device,
            device_id_type=MESH,
        )

    def send(self, key, source, target, device, when=None, recv=None):
        copy = self.copy(key, source, target, device, recv=recv)
        if when is None:
            copy.start()
        else:
            pl.when(when)(copy.start)
        self.sent.append((copy, when))

    def send_to_slot(self, key, source, target, device, slot, span, when):
        copy = self.copy(key, source, target, device, slot, span)
        pl.when(when)(copy.start)
        self.sent.append((copy, when))

    def arrive(self, key, target, device, when=None):
        copy = self.copy(key, target, target, device)
        if when is None:
            copy.wait_recv()
        else:
            pl.when(when)(copy.wait_recv)

    def arrive_slot(self, key, target, device, slot, span, when):
        pl.when(when)(self.copy(key, target, target, device, slot, span).wait_recv)

    def drain(self):
        for copy, when in self.sent:
            if when is None:
                copy.wait_send()
            else:
                pl.when(when)(copy.wait_send)


def flip(value, bit):
    return 1 - value if bit else value


def enter(devices):
    barrier = pltpu.get_barrier_semaphore()
    for device in devices:
        pl.semaphore_signal(barrier, inc=1, device_id=device, device_id_type=MESH)
    pl.semaphore_wait(barrier, len(devices))


class Place:
    def __init__(self):
        self.zo, self.zi, self.x, self.y, self.c = (lax.axis_index(name) for name in ALL)
        self.rank = self.x * 4 + self.y * 2 + self.c
        self.unit = self.zi * 2 + self.c

    def plane(self, delta):
        dx, dy, dc = delta >> 2 & 1, delta >> 1 & 1, delta & 1
        x, y, c = flip(self.x, dx), flip(self.y, dy), flip(self.c, dc)
        return (self.zo, self.zi, x, y, c), x * 4 + y * 2 + c

    def column(self, step):
        other = lax.rem(self.unit + step + 8, 8)
        return (self.zo, other // 2, self.x, self.y, lax.rem(other, 2)), other

    def ends(self):
        return self.line(jnp.minimum(self.zi + 1, 3)), self.line(jnp.maximum(self.zi - 1, 0))

    def line(self, z):
        return (self.zo, z, self.x, self.y, self.c)

    def column_neighbours(self):
        return [self.line(z) for z in self.others()] + [self.plane(1)[0]]

    def others(self):
        return [lax.rem(self.zi + step, 4) for step in (1, 2, 3)]

    def neighbours(self):
        plane = [self.plane(delta)[0] for delta in range(1, 8)]
        column = []
        for dz in range(1, 4):
            z = lax.rem(self.zi + dz, 4)
            column += [(self.zo, z, self.x, self.y, core) for core in (0, 1)]
        return plane + column


def gather_kernel(
    qkv_in,
    ffn_in,
    proj_in,
    x_in,
    small_in,
    qkv_out,
    ffn_out,
    proj_out,
    x_out,
    small_out,
    send_sems,
    recv_sems,
    own_sems,
):
    at = Place()
    wire = Wire(send_sems, recv_sems)
    enter(at.neighbours())
    x_side, y_side, core_side = at.plane(4)[0], at.plane(2)[0], at.plane(1)[0]
    half = x_in.shape[0] // 2

    own = [
        pltpu.make_async_copy(x_in, x_out.at[at.rank], own_sems.at[0]),
        pltpu.make_async_copy(qkv_in.at[at.rank], qkv_out.at[at.zi, at.rank], own_sems.at[1]),
        pltpu.make_async_copy(
            ffn_in.at[at.unit], ffn_out.at[:, at.zi, at.x, at.y, at.c], own_sems.at[2]
        ),
        pltpu.make_async_copy(small_in, small_out.at[at.zi, at.rank], own_sems.at[3]),
    ]
    for copy in own:
        copy.start()

    chunk = at.y * 2 + at.c
    holder = at.zi * 2 + at.x
    proj_home = at.rank // 2
    proj_first = at.rank == holder
    proj_own = pltpu.make_async_copy(proj_in, proj_out.at[chunk], own_sems.at[4])
    pl.when(proj_first)(proj_own.start)

    def small_first():
        for delta in range(1, 8):
            device, _ = at.plane(delta)
            slot = small_out.at[at.zi, at.rank]
            wire.send(("s", delta), small_in, slot, device)

    small_first()

    for step in (1, 7, 2, 6, 3, 5, 4):
        device, other = at.column(step)
        slot = ffn_out.at[:, at.zi, at.x, at.y, at.c]
        wire.send(("f", step), ffn_in.at[other], slot, device)
    for delta in range(1, 8):
        device, other = at.plane(delta)
        wire.send(("q", delta), qkv_in.at[other], qkv_out.at[at.zi, at.rank], device)
    holder_device = (at.zo, at.zi, holder // 4, lax.rem(holder // 2, 2), lax.rem(holder, 2))
    wire.send_to_slot("p", proj_in, proj_out.at[chunk], holder_device, chunk, 4, at.rank != holder)
    wire.send("xx", x_in, x_out.at[at.rank], x_side)
    wire.send("xy", x_in, x_out.at[at.rank], y_side)
    wire.send("xc0", x_in, x_out.at[at.rank], core_side)
    for copy in own:
        copy.wait()
    pl.when(proj_first)(proj_own.wait)

    def small_second():
        for delta in range(1, 8):
            device, other = at.plane(delta)
            wire.arrive(("s", delta), small_out.at[at.zi, other], device)
        for dz in range(1, 4):
            device = at.line(lax.rem(at.zi + dz, 4))
            wire.send(("t", dz), small_out.at[at.zi], small_out.at[at.zi], device)

    def small_last():
        for dz in range(1, 4):
            z = lax.rem(at.zi - dz + 4, 4)
            wire.arrive(("t", dz), small_out.at[z], at.line(z))

    def proj_start():
        for slot in range(4):
            source = (at.zo, at.zi, lax.rem(at.rank, 2), slot // 2, slot % 2)
            mine = (at.zi == proj_home) & ((chunk != slot) | (at.rank != holder))
            wire.arrive_slot("p", proj_out.at[slot], source, slot, 4, mine)
        wire.send("pu0", proj_out, proj_out, up, (at.zi == proj_home) & (at.zi < 3))
        wire.send("pd0", proj_out, proj_out, down, (at.zi == proj_home) & (at.zi > 0))

    def proj_relay():
        above, below = at.zi > proj_home, at.zi < proj_home
        wire.arrive("pu0", proj_out, down, above)
        wire.arrive("pd0", proj_out, up, below)
        wire.send("pu1", proj_out, proj_out, up, above & (at.zi < 3), recv="pu0")
        wire.send("pd1", proj_out, proj_out, down, below & (at.zi > 0), recv="pd0")

    def qkv_slot(z, delta):
        return qkv_out.at[jnp.clip(z, 0, 3), at.plane(delta)[1]]

    up, down = at.line(jnp.minimum(at.zi + 1, 3)), at.line(jnp.maximum(at.zi - 1, 0))

    def qkv_hop(hop, delta):
        below, above = qkv_slot(at.zi - hop, delta), qkv_slot(at.zi + hop, delta)
        if hop == 0:
            if delta:
                wire.arrive(("q", delta), below, at.plane(delta)[0])
        else:
            wire.arrive(("up", hop - 1, delta), below, down, at.zi >= hop)
            wire.arrive(("down", hop - 1, delta), above, up, at.zi <= 3 - hop)
        if hop < 3:
            wire.send(("up", hop, delta), below, below, up, (at.zi >= hop) & (at.zi < 3))
            wire.send(("down", hop, delta), above, above, down, (at.zi <= 3 - hop) & (at.zi > 0))

    def ffn_slot(step, x, y):
        source = lax.rem(at.unit - step + 8, 8)
        return ffn_out.at[:, source // 2, x, y, lax.rem(source, 2)]

    def ffn_first(step):
        slot = ffn_slot(step, at.x, at.y)
        if step:
            wire.arrive(("f", step), slot, at.column(-step)[0])
        wire.send(("fx", step), slot, slot, x_side)
        wire.send(("fy", step), slot, slot, y_side)

    def ffn_second(step, turn):
        from_x, from_y = ffn_slot(step, 1 - at.x, at.y), ffn_slot(step, at.x, 1 - at.y)
        wire.arrive(("fx", step), from_x, x_side)
        wire.arrive(("fy", step), from_y, y_side)
        if turn % 2:
            wire.send(("fd", step), from_x, from_x, y_side)
        else:
            wire.send(("fd", step), from_y, from_y, x_side)

    from_x, from_y, from_xy = (at.plane(delta)[1] for delta in (4, 2, 6))
    low_half, high_half = pl.ds(0, half), pl.ds(half, half)
    ffn_first(0)
    wire.arrive("xx", x_out.at[from_x], x_side)
    wire.send("xd0", x_out.at[from_x, low_half], x_out.at[from_x, low_half], y_side)
    wire.send("xc1", x_out.at[from_x], x_out.at[from_x], core_side)
    wire.arrive("xy", x_out.at[from_y], y_side)
    wire.send("xd1", x_out.at[from_y, high_half], x_out.at[from_y, high_half], x_side)
    wire.send("xc2", x_out.at[from_y], x_out.at[from_y], core_side)
    small_second()
    for delta in range(8):
        qkv_hop(0, delta)
    proj_start()
    wire.arrive("xd0", x_out.at[from_xy, low_half], y_side)
    wire.arrive("xd1", x_out.at[from_xy, high_half], x_side)
    wire.send("xc3", x_out.at[from_xy], x_out.at[from_xy], core_side)

    steps = (1, 7, 2, 6, 3, 5, 4)
    ffn_second(0, 0)
    for turn, step in enumerate(steps):
        ffn_first(step)
        qkv_hop(1, turn)
        if turn >= 2:
            ffn_second(steps[turn - 2], turn - 2 + 1)
    qkv_hop(1, 7)
    proj_relay()
    for delta in range(8):
        qkv_hop(2, delta)
        if delta < 2:
            ffn_second(steps[5 + delta], 5 + delta + 1)
    for delta in range(8):
        qkv_hop(3, delta)
    for index, delta in enumerate((1, 5, 3, 7)):
        other = at.plane(delta)[1]
        wire.arrive("xc%d" % index, x_out.at[other], core_side)
    for step in range(8):
        wire.arrive(("fd", step), ffn_slot(step, 1 - at.x, 1 - at.y), x_side)
    small_last()
    wire.drain()


ANY = pl.BlockSpec(memory_space=pl.ANY)
VMEM = pl.BlockSpec(memory_space=pltpu.VMEM)


def comm_params(number):
    return pltpu.CompilerParams(
        collective_id=number, has_side_effects=True, vmem_limit_bytes=63 * 2**20
    )


def gather_weights(qkv_parts, ffn_parts, proj_own, x_own, small):
    _, rows_own, qkv_width = qkv_parts.shape
    unit_width = ffn_parts.shape[-1]
    own, width = x_own.shape
    low_type = jnp.bfloat16
    return pl.pallas_call(
        gather_kernel,
        out_shape=(
            jax.ShapeDtypeStruct((4, 8, rows_own, qkv_width), low_type),
            jax.ShapeDtypeStruct((3, 4, 2, 2, 2, rows_own, unit_width), low_type),
            jax.ShapeDtypeStruct((4, rows_own, width), low_type),
            jax.ShapeDtypeStruct((8, own, width), low_type),
            jax.ShapeDtypeStruct((4, 8) + small.shape, small.dtype),
        ),
        in_specs=[VMEM] * 5,
        out_specs=(ANY,) * 5,
        scratch_shapes=[
            pltpu.SemaphoreType.DMA((128,)),
            pltpu.SemaphoreType.DMA((128,)),
            pltpu.SemaphoreType.DMA((5,)),
        ],
        compiler_params=comm_params(1),
        cost_estimate=pl.CostEstimate(
            flops=0, bytes_accessed=400_000_000, transcendentals=0
        ),
        name="gather_weights",
    )(qkv_parts, ffn_parts, proj_own, x_own, small)


def add_rows(out, *terms):
    step = 32

    @pl.loop(0, out.shape[0] // step)
    def _(index):
        part = pl.ds(pl.multiple_of(index * step, step), step)
        whole = terms[0][part].astype(jnp.float32)
        for term in terms[1:]:
            whole = whole + term[part].astype(jnp.float32)
        out[part] = whole.astype(out.dtype)


def column_scatter_flow(
    at, wire, tag, part, out, core_in, core_sum, up_in, down_in, up_sum, down_sum
):
    core_side = at.plane(1)[0]
    up, down = at.ends()
    for goal in (3, 0, 2, 1):
        source = part.at[goal * 2 + 1 - at.c]
        wire.send(("rc", tag, goal), source, core_in.at[goal], core_side)
    yield
    for goal in (3, 0, 2, 1):
        wire.arrive(("rc", tag, goal), core_in.at[goal], core_side)
        add_rows(core_sum.at[goal], part.at[goal * 2 + at.c], core_in.at[goal])
        source = core_sum.at[goal]
        if goal > 0:
            wire.send(("ru", tag, goal), source, up_in.at[goal], up, at.zi == 0)
        if goal < 3:
            wire.send(("rd", tag, goal), source, down_in.at[goal], down, at.zi == 3)

    def climb(goal):
        wire.arrive(("ru", tag, goal), up_in.at[goal], down)
        add_rows(up_sum.at[goal], core_sum.at[goal], up_in.at[goal])

    def descend(goal):
        wire.arrive(("rd", tag, goal), down_in.at[goal], up)
        add_rows(down_sum.at[goal], core_sum.at[goal], down_in.at[goal])

    for goal in (3, 2):
        yield
        back = 3 - goal
        passing = (at.zi > 0) & (at.zi < goal)
        pl.when(passing)(lambda: climb(goal))
        key = "ru", tag, goal
        wire.send(("ru2", tag, goal), up_sum.at[goal], up_in.at[goal], up, passing, recv=key)
        passing = (at.zi < 3) & (at.zi > back)
        pl.when(passing)(lambda: descend(back))
        key = "rd", tag, back
        wire.send(("rd2", tag, back), down_sum.at[back], down_in.at[back], down, passing, recv=key)
    yield
    add_rows(out, core_sum.at[at.zi])

    def last(key, source, device):
        wire.arrive(key, source, device)
        add_rows(out, out, source)

    for goal in range(4):
        if goal > 0:
            pl.when(at.zi == goal)(lambda: last(("ru", tag, goal), up_in.at[goal], down))
        if goal < 3:
            pl.when(at.zi == goal)(lambda: last(("rd", tag, goal), down_in.at[goal], up))


def column_gather_flow(at, wire, tag, own_in, out, own_sem):
    core_side = at.plane(1)[0]
    up, down = at.ends()

    def slot(z, c):
        return out.at[jnp.clip(z, 0, 3) * 2 + c]

    mine = slot(at.zi, at.c)
    wire.send(("gu", tag, 0), own_in, mine, up, at.zi < 3)
    wire.send(("gd", tag, 0), own_in, mine, down, at.zi > 0)
    wire.send(("gc", tag), own_in, mine, core_side)
    own = pltpu.make_async_copy(own_in, mine, own_sem)
    own.start()
    for hop in (1, 2, 3):
        yield
        below, above = slot(at.zi - hop, at.c), slot(at.zi + hop, at.c)
        has_below, has_above = at.zi >= hop, at.zi <= 3 - hop
        wire.arrive(("gu", tag, hop - 1), below, down, has_below)
        if hop < 3:
            wire.send(("gu", tag, hop), below, below, up, has_below & (at.zi < 3))
        wire.send(("gcu", tag, hop), below, below, core_side, has_below)
        wire.arrive(("gd", tag, hop - 1), above, up, has_above)
        if hop < 3:
            wire.send(("gd", tag, hop), above, above, down, has_above & (at.zi > 0))
        wire.send(("gcd", tag, hop), above, above, core_side, has_above)
    yield
    own.wait()
    wire.arrive(("gc", tag), slot(at.zi, 1 - at.c), core_side)
    for hop in (1, 2, 3):
        below, above = slot(at.zi - hop, 1 - at.c), slot(at.zi + hop, 1 - at.c)
        wire.arrive(("gcu", tag, hop), below, core_side, at.zi >= hop)
        wire.arrive(("gcd", tag, hop), above, core_side, at.zi <= 3 - hop)


def column_scratch(own, width):
    return [pltpu.VMEM((4, own, width), jnp.bfloat16)] * 6


def plane_scatter_flow(at, wire, part, out, core_in, core_sum, side_in, side_sum, last_in):
    x_side, y_side, core_side = at.plane(4)[0], at.plane(2)[0], at.plane(1)[0]
    half = out.shape[1] // 2
    halves = (pl.ds(0, half), pl.ds(half, half))
    order = ((1, 1), (1, 0), (0, 1), (0, 0))

    def place(dx, dy):
        return flip(at.x, dx), flip(at.y, dy)

    for dx, dy in order:
        x, y = place(dx, dy)
        other = x * 4 + y * 2 + 1 - at.c
        wire.send(("c", dx, dy), part.at[other], core_in.at[dx * 2 + dy], core_side)
    yield
    for dx, dy in order:
        x, y = place(dx, dy)
        mine = x * 4 + y * 2 + at.c
        slot = dx * 2 + dy
        wire.arrive(("c", dx, dy), core_in.at[slot], core_side)
        add_rows(core_sum.at[slot], part.at[mine], core_in.at[slot])
        if dx:
            source = core_sum.at[slot, :, halves[0]]
            wire.send(("sa", dy), source, side_in.at[0, dy], x_side)
        if dy:
            source = core_sum.at[slot, :, halves[1]]
            wire.send(("sb", dx), source, side_in.at[1, dx], y_side)
    yield
    wire.arrive(("sa", 1), side_in.at[0, 1], x_side)
    add_rows(side_sum.at[0], core_sum.at[1, :, halves[0]], side_in.at[0, 1])
    wire.send("sy", side_sum.at[0], last_in.at[0], y_side)
    wire.arrive(("sb", 1), side_in.at[1, 1], y_side)
    add_rows(side_sum.at[1], core_sum.at[2, :, halves[1]], side_in.at[1, 1])
    wire.send("sx", side_sum.at[1], last_in.at[1], x_side)
    yield
    wire.arrive(("sa", 0), side_in.at[0, 0], x_side)
    wire.arrive(("sb", 0), side_in.at[1, 0], y_side)
    wire.arrive("sy", last_in.at[0], y_side)
    terms = core_sum.at[0, :, halves[0]], side_in.at[0, 0], last_in.at[0]
    add_rows(out.at[:, halves[0]], *terms)
    wire.arrive("sx", last_in.at[1], x_side)
    terms = core_sum.at[0, :, halves[1]], side_in.at[1, 0], last_in.at[1]
    add_rows(out.at[:, halves[1]], *terms)


def plane_scratch(own, width):
    return [
        pltpu.VMEM((4, own, width), jnp.bfloat16),
        pltpu.VMEM((4, own, width), jnp.bfloat16),
        pltpu.VMEM((2, 2, own, width // 2), jnp.bfloat16),
        pltpu.VMEM((2, own, width // 2), jnp.bfloat16),
        pltpu.VMEM((2, own, width // 2), jnp.bfloat16),
    ]


def plane_gather_flow(at, wire, own_in, out, own_sem):
    x_side, y_side, core_side = at.plane(4)[0], at.plane(2)[0], at.plane(1)[0]
    half = own_in.shape[0] // 2
    mine = out.at[at.rank]
    wire.send("gx", own_in, mine, x_side)
    wire.send("gy", own_in, mine, y_side)
    wire.send("gc0", own_in, mine, core_side)
    own = pltpu.make_async_copy(own_in, mine, own_sem)
    own.start()
    yield
    from_x, from_y, from_xy = (at.plane(delta)[1] for delta in (4, 2, 6))
    low_half, high_half = pl.ds(0, half), pl.ds(half, half)
    wire.arrive("gx", out.at[from_x], x_side)
    wire.send("gd0", out.at[from_x, low_half], out.at[from_x, low_half], y_side)
    wire.send("gc1", out.at[from_x], out.at[from_x], core_side)
    wire.arrive("gy", out.at[from_y], y_side)
    wire.send("gd1", out.at[from_y, high_half], out.at[from_y, high_half], x_side)
    wire.send("gc2", out.at[from_y], out.at[from_y], core_side)
    yield
    wire.arrive("gd0", out.at[from_xy, low_half], y_side)
    wire.arrive("gd1", out.at[from_xy, high_half], x_side)
    wire.send("gc3", out.at[from_xy], out.at[from_xy], core_side)
    own.wait()
    for index, delta in enumerate((1, 5, 3, 7)):
        wire.arrive("gc%d" % index, out.at[at.plane(delta)[1]], core_side)


def turn_kernel(
    part,
    normed,
    out_grad,
    gain,
    shift,
    layer_out,
    d_second,
    down_out,
    norm_out,
    second,
    down_low,
    core_in,
    core_sum,
    up_in,
    down_in,
    up_sum,
    down_sum,
    send_sems,
    recv_sems,
    own_sems,
):
    at = Place()
    wire = Wire(send_sems, recv_sems)
    enter(at.column_neighbours())
    half = normed.shape[0] // 2
    scratch = core_in, core_sum, up_in, down_in, up_sum, down_sum

    def norm_rows(start):
        count = 16

        @pl.loop(0, half // count)
        def _(index):
            rows = pl.ds(pl.multiple_of(start + index * count, count), count)
            whole = deep_alpha * normed[rows].astype(jnp.float32) + second[rows]
            near, inverse = norm_parts(whole)
            layer_out[rows] = (near * gain[...] + shift[...]).astype(jnp.bfloat16)
            cotangent = out_grad[rows].astype(jnp.float32)
            result = norm_back(cotangent, near, inverse, gain[...])
            d_second[rows] = result
            down_low[rows] = result.astype(jnp.bfloat16)
            along = cotangent * near
            norm_out[0] += along[:8] + along[8:]
            norm_out[1] += cotangent[:8] + cotangent[8:]

    scatters, gathers = [], []
    for index in range(2):
        rows = pl.ds(index * half, half)
        views = [ref.at[:, rows] for ref in scratch]
        scatters.append(
            column_scatter_flow(at, wire, index, part.at[:, rows], second.at[rows], *views)
        )
        gathers.append(
            column_gather_flow(
                at, wire, index, down_low.at[rows], down_out.at[:, rows], own_sems.at[index]
            )
        )
    norm_out[...] = jnp.zeros_like(norm_out)
    for flow in scatters:
        next(flow)
    for flow in scatters:
        next(flow)
    for _ in scatters[0]:
        pass
    norm_rows(0)
    next(gathers[0])
    next(scatters[1])
    next(gathers[0])
    for _ in scatters[1]:
        pass
    norm_rows(half)
    next(gathers[1])
    next(gathers[0])
    next(gathers[1])
    next(gathers[0])
    for flow in gathers[::-1]:
        for _ in flow:
            pass
    wire.drain()


def turn(part, normed, out_grad, gain, shift):
    _, own, width = part.shape
    low_type = jnp.bfloat16
    return pl.pallas_call(
        turn_kernel,
        out_shape=(
            jax.ShapeDtypeStruct((own, width), low_type),
            jax.ShapeDtypeStruct((own, width), jnp.float32),
            jax.ShapeDtypeStruct((8, own, width), low_type),
            jax.ShapeDtypeStruct((2, 8, width), jnp.float32),
        ),
        in_specs=[VMEM] * 5,
        out_specs=(VMEM, VMEM, ANY, VMEM),
        scratch_shapes=[
            pltpu.VMEM((own, width), jnp.float32),
            pltpu.VMEM((own, width), low_type),
        ]
        + column_scratch(own, width)
        + [
            pltpu.SemaphoreType.DMA((72,)),
            pltpu.SemaphoreType.DMA((72,)),
            pltpu.SemaphoreType.DMA((2,)),
        ],
        compiler_params=comm_params(5),
        name="turn",
    )(part, normed, out_grad, gain, shift)


def close_units_kernel(
    gate_in,
    raise_in,
    lower_in,
    part,
    d_second,
    hat,
    inverse,
    gain,
    ffn_out,
    branch_out,
    d_first,
    norm_out,
    first_in,
    second_sum,
    second_in,
    total,
    d_normed,
    branch_low,
    core_in,
    core_sum,
    up_in,
    down_in,
    up_sum,
    down_sum,
    send_sems,
    recv_sems,
    own_sems,
):
    at = Place()
    wire = Wire(send_sems, recv_sems)
    enter(at.neighbours())
    x_side, y_side = at.plane(4)[0], at.plane(2)[0]
    steps = (4, 3, 5, 2, 6, 1, 7, 0)
    sources = gate_in, raise_in, lower_in

    def owner(step):
        other = at.column(step)[1]
        return other // 2, lax.rem(other, 2)

    def ffn_first(turn):
        step = steps[turn]
        z, c = owner(step)
        for index, source in enumerate(sources):
            if turn % 2:
                block, device = source.at[z, 1 - at.x, :, c], x_side
            else:
                block, device = source.at[z, :, 1 - at.y, c], y_side
            wire.send(("a", step, index), block, first_in.at[step, index], device)

    def ffn_second(turn):
        step = steps[turn]
        z, c = owner(step)
        for index, source in enumerate(sources):
            if turn % 2:
                wire.arrive(("a", step, index), first_in.at[step, index], x_side)
                terms = source.at[z, at.x, 1 - at.y, c], first_in.at[step, index, 1 - at.y]
            else:
                wire.arrive(("a", step, index), first_in.at[step, index], y_side)
                terms = source.at[z, 1 - at.x, at.y, c], first_in.at[step, index, 1 - at.x]
            add_rows(second_sum.at[step, index], *terms)
        wire.send(
            ("b", step), second_sum.at[step], second_in.at[step], y_side if turn % 2 else x_side
        )

    own_total = pltpu.make_async_copy(total.at[0], ffn_out.at[at.unit], own_sems.at[0])

    def ffn_last(turn):
        step = steps[turn]
        z, c = owner(step)
        near = at.y if turn % 2 else at.x
        wire.arrive(("b", step), second_in.at[step], x_side)
        for index, source in enumerate(sources):
            add_rows(
                total.at[step, index],
                source.at[z, at.x, at.y, c],
                first_in.at[step, index, near],
                second_in.at[step, index],
            )
        if step:
            wire.send(("f", step), total.at[step], ffn_out.at[at.unit], at.column(step)[0])
        else:
            own_total.start()

    def norm_rows():
        count = 16
        norm_out[...] = jnp.zeros_like(norm_out)

        @pl.loop(0, hat.shape[0] // count)
        def _(index):
            rows = pl.ds(pl.multiple_of(index * count, count), count)
            cotangent = deep_alpha * d_second[rows] + d_normed[rows]
            near = hat[rows]
            result = norm_back(cotangent, near, inverse[rows], gain[...])
            d_first[rows] = result
            branch_low[rows] = result.astype(jnp.bfloat16)
            along = cotangent * near
            norm_out[0] += along[:8] + along[8:]
            norm_out[1] += cotangent[:8] + cotangent[8:]

    scatter = column_scatter_flow(
        at, wire, 0, part, d_normed, core_in, core_sum, up_in, down_in, up_sum, down_sum
    )
    next(scatter)
    for turn in range(5):
        ffn_first(turn)
    next(scatter)
    next(scatter)
    ffn_second(0)
    ffn_first(5)
    ffn_second(1)
    ffn_first(6)
    next(scatter)
    ffn_second(2)
    ffn_first(7)
    ffn_second(3)
    for _ in scatter:
        pass
    norm_rows()
    spread = plane_gather_flow(at, wire, branch_low, branch_out, own_sems.at[1])
    next(spread)
    ffn_last(0)
    ffn_last(1)
    ffn_second(4)
    ffn_last(2)
    ffn_second(5)
    ffn_last(3)
    next(spread)
    ffn_second(6)
    ffn_second(7)
    ffn_last(4)
    for _ in spread:
        pass
    for turn in range(5, 8):
        ffn_last(turn)
    own_total.wait()
    for step in steps:
        if step:
            device, other = at.column(-step)
            wire.arrive(("f", step), ffn_out.at[other], device)
    wire.drain()


def close_units(grads, part, d_second, hat, inverse, gain):
    rows_own, unit_width = grads[0].shape[-2:]
    _, own, width = part.shape
    low_type = jnp.bfloat16
    block = (rows_own, unit_width)
    return pl.pallas_call(
        close_units_kernel,
        out_shape=(
            jax.ShapeDtypeStruct((8, 3) + block, low_type),
            jax.ShapeDtypeStruct((8, own, width), low_type),
            jax.ShapeDtypeStruct((own, width), jnp.float32),
            jax.ShapeDtypeStruct((2, 8, width), jnp.float32),
        ),
        in_specs=[VMEM] * 8,
        out_specs=(ANY, ANY, VMEM, VMEM),
        scratch_shapes=[
            pltpu.VMEM((8, 3, 2) + block, low_type),
            pltpu.VMEM((8, 3) + block, low_type),
            pltpu.VMEM((8, 3) + block, low_type),
            pltpu.VMEM((8, 3) + block, low_type),
            pltpu.VMEM((own, width), jnp.float32),
            pltpu.VMEM((own, width), low_type),
        ]
        + column_scratch(own, width)
        + [
            pltpu.SemaphoreType.DMA((80,)),
            pltpu.SemaphoreType.DMA((80,)),
            pltpu.SemaphoreType.DMA((2,)),
        ],
        compiler_params=comm_params(3),
        name="close_units",
    )(*grads, part, d_second, hat, inverse, gain)


def close_heads_kernel(
    qkv_in,
    proj_in,
    small_in,
    part,
    qkv_out,
    proj_out,
    small_out,
    d_input,
    proj_below,
    proj_above,
    proj_sum,
    small_plane,
    small_mid,
    small_line,
    up_in,
    down_in,
    up_sum,
    down_sum,
    qkv_total,
    core_in,
    core_sum,
    side_in,
    side_sum,
    last_in,
    send_sems,
    recv_sems,
    own_sems,
):
    at = Place()
    wire = Wire(send_sems, recv_sems)
    enter(at.neighbours())
    scatter = plane_scatter_flow(
        at, wire, part, d_input, core_in, core_sum, side_in, side_sum, last_in
    )
    next(scatter)

    def add(*terms):
        whole = terms[0].astype(jnp.float32)
        for term in terms[1:]:
            whole = whole + term.astype(jnp.float32)
        return whole.astype(jnp.bfloat16)

    for delta in range(1, 8):
        device, other = at.plane(delta)
        wire.send(("s", delta), small_in.at[other], small_plane.at[at.rank], device)

    def small_second():
        whole = small_in[at.rank]
        for delta in range(1, 8):
            device, other = at.plane(delta)
            wire.arrive(("s", delta), small_plane.at[other], device)
            whole = whole + small_plane[other]
        small_mid[...] = whole
        for dz in range(1, 4):
            z = lax.rem(at.zi + dz, 4)
            wire.send(("t", dz), small_mid.at[z], small_line.at[at.zi], at.line(z))

    def small_last():
        whole = small_mid[at.zi]
        for dz in range(1, 4):
            z = lax.rem(at.zi - dz + 4, 4)
            wire.arrive(("t", dz), small_line.at[z], at.line(z))
            whole = whole + small_line[z]
        small_out[...] = whole

    pieces = 4
    wide = 8 // pieces
    up, down = at.line(jnp.minimum(at.zi + 1, 3)), at.line(jnp.maximum(at.zi - 1, 0))

    def qkv_pass(goal, piece):
        part = pl.ds(piece * wide, wide)

        if goal > 0:

            @pl.when(at.zi < goal)
            def _():
                @pl.when(at.zi == 0)
                def _():
                    up_sum[goal, part] = qkv_in[goal, part]

                @pl.when(at.zi > 0)
                def _():
                    wire.arrive(("u", goal, piece), up_in.at[goal, part], down)
                    up_sum[goal, part] = add(qkv_in[goal, part], up_in[goal, part])

            wire.send(
                ("u", goal, piece),
                up_sum.at[goal, part],
                up_in.at[goal, part],
                up,
                at.zi < goal,
            )
        back = 3 - goal
        if back < 3:

            @pl.when(at.zi > back)
            def _():
                @pl.when(at.zi == 3)
                def _():
                    down_sum[back, part] = qkv_in[back, part]

                @pl.when(at.zi < 3)
                def _():
                    wire.arrive(("d", back, piece), down_in.at[back, part], up)
                    down_sum[back, part] = add(qkv_in[back, part], down_in[back, part])

            wire.send(
                ("d", back, piece),
                down_sum.at[back, part],
                down_in.at[back, part],
                down,
                at.zi > back,
            )

    proj_home = at.rank // 2

    def proj_add(slot, *terms):
        add_rows(proj_sum.at[slot], *(term.at[slot] for term in terms))

    below, above = at.zi < proj_home, at.zi > proj_home
    ends = (at.zi == 0) | (at.zi == 3)

    def proj_pass(slot):
        under, over = proj_below.at[slot], proj_above.at[slot]
        wire.send(("pu", slot), proj_in.at[slot], under, up, below & ends)
        wire.send(("pd", slot), proj_in.at[slot], over, down, above & ends)

        def climb():
            wire.arrive(("pu", slot), under, down)
            proj_add(slot, proj_in, proj_below)

        def descend():
            wire.arrive(("pd", slot), over, up)
            proj_add(slot, proj_in, proj_above)

        pl.when(below & (at.zi > 0))(climb)
        pl.when(above & (at.zi < 3))(descend)
        source = proj_sum.at[slot]
        key = "pu", slot
        wire.send(("pu2", slot), source, under, up, below & (at.zi > 0), recv=key)
        key = "pd", slot
        wire.send(("pd2", slot), source, over, down, above & (at.zi < 3), recv=key)

    holder = at.zi * 2 + at.x
    chunk = at.y * 2 + at.c
    holder_device = (at.zo, at.zi, holder // 4, lax.rem(holder // 2, 2), lax.rem(holder, 2))

    def proj_last():
        home = at.zi == proj_home
        for slot in range(4):
            under, over = proj_below.at[slot], proj_above.at[slot]

            def first():
                wire.arrive(("pu", slot), under, down)
                proj_add(slot, proj_in, proj_below)

            def only():
                wire.arrive(("pd", slot), over, up)
                proj_add(slot, proj_in, proj_above)

            def both():
                wire.arrive(("pd", slot), over, up)
                proj_add(slot, proj_sum, proj_above)

            pl.when(home & (at.zi > 0))(first)
            pl.when(home & (at.zi == 0))(only)
            pl.when(home & (at.zi > 0) & (at.zi < 3))(both)
            target = (at.zo, at.zi, lax.rem(at.rank, 2), slot // 2, slot % 2)
            other = (chunk != slot) | (at.rank != holder)
            wire.send(("o", slot), proj_sum.at[slot], proj_out, target, home & other, recv="o")
        own = pltpu.make_async_copy(proj_sum.at[chunk], proj_out, own_sems.at[2])
        pl.when(home & (at.rank == holder))(own.start)
        pl.when(home & (at.rank == holder))(own.wait)

    def qkv_last(piece):
        part = pl.ds(piece * wide, wide)
        for goal in range(4):

            @pl.when(at.zi == goal)
            def _():
                terms = [qkv_in[goal, part]]
                if goal > 0:
                    wire.arrive(("u", goal, piece), up_in.at[goal, part], down)
                    terms.append(up_in[goal, part])
                if goal < 3:
                    wire.arrive(("d", goal, piece), down_in.at[goal, part], up)
                    terms.append(down_in[goal, part])
                qkv_total[part] = add(*terms)

    for piece in range(pieces):
        qkv_pass(3, piece)
        if piece == 0:
            next(scatter)
    for slot in range(4):
        proj_pass(slot)
    next(scatter)
    small_second()
    for piece in range(pieces):
        qkv_pass(2, piece)
    for _ in scatter:
        pass
    for piece in range(pieces):
        qkv_pass(1, piece)
    proj_last()
    for piece in range(pieces):
        qkv_last(piece)
    own_qkv = pltpu.make_async_copy(
        qkv_total.at[at.rank], qkv_out.at[at.rank], own_sems.at[1]
    )
    own_qkv.start()
    for delta in range(1, 8):
        device, other = at.plane(delta)
        wire.send(("q", delta), qkv_total.at[other], qkv_out.at[at.rank], device)
    own_qkv.wait()
    for delta in range(1, 8):
        device, other = at.plane(delta)
        wire.arrive(("q", delta), qkv_out.at[other], device)
    small_last()
    wire.arrive("o", proj_out, holder_device, at.rank != holder)
    wire.drain()


def close_heads(qkv_part, proj_part, small_part, part):
    _, _, rows_own, qkv_width = qkv_part.shape
    _, own, width = part.shape
    low_type = jnp.bfloat16
    line = (4, 8, rows_own, qkv_width)
    small_shape = small_part.shape[1:]
    return pl.pallas_call(
        close_heads_kernel,
        out_shape=(
            jax.ShapeDtypeStruct((8, rows_own, qkv_width), low_type),
            jax.ShapeDtypeStruct((rows_own, width), low_type),
            jax.ShapeDtypeStruct(small_shape[1:], small_part.dtype),
            jax.ShapeDtypeStruct((own, width), jnp.float32),
        ),
        in_specs=[VMEM] * 4,
        out_specs=(ANY, ANY, VMEM, VMEM),
        scratch_shapes=[
            pltpu.VMEM((4, rows_own, width), low_type),
            pltpu.VMEM((4, rows_own, width), low_type),
            pltpu.VMEM((4, rows_own, width), low_type),
            pltpu.VMEM(small_part.shape, small_part.dtype),
            pltpu.VMEM(small_shape, small_part.dtype),
            pltpu.VMEM(small_shape, small_part.dtype),
            pltpu.VMEM(line, low_type),
            pltpu.VMEM(line, low_type),
            pltpu.VMEM(line, low_type),
            pltpu.VMEM(line, low_type),
            pltpu.VMEM(line[1:], low_type),
        ]
        + plane_scratch(own, width)
        + [
            pltpu.SemaphoreType.DMA((80,)),
            pltpu.SemaphoreType.DMA((80,)),
            pltpu.SemaphoreType.DMA((3,)),
        ],
        compiler_params=comm_params(2),
        name="close_heads",
    )(qkv_part, proj_part, small_part, part)


def plane_scatter_kernel(part, out, *rest):
    at = Place()
    wire = Wire(*rest[-2:])
    enter([at.plane(delta)[0] for delta in (4, 2, 1)])
    for _ in plane_scatter_flow(at, wire, part, out, *rest[:-2]):
        pass
    wire.drain()


def plane_scatter(part, number):
    _, own, width = part.shape
    return pl.pallas_call(
        plane_scatter_kernel,
        out_shape=jax.ShapeDtypeStruct((own, width), jnp.float32),
        in_specs=[VMEM],
        out_specs=VMEM,
        scratch_shapes=plane_scratch(own, width)
        + [pltpu.SemaphoreType.DMA((16,)), pltpu.SemaphoreType.DMA((16,))],
        compiler_params=comm_params(number),
        name="plane_scatter_%d" % number,
    )(part)


def group_body(
    hidden_in,
    token_marks,
    out_grad,
    qkv_weight,
    proj_weight,
    gate_weight,
    up_weight,
    down_weight,
    first_gain,
    first_shift,
    second_gain,
    second_shift,
):
    micro_count, _, pos_count, width = hidden_in.shape
    rows_own = qkv_weight.shape[0]
    units = gate_weight.shape[1]
    head_ways = math.prod(lax.axis_size(name) for name in HEAD_AXES)
    unit_ways = math.prod(lax.axis_size(name) for name in UNIT_AXES)
    chunk_count = lax.axis_size("y") * lax.axis_size("c")
    row_length = pos_count * chunk_count
    x_size = lax.axis_size("x")
    marks_own = token_marks.astype(jnp.float32)
    own = micro_count * pos_count
    head_width = width // head_ways
    heads_here = head_width // HEAD_DIM
    unit_width = -(-units // (unit_ways * LANES)) * LANES
    unit_pad = unit_width * unit_ways - units
    x_own = hidden_in.reshape(own, width)

    params = jnp.stack([first_gain, first_shift, second_gain, second_shift])
    small = jnp.concatenate([params.astype(jnp.float32).ravel(), marks_own.ravel()])
    small = jnp.pad(small, (0, -small.size % (8 * LANES))).reshape(-1, LANES)

    qkv_parts = (
        qkv_weight.reshape(rows_own, 3, head_ways, head_width)
        .transpose(2, 0, 1, 3)
        .reshape(head_ways, rows_own, 3 * head_width)
    )
    ffn = jnp.stack([gate_weight, up_weight, down_weight])
    ffn = jnp.pad(ffn, ((0, 0), (0, 0), (0, unit_pad)))
    ffn = ffn.reshape(3, rows_own, unit_ways, unit_width).transpose(2, 0, 1, 3)

    qkv_here, ffn, proj_here, x_all, small = gather_weights(
        qkv_parts, ffn, proj_weight, x_own, small
    )
    qkv_here = qkv_here.reshape(-1, 3 * head_width)
    ffn = ffn.reshape(3, -1, unit_width)
    x_all = x_all.reshape(-1, width)
    proj_here = proj_here.reshape(head_width, width)
    gate_here, up_here, down_here = ffn[0], ffn[1], ffn[2]
    small = small.reshape(unit_ways * 4, -1)
    params = small[:, : 4 * rows_own].reshape(-1, 4, rows_own).transpose(1, 0, 2)
    gain_one, shift_one, gain_two, shift_two = params.reshape(4, 1, width)
    marks = small.reshape(4, head_ways, -1)[lax.axis_index("zi")]
    marks = marks[:, 4 * rows_own : 4 * rows_own + own * 3].astype(jnp.int32)

    mixed = dot(x_all, qkv_here)

    def to_rows(values):
        inner = values.shape[1:]
        values = values.reshape((x_size, chunk_count, micro_count, pos_count) + inner)
        return jnp.swapaxes(values, 1, 2).reshape((x_size * micro_count, row_length) + inner)

    def from_rows(values):
        inner = values.shape[2:]
        values = values.reshape((x_size, micro_count, chunk_count, pos_count) + inner)
        return jnp.swapaxes(values, 1, 2).reshape((head_ways * own,) + inner)

    row_marks = to_rows(marks.reshape(head_ways * own, 3))
    cosine, sine = rotary_tables(row_marks[..., 2])
    cosine, sine = cosine[:, :, None, :], sine[:, :, None, :]
    mixed = to_rows(mixed).reshape(x_size * micro_count, row_length, 3, heads_here, HEAD_DIM)
    queries = low(rotate(mixed[:, :, 0], cosine, sine))
    key_rows = low(rotate(mixed[:, :, 1], cosine, sine))
    value_rows = low(mixed[:, :, 2])
    place = jnp.arange(row_length, dtype=jnp.int32)
    allowed = (row_marks[:, :, None, 0] == row_marks[:, None, :, 0]) & (
        (place[None, None, :] <= place[None, :, None])
        | (place[None, :] < row_marks[:, :, 1])[:, None, :]
    )
    score_scale = 1.0 / math.sqrt(HEAD_DIM)

    def pair(spec, left_side, right_side):
        return jnp.einsum(spec, left_side, right_side, preferred_element_type=jnp.float32)

    scores = pair("rqhd,rkhd->rhqk", queries, key_rows) * score_scale
    scores = jnp.where(allowed[:, None], scores, masked_score)
    exp_scores = jnp.exp(scores - jnp.max(scores, axis=-1, keepdims=True))
    probs = exp_scores / jnp.sum(exp_scores, axis=-1, keepdims=True)
    probs_low = low(probs)
    context = low(pair("rhqk,rkhd->rqhd", probs_low, value_rows))

    context = from_rows(context).reshape(-1, head_width)
    branch = plane_scatter(low(dot(context, proj_here)).reshape(head_ways, own, width), 4)
    first_sum = deep_alpha * x_own.astype(jnp.float32) + branch
    hat_one, inverse_one = norm_parts(first_sum)
    normed = low(hat_one * gain_one + shift_one)

    normed_all = gather(normed, UNIT_AXES)
    gate_val = dot(normed_all, gate_here)
    up_val = dot(normed_all, up_here)
    gelu_val, gelu_slope = gelu_parts(gate_val)
    active = low(gelu_val * up_val)
    down_part = low(contract_last(active, down_here)).reshape(unit_ways, own, width)
    layer_rows, d_second, down_low, norm_grads = turn(
        down_part, normed, out_grad.reshape(own, width), gain_two, shift_two
    )
    gain_two_grad, shift_two_grad = jnp.sum(norm_grads, axis=1)
    down_low = down_low.reshape(-1, width)
    d_active = dot(down_low, down_here)
    gate_low = low(d_active * up_val * gelu_slope)
    up_low = low(d_active * gelu_val)
    d_normed_part = low(contract_last(gate_low, gate_here) + contract_last(up_low, up_here))

    def unit_grad(left_side, right_side):
        part = low(contract_first(left_side, right_side))
        return part.reshape(4, 2, 2, 2, rows_own, unit_width)

    ffn_grads = (
        unit_grad(normed_all, gate_low),
        unit_grad(normed_all, up_low),
        unit_grad(down_low, active),
    )
    ffn_part, branch_all, d_first, norm_grads = close_units(
        ffn_grads,
        d_normed_part.reshape(unit_ways, own, width),
        d_second,
        hat_one,
        inverse_one,
        gain_one,
    )
    gain_one_grad, shift_one_grad = jnp.sum(norm_grads, axis=1)
    branch_all = branch_all.reshape(-1, width)
    small_grads = jnp.stack([gain_one_grad, shift_one_grad, gain_two_grad, shift_two_grad])
    small_grads = small_grads.reshape(4, 4, head_ways, rows_own).transpose(2, 1, 0, 3)
    small_grads = small_grads.reshape(head_ways, 4, 4 * rows_own // LANES, LANES)
    small_grads = jnp.pad(small_grads, ((0, 0), (0, 0), (0, -small_grads.shape[2] % 8), (0, 0)))

    proj_part = low(contract_first(context, branch_all)).reshape(4, rows_own, width)
    d_context = to_rows(low(contract_last(branch_all, proj_here)))
    d_context = d_context.reshape(x_size * micro_count, row_length, heads_here, HEAD_DIM)
    d_probs = pair("rqhd,rkhd->rhqk", d_context, value_rows)
    d_scores = low(probs * (d_probs - jnp.sum(probs * d_probs, axis=-1, keepdims=True)))
    d_query = pair("rhqk,rkhd->rqhd", d_scores, key_rows) * score_scale
    d_keys = pair("rhqk,rqhd->rkhd", d_scores, queries) * score_scale
    d_values = pair("rhqk,rqhd->rkhd", probs_low, d_context)
    d_mixed = low(
        jnp.stack(
            [rotate(d_query, cosine, -sine), rotate(d_keys, cosine, -sine), d_values], axis=2
        )
    )
    d_mixed = from_rows(d_mixed.reshape(x_size * micro_count, row_length, 3 * head_width))
    d_input = low(contract_last(d_mixed, qkv_here)).reshape(head_ways, own, width)
    qkv_part = low(contract_first(x_all, d_mixed))
    qkv_part, proj_part, small_grads, d_input = close_heads(
        qkv_part.reshape(4, 8, rows_own, 3 * head_width), proj_part, small_grads, d_input
    )
    d_input = deep_alpha * d_first + d_input
    small_grads = small_grads.ravel()[: 4 * rows_own].reshape(4, rows_own)
    qkv_grad = (
        qkv_part.reshape(head_ways, rows_own, 3, head_width)
        .transpose(1, 2, 0, 3)
        .reshape(rows_own, 3 * width)
        .astype(jnp.float32)
    )
    ffn_part = ffn_part.transpose(1, 2, 0, 3).reshape(3, rows_own, unit_ways * unit_width)
    gate_grad, up_grad, down_grad = (
        ffn_part[index, :, :units].astype(jnp.float32) for index in range(3)
    )
    return (
        layer_rows.reshape(micro_count, 1, pos_count, width),
        low(d_input).reshape(micro_count, 1, pos_count, width),
        qkv_grad,
        proj_part.astype(jnp.float32),
        gate_grad,
        up_grad,
        down_grad,
        small_grads[0],
        small_grads[1],
        small_grads[2],
        small_grads[3],
    )


def body(hidden_in, token_marks, out_grad, *weights):
    joined = lax.axis_size("zo")
    if joined == 1:
        return group_body(hidden_in, token_marks, out_grad, *weights)
    rows = weights[0].shape[0]
    width = hidden_in.shape[-1]
    groups = width // (joined * rows)
    group_place = lax.axis_index(ALL[1:])

    def inward(values):
        shape = values.shape
        values = values.reshape(shape[:-1] + (joined, groups, rows))
        return jnp.swapaxes(values, -3, -2).reshape(shape)

    def outward(values):
        shape = values.shape
        values = values.reshape(shape[:-1] + (groups, joined, rows))
        return jnp.swapaxes(values, -3, -2).reshape(shape)

    proj = gather(weights[1], ALL)
    proj = inward(lax.dynamic_slice_in_dim(proj, group_place * joined * rows, joined * rows))
    weights = [gather(weight, "zo") for weight in weights]
    weights[1] = proj
    outs = list(group_body(inward(hidden_in), token_marks, inward(out_grad), *weights))
    outs[:2] = outward(outs[0]), outward(outs[1])
    proj_grad = jnp.zeros((width, width), jnp.float32)
    proj_grad = lax.dynamic_update_slice_in_dim(
        proj_grad, outward(outs[3]), group_place * joined * rows, 0
    )
    outs[2:] = [scatter_sum(grad, "zo") for grad in outs[2:]]
    outs[3] = scatter_sum(proj_grad, ALL)
    return tuple(outs)


def solution(mesh):
    seq_size, ctx_size = mesh.shape["seq"], mesh.shape["ctx"]
    cores, x_size = 2, 2
    zi_size = math.gcd(4, seq_size // x_size)
    zo_size = seq_size // (x_size * zi_size)
    devices = np.asarray(mesh.devices).reshape(
        zo_size, zi_size, x_size, ctx_size // cores, cores
    )
    inner = Mesh(devices, ALL)
    tokens = P(None, ("zo", "zi", "x"), ("y", "c"), None)
    matrix = P(ALL, None)
    vector = P(ALL)
    return jax.shard_map(
        body,
        mesh=inner,
        in_specs=(tokens,) * 3 + (matrix,) * 5 + (vector,) * 4,
        out_specs=(tokens,) * 2 + (matrix,) * 5 + (vector,) * 4,
        check_vma=False,
    )
```

```python
import math

import jax
import jax.numpy as jnp
import numpy as np
from jax import lax
from jax.experimental import pallas as pl
from jax.experimental.pallas import tpu as pltpu
from jax.sharding import Mesh
from jax.sharding import PartitionSpec as P

HEAD_DIM = 128
LANES = 128

deep_alpha = 48.0**0.25
norm_eps = 1e-05
masked_score = -1e30

ALL = ("zo", "zi", "x", "y", "c")
HEAD_AXES = ("x", "y", "c")
UNIT_AXES = ("zi", "c")
HEAD_COPIES = ("zo", "zi")
UNIT_COPIES = ("zo", "x", "y")


def contract_last(left_side, right_side):
    return lax.dot_general(
        left_side, right_side, (((1,), (1,)), ((), ())), preferred_element_type=jnp.float32
    )


def contract_first(left_side, right_side):
    return lax.dot_general(
        left_side, right_side, (((0,), (0,)), ((), ())), preferred_element_type=jnp.float32
    )


def dot(left_side, right_side):
    return jnp.dot(left_side, right_side, preferred_element_type=jnp.float32)


def low(values):
    return values.astype(jnp.bfloat16)


def norm_parts(values):
    center = values - jnp.mean(values, axis=-1, keepdims=True)
    spread = jnp.mean(center * center, axis=-1, keepdims=True)
    inverse = lax.rsqrt(spread + norm_eps)
    return center * inverse, inverse


def norm_back(cotangent, hat, inverse, gain_vec):
    scaled = cotangent * gain_vec
    return (
        scaled
        - jnp.mean(scaled, axis=-1, keepdims=True)
        - hat * jnp.mean(scaled * hat, axis=-1, keepdims=True)
    ) * inverse


def rotary_tables(positions):
    half = HEAD_DIM // 2
    exponent = jnp.arange(half, dtype=jnp.float32) * (2.0 / HEAD_DIM)
    angles = positions.astype(jnp.float32)[..., None] * jnp.exp(-math.log(10000.0) * exponent)
    return (jnp.cos(angles), jnp.sin(angles))


def rotate(values, cosine, sine):
    half = HEAD_DIM // 2
    front, back = values[..., :half], values[..., half:]
    return jnp.concatenate(
        [front * cosine - back * sine, back * cosine + front * sine], axis=-1
    )


def gather(values, axes):
    return lax.all_gather(values, axes, axis=0, tiled=True)


def scatter_sum(values, axes):
    return lax.psum_scatter(values, axes, scatter_dimension=0, tiled=True)


def gelu_parts(value):
    phi = 0.5 * lax.erfc(-value * math.sqrt(0.5))
    density = jnp.exp(-0.5 * value * value) * (1.0 / math.sqrt(2.0 * math.pi))
    return value * phi, phi + value * density


MESH = pl.DeviceIdType.MESH


class Wire:
    def __init__(self, send_sems, recv_sems):
        self.send_sems, self.recv_sems = send_sems, recv_sems
        self.keys, self.sent = {}, []

    def number(self, key, span=1):
        if key not in self.keys:
            self.keys[key] = sum(size for _, size in self.keys.values()), span
        return self.keys[key][0]

    def copy(self, key, source, target, device, slot=0, span=1, recv=None):
        send = self.number(key, span)
        receive = send if recv is None else self.number(recv)
        return pltpu.make_async_remote_copy(
            src_ref=source,
            dst_ref=target,
            send_sem=self.send_sems.at[send],
            recv_sem=self.recv_sems.at[receive + slot],
            device_id=device,
            device_id_type=MESH,
        )

    def send(self, key, source, target, device, when=None, recv=None):
        copy = self.copy(key, source, target, device, recv=recv)
        if when is None:
            copy.start()
        else:
            pl.when(when)(copy.start)
        self.sent.append((copy, when))

    def send_to_slot(self, key, source, target, device, slot, span, when):
        copy = self.copy(key, source, target, device, slot, span)
        pl.when(when)(copy.start)
        self.sent.append((copy, when))

    def arrive(self, key, target, device, when=None):
        copy = self.copy(key, target, target, device)
        if when is None:
            copy.wait_recv()
        else:
            pl.when(when)(copy.wait_recv)

    def arrive_slot(self, key, target, device, slot, span, when):
        pl.when(when)(self.copy(key, target, target, device, slot, span).wait_recv)

    def drain(self):
        for copy, when in self.sent:
            if when is None:
                copy.wait_send()
            else:
                pl.when(when)(copy.wait_send)


def flip(value, bit):
    return 1 - value if bit else value


def enter(devices):
    barrier = pltpu.get_barrier_semaphore()
    for device in devices:
        pl.semaphore_signal(barrier, inc=1, device_id=device, device_id_type=MESH)
    pl.semaphore_wait(barrier, len(devices))


class Place:
    def __init__(self):
        self.zo, self.zi, self.x, self.y, self.c = (lax.axis_index(name) for name in ALL)
        self.rank = self.x * 4 + self.y * 2 + self.c
        self.unit = self.zi * 2 + self.c

    def head_home(self):
        return self.y + self.c * (3 - 2 * self.y)

    def holder(self):
        y, c = lax.rem((self.zi + 1) // 2, 2), self.zi // 2
        return (self.zo, self.zi, self.x, y, c), self.x * 4 + y * 2 + c

    def plane(self, delta):
        dx, dy, dc = delta >> 2 & 1, delta >> 1 & 1, delta & 1
        x, y, c = flip(self.x, dx), flip(self.y, dy), flip(self.c, dc)
        return (self.zo, self.zi, x, y, c), x * 4 + y * 2 + c

    def column(self, step):
        other = lax.rem(self.unit + step + 8, 8)
        return (self.zo, other // 2, self.x, self.y, lax.rem(other, 2)), other

    def ends(self):
        return self.line(jnp.minimum(self.zi + 1, 3)), self.line(jnp.maximum(self.zi - 1, 0))

    def line(self, z):
        return (self.zo, z, self.x, self.y, self.c)

    def column_neighbours(self):
        return [self.line(z) for z in self.others()] + [self.plane(1)[0]]

    def others(self):
        return [lax.rem(self.zi + step, 4) for step in (1, 2, 3)]

    def neighbours(self):
        plane = [self.plane(delta)[0] for delta in range(1, 8)]
        column = []
        for dz in range(1, 4):
            z = lax.rem(self.zi + dz, 4)
            column += [(self.zo, z, self.x, self.y, core) for core in (0, 1)]
        return plane + column


def unit_gather_flow(at, wire, ffn_in, ffn_out, own_sem):
    x_side, y_side = at.plane(4)[0], at.plane(2)[0]
    steps = (1, 7, 2, 6, 3, 5, 4)
    mine = ffn_out.at[:, at.zi, at.x, at.y, at.c]
    own = pltpu.make_async_copy(ffn_in.at[at.unit], mine, own_sem)
    own.start()
    for step in (4, 3, 5, 2, 6, 1, 7):
        device, other = at.column(step)
        wire.send(("f", step), ffn_in.at[other], mine, device)
    own.wait()

    def slot(step, x, y):
        source = lax.rem(at.unit - step + 8, 8)
        return ffn_out.at[:, source // 2, x, y, lax.rem(source, 2)]

    def first(step):
        here = slot(step, at.x, at.y)
        if step:
            wire.arrive(("f", step), here, at.column(-step)[0])
        wire.send(("fx", step), here, here, x_side)
        wire.send(("fy", step), here, here, y_side)

    def second(step, turn):
        from_x, from_y = slot(step, 1 - at.x, at.y), slot(step, at.x, 1 - at.y)
        wire.arrive(("fx", step), from_x, x_side)
        wire.arrive(("fy", step), from_y, y_side)
        if turn % 2:
            wire.send(("fd", step), from_x, from_x, y_side)
        else:
            wire.send(("fd", step), from_y, from_y, x_side)

    yield
    first(0)
    for turn, step in enumerate(steps):
        yield
        first(step)
        if turn >= 1:
            second(((0,) + steps)[turn - 1], turn - 1)
    yield
    second(steps[5], 6)
    second(steps[6], 7)
    yield
    for step in (0,) + steps:
        wire.arrive(("fd", step), slot(step, 1 - at.x, 1 - at.y), x_side)


def open_heads_kernel(
    qkv_in,
    ffn_in,
    proj_in,
    x_in,
    small_in,
    qkv_out,
    ffn_out,
    proj_out,
    x_out,
    small_out,
    send_sems,
    recv_sems,
    own_sems,
):
    at = Place()
    wire = Wire(send_sems, recv_sems)
    enter(at.neighbours())
    up, down = at.ends()
    chunk = at.y * 2 + at.c
    holder_device, holder = at.holder()
    proj_home = at.head_home()
    own = [
        pltpu.make_async_copy(qkv_in.at[at.rank], qkv_out.at[at.zi, at.rank], own_sems.at[1]),
        pltpu.make_async_copy(small_in, small_out.at[at.zi, at.rank], own_sems.at[3]),
    ]
    for copy in own:
        copy.start()
    for delta in range(1, 8):
        device, other = at.plane(delta)
        wire.send(("q", delta), qkv_in.at[other], qkv_out.at[at.zi, at.rank], device)
    wire.send_to_slot("p", proj_in, proj_out.at[chunk], holder_device, chunk, 4, at.rank != holder)
    proj_own = pltpu.make_async_copy(proj_in, proj_out.at[chunk], own_sems.at[4])
    pl.when(at.rank == holder)(proj_own.start)
    for delta in range(1, 8):
        device, _ = at.plane(delta)
        wire.send(("s", delta), small_in, small_out.at[at.zi, at.rank], device)
    spread = plane_gather_flow(at, wire, x_in, x_out, own_sems.at[0])
    next(spread)
    for copy in own:
        copy.wait()
    pl.when(at.rank == holder)(proj_own.wait)

    def small_second():
        for delta in range(1, 8):
            device, other = at.plane(delta)
            wire.arrive(("s", delta), small_out.at[at.zi, other], device)
        for dz in range(1, 4):
            device = at.line(lax.rem(at.zi + dz, 4))
            wire.send(("t", dz), small_out.at[at.zi], small_out.at[at.zi], device)

    def small_last():
        for dz in range(1, 4):
            z = lax.rem(at.zi - dz + 4, 4)
            wire.arrive(("t", dz), small_out.at[z], at.line(z))

    def proj_start(slot):
        block = proj_out.at[slot]
        source = (at.zo, at.zi, at.x, slot // 2, slot % 2)
        home = at.zi == proj_home
        mine = home & ((chunk != slot) | (at.rank != holder))
        wire.arrive_slot("p", block, source, slot, 4, mine)
        wire.send(("pu", slot), block, block, up, home & (at.zi < 3))
        wire.send(("pd", slot), block, block, down, home & (at.zi > 0))

    def proj_relay(slot):
        block = proj_out.at[slot]
        above, below = at.zi > proj_home, at.zi < proj_home
        wire.arrive(("pu", slot), block, down, above)
        wire.arrive(("pd", slot), block, up, below)
        key = "pu", slot
        wire.send(("pu2", slot), block, block, up, above & (at.zi < 3), recv=key)
        key = "pd", slot
        wire.send(("pd2", slot), block, block, down, below & (at.zi > 0), recv=key)

    def qkv_slot(z, delta):
        return qkv_out.at[jnp.clip(z, 0, 3), at.plane(delta)[1]]

    def qkv_hop(hop, delta):
        below, above = qkv_slot(at.zi - hop, delta), qkv_slot(at.zi + hop, delta)
        if hop == 0:
            if delta:
                wire.arrive(("q", delta), below, at.plane(delta)[0])
        else:
            wire.arrive(("up", hop - 1, delta), below, down, at.zi >= hop)
            wire.arrive(("down", hop - 1, delta), above, up, at.zi <= 3 - hop)
        if hop < 3:
            wire.send(("up", hop, delta), below, below, up, (at.zi >= hop) & (at.zi < 3))
            wire.send(("down", hop, delta), above, above, down, (at.zi <= 3 - hop) & (at.zi > 0))

    for delta in range(8):
        qkv_hop(0, delta)
    units = unit_gather_flow(at, wire, ffn_in, ffn_out, own_sems.at[2])
    for slot in range(4):
        proj_start(slot)
    next(units)
    next(spread)
    small_second()
    next(units)
    for _ in spread:
        pass
    for delta in range(8):
        qkv_hop(1, delta)
        if delta % 2:
            proj_relay(delta // 2)
            next(units)
    for delta in range(8):
        qkv_hop(2, delta)
        if delta % 2:
            next(units)
    for delta in range(8):
        qkv_hop(3, delta)
    for _ in units:
        pass
    small_last()
    wire.drain()


def open_units_kernel(
    part,
    x_own,
    gain,
    shift,
    ffn_in,
    normed,
    hat,
    inverse_out,
    normed_all,
    ffn_out,
    branch,
    *rest,
):
    at = Place()
    *scratch, send_sems, recv_sems, own_sems = rest
    wire = Wire(send_sems, recv_sems)
    enter(at.neighbours())

    def norm_rows():
        count = 16

        @pl.loop(0, x_own.shape[0] // count)
        def _(index):
            rows = pl.ds(pl.multiple_of(index * count, count), count)
            whole = deep_alpha * x_own[rows].astype(jnp.float32) + branch[rows]
            near, inverse = norm_parts(whole)
            hat[rows] = near
            inverse_out[rows] = jnp.broadcast_to(inverse, (count, LANES))
            normed[rows] = (near * gain[...] + shift[...]).astype(jnp.bfloat16)

    scatter = plane_scatter_flow(at, wire, part, branch, *scratch)
    units = unit_gather_flow(at, wire, ffn_in, ffn_out, own_sems.at[0])
    next(scatter)
    next(units)
    next(scatter)
    next(scatter)
    next(units)
    for _ in scatter:
        pass
    norm_rows()
    spread = column_gather_flow(at, wire, 0, normed, normed_all, own_sems.at[1])
    next(spread)
    next(units)
    next(units)
    next(spread)
    next(units)
    next(units)
    next(spread)
    next(units)
    next(units)
    next(spread)
    next(units)
    for _ in spread:
        pass
    for _ in units:
        pass
    wire.drain()


ANY = pl.BlockSpec(memory_space=pl.ANY)
VMEM = pl.BlockSpec(memory_space=pltpu.VMEM)


def comm_params(number):
    return pltpu.CompilerParams(
        collective_id=number, has_side_effects=True, vmem_limit_bytes=63 * 2**20
    )


def open_heads(qkv_parts, ffn_parts, proj_own, x_own, small):
    _, rows_own, qkv_width = qkv_parts.shape
    _, matrices, _, unit_width = ffn_parts.shape
    own, width = x_own.shape
    low_type = jnp.bfloat16
    return pl.pallas_call(
        open_heads_kernel,
        out_shape=(
            jax.ShapeDtypeStruct((4, 8, rows_own, qkv_width), low_type),
            jax.ShapeDtypeStruct((matrices, 4, 2, 2, 2, rows_own, unit_width), low_type),
            jax.ShapeDtypeStruct((4, rows_own, width), low_type),
            jax.ShapeDtypeStruct((8, own, width), low_type),
            jax.ShapeDtypeStruct((4, 8) + small.shape, small.dtype),
        ),
        in_specs=[VMEM] * 5,
        out_specs=(ANY,) * 5,
        scratch_shapes=[
            pltpu.SemaphoreType.DMA((136,)),
            pltpu.SemaphoreType.DMA((136,)),
            pltpu.SemaphoreType.DMA((5,)),
        ],
        compiler_params=comm_params(1),
        name="open_heads",
    )(qkv_parts, ffn_parts, proj_own, x_own, small)


def open_units(part, x_own, gain, shift, ffn_parts):
    _, matrices, rows_own, unit_width = ffn_parts.shape
    own, width = x_own.shape
    low_type = jnp.bfloat16
    return pl.pallas_call(
        open_units_kernel,
        out_shape=(
            jax.ShapeDtypeStruct((own, width), low_type),
            jax.ShapeDtypeStruct((own, width), jnp.float32),
            jax.ShapeDtypeStruct((own, LANES), jnp.float32),
            jax.ShapeDtypeStruct((8, own, width), low_type),
            jax.ShapeDtypeStruct((matrices, 4, 2, 2, 2, rows_own, unit_width), low_type),
        ),
        in_specs=[VMEM] * 5,
        out_specs=(VMEM, VMEM, VMEM, ANY, ANY),
        scratch_shapes=[pltpu.VMEM((own, width), jnp.float32)]
        + plane_scratch(own, width)
        + [
            pltpu.SemaphoreType.DMA((64,)),
            pltpu.SemaphoreType.DMA((64,)),
            pltpu.SemaphoreType.DMA((2,)),
        ],
        compiler_params=comm_params(4),
        name="open_units",
    )(part, x_own, gain, shift, ffn_parts)


def add_rows(out, *terms):
    step = 32

    @pl.loop(0, out.shape[0] // step)
    def _(index):
        part = pl.ds(pl.multiple_of(index * step, step), step)
        whole = terms[0][part].astype(jnp.float32)
        for term in terms[1:]:
            whole = whole + term[part].astype(jnp.float32)
        out[part] = whole.astype(out.dtype)


def column_scatter_flow(
    at, wire, tag, part, out, core_in, core_sum, up_in, down_in, up_sum, down_sum
):
    core_side = at.plane(1)[0]
    up, down = at.ends()
    for goal in (3, 0, 2, 1):
        source = part.at[goal * 2 + 1 - at.c]
        wire.send(("rc", tag, goal), source, core_in.at[goal], core_side)
    yield
    for goal in (3, 0, 2, 1):
        wire.arrive(("rc", tag, goal), core_in.at[goal], core_side)
        add_rows(core_sum.at[goal], part.at[goal * 2 + at.c], core_in.at[goal])
        source = core_sum.at[goal]
        if goal > 0:
            wire.send(("ru", tag, goal), source, up_in.at[goal], up, at.zi == 0)
        if goal < 3:
            wire.send(("rd", tag, goal), source, down_in.at[goal], down, at.zi == 3)

    def climb(goal):
        wire.arrive(("ru", tag, goal), up_in.at[goal], down)
        add_rows(up_sum.at[goal], core_sum.at[goal], up_in.at[goal])

    def descend(goal):
        wire.arrive(("rd", tag, goal), down_in.at[goal], up)
        add_rows(down_sum.at[goal], core_sum.at[goal], down_in.at[goal])

    for goal in (3, 2):
        yield
        back = 3 - goal
        passing = (at.zi > 0) & (at.zi < goal)
        pl.when(passing)(lambda: climb(goal))
        key = "ru", tag, goal
        wire.send(("ru2", tag, goal), up_sum.at[goal], up_in.at[goal], up, passing, recv=key)
        passing = (at.zi < 3) & (at.zi > back)
        pl.when(passing)(lambda: descend(back))
        key = "rd", tag, back
        wire.send(("rd2", tag, back), down_sum.at[back], down_in.at[back], down, passing, recv=key)
    yield
    add_rows(out, core_sum.at[at.zi])

    def last(key, source, device):
        wire.arrive(key, source, device)
        add_rows(out, out, source)

    for goal in range(4):
        if goal > 0:
            pl.when(at.zi == goal)(lambda: last(("ru", tag, goal), up_in.at[goal], down))
        if goal < 3:
            pl.when(at.zi == goal)(lambda: last(("rd", tag, goal), down_in.at[goal], up))


def column_gather_flow(at, wire, tag, own_in, out, own_sem):
    core_side = at.plane(1)[0]
    up, down = at.ends()

    def slot(z, c):
        return out.at[jnp.clip(z, 0, 3) * 2 + c]

    mine = slot(at.zi, at.c)
    wire.send(("gu", tag, 0), own_in, mine, up, at.zi < 3)
    wire.send(("gd", tag, 0), own_in, mine, down, at.zi > 0)
    wire.send(("gc", tag), own_in, mine, core_side)
    own = pltpu.make_async_copy(own_in, mine, own_sem)
    own.start()
    for hop in (1, 2, 3):
        yield
        below, above = slot(at.zi - hop, at.c), slot(at.zi + hop, at.c)
        has_below, has_above = at.zi >= hop, at.zi <= 3 - hop
        wire.arrive(("gu", tag, hop - 1), below, down, has_below)
        if hop < 3:
            wire.send(("gu", tag, hop), below, below, up, has_below & (at.zi < 3))
        wire.send(("gcu", tag, hop), below, below, core_side, has_below)
        wire.arrive(("gd", tag, hop - 1), above, up, has_above)
        if hop < 3:
            wire.send(("gd", tag, hop), above, above, down, has_above & (at.zi > 0))
        wire.send(("gcd", tag, hop), above, above, core_side, has_above)
    yield
    own.wait()
    wire.arrive(("gc", tag), slot(at.zi, 1 - at.c), core_side)
    for hop in (1, 2, 3):
        below, above = slot(at.zi - hop, 1 - at.c), slot(at.zi + hop, 1 - at.c)
        wire.arrive(("gcu", tag, hop), below, core_side, at.zi >= hop)
        wire.arrive(("gcd", tag, hop), above, core_side, at.zi <= 3 - hop)


def column_scratch(own, width):
    return [pltpu.VMEM((4, own, width), jnp.bfloat16)] * 6


def plane_scatter_flow(at, wire, part, out, core_in, core_sum, side_in, side_sum, last_in):
    x_side, y_side, core_side = at.plane(4)[0], at.plane(2)[0], at.plane(1)[0]
    half = out.shape[1] // 2
    halves = (pl.ds(0, half), pl.ds(half, half))
    order = ((1, 1), (1, 0), (0, 1), (0, 0))

    def place(dx, dy):
        return flip(at.x, dx), flip(at.y, dy)

    for dx, dy in order:
        x, y = place(dx, dy)
        other = x * 4 + y * 2 + 1 - at.c
        wire.send(("c", dx, dy), part.at[other], core_in.at[dx * 2 + dy], core_side)
    yield
    for dx, dy in order:
        x, y = place(dx, dy)
        mine = x * 4 + y * 2 + at.c
        slot = dx * 2 + dy
        wire.arrive(("c", dx, dy), core_in.at[slot], core_side)
        add_rows(core_sum.at[slot], part.at[mine], core_in.at[slot])
        if dx:
            source = core_sum.at[slot, :, halves[0]]
            wire.send(("sa", dy), source, side_in.at[0, dy], x_side)
        if dy:
            source = core_sum.at[slot, :, halves[1]]
            wire.send(("sb", dx), source, side_in.at[1, dx], y_side)
    yield
    wire.arrive(("sa", 1), side_in.at[0, 1], x_side)
    add_rows(side_sum.at[0], core_sum.at[1, :, halves[0]], side_in.at[0, 1])
    wire.send("sy", side_sum.at[0], last_in.at[0], y_side)
    wire.arrive(("sb", 1), side_in.at[1, 1], y_side)
    add_rows(side_sum.at[1], core_sum.at[2, :, halves[1]], side_in.at[1, 1])
    wire.send("sx", side_sum.at[1], last_in.at[1], x_side)
    yield
    wire.arrive(("sa", 0), side_in.at[0, 0], x_side)
    wire.arrive(("sb", 0), side_in.at[1, 0], y_side)
    wire.arrive("sy", last_in.at[0], y_side)
    terms = core_sum.at[0, :, halves[0]], side_in.at[0, 0], last_in.at[0]
    add_rows(out.at[:, halves[0]], *terms)
    wire.arrive("sx", last_in.at[1], x_side)
    terms = core_sum.at[0, :, halves[1]], side_in.at[1, 0], last_in.at[1]
    add_rows(out.at[:, halves[1]], *terms)


def plane_scratch(own, width):
    return [
        pltpu.VMEM((4, own, width), jnp.bfloat16),
        pltpu.VMEM((4, own, width), jnp.bfloat16),
        pltpu.VMEM((2, 2, own, width // 2), jnp.bfloat16),
        pltpu.VMEM((2, own, width // 2), jnp.bfloat16),
        pltpu.VMEM((2, own, width // 2), jnp.bfloat16),
    ]


def plane_gather_flow(at, wire, own_in, out, own_sem):
    x_side, y_side, core_side = at.plane(4)[0], at.plane(2)[0], at.plane(1)[0]
    half = own_in.shape[0] // 2
    mine = out.at[at.rank]
    wire.send("gx", own_in, mine, x_side)
    wire.send("gy", own_in, mine, y_side)
    wire.send("gc0", own_in, mine, core_side)
    own = pltpu.make_async_copy(own_in, mine, own_sem)
    own.start()
    yield
    from_x, from_y, from_xy = (at.plane(delta)[1] for delta in (4, 2, 6))
    low_half, high_half = pl.ds(0, half), pl.ds(half, half)
    wire.arrive("gx", out.at[from_x], x_side)
    wire.send("gd0", out.at[from_x, low_half], out.at[from_x, low_half], y_side)
    wire.send("gc1", out.at[from_x], out.at[from_x], core_side)
    wire.arrive("gy", out.at[from_y], y_side)
    wire.send("gd1", out.at[from_y, high_half], out.at[from_y, high_half], x_side)
    wire.send("gc2", out.at[from_y], out.at[from_y], core_side)
    yield
    wire.arrive("gd0", out.at[from_xy, low_half], y_side)
    wire.arrive("gd1", out.at[from_xy, high_half], x_side)
    wire.send("gc3", out.at[from_xy], out.at[from_xy], core_side)
    own.wait()
    for index, delta in enumerate((1, 5, 3, 7)):
        wire.arrive("gc%d" % index, out.at[at.plane(delta)[1]], core_side)


def turn_kernel(
    part,
    normed,
    out_grad,
    gain,
    shift,
    layer_out,
    d_second,
    down_out,
    norm_out,
    second,
    down_low,
    core_in,
    core_sum,
    up_in,
    down_in,
    up_sum,
    down_sum,
    send_sems,
    recv_sems,
    own_sems,
):
    at = Place()
    wire = Wire(send_sems, recv_sems)
    enter(at.column_neighbours())
    half = normed.shape[0] // 2
    scratch = core_in, core_sum, up_in, down_in, up_sum, down_sum

    def norm_rows(start):
        count = 16

        @pl.loop(0, half // count)
        def _(index):
            rows = pl.ds(pl.multiple_of(start + index * count, count), count)
            whole = deep_alpha * normed[rows].astype(jnp.float32) + second[rows]
            near, inverse = norm_parts(whole)
            layer_out[rows] = (near * gain[...] + shift[...]).astype(jnp.bfloat16)
            cotangent = out_grad[rows].astype(jnp.float32)
            result = norm_back(cotangent, near, inverse, gain[...])
            d_second[rows] = result
            down_low[rows] = result.astype(jnp.bfloat16)
            along = cotangent * near
            norm_out[0] += along[:8] + along[8:]
            norm_out[1] += cotangent[:8] + cotangent[8:]

    scatters, gathers = [], []
    for index in range(2):
        rows = pl.ds(index * half, half)
        views = [ref.at[:, rows] for ref in scratch]
        scatters.append(
            column_scatter_flow(at, wire, index, part.at[:, rows], second.at[rows], *views)
        )
        gathers.append(
            column_gather_flow(
                at, wire, index, down_low.at[rows], down_out.at[:, rows], own_sems.at[index]
            )
        )
    norm_out[...] = jnp.zeros_like(norm_out)
    for flow in scatters:
        next(flow)
    for flow in scatters:
        next(flow)
    for _ in scatters[0]:
        pass
    norm_rows(0)
    next(gathers[0])
    next(scatters[1])
    next(gathers[0])
    for _ in scatters[1]:
        pass
    norm_rows(half)
    next(gathers[1])
    next(gathers[0])
    next(gathers[1])
    next(gathers[0])
    for flow in gathers[::-1]:
        for _ in flow:
            pass
    wire.drain()


def turn(part, normed, out_grad, gain, shift):
    _, own, width = part.shape
    low_type = jnp.bfloat16
    return pl.pallas_call(
        turn_kernel,
        out_shape=(
            jax.ShapeDtypeStruct((own, width), low_type),
            jax.ShapeDtypeStruct((own, width), jnp.float32),
            jax.ShapeDtypeStruct((8, own, width), low_type),
            jax.ShapeDtypeStruct((2, 8, width), jnp.float32),
        ),
        in_specs=[VMEM] * 5,
        out_specs=(VMEM, VMEM, ANY, VMEM),
        scratch_shapes=[
            pltpu.VMEM((own, width), jnp.float32),
            pltpu.VMEM((own, width), low_type),
        ]
        + column_scratch(own, width)
        + [
            pltpu.SemaphoreType.DMA((72,)),
            pltpu.SemaphoreType.DMA((72,)),
            pltpu.SemaphoreType.DMA((2,)),
        ],
        compiler_params=comm_params(5),
        name="turn",
    )(part, normed, out_grad, gain, shift)


def close_units_kernel(
    gate_in,
    raise_in,
    lower_in,
    part,
    d_second,
    hat,
    inverse,
    gain,
    ffn_out,
    branch_out,
    d_first,
    norm_out,
    first_in,
    second_sum,
    second_in,
    total,
    d_normed,
    branch_low,
    core_in,
    core_sum,
    up_in,
    down_in,
    up_sum,
    down_sum,
    send_sems,
    recv_sems,
    own_sems,
):
    at = Place()
    wire = Wire(send_sems, recv_sems)
    enter(at.neighbours())
    x_side, y_side = at.plane(4)[0], at.plane(2)[0]
    steps = (4, 3, 5, 2, 6, 1, 7, 0)
    sources = gate_in, raise_in, lower_in

    def owner(step):
        other = at.column(step)[1]
        return other // 2, lax.rem(other, 2)

    def ffn_first(turn):
        step = steps[turn]
        z, c = owner(step)
        for index, source in enumerate(sources):
            if turn % 2:
                block, device = source.at[z, 1 - at.x, :, c], x_side
            else:
                block, device = source.at[z, :, 1 - at.y, c], y_side
            wire.send(("a", step, index), block, first_in.at[step, index], device)

    def ffn_second(turn):
        step = steps[turn]
        z, c = owner(step)
        for index, source in enumerate(sources):
            if turn % 2:
                wire.arrive(("a", step, index), first_in.at[step, index], x_side)
                terms = source.at[z, at.x, 1 - at.y, c], first_in.at[step, index, 1 - at.y]
            else:
                wire.arrive(("a", step, index), first_in.at[step, index], y_side)
                terms = source.at[z, 1 - at.x, at.y, c], first_in.at[step, index, 1 - at.x]
            add_rows(second_sum.at[step, index], *terms)
        wire.send(
            ("b", step), second_sum.at[step], second_in.at[step], y_side if turn % 2 else x_side
        )

    own_total = pltpu.make_async_copy(total.at[0], ffn_out.at[at.unit], own_sems.at[0])

    def ffn_last(turn):
        step = steps[turn]
        z, c = owner(step)
        near = at.y if turn % 2 else at.x
        wire.arrive(("b", step), second_in.at[step], x_side)
        for index, source in enumerate(sources):
            add_rows(
                total.at[step, index],
                source.at[z, at.x, at.y, c],
                first_in.at[step, index, near],
                second_in.at[step, index],
            )
        if step:
            wire.send(("f", step), total.at[step], ffn_out.at[at.unit], at.column(step)[0])
        else:
            own_total.start()

    def norm_rows():
        count = 16
        norm_out[...] = jnp.zeros_like(norm_out)

        @pl.loop(0, hat.shape[0] // count)
        def _(index):
            rows = pl.ds(pl.multiple_of(index * count, count), count)
            cotangent = deep_alpha * d_second[rows] + d_normed[rows]
            near = hat[rows]
            result = norm_back(cotangent, near, inverse[rows, :1], gain[...])
            d_first[rows] = result
            branch_low[rows] = result.astype(jnp.bfloat16)
            along = cotangent * near
            norm_out[0] += along[:8] + along[8:]
            norm_out[1] += cotangent[:8] + cotangent[8:]

    scatter = column_scatter_flow(
        at, wire, 0, part, d_normed, core_in, core_sum, up_in, down_in, up_sum, down_sum
    )
    next(scatter)
    for turn in range(5):
        ffn_first(turn)
    next(scatter)
    next(scatter)
    ffn_second(0)
    ffn_first(5)
    ffn_second(1)
    ffn_first(6)
    next(scatter)
    ffn_second(2)
    ffn_first(7)
    ffn_second(3)
    for _ in scatter:
        pass
    norm_rows()
    spread = plane_gather_flow(at, wire, branch_low, branch_out, own_sems.at[1])
    next(spread)
    ffn_last(0)
    ffn_last(1)
    ffn_second(4)
    ffn_last(2)
    ffn_second(5)
    ffn_last(3)
    next(spread)
    ffn_second(6)
    ffn_second(7)
    ffn_last(4)
    for _ in spread:
        pass
    for turn in range(5, 8):
        ffn_last(turn)
    own_total.wait()
    for step in steps:
        if step:
            device, other = at.column(-step)
            wire.arrive(("f", step), ffn_out.at[other], device)
    wire.drain()


def close_units(grads, part, d_second, hat, inverse, gain):
    rows_own, unit_width = grads[0].shape[-2:]
    _, own, width = part.shape
    low_type = jnp.bfloat16
    block = (rows_own, unit_width)
    return pl.pallas_call(
        close_units_kernel,
        out_shape=(
            jax.ShapeDtypeStruct((8, 3) + block, low_type),
            jax.ShapeDtypeStruct((8, own, width), low_type),
            jax.ShapeDtypeStruct((own, width), jnp.float32),
            jax.ShapeDtypeStruct((2, 8, width), jnp.float32),
        ),
        in_specs=[VMEM] * 8,
        out_specs=(ANY, ANY, VMEM, VMEM),
        scratch_shapes=[
            pltpu.VMEM((8, 3, 2) + block, low_type),
            pltpu.VMEM((8, 3) + block, low_type),
            pltpu.VMEM((8, 3) + block, low_type),
            pltpu.VMEM((8, 3) + block, low_type),
            pltpu.VMEM((own, width), jnp.float32),
            pltpu.VMEM((own, width), low_type),
        ]
        + column_scratch(own, width)
        + [
            pltpu.SemaphoreType.DMA((80,)),
            pltpu.SemaphoreType.DMA((80,)),
            pltpu.SemaphoreType.DMA((2,)),
        ],
        compiler_params=comm_params(3),
        name="close_units",
    )(*grads, part, d_second, hat, inverse, gain)


def close_heads_kernel(
    qkv_in,
    proj_in,
    small_in,
    part,
    qkv_out,
    proj_out,
    small_out,
    d_input,
    proj_below,
    proj_above,
    proj_sum,
    small_plane,
    small_mid,
    small_line,
    up_in,
    down_in,
    up_sum,
    down_sum,
    qkv_total,
    core_in,
    core_sum,
    side_in,
    side_sum,
    last_in,
    send_sems,
    recv_sems,
    own_sems,
):
    at = Place()
    wire = Wire(send_sems, recv_sems)
    enter(at.neighbours())
    scatter = plane_scatter_flow(
        at, wire, part, d_input, core_in, core_sum, side_in, side_sum, last_in
    )
    next(scatter)

    def add(*terms):
        whole = terms[0].astype(jnp.float32)
        for term in terms[1:]:
            whole = whole + term.astype(jnp.float32)
        return whole.astype(jnp.bfloat16)

    for delta in range(1, 8):
        device, other = at.plane(delta)
        wire.send(("s", delta), small_in.at[other], small_plane.at[at.rank], device)

    def small_second():
        whole = small_in[at.rank]
        for delta in range(1, 8):
            device, other = at.plane(delta)
            wire.arrive(("s", delta), small_plane.at[other], device)
            whole = whole + small_plane[other]
        small_mid[...] = whole
        for dz in range(1, 4):
            z = lax.rem(at.zi + dz, 4)
            wire.send(("t", dz), small_mid.at[z], small_line.at[at.zi], at.line(z))

    def small_last():
        whole = small_mid[at.zi]
        for dz in range(1, 4):
            z = lax.rem(at.zi - dz + 4, 4)
            wire.arrive(("t", dz), small_line.at[z], at.line(z))
            whole = whole + small_line[z]
        small_out[...] = whole

    pieces = 4
    wide = 8 // pieces
    up, down = at.line(jnp.minimum(at.zi + 1, 3)), at.line(jnp.maximum(at.zi - 1, 0))

    def qkv_pass(goal, piece):
        part = pl.ds(piece * wide, wide)

        if goal > 0:

            @pl.when(at.zi < goal)
            def _():
                @pl.when(at.zi == 0)
                def _():
                    up_sum[goal, part] = qkv_in[goal, part]

                @pl.when(at.zi > 0)
                def _():
                    wire.arrive(("u", goal, piece), up_in.at[goal, part], down)
                    up_sum[goal, part] = add(qkv_in[goal, part], up_in[goal, part])

            wire.send(
                ("u", goal, piece),
                up_sum.at[goal, part],
                up_in.at[goal, part],
                up,
                at.zi < goal,
            )
        back = 3 - goal
        if back < 3:

            @pl.when(at.zi > back)
            def _():
                @pl.when(at.zi == 3)
                def _():
                    down_sum[back, part] = qkv_in[back, part]

                @pl.when(at.zi < 3)
                def _():
                    wire.arrive(("d", back, piece), down_in.at[back, part], up)
                    down_sum[back, part] = add(qkv_in[back, part], down_in[back, part])

            wire.send(
                ("d", back, piece),
                down_sum.at[back, part],
                down_in.at[back, part],
                down,
                at.zi > back,
            )

    proj_home = at.head_home()

    def proj_add(slot, *terms):
        add_rows(proj_sum.at[slot], *(term.at[slot] for term in terms))

    below, above = at.zi < proj_home, at.zi > proj_home
    ends = (at.zi == 0) | (at.zi == 3)

    def proj_pass(slot):
        under, over = proj_below.at[slot], proj_above.at[slot]
        wire.send(("pu", slot), proj_in.at[slot], under, up, below & ends)
        wire.send(("pd", slot), proj_in.at[slot], over, down, above & ends)

        def climb():
            wire.arrive(("pu", slot), under, down)
            proj_add(slot, proj_in, proj_below)

        def descend():
            wire.arrive(("pd", slot), over, up)
            proj_add(slot, proj_in, proj_above)

        pl.when(below & (at.zi > 0))(climb)
        pl.when(above & (at.zi < 3))(descend)
        source = proj_sum.at[slot]
        key = "pu", slot
        wire.send(("pu2", slot), source, under, up, below & (at.zi > 0), recv=key)
        key = "pd", slot
        wire.send(("pd2", slot), source, over, down, above & (at.zi < 3), recv=key)

    chunk = at.y * 2 + at.c
    holder_device, holder = at.holder()

    def proj_last():
        home = at.zi == proj_home
        for slot in range(4):
            under, over = proj_below.at[slot], proj_above.at[slot]

            def first():
                wire.arrive(("pu", slot), under, down)
                proj_add(slot, proj_in, proj_below)

            def only():
                wire.arrive(("pd", slot), over, up)
                proj_add(slot, proj_in, proj_above)

            def both():
                wire.arrive(("pd", slot), over, up)
                proj_add(slot, proj_sum, proj_above)

            pl.when(home & (at.zi > 0))(first)
            pl.when(home & (at.zi == 0))(only)
            pl.when(home & (at.zi > 0) & (at.zi < 3))(both)
            target = (at.zo, at.zi, at.x, slot // 2, slot % 2)
            other = (chunk != slot) | (at.rank != holder)
            wire.send(("o", slot), proj_sum.at[slot], proj_out, target, home & other, recv="o")
        own = pltpu.make_async_copy(proj_sum.at[chunk], proj_out, own_sems.at[2])
        pl.when(home & (at.rank == holder))(own.start)
        pl.when(home & (at.rank == holder))(own.wait)

    def qkv_last(piece):
        part = pl.ds(piece * wide, wide)
        for goal in range(4):

            @pl.when(at.zi == goal)
            def _():
                terms = [qkv_in[goal, part]]
                if goal > 0:
                    wire.arrive(("u", goal, piece), up_in.at[goal, part], down)
                    terms.append(up_in[goal, part])
                if goal < 3:
                    wire.arrive(("d", goal, piece), down_in.at[goal, part], up)
                    terms.append(down_in[goal, part])
                qkv_total[part] = add(*terms)

    for piece in range(pieces):
        qkv_pass(3, piece)
        if piece == 0:
            next(scatter)
    for slot in range(4):
        proj_pass(slot)
    next(scatter)
    small_second()
    for piece in range(pieces):
        qkv_pass(2, piece)
    for _ in scatter:
        pass
    for piece in range(pieces):
        qkv_pass(1, piece)
    proj_last()
    for piece in range(pieces):
        qkv_last(piece)
    own_qkv = pltpu.make_async_copy(
        qkv_total.at[at.rank], qkv_out.at[at.rank], own_sems.at[1]
    )
    own_qkv.start()
    for delta in range(1, 8):
        device, other = at.plane(delta)
        wire.send(("q", delta), qkv_total.at[other], qkv_out.at[at.rank], device)
    own_qkv.wait()
    for delta in range(1, 8):
        device, other = at.plane(delta)
        wire.arrive(("q", delta), qkv_out.at[other], device)
    small_last()
    wire.arrive("o", proj_out, holder_device, at.rank != holder)
    wire.drain()


def close_heads(qkv_part, proj_part, small_part, part):
    _, _, rows_own, qkv_width = qkv_part.shape
    _, own, width = part.shape
    low_type = jnp.bfloat16
    line = (4, 8, rows_own, qkv_width)
    small_shape = small_part.shape[1:]
    return pl.pallas_call(
        close_heads_kernel,
        out_shape=(
            jax.ShapeDtypeStruct((8, rows_own, qkv_width), low_type),
            jax.ShapeDtypeStruct((rows_own, width), low_type),
            jax.ShapeDtypeStruct(small_shape[1:], small_part.dtype),
            jax.ShapeDtypeStruct((own, width), jnp.float32),
        ),
        in_specs=[VMEM] * 4,
        out_specs=(ANY, ANY, VMEM, VMEM),
        scratch_shapes=[
            pltpu.VMEM((4, rows_own, width), low_type),
            pltpu.VMEM((4, rows_own, width), low_type),
            pltpu.VMEM((4, rows_own, width), low_type),
            pltpu.VMEM(small_part.shape, small_part.dtype),
            pltpu.VMEM(small_shape, small_part.dtype),
            pltpu.VMEM(small_shape, small_part.dtype),
            pltpu.VMEM(line, low_type),
            pltpu.VMEM(line, low_type),
            pltpu.VMEM(line, low_type),
            pltpu.VMEM(line, low_type),
            pltpu.VMEM(line[1:], low_type),
        ]
        + plane_scratch(own, width)
        + [
            pltpu.SemaphoreType.DMA((80,)),
            pltpu.SemaphoreType.DMA((80,)),
            pltpu.SemaphoreType.DMA((3,)),
        ],
        compiler_params=comm_params(2),
        name="close_heads",
    )(qkv_part, proj_part, small_part, part)


def group_body(
    hidden_in,
    token_marks,
    out_grad,
    qkv_weight,
    proj_weight,
    gate_weight,
    up_weight,
    down_weight,
    first_gain,
    first_shift,
    second_gain,
    second_shift,
):
    micro_count, _, pos_count, width = hidden_in.shape
    rows_own = qkv_weight.shape[0]
    units = gate_weight.shape[1]
    head_ways = math.prod(lax.axis_size(name) for name in HEAD_AXES)
    unit_ways = math.prod(lax.axis_size(name) for name in UNIT_AXES)
    chunk_count = lax.axis_size("y") * lax.axis_size("c")
    row_length = pos_count * chunk_count
    x_size = lax.axis_size("x")
    marks_own = token_marks.astype(jnp.float32)
    own = micro_count * pos_count
    head_width = width // head_ways
    heads_here = head_width // HEAD_DIM
    unit_width = -(-units // (unit_ways * LANES)) * LANES
    unit_pad = unit_width * unit_ways - units
    x_own = hidden_in.reshape(own, width)

    params = jnp.stack([first_gain, first_shift, second_gain, second_shift])
    small = jnp.concatenate([params.astype(jnp.float32).ravel(), marks_own.ravel()])
    small = jnp.pad(small, (0, -small.size % (8 * LANES))).reshape(-1, LANES)

    qkv_parts = qkv_weight.reshape(rows_own, 3, 4, 2, head_width)
    qkv_parts = jnp.stack([qkv_parts[:, :, home] for home in (0, 3, 1, 2)])
    qkv_parts = qkv_parts.transpose(3, 0, 1, 2, 4).reshape(head_ways, rows_own, 3 * head_width)

    def unit_parts(*matrices):
        parts = jnp.stack(matrices)
        parts = jnp.pad(parts, ((0, 0), (0, 0), (0, unit_pad)))
        parts = parts.reshape(len(matrices), rows_own, unit_ways, unit_width)
        return parts.transpose(2, 0, 1, 3)

    qkv_here, gate_here, proj_here, x_all, small = open_heads(
        qkv_parts, unit_parts(gate_weight), proj_weight, x_own, small
    )
    qkv_here = qkv_here.reshape(-1, 3 * head_width)
    gate_here = gate_here.reshape(-1, unit_width)
    x_all = x_all.reshape(-1, width)
    proj_here = proj_here.reshape(head_width, width)
    small = small.reshape(unit_ways * 4, -1)
    params = small[:, : 4 * rows_own].reshape(-1, 4, rows_own).transpose(1, 0, 2)
    gain_one, shift_one, gain_two, shift_two = params.reshape(4, 1, width)
    marks = small.reshape(4, head_ways, -1)[lax.axis_index("zi")]
    marks = marks[:, 4 * rows_own : 4 * rows_own + own * 3].astype(jnp.int32)

    mixed = dot(x_all, qkv_here)

    def to_rows(values):
        inner = values.shape[1:]
        values = values.reshape((x_size, chunk_count, micro_count, pos_count) + inner)
        return jnp.swapaxes(values, 1, 2).reshape((x_size * micro_count, row_length) + inner)

    def from_rows(values):
        inner = values.shape[2:]
        values = values.reshape((x_size, micro_count, chunk_count, pos_count) + inner)
        return jnp.swapaxes(values, 1, 2).reshape((head_ways * own,) + inner)

    row_marks = to_rows(marks.reshape(head_ways * own, 3))
    cosine, sine = rotary_tables(row_marks[..., 2])
    cosine, sine = cosine[:, :, None, :], sine[:, :, None, :]
    mixed = to_rows(mixed).reshape(x_size * micro_count, row_length, 3, heads_here, HEAD_DIM)
    queries = low(rotate(mixed[:, :, 0], cosine, sine))
    key_rows = low(rotate(mixed[:, :, 1], cosine, sine))
    value_rows = low(mixed[:, :, 2])
    place = jnp.arange(row_length, dtype=jnp.int32)
    allowed = (row_marks[:, :, None, 0] == row_marks[:, None, :, 0]) & (
        (place[None, None, :] <= place[None, :, None])
        | (place[None, :] < row_marks[:, :, 1])[:, None, :]
    )
    score_scale = 1.0 / math.sqrt(HEAD_DIM)

    def pair(spec, left_side, right_side):
        return jnp.einsum(spec, left_side, right_side, preferred_element_type=jnp.float32)

    scores = pair("rqhd,rkhd->rhqk", queries, key_rows) * score_scale
    scores = jnp.where(allowed[:, None], scores, masked_score)
    exp_scores = jnp.exp(scores - jnp.max(scores, axis=-1, keepdims=True))
    probs = exp_scores / jnp.sum(exp_scores, axis=-1, keepdims=True)
    probs_low = low(probs)
    context = low(pair("rhqk,rkhd->rqhd", probs_low, value_rows))

    context = from_rows(context).reshape(-1, head_width)
    branch_part = low(dot(context, proj_here)).reshape(head_ways, own, width)
    normed, hat_one, inverse_one, normed_all, ffn = open_units(
        branch_part, x_own, gain_one, shift_one, unit_parts(up_weight, down_weight)
    )
    normed_all = normed_all.reshape(-1, width)
    up_here, down_here = ffn.reshape(2, -1, unit_width)

    gate_val = dot(normed_all, gate_here)
    up_val = dot(normed_all, up_here)
    gelu_val, gelu_slope = gelu_parts(gate_val)
    active = low(gelu_val * up_val)
    down_part = low(contract_last(active, down_here)).reshape(unit_ways, own, width)
    layer_rows, d_second, down_low, norm_grads = turn(
        down_part, normed, out_grad.reshape(own, width), gain_two, shift_two
    )
    gain_two_grad, shift_two_grad = jnp.sum(norm_grads, axis=1)
    down_low = down_low.reshape(-1, width)
    d_active = dot(down_low, down_here)
    gate_low = low(d_active * up_val * gelu_slope)
    up_low = low(d_active * gelu_val)
    d_normed_part = low(contract_last(gate_low, gate_here) + contract_last(up_low, up_here))

    def unit_grad(left_side, right_side):
        part = low(contract_first(left_side, right_side))
        return part.reshape(4, 2, 2, 2, rows_own, unit_width)

    ffn_grads = (
        unit_grad(normed_all, gate_low),
        unit_grad(normed_all, up_low),
        unit_grad(down_low, active),
    )
    ffn_part, branch_all, d_first, norm_grads = close_units(
        ffn_grads,
        d_normed_part.reshape(unit_ways, own, width),
        d_second,
        hat_one,
        inverse_one,
        gain_one,
    )
    gain_one_grad, shift_one_grad = jnp.sum(norm_grads, axis=1)
    branch_all = branch_all.reshape(-1, width)
    small_grads = jnp.stack([gain_one_grad, shift_one_grad, gain_two_grad, shift_two_grad])
    small_grads = small_grads.reshape(4, 4, head_ways, rows_own).transpose(2, 1, 0, 3)
    small_grads = small_grads.reshape(head_ways, 4, 4 * rows_own // LANES, LANES)
    small_grads = jnp.pad(small_grads, ((0, 0), (0, 0), (0, -small_grads.shape[2] % 8), (0, 0)))

    proj_part = low(contract_first(context, branch_all)).reshape(4, rows_own, width)
    d_context = to_rows(low(contract_last(branch_all, proj_here)))
    d_context = d_context.reshape(x_size * micro_count, row_length, heads_here, HEAD_DIM)
    d_probs = pair("rqhd,rkhd->rhqk", d_context, value_rows)
    d_scores = low(probs * (d_probs - jnp.sum(probs * d_probs, axis=-1, keepdims=True)))
    d_query = pair("rhqk,rkhd->rqhd", d_scores, key_rows) * score_scale
    d_keys = pair("rhqk,rqhd->rkhd", d_scores, queries) * score_scale
    d_values = pair("rhqk,rqhd->rkhd", probs_low, d_context)
    d_mixed = low(
        jnp.stack(
            [rotate(d_query, cosine, -sine), rotate(d_keys, cosine, -sine), d_values], axis=2
        )
    )
    d_mixed = from_rows(d_mixed.reshape(x_size * micro_count, row_length, 3 * head_width))
    d_input = low(contract_last(d_mixed, qkv_here)).reshape(head_ways, own, width)
    qkv_part = low(contract_first(x_all, d_mixed))
    qkv_part, proj_part, small_grads, d_input = close_heads(
        qkv_part.reshape(4, 8, rows_own, 3 * head_width), proj_part, small_grads, d_input
    )
    d_input = deep_alpha * d_first + d_input
    small_grads = small_grads.ravel()[: 4 * rows_own].reshape(4, rows_own)
    qkv_grad = qkv_part.reshape(2, 4, rows_own, 3, head_width)
    qkv_grad = jnp.stack([qkv_grad[:, place] for place in (0, 2, 3, 1)])
    qkv_grad = qkv_grad.transpose(2, 3, 0, 1, 4).reshape(rows_own, 3 * width).astype(jnp.float32)
    ffn_part = ffn_part.transpose(1, 2, 0, 3).reshape(3, rows_own, unit_ways * unit_width)
    gate_grad, up_grad, down_grad = (
        ffn_part[index, :, :units].astype(jnp.float32) for index in range(3)
    )
    return (
        layer_rows.reshape(micro_count, 1, pos_count, width),
        low(d_input).reshape(micro_count, 1, pos_count, width),
        qkv_grad,
        proj_part.astype(jnp.float32),
        gate_grad,
        up_grad,
        down_grad,
        small_grads[0],
        small_grads[1],
        small_grads[2],
        small_grads[3],
    )


def body(hidden_in, token_marks, out_grad, *weights):
    joined = lax.axis_size("zo")
    if joined == 1:
        return group_body(hidden_in, token_marks, out_grad, *weights)
    rows = weights[0].shape[0]
    width = hidden_in.shape[-1]
    groups = width // (joined * rows)
    group_place = lax.axis_index(ALL[1:])

    def inward(values):
        shape = values.shape
        values = values.reshape(shape[:-1] + (joined, groups, rows))
        return jnp.swapaxes(values, -3, -2).reshape(shape)

    def outward(values):
        shape = values.shape
        values = values.reshape(shape[:-1] + (groups, joined, rows))
        return jnp.swapaxes(values, -3, -2).reshape(shape)

    proj = gather(weights[1], ALL)
    proj = inward(lax.dynamic_slice_in_dim(proj, group_place * joined * rows, joined * rows))
    weights = [gather(weight, "zo") for weight in weights]
    weights[1] = proj
    outs = list(group_body(inward(hidden_in), token_marks, inward(out_grad), *weights))
    outs[:2] = outward(outs[0]), outward(outs[1])
    proj_grad = jnp.zeros((width, width), jnp.float32)
    proj_grad = lax.dynamic_update_slice_in_dim(
        proj_grad, outward(outs[3]), group_place * joined * rows, 0
    )
    outs[2:] = [scatter_sum(grad, "zo") for grad in outs[2:]]
    outs[3] = scatter_sum(proj_grad, ALL)
    return tuple(outs)


def solution(mesh):
    seq_size, ctx_size = mesh.shape["seq"], mesh.shape["ctx"]
    cores, x_size = 2, 2
    zi_size = math.gcd(4, seq_size // x_size)
    zo_size = seq_size // (x_size * zi_size)
    devices = np.asarray(mesh.devices).reshape(
        zo_size, zi_size, x_size, ctx_size // cores, cores
    )
    inner = Mesh(devices, ALL)
    tokens = P(None, ("zo", "zi", "x"), ("y", "c"), None)
    matrix = P(ALL, None)
    vector = P(ALL)
    return jax.shard_map(
        body,
        mesh=inner,
        in_specs=(tokens,) * 3 + (matrix,) * 5 + (vector,) * 4,
        out_specs=(tokens,) * 2 + (matrix,) * 5 + (vector,) * 4,
        check_vma=False,
    )
```

```python
import math

import jax
import jax.numpy as jnp
import numpy as np
from jax import lax
from jax.experimental import pallas as pl
from jax.experimental.pallas import tpu as pltpu
from jax.sharding import Mesh
from jax.sharding import PartitionSpec as P

HEAD_DIM = 128
LANES = 128

deep_alpha = 48.0**0.25
norm_eps = 1e-05
masked_score = -1e30

ALL = ("zo", "zi", "x", "y", "c")
HEAD_AXES = ("x", "y", "c")
UNIT_AXES = ("zi", "c")
HEAD_COPIES = ("zo", "zi")
UNIT_COPIES = ("zo", "x", "y")


def contract_last(left_side, right_side):
    return lax.dot_general(
        left_side, right_side, (((1,), (1,)), ((), ())), preferred_element_type=jnp.float32
    )


def contract_first(left_side, right_side):
    return lax.dot_general(
        left_side, right_side, (((0,), (0,)), ((), ())), preferred_element_type=jnp.float32
    )


def dot(left_side, right_side):
    return jnp.dot(left_side, right_side, preferred_element_type=jnp.float32)


def low(values):
    return values.astype(jnp.bfloat16)


def norm_parts(values):
    center = values - jnp.mean(values, axis=-1, keepdims=True)
    spread = jnp.mean(center * center, axis=-1, keepdims=True)
    inverse = lax.rsqrt(spread + norm_eps)
    return center * inverse, inverse


def norm_back(cotangent, hat, inverse, gain_vec):
    scaled = cotangent * gain_vec
    return (
        scaled
        - jnp.mean(scaled, axis=-1, keepdims=True)
        - hat * jnp.mean(scaled * hat, axis=-1, keepdims=True)
    ) * inverse


def rotary_tables(positions):
    half = HEAD_DIM // 2
    exponent = jnp.arange(half, dtype=jnp.float32) * (2.0 / HEAD_DIM)
    angles = positions.astype(jnp.float32)[..., None] * jnp.exp(-math.log(10000.0) * exponent)
    return (jnp.cos(angles), jnp.sin(angles))


def rotate(values, cosine, sine):
    half = HEAD_DIM // 2
    front, back = values[..., :half], values[..., half:]
    return jnp.concatenate(
        [front * cosine - back * sine, back * cosine + front * sine], axis=-1
    )


def gather(values, axes):
    return lax.all_gather(values, axes, axis=0, tiled=True)


def scatter_sum(values, axes):
    return lax.psum_scatter(values, axes, scatter_dimension=0, tiled=True)


def gelu_parts(value):
    phi = 0.5 * lax.erfc(-value * math.sqrt(0.5))
    density = jnp.exp(-0.5 * value * value) * (1.0 / math.sqrt(2.0 * math.pi))
    return value * phi, phi + value * density


MESH = pl.DeviceIdType.MESH


class Wire:
    def __init__(self, send_sems, recv_sems):
        self.send_sems, self.recv_sems = send_sems, recv_sems
        self.keys, self.sent = {}, []

    def number(self, key, span=1):
        if key not in self.keys:
            self.keys[key] = sum(size for _, size in self.keys.values()), span
        return self.keys[key][0]

    def copy(self, key, source, target, device, slot=0, span=1, recv=None):
        send = self.number(key, span)
        receive = send if recv is None else self.number(recv)
        return pltpu.make_async_remote_copy(
            src_ref=source,
            dst_ref=target,
            send_sem=self.send_sems.at[send],
            recv_sem=self.recv_sems.at[receive + slot],
            device_id=device,
            device_id_type=MESH,
        )

    def send(self, key, source, target, device, when=None, recv=None):
        copy = self.copy(key, source, target, device, recv=recv)
        if when is None:
            copy.start()
        else:
            pl.when(when)(copy.start)
        self.sent.append((copy, when))

    def send_to_slot(self, key, source, target, device, slot, span, when):
        copy = self.copy(key, source, target, device, slot, span)
        pl.when(when)(copy.start)
        self.sent.append((copy, when))

    def arrive(self, key, target, device, when=None):
        copy = self.copy(key, target, target, device)
        if when is None:
            copy.wait_recv()
        else:
            pl.when(when)(copy.wait_recv)

    def arrive_slot(self, key, target, device, slot, span, when):
        pl.when(when)(self.copy(key, target, target, device, slot, span).wait_recv)

    def drain(self):
        for copy, when in self.sent:
            if when is None:
                copy.wait_send()
            else:
                pl.when(when)(copy.wait_send)


def flip(value, bit):
    return 1 - value if bit else value


def enter(devices):
    barrier = pltpu.get_barrier_semaphore()
    for device in devices:
        pl.semaphore_signal(barrier, inc=1, device_id=device, device_id_type=MESH)
    pl.semaphore_wait(barrier, len(devices))


class Place:
    def __init__(self):
        self.zo, self.zi, self.x, self.y, self.c = (lax.axis_index(name) for name in ALL)
        self.rank = self.x * 4 + self.y * 2 + self.c
        self.unit = self.zi * 2 + self.c

    def head_home(self):
        return self.y + self.c * (3 - 2 * self.y)

    def holder(self):
        y, c = lax.rem((self.zi + 1) // 2, 2), self.zi // 2
        return (self.zo, self.zi, self.x, y, c), self.x * 4 + y * 2 + c

    def plane(self, delta):
        dx, dy, dc = delta >> 2 & 1, delta >> 1 & 1, delta & 1
        x, y, c = flip(self.x, dx), flip(self.y, dy), flip(self.c, dc)
        return (self.zo, self.zi, x, y, c), x * 4 + y * 2 + c

    def column(self, step):
        other = lax.rem(self.unit + step + 8, 8)
        return (self.zo, other // 2, self.x, self.y, lax.rem(other, 2)), other

    def ends(self):
        return self.line(jnp.minimum(self.zi + 1, 3)), self.line(jnp.maximum(self.zi - 1, 0))

    def line(self, z):
        return (self.zo, z, self.x, self.y, self.c)

    def column_neighbours(self):
        return [self.line(z) for z in self.others()] + [self.plane(1)[0]]

    def others(self):
        return [lax.rem(self.zi + step, 4) for step in (1, 2, 3)]

    def neighbours(self):
        plane = [self.plane(delta)[0] for delta in range(1, 8)]
        column = []
        for dz in range(1, 4):
            z = lax.rem(self.zi + dz, 4)
            column += [(self.zo, z, self.x, self.y, core) for core in (0, 1)]
        return plane + column


def unit_gather_flow(at, wire, ffn_in, ffn_out, own_sem):
    x_side, y_side = at.plane(4)[0], at.plane(2)[0]
    steps = (1, 7, 2, 6, 3, 5, 4)
    mine = ffn_out.at[:, at.zi, at.x, at.y, at.c]
    own = pltpu.make_async_copy(ffn_in.at[at.unit], mine, own_sem)
    own.start()
    for step in (4, 3, 5, 2, 6, 1, 7):
        device, other = at.column(step)
        wire.send(("f", step), ffn_in.at[other], mine, device)
    own.wait()

    def slot(step, x, y):
        source = lax.rem(at.unit - step + 8, 8)
        return ffn_out.at[:, source // 2, x, y, lax.rem(source, 2)]

    def first(step):
        here = slot(step, at.x, at.y)
        if step:
            wire.arrive(("f", step), here, at.column(-step)[0])
        wire.send(("fx", step), here, here, x_side)
        wire.send(("fy", step), here, here, y_side)

    def second(step, turn):
        from_x, from_y = slot(step, 1 - at.x, at.y), slot(step, at.x, 1 - at.y)
        wire.arrive(("fx", step), from_x, x_side)
        wire.arrive(("fy", step), from_y, y_side)
        if turn % 2:
            wire.send(("fd", step), from_x, from_x, y_side)
        else:
            wire.send(("fd", step), from_y, from_y, x_side)

    yield
    first(0)
    for turn, step in enumerate(steps):
        yield
        first(step)
        if turn >= 1:
            second(((0,) + steps)[turn - 1], turn - 1)
    yield
    second(steps[5], 6)
    second(steps[6], 7)
    yield
    for step in (0,) + steps:
        wire.arrive(("fd", step), slot(step, 1 - at.x, 1 - at.y), x_side)


def open_heads_kernel(
    qkv_in,
    ffn_in,
    proj_in,
    x_in,
    small_in,
    qkv_out,
    ffn_out,
    proj_out,
    x_out,
    small_out,
    send_sems,
    recv_sems,
    own_sems,
):
    at = Place()
    wire = Wire(send_sems, recv_sems)
    enter(at.neighbours())
    up, down = at.ends()
    chunk = at.y * 2 + at.c
    holder_device, holder = at.holder()
    proj_home = at.head_home()
    own = [
        pltpu.make_async_copy(qkv_in.at[at.rank], qkv_out.at[at.zi, at.rank], own_sems.at[1]),
        pltpu.make_async_copy(small_in, small_out.at[at.zi, at.rank], own_sems.at[3]),
    ]
    for copy in own:
        copy.start()
    for delta in range(1, 8):
        device, other = at.plane(delta)
        wire.send(("q", delta), qkv_in.at[other], qkv_out.at[at.zi, at.rank], device)
    wire.send_to_slot("p", proj_in, proj_out.at[chunk], holder_device, chunk, 4, at.rank != holder)
    proj_own = pltpu.make_async_copy(proj_in, proj_out.at[chunk], own_sems.at[4])
    pl.when(at.rank == holder)(proj_own.start)
    for delta in range(1, 8):
        device, _ = at.plane(delta)
        wire.send(("s", delta), small_in, small_out.at[at.zi, at.rank], device)
    spread = plane_gather_flow(at, wire, x_in, x_out, own_sems.at[0])
    next(spread)
    for copy in own:
        copy.wait()
    pl.when(at.rank == holder)(proj_own.wait)

    def small_second():
        for delta in range(1, 8):
            device, other = at.plane(delta)
            wire.arrive(("s", delta), small_out.at[at.zi, other], device)
        for dz in range(1, 4):
            device = at.line(lax.rem(at.zi + dz, 4))
            wire.send(("t", dz), small_out.at[at.zi], small_out.at[at.zi], device)

    def small_last():
        for dz in range(1, 4):
            z = lax.rem(at.zi - dz + 4, 4)
            wire.arrive(("t", dz), small_out.at[z], at.line(z))

    def proj_start(slot):
        block = proj_out.at[slot]
        source = (at.zo, at.zi, at.x, slot // 2, slot % 2)
        home = at.zi == proj_home
        mine = home & ((chunk != slot) | (at.rank != holder))
        wire.arrive_slot("p", block, source, slot, 4, mine)
        wire.send(("pu", slot), block, block, up, home & (at.zi < 3))
        wire.send(("pd", slot), block, block, down, home & (at.zi > 0))

    def proj_relay(slot):
        block = proj_out.at[slot]
        above, below = at.zi > proj_home, at.zi < proj_home
        wire.arrive(("pu", slot), block, down, above)
        wire.arrive(("pd", slot), block, up, below)
        key = "pu", slot
        wire.send(("pu2", slot), block, block, up, above & (at.zi < 3), recv=key)
        key = "pd", slot
        wire.send(("pd2", slot), block, block, down, below & (at.zi > 0), recv=key)

    def qkv_slot(z, delta):
        return qkv_out.at[jnp.clip(z, 0, 3), at.plane(delta)[1]]

    def qkv_hop(hop, delta):
        below, above = qkv_slot(at.zi - hop, delta), qkv_slot(at.zi + hop, delta)
        if hop == 0:
            if delta:
                wire.arrive(("q", delta), below, at.plane(delta)[0])
        else:
            wire.arrive(("up", hop - 1, delta), below, down, at.zi >= hop)
            wire.arrive(("down", hop - 1, delta), above, up, at.zi <= 3 - hop)
        if hop < 3:
            wire.send(("up", hop, delta), below, below, up, (at.zi >= hop) & (at.zi < 3))
            wire.send(("down", hop, delta), above, above, down, (at.zi <= 3 - hop) & (at.zi > 0))

    for delta in range(8):
        qkv_hop(0, delta)
    units = unit_gather_flow(at, wire, ffn_in, ffn_out, own_sems.at[2])
    for slot in range(4):
        proj_start(slot)
    next(units)
    next(spread)
    small_second()
    next(units)
    for _ in spread:
        pass
    for delta in range(8):
        qkv_hop(1, delta)
        if delta % 2:
            proj_relay(delta // 2)
            next(units)
    for delta in range(8):
        qkv_hop(2, delta)
        if delta % 2:
            next(units)
    for delta in range(8):
        qkv_hop(3, delta)
    for _ in units:
        pass
    small_last()
    wire.drain()


def turned(values, cosine, sine):
    return values * cosine + pltpu.roll(values, HEAD_DIM // 2, 1) * sine


def row_place(rank, micro):
    piece = rank % 4
    return (rank // 4) * 2 + micro, piece


def open_units_kernel(
    x_all,
    qkv,
    proj,
    cosine,
    sine,
    start_query,
    start_key,
    end_key,
    x_own,
    gain,
    shift,
    ffn_in,
    queries,
    key_rows,
    value_rows,
    probs_out,
    context,
    normed,
    hat,
    inverse_out,
    normed_all,
    ffn_out,
    part,
    branch,
    *rest,
):
    at = Place()
    *scratch, send_sems, recv_sems, own_sems = rest
    wire = Wire(send_sems, recv_sems)
    enter(at.neighbours())
    own = x_own.shape[0]
    pos = own // 2
    length = 4 * pos
    heads = context.shape[-1] // HEAD_DIM
    wide = heads * HEAD_DIM

    def project():
        @pl.loop(0, 8)
        def _(rank):
            mixed = dot(x_all[rank], qkv[...])
            for micro in range(2):
                row, piece = row_place(rank, micro)
                place = pl.ds(pl.multiple_of(piece * pos, pos), pos)
                near = mixed[micro * pos : (micro + 1) * pos]
                cos, sin = cosine[row, place], sine[row, place]
                for head in range(heads):
                    cols = pl.ds(head * HEAD_DIM, HEAD_DIM)
                    for kind, target in enumerate((queries, key_rows, value_rows)):
                        first = kind * wide + head * HEAD_DIM
                        values = near[:, first : first + HEAD_DIM]
                        if kind < 2:
                            values = turned(values, cos, sin)
                        target[row, place, cols] = values.astype(jnp.bfloat16)

    def attend():
        scale = 1.0 / math.sqrt(HEAD_DIM)
        here = lax.broadcasted_iota(jnp.int32, (length, length), 0)
        there = lax.broadcasted_iota(jnp.int32, (length, length), 1)

        @pl.loop(0, 4)
        def _(row):
            bound = end_key[row].astype(jnp.int32)
            seen = (start_query[row] == start_key[row]) & ((there <= here) | (there < bound))
            for head in range(heads):
                cols = pl.ds(head * HEAD_DIM, HEAD_DIM)
                scores = contract_last(queries[row, :, cols], key_rows[row, :, cols]) * scale
                scores = jnp.where(seen, scores, masked_score)
                scores = jnp.exp(scores - jnp.max(scores, axis=-1, keepdims=True))
                probs = scores / jnp.sum(scores, axis=-1, keepdims=True)
                probs_out[row, head] = probs
                result = dot(probs.astype(jnp.bfloat16), value_rows[row, :, cols])
                result = result.astype(jnp.bfloat16)
                for piece in range(4):
                    target = pl.ds(pl.multiple_of((row % 2) * pos, pos), pos)
                    source = result[piece * pos : (piece + 1) * pos]
                    context[(row // 2) * 4 + piece, target, cols] = source

    def branch_parts():
        @pl.loop(0, 8)
        def _(rank):
            part[rank] = dot(context[rank], proj[...]).astype(jnp.bfloat16)

    def norm_rows():
        count = 16

        @pl.loop(0, own // count)
        def _(index):
            rows = pl.ds(pl.multiple_of(index * count, count), count)
            whole = deep_alpha * x_own[rows].astype(jnp.float32) + branch[rows]
            near, inverse = norm_parts(whole)
            hat[rows] = near
            inverse_out[rows] = jnp.broadcast_to(inverse, (count, LANES))
            normed[rows] = (near * gain[...] + shift[...]).astype(jnp.bfloat16)

    scatter = plane_scatter_flow(at, wire, part, branch, *scratch)
    units = unit_gather_flow(at, wire, ffn_in, ffn_out, own_sems.at[0])
    next(units)
    next(units)
    project()
    next(units)
    next(units)
    attend()
    next(units)
    branch_parts()
    next(scatter)
    next(units)
    next(scatter)
    next(scatter)
    for _ in scatter:
        pass
    norm_rows()
    spread = column_gather_flow(at, wire, 0, normed, normed_all, own_sems.at[1])
    next(spread)
    next(units)
    next(units)
    next(spread)
    next(units)
    next(spread)
    for _ in spread:
        next(units, None)
    for _ in units:
        pass
    wire.drain()


ANY = pl.BlockSpec(memory_space=pl.ANY)
VMEM = pl.BlockSpec(memory_space=pltpu.VMEM)


def comm_params(number):
    return pltpu.CompilerParams(
        collective_id=number, has_side_effects=True, vmem_limit_bytes=63 * 2**20
    )


def open_heads(qkv_parts, ffn_parts, proj_own, x_own, small):
    _, rows_own, qkv_width = qkv_parts.shape
    _, matrices, _, unit_width = ffn_parts.shape
    own, width = x_own.shape
    low_type = jnp.bfloat16
    return pl.pallas_call(
        open_heads_kernel,
        out_shape=(
            jax.ShapeDtypeStruct((4, 8, rows_own, qkv_width), low_type),
            jax.ShapeDtypeStruct((matrices, 4, 2, 2, 2, rows_own, unit_width), low_type),
            jax.ShapeDtypeStruct((4, rows_own, width), low_type),
            jax.ShapeDtypeStruct((8, own, width), low_type),
            jax.ShapeDtypeStruct((4, 8) + small.shape, small.dtype),
        ),
        in_specs=[VMEM] * 5,
        out_specs=(ANY,) * 5,
        scratch_shapes=[
            pltpu.SemaphoreType.DMA((136,)),
            pltpu.SemaphoreType.DMA((136,)),
            pltpu.SemaphoreType.DMA((5,)),
        ],
        compiler_params=comm_params(1),
        name="open_heads",
    )(qkv_parts, ffn_parts, proj_own, x_own, small)


def open_units(x_all, qkv, proj, tables, x_own, gain, shift, ffn_parts):
    _, matrices, rows_own, unit_width = ffn_parts.shape
    own, width = x_own.shape
    head_width = proj.shape[0]
    length = 2 * own
    low_type = jnp.bfloat16
    rows = jax.ShapeDtypeStruct((4, length, head_width), low_type)
    return pl.pallas_call(
        open_units_kernel,
        out_shape=(
            rows,
            rows,
            rows,
            jax.ShapeDtypeStruct((4, head_width // HEAD_DIM, length, length), jnp.float32),
            jax.ShapeDtypeStruct((8, own, head_width), low_type),
            jax.ShapeDtypeStruct((own, width), low_type),
            jax.ShapeDtypeStruct((own, width), jnp.float32),
            jax.ShapeDtypeStruct((own, LANES), jnp.float32),
            jax.ShapeDtypeStruct((8, own, width), low_type),
            jax.ShapeDtypeStruct((matrices, 4, 2, 2, 2, rows_own, unit_width), low_type),
        ),
        in_specs=[VMEM] * 12,
        out_specs=(VMEM,) * 8 + (ANY, ANY),
        scratch_shapes=[
            pltpu.VMEM((8, own, width), low_type),
            pltpu.VMEM((own, width), jnp.float32),
        ]
        + plane_scratch(own, width)
        + [
            pltpu.SemaphoreType.DMA((64,)),
            pltpu.SemaphoreType.DMA((64,)),
            pltpu.SemaphoreType.DMA((2,)),
        ],
        compiler_params=comm_params(4),
        name="open_units",
    )(x_all, qkv, proj, *tables, x_own, gain, shift, ffn_parts)


def add_rows(out, *terms):
    step = 32

    @pl.loop(0, out.shape[0] // step)
    def _(index):
        part = pl.ds(pl.multiple_of(index * step, step), step)
        whole = terms[0][part].astype(jnp.float32)
        for term in terms[1:]:
            whole = whole + term[part].astype(jnp.float32)
        out[part] = whole.astype(out.dtype)


def column_scatter_flow(
    at, wire, tag, part, out, core_in, core_sum, up_in, down_in, up_sum, down_sum
):
    core_side = at.plane(1)[0]
    up, down = at.ends()
    for goal in (3, 0, 2, 1):
        source = part.at[goal * 2 + 1 - at.c]
        wire.send(("rc", tag, goal), source, core_in.at[goal], core_side)
    yield
    for goal in (3, 0, 2, 1):
        wire.arrive(("rc", tag, goal), core_in.at[goal], core_side)
        add_rows(core_sum.at[goal], part.at[goal * 2 + at.c], core_in.at[goal])
        source = core_sum.at[goal]
        if goal > 0:
            wire.send(("ru", tag, goal), source, up_in.at[goal], up, at.zi == 0)
        if goal < 3:
            wire.send(("rd", tag, goal), source, down_in.at[goal], down, at.zi == 3)

    def climb(goal):
        wire.arrive(("ru", tag, goal), up_in.at[goal], down)
        add_rows(up_sum.at[goal], core_sum.at[goal], up_in.at[goal])

    def descend(goal):
        wire.arrive(("rd", tag, goal), down_in.at[goal], up)
        add_rows(down_sum.at[goal], core_sum.at[goal], down_in.at[goal])

    for goal in (3, 2):
        yield
        back = 3 - goal
        passing = (at.zi > 0) & (at.zi < goal)
        pl.when(passing)(lambda: climb(goal))
        key = "ru", tag, goal
        wire.send(("ru2", tag, goal), up_sum.at[goal], up_in.at[goal], up, passing, recv=key)
        passing = (at.zi < 3) & (at.zi > back)
        pl.when(passing)(lambda: descend(back))
        key = "rd", tag, back
        wire.send(("rd2", tag, back), down_sum.at[back], down_in.at[back], down, passing, recv=key)
    yield
    add_rows(out, core_sum.at[at.zi])

    def last(key, source, device):
        wire.arrive(key, source, device)
        add_rows(out, out, source)

    for goal in range(4):
        if goal > 0:
            pl.when(at.zi == goal)(lambda: last(("ru", tag, goal), up_in.at[goal], down))
        if goal < 3:
            pl.when(at.zi == goal)(lambda: last(("rd", tag, goal), down_in.at[goal], up))


def column_gather_flow(at, wire, tag, own_in, out, own_sem):
    core_side = at.plane(1)[0]
    up, down = at.ends()

    def slot(z, c):
        return out.at[jnp.clip(z, 0, 3) * 2 + c]

    mine = slot(at.zi, at.c)
    wire.send(("gu", tag, 0), own_in, mine, up, at.zi < 3)
    wire.send(("gd", tag, 0), own_in, mine, down, at.zi > 0)
    wire.send(("gc", tag), own_in, mine, core_side)
    own = pltpu.make_async_copy(own_in, mine, own_sem)
    own.start()
    for hop in (1, 2, 3):
        yield
        below, above = slot(at.zi - hop, at.c), slot(at.zi + hop, at.c)
        has_below, has_above = at.zi >= hop, at.zi <= 3 - hop
        wire.arrive(("gu", tag, hop - 1), below, down, has_below)
        if hop < 3:
            wire.send(("gu", tag, hop), below, below, up, has_below & (at.zi < 3))
        wire.send(("gcu", tag, hop), below, below, core_side, has_below)
        wire.arrive(("gd", tag, hop - 1), above, up, has_above)
        if hop < 3:
            wire.send(("gd", tag, hop), above, above, down, has_above & (at.zi > 0))
        wire.send(("gcd", tag, hop), above, above, core_side, has_above)
    yield
    own.wait()
    wire.arrive(("gc", tag), slot(at.zi, 1 - at.c), core_side)
    for hop in (1, 2, 3):
        below, above = slot(at.zi - hop, 1 - at.c), slot(at.zi + hop, 1 - at.c)
        wire.arrive(("gcu", tag, hop), below, core_side, at.zi >= hop)
        wire.arrive(("gcd", tag, hop), above, core_side, at.zi <= 3 - hop)


def column_scratch(own, width):
    return [pltpu.VMEM((4, own, width), jnp.bfloat16)] * 6


def plane_scatter_flow(at, wire, part, out, core_in, core_sum, side_in, side_sum, last_in):
    x_side, y_side, core_side = at.plane(4)[0], at.plane(2)[0], at.plane(1)[0]
    half = out.shape[1] // 2
    halves = (pl.ds(0, half), pl.ds(half, half))
    order = ((1, 1), (1, 0), (0, 1), (0, 0))

    def place(dx, dy):
        return flip(at.x, dx), flip(at.y, dy)

    for dx, dy in order:
        x, y = place(dx, dy)
        other = x * 4 + y * 2 + 1 - at.c
        wire.send(("c", dx, dy), part.at[other], core_in.at[dx * 2 + dy], core_side)
    yield
    for dx, dy in order:
        x, y = place(dx, dy)
        mine = x * 4 + y * 2 + at.c
        slot = dx * 2 + dy
        wire.arrive(("c", dx, dy), core_in.at[slot], core_side)
        add_rows(core_sum.at[slot], part.at[mine], core_in.at[slot])
        if dx:
            source = core_sum.at[slot, :, halves[0]]
            wire.send(("sa", dy), source, side_in.at[0, dy], x_side)
        if dy:
            source = core_sum.at[slot, :, halves[1]]
            wire.send(("sb", dx), source, side_in.at[1, dx], y_side)
    yield
    wire.arrive(("sa", 1), side_in.at[0, 1], x_side)
    add_rows(side_sum.at[0], core_sum.at[1, :, halves[0]], side_in.at[0, 1])
    wire.send("sy", side_sum.at[0], last_in.at[0], y_side)
    wire.arrive(("sb", 1), side_in.at[1, 1], y_side)
    add_rows(side_sum.at[1], core_sum.at[2, :, halves[1]], side_in.at[1, 1])
    wire.send("sx", side_sum.at[1], last_in.at[1], x_side)
    yield
    wire.arrive(("sa", 0), side_in.at[0, 0], x_side)
    wire.arrive(("sb", 0), side_in.at[1, 0], y_side)
    wire.arrive("sy", last_in.at[0], y_side)
    terms = core_sum.at[0, :, halves[0]], side_in.at[0, 0], last_in.at[0]
    add_rows(out.at[:, halves[0]], *terms)
    wire.arrive("sx", last_in.at[1], x_side)
    terms = core_sum.at[0, :, halves[1]], side_in.at[1, 0], last_in.at[1]
    add_rows(out.at[:, halves[1]], *terms)


def plane_scratch(own, width):
    return [
        pltpu.VMEM((4, own, width), jnp.bfloat16),
        pltpu.VMEM((4, own, width), jnp.bfloat16),
        pltpu.VMEM((2, 2, own, width // 2), jnp.bfloat16),
        pltpu.VMEM((2, own, width // 2), jnp.bfloat16),
        pltpu.VMEM((2, own, width // 2), jnp.bfloat16),
    ]


def plane_gather_flow(at, wire, own_in, out, own_sem):
    x_side, y_side, core_side = at.plane(4)[0], at.plane(2)[0], at.plane(1)[0]
    half = own_in.shape[0] // 2
    mine = out.at[at.rank]
    wire.send("gx", own_in, mine, x_side)
    wire.send("gy", own_in, mine, y_side)
    wire.send("gc0", own_in, mine, core_side)
    own = pltpu.make_async_copy(own_in, mine, own_sem)
    own.start()
    yield
    from_x, from_y, from_xy = (at.plane(delta)[1] for delta in (4, 2, 6))
    low_half, high_half = pl.ds(0, half), pl.ds(half, half)
    wire.arrive("gx", out.at[from_x], x_side)
    wire.send("gd0", out.at[from_x, low_half], out.at[from_x, low_half], y_side)
    wire.send("gc1", out.at[from_x], out.at[from_x], core_side)
    wire.arrive("gy", out.at[from_y], y_side)
    wire.send("gd1", out.at[from_y, high_half], out.at[from_y, high_half], x_side)
    wire.send("gc2", out.at[from_y], out.at[from_y], core_side)
    yield
    wire.arrive("gd0", out.at[from_xy, low_half], y_side)
    wire.arrive("gd1", out.at[from_xy, high_half], x_side)
    wire.send("gc3", out.at[from_xy], out.at[from_xy], core_side)
    own.wait()
    for index, delta in enumerate((1, 5, 3, 7)):
        wire.arrive("gc%d" % index, out.at[at.plane(delta)[1]], core_side)


def turn_kernel(
    part,
    normed,
    out_grad,
    gain,
    shift,
    layer_out,
    d_second,
    down_out,
    norm_out,
    second,
    down_low,
    core_in,
    core_sum,
    up_in,
    down_in,
    up_sum,
    down_sum,
    send_sems,
    recv_sems,
    own_sems,
):
    at = Place()
    wire = Wire(send_sems, recv_sems)
    enter(at.column_neighbours())
    pieces = 4
    height = normed.shape[0] // pieces
    scratch = core_in, core_sum, up_in, down_in, up_sum, down_sum

    def norm_rows(start):
        count = 16

        @pl.loop(0, height // count)
        def _(index):
            rows = pl.ds(pl.multiple_of(start + index * count, count), count)
            whole = deep_alpha * normed[rows].astype(jnp.float32) + second[rows]
            near, inverse = norm_parts(whole)
            layer_out[rows] = (near * gain[...] + shift[...]).astype(jnp.bfloat16)
            cotangent = out_grad[rows].astype(jnp.float32)
            result = norm_back(cotangent, near, inverse, gain[...])
            d_second[rows] = result
            down_low[rows] = result.astype(jnp.bfloat16)
            along = cotangent * near
            norm_out[0] += along[:8] + along[8:]
            norm_out[1] += cotangent[:8] + cotangent[8:]

    scatters, gathers = [], []
    for index in range(pieces):
        rows = pl.ds(index * height, height)
        views = [ref.at[:, rows] for ref in scratch]
        scatters.append(
            column_scatter_flow(at, wire, index, part.at[:, rows], second.at[rows], *views)
        )
        gathers.append(
            column_gather_flow(
                at, wire, index, down_low.at[rows], down_out.at[:, rows], own_sems.at[index]
            )
        )
    norm_out[...] = jnp.zeros_like(norm_out)
    for flow in scatters:
        next(flow)
    for flow in scatters:
        next(flow)
    for index in range(pieces):
        for _ in scatters[index]:
            for flow in gathers[:index]:
                next(flow, None)
        norm_rows(index * height)
        next(gathers[index])
    for _ in range(4):
        for flow in gathers:
            next(flow, None)
    for flow in gathers:
        for _ in flow:
            pass
    wire.drain()


def turn(part, normed, out_grad, gain, shift):
    _, own, width = part.shape
    low_type = jnp.bfloat16
    return pl.pallas_call(
        turn_kernel,
        out_shape=(
            jax.ShapeDtypeStruct((own, width), low_type),
            jax.ShapeDtypeStruct((own, width), jnp.float32),
            jax.ShapeDtypeStruct((8, own, width), low_type),
            jax.ShapeDtypeStruct((2, 8, width), jnp.float32),
        ),
        in_specs=[VMEM] * 5,
        out_specs=(VMEM, VMEM, ANY, VMEM),
        scratch_shapes=[
            pltpu.VMEM((own, width), jnp.float32),
            pltpu.VMEM((own, width), low_type),
        ]
        + column_scratch(own, width)
        + [
            pltpu.SemaphoreType.DMA((112,)),
            pltpu.SemaphoreType.DMA((112,)),
            pltpu.SemaphoreType.DMA((4,)),
        ],
        compiler_params=comm_params(5),
        name="turn",
    )(part, normed, out_grad, gain, shift)


def close_units_kernel(
    gate_in,
    raise_in,
    lower_in,
    part,
    d_second,
    hat,
    inverse,
    gain,
    ffn_out,
    branch_out,
    d_first,
    norm_out,
    first_in,
    second_sum,
    second_in,
    total,
    d_normed,
    branch_low,
    core_in,
    core_sum,
    up_in,
    down_in,
    up_sum,
    down_sum,
    send_sems,
    recv_sems,
    own_sems,
):
    at = Place()
    wire = Wire(send_sems, recv_sems)
    enter(at.neighbours())
    x_side, y_side = at.plane(4)[0], at.plane(2)[0]
    steps = (4, 3, 5, 2, 6, 1, 7, 0)
    sources = gate_in, raise_in, lower_in

    def owner(step):
        other = at.column(step)[1]
        return other // 2, lax.rem(other, 2)

    def ffn_first(turn):
        step = steps[turn]
        z, c = owner(step)
        for index, source in enumerate(sources):
            if turn % 2:
                block, device = source.at[z, 1 - at.x, :, c], x_side
            else:
                block, device = source.at[z, :, 1 - at.y, c], y_side
            wire.send(("a", step, index), block, first_in.at[step, index], device)

    def ffn_second(turn):
        step = steps[turn]
        z, c = owner(step)
        for index, source in enumerate(sources):
            if turn % 2:
                wire.arrive(("a", step, index), first_in.at[step, index], x_side)
                terms = source.at[z, at.x, 1 - at.y, c], first_in.at[step, index, 1 - at.y]
            else:
                wire.arrive(("a", step, index), first_in.at[step, index], y_side)
                terms = source.at[z, 1 - at.x, at.y, c], first_in.at[step, index, 1 - at.x]
            add_rows(second_sum.at[step, index], *terms)
        wire.send(
            ("b", step), second_sum.at[step], second_in.at[step], y_side if turn % 2 else x_side
        )

    own_total = pltpu.make_async_copy(total.at[0], ffn_out.at[at.unit], own_sems.at[0])

    def ffn_last(turn):
        step = steps[turn]
        z, c = owner(step)
        near = at.y if turn % 2 else at.x
        wire.arrive(("b", step), second_in.at[step], x_side)
        for index, source in enumerate(sources):
            add_rows(
                total.at[step, index],
                source.at[z, at.x, at.y, c],
                first_in.at[step, index, near],
                second_in.at[step, index],
            )
        if step:
            wire.send(("f", step), total.at[step], ffn_out.at[at.unit], at.column(step)[0])
        else:
            own_total.start()

    def norm_rows():
        count = 16
        norm_out[...] = jnp.zeros_like(norm_out)

        @pl.loop(0, hat.shape[0] // count)
        def _(index):
            rows = pl.ds(pl.multiple_of(index * count, count), count)
            cotangent = deep_alpha * d_second[rows] + d_normed[rows]
            near = hat[rows]
            result = norm_back(cotangent, near, inverse[rows, :1], gain[...])
            d_first[rows] = result
            branch_low[rows] = result.astype(jnp.bfloat16)
            along = cotangent * near
            norm_out[0] += along[:8] + along[8:]
            norm_out[1] += cotangent[:8] + cotangent[8:]

    scatter = column_scatter_flow(
        at, wire, 0, part, d_normed, core_in, core_sum, up_in, down_in, up_sum, down_sum
    )
    next(scatter)
    for turn in range(5):
        ffn_first(turn)
    next(scatter)
    next(scatter)
    ffn_second(0)
    ffn_first(5)
    ffn_second(1)
    ffn_first(6)
    next(scatter)
    ffn_second(2)
    ffn_first(7)
    ffn_second(3)
    for _ in scatter:
        pass
    norm_rows()
    spread = plane_gather_flow(at, wire, branch_low, branch_out, own_sems.at[1])
    next(spread)
    ffn_last(0)
    ffn_last(1)
    ffn_second(4)
    ffn_last(2)
    ffn_second(5)
    ffn_last(3)
    next(spread)
    ffn_second(6)
    ffn_second(7)
    ffn_last(4)
    for _ in spread:
        pass
    for turn in range(5, 8):
        ffn_last(turn)
    own_total.wait()
    for step in steps:
        if step:
            device, other = at.column(-step)
            wire.arrive(("f", step), ffn_out.at[other], device)
    wire.drain()


def close_units(grads, part, d_second, hat, inverse, gain):
    rows_own, unit_width = grads[0].shape[-2:]
    _, own, width = part.shape
    low_type = jnp.bfloat16
    block = (rows_own, unit_width)
    return pl.pallas_call(
        close_units_kernel,
        out_shape=(
            jax.ShapeDtypeStruct((8, 3) + block, low_type),
            jax.ShapeDtypeStruct((8, own, width), low_type),
            jax.ShapeDtypeStruct((own, width), jnp.float32),
            jax.ShapeDtypeStruct((2, 8, width), jnp.float32),
        ),
        in_specs=[VMEM] * 8,
        out_specs=(ANY, ANY, VMEM, VMEM),
        scratch_shapes=[
            pltpu.VMEM((8, 3, 2) + block, low_type),
            pltpu.VMEM((8, 3) + block, low_type),
            pltpu.VMEM((8, 3) + block, low_type),
            pltpu.VMEM((8, 3) + block, low_type),
            pltpu.VMEM((own, width), jnp.float32),
            pltpu.VMEM((own, width), low_type),
        ]
        + column_scratch(own, width)
        + [
            pltpu.SemaphoreType.DMA((80,)),
            pltpu.SemaphoreType.DMA((80,)),
            pltpu.SemaphoreType.DMA((2,)),
        ],
        compiler_params=comm_params(3),
        name="close_units",
    )(*grads, part, d_second, hat, inverse, gain)


def close_heads_kernel(
    qkv_in,
    proj_in,
    small_in,
    part,
    qkv_out,
    proj_out,
    small_out,
    d_input,
    proj_below,
    proj_above,
    proj_sum,
    small_plane,
    small_mid,
    small_line,
    up_in,
    down_in,
    up_sum,
    down_sum,
    qkv_total,
    core_in,
    core_sum,
    side_in,
    side_sum,
    last_in,
    send_sems,
    recv_sems,
    own_sems,
):
    at = Place()
    wire = Wire(send_sems, recv_sems)
    enter(at.neighbours())
    scatter = plane_scatter_flow(
        at, wire, part, d_input, core_in, core_sum, side_in, side_sum, last_in
    )
    next(scatter)

    def add(*terms):
        whole = terms[0].astype(jnp.float32)
        for term in terms[1:]:
            whole = whole + term.astype(jnp.float32)
        return whole.astype(jnp.bfloat16)

    for delta in range(1, 8):
        device, other = at.plane(delta)
        wire.send(("s", delta), small_in.at[other], small_plane.at[at.rank], device)

    def small_second():
        whole = small_in[at.rank]
        for delta in range(1, 8):
            device, other = at.plane(delta)
            wire.arrive(("s", delta), small_plane.at[other], device)
            whole = whole + small_plane[other]
        small_mid[...] = whole
        for dz in range(1, 4):
            z = lax.rem(at.zi + dz, 4)
            wire.send(("t", dz), small_mid.at[z], small_line.at[at.zi], at.line(z))

    def small_last():
        whole = small_mid[at.zi]
        for dz in range(1, 4):
            z = lax.rem(at.zi - dz + 4, 4)
            wire.arrive(("t", dz), small_line.at[z], at.line(z))
            whole = whole + small_line[z]
        small_out[...] = whole

    pieces = 4
    wide = 8 // pieces
    up, down = at.line(jnp.minimum(at.zi + 1, 3)), at.line(jnp.maximum(at.zi - 1, 0))

    def qkv_pass(goal, piece):
        part = pl.ds(piece * wide, wide)

        if goal > 0:

            @pl.when(at.zi < goal)
            def _():
                @pl.when(at.zi == 0)
                def _():
                    up_sum[goal, part] = qkv_in[goal, part]

                @pl.when(at.zi > 0)
                def _():
                    wire.arrive(("u", goal, piece), up_in.at[goal, part], down)
                    up_sum[goal, part] = add(qkv_in[goal, part], up_in[goal, part])

            wire.send(
                ("u", goal, piece),
                up_sum.at[goal, part],
                up_in.at[goal, part],
                up,
                at.zi < goal,
            )
        back = 3 - goal
        if back < 3:

            @pl.when(at.zi > back)
            def _():
                @pl.when(at.zi == 3)
                def _():
                    down_sum[back, part] = qkv_in[back, part]

                @pl.when(at.zi < 3)
                def _():
                    wire.arrive(("d", back, piece), down_in.at[back, part], up)
                    down_sum[back, part] = add(qkv_in[back, part], down_in[back, part])

            wire.send(
                ("d", back, piece),
                down_sum.at[back, part],
                down_in.at[back, part],
                down,
                at.zi > back,
            )

    proj_home = at.head_home()

    def proj_add(slot, *terms):
        add_rows(proj_sum.at[slot], *(term.at[slot] for term in terms))

    below, above = at.zi < proj_home, at.zi > proj_home
    ends = (at.zi == 0) | (at.zi == 3)

    def proj_pass(slot):
        under, over = proj_below.at[slot], proj_above.at[slot]
        wire.send(("pu", slot), proj_in.at[slot], under, up, below & ends)
        wire.send(("pd", slot), proj_in.at[slot], over, down, above & ends)

        def climb():
            wire.arrive(("pu", slot), under, down)
            proj_add(slot, proj_in, proj_below)

        def descend():
            wire.arrive(("pd", slot), over, up)
            proj_add(slot, proj_in, proj_above)

        pl.when(below & (at.zi > 0))(climb)
        pl.when(above & (at.zi < 3))(descend)
        source = proj_sum.at[slot]
        key = "pu", slot
        wire.send(("pu2", slot), source, under, up, below & (at.zi > 0), recv=key)
        key = "pd", slot
        wire.send(("pd2", slot), source, over, down, above & (at.zi < 3), recv=key)

    chunk = at.y * 2 + at.c
    holder_device, holder = at.holder()

    def proj_last():
        home = at.zi == proj_home
        for slot in range(4):
            under, over = proj_below.at[slot], proj_above.at[slot]

            def first():
                wire.arrive(("pu", slot), under, down)
                proj_add(slot, proj_in, proj_below)

            def only():
                wire.arrive(("pd", slot), over, up)
                proj_add(slot, proj_in, proj_above)

            def both():
                wire.arrive(("pd", slot), over, up)
                proj_add(slot, proj_sum, proj_above)

            pl.when(home & (at.zi > 0))(first)
            pl.when(home & (at.zi == 0))(only)
            pl.when(home & (at.zi > 0) & (at.zi < 3))(both)
            target = (at.zo, at.zi, at.x, slot // 2, slot % 2)
            other = (chunk != slot) | (at.rank != holder)
            wire.send(("o", slot), proj_sum.at[slot], proj_out, target, home & other, recv="o")
        own = pltpu.make_async_copy(proj_sum.at[chunk], proj_out, own_sems.at[2])
        pl.when(home & (at.rank == holder))(own.start)
        pl.when(home & (at.rank == holder))(own.wait)

    def qkv_last(piece):
        part = pl.ds(piece * wide, wide)
        for goal in range(4):

            @pl.when(at.zi == goal)
            def _():
                terms = [qkv_in[goal, part]]
                if goal > 0:
                    wire.arrive(("u", goal, piece), up_in.at[goal, part], down)
                    terms.append(up_in[goal, part])
                if goal < 3:
                    wire.arrive(("d", goal, piece), down_in.at[goal, part], up)
                    terms.append(down_in[goal, part])
                qkv_total[part] = add(*terms)

    for piece in range(pieces):
        qkv_pass(3, piece)
        if piece == 0:
            next(scatter)
    for slot in range(4):
        proj_pass(slot)
    next(scatter)
    small_second()
    for piece in range(pieces):
        qkv_pass(2, piece)
    for _ in scatter:
        pass
    for piece in range(pieces):
        qkv_pass(1, piece)
    proj_last()
    for piece in range(pieces):
        qkv_last(piece)
    own_qkv = pltpu.make_async_copy(
        qkv_total.at[at.rank], qkv_out.at[at.rank], own_sems.at[1]
    )
    own_qkv.start()
    for delta in range(1, 8):
        device, other = at.plane(delta)
        wire.send(("q", delta), qkv_total.at[other], qkv_out.at[at.rank], device)
    own_qkv.wait()
    for delta in range(1, 8):
        device, other = at.plane(delta)
        wire.arrive(("q", delta), qkv_out.at[other], device)
    small_last()
    wire.arrive("o", proj_out, holder_device, at.rank != holder)
    wire.drain()


def close_heads(qkv_part, proj_part, small_part, part):
    _, _, rows_own, qkv_width = qkv_part.shape
    _, own, width = part.shape
    low_type = jnp.bfloat16
    line = (4, 8, rows_own, qkv_width)
    small_shape = small_part.shape[1:]
    return pl.pallas_call(
        close_heads_kernel,
        out_shape=(
            jax.ShapeDtypeStruct((8, rows_own, qkv_width), low_type),
            jax.ShapeDtypeStruct((rows_own, width), low_type),
            jax.ShapeDtypeStruct(small_shape[1:], small_part.dtype),
            jax.ShapeDtypeStruct((own, width), jnp.float32),
        ),
        in_specs=[VMEM] * 4,
        out_specs=(ANY, ANY, VMEM, VMEM),
        scratch_shapes=[
            pltpu.VMEM((4, rows_own, width), low_type),
            pltpu.VMEM((4, rows_own, width), low_type),
            pltpu.VMEM((4, rows_own, width), low_type),
            pltpu.VMEM(small_part.shape, small_part.dtype),
            pltpu.VMEM(small_shape, small_part.dtype),
            pltpu.VMEM(small_shape, small_part.dtype),
            pltpu.VMEM(line, low_type),
            pltpu.VMEM(line, low_type),
            pltpu.VMEM(line, low_type),
            pltpu.VMEM(line, low_type),
            pltpu.VMEM(line[1:], low_type),
        ]
        + plane_scratch(own, width)
        + [
            pltpu.SemaphoreType.DMA((80,)),
            pltpu.SemaphoreType.DMA((80,)),
            pltpu.SemaphoreType.DMA((3,)),
        ],
        compiler_params=comm_params(2),
        name="close_heads",
    )(qkv_part, proj_part, small_part, part)


def group_body(
    hidden_in,
    token_marks,
    out_grad,
    qkv_weight,
    proj_weight,
    gate_weight,
    up_weight,
    down_weight,
    first_gain,
    first_shift,
    second_gain,
    second_shift,
):
    micro_count, _, pos_count, width = hidden_in.shape
    rows_own = qkv_weight.shape[0]
    units = gate_weight.shape[1]
    head_ways = math.prod(lax.axis_size(name) for name in HEAD_AXES)
    unit_ways = math.prod(lax.axis_size(name) for name in UNIT_AXES)
    chunk_count = lax.axis_size("y") * lax.axis_size("c")
    row_length = pos_count * chunk_count
    x_size = lax.axis_size("x")
    marks_own = token_marks.astype(jnp.float32)
    own = micro_count * pos_count
    head_width = width // head_ways
    heads_here = head_width // HEAD_DIM
    unit_width = -(-units // (unit_ways * LANES)) * LANES
    unit_pad = unit_width * unit_ways - units
    x_own = hidden_in.reshape(own, width)

    params = jnp.stack([first_gain, first_shift, second_gain, second_shift])
    small = jnp.concatenate([params.astype(jnp.float32).ravel(), marks_own.ravel()])
    small = jnp.pad(small, (0, -small.size % (8 * LANES))).reshape(-1, LANES)

    qkv_parts = qkv_weight.reshape(rows_own, 3, 4, 2, head_width)
    qkv_parts = jnp.stack([qkv_parts[:, :, home] for home in (0, 3, 1, 2)])
    qkv_parts = qkv_parts.transpose(3, 0, 1, 2, 4).reshape(head_ways, rows_own, 3 * head_width)

    def unit_parts(*matrices):
        parts = jnp.stack(matrices)
        parts = jnp.pad(parts, ((0, 0), (0, 0), (0, unit_pad)))
        parts = parts.reshape(len(matrices), rows_own, unit_ways, unit_width)
        return parts.transpose(2, 0, 1, 3)

    qkv_here, gate_here, proj_here, x_all, small = open_heads(
        qkv_parts, unit_parts(gate_weight), proj_weight, x_own, small
    )
    qkv_here = qkv_here.reshape(-1, 3 * head_width)
    gate_here = gate_here.reshape(-1, unit_width)
    x_all = x_all.reshape(-1, width)
    proj_here = proj_here.reshape(head_width, width)
    small = small.reshape(unit_ways * 4, -1)
    params = small[:, : 4 * rows_own].reshape(-1, 4, rows_own).transpose(1, 0, 2)
    gain_one, shift_one, gain_two, shift_two = params.reshape(4, 1, width)
    marks = small.reshape(4, head_ways, -1)[lax.axis_index("zi")]
    marks = marks[:, 4 * rows_own : 4 * rows_own + own * 3]

    def to_rows(values):
        inner = values.shape[1:]
        values = values.reshape((x_size, chunk_count, micro_count, pos_count) + inner)
        return jnp.swapaxes(values, 1, 2).reshape((x_size * micro_count, row_length) + inner)

    def from_rows(values):
        inner = values.shape[2:]
        values = values.reshape((x_size, micro_count, chunk_count, pos_count) + inner)
        return jnp.swapaxes(values, 1, 2).reshape((head_ways * own,) + inner)

    row_marks = to_rows(marks.reshape(head_ways * own, 3))
    cosine, sine = rotary_tables(row_marks[..., 2])
    tables = (
        jnp.concatenate([cosine, cosine], axis=-1),
        jnp.concatenate([-sine, sine], axis=-1),
        row_marks[:, :, :1],
        row_marks[:, None, :, 0],
        row_marks[:, None, :, 1],
    )
    queries, key_rows, value_rows, probs, context, normed, hat_one, inverse_one, normed_all, ffn = (
        open_units(
            x_all.reshape(head_ways, own, width),
            qkv_here,
            proj_here,
            tables,
            x_own,
            gain_one,
            shift_one,
            unit_parts(up_weight, down_weight),
        )
    )
    rows_shape = (x_size * micro_count, row_length, heads_here, HEAD_DIM)
    queries, key_rows, value_rows = (
        values.reshape(rows_shape) for values in (queries, key_rows, value_rows)
    )
    probs_low = low(probs)
    context = context.reshape(-1, head_width)
    cosine, sine = cosine[:, :, None, :], sine[:, :, None, :]
    score_scale = 1.0 / math.sqrt(HEAD_DIM)

    def pair(spec, left_side, right_side):
        return jnp.einsum(spec, left_side, right_side, preferred_element_type=jnp.float32)

    normed_all = normed_all.reshape(-1, width)
    up_here, down_here = ffn.reshape(2, -1, unit_width)

    gate_val = dot(normed_all, gate_here)
    up_val = dot(normed_all, up_here)
    gelu_val, gelu_slope = gelu_parts(gate_val)
    active = low(gelu_val * up_val)
    down_part = low(contract_last(active, down_here)).reshape(unit_ways, own, width)
    layer_rows, d_second, down_low, norm_grads = turn(
        down_part, normed, out_grad.reshape(own, width), gain_two, shift_two
    )
    gain_two_grad, shift_two_grad = jnp.sum(norm_grads, axis=1)
    down_low = down_low.reshape(-1, width)
    d_active = dot(down_low, down_here)
    gate_low = low(d_active * up_val * gelu_slope)
    up_low = low(d_active * gelu_val)
    d_normed_part = low(contract_last(gate_low, gate_here) + contract_last(up_low, up_here))

    def unit_grad(left_side, right_side):
        part = low(contract_first(left_side, right_side))
        return part.reshape(4, 2, 2, 2, rows_own, unit_width)

    ffn_grads = (
        unit_grad(normed_all, gate_low),
        unit_grad(normed_all, up_low),
        unit_grad(down_low, active),
    )
    ffn_part, branch_all, d_first, norm_grads = close_units(
        ffn_grads,
        d_normed_part.reshape(unit_ways, own, width),
        d_second,
        hat_one,
        inverse_one,
        gain_one,
    )
    gain_one_grad, shift_one_grad = jnp.sum(norm_grads, axis=1)
    branch_all = branch_all.reshape(-1, width)
    small_grads = jnp.stack([gain_one_grad, shift_one_grad, gain_two_grad, shift_two_grad])
    small_grads = small_grads.reshape(4, 4, head_ways, rows_own).transpose(2, 1, 0, 3)
    small_grads = small_grads.reshape(head_ways, 4, 4 * rows_own // LANES, LANES)
    small_grads = jnp.pad(small_grads, ((0, 0), (0, 0), (0, -small_grads.shape[2] % 8), (0, 0)))

    proj_part = low(contract_first(context, branch_all)).reshape(4, rows_own, width)
    d_context = to_rows(low(contract_last(branch_all, proj_here)))
    d_context = d_context.reshape(x_size * micro_count, row_length, heads_here, HEAD_DIM)
    d_probs = pair("rqhd,rkhd->rhqk", d_context, value_rows)
    d_scores = low(probs * (d_probs - jnp.sum(probs * d_probs, axis=-1, keepdims=True)))
    d_query = pair("rhqk,rkhd->rqhd", d_scores, key_rows) * score_scale
    d_keys = pair("rhqk,rqhd->rkhd", d_scores, queries) * score_scale
    d_values = pair("rhqk,rqhd->rkhd", probs_low, d_context)
    d_mixed = low(
        jnp.stack(
            [rotate(d_query, cosine, -sine), rotate(d_keys, cosine, -sine), d_values], axis=2
        )
    )
    d_mixed = from_rows(d_mixed.reshape(x_size * micro_count, row_length, 3 * head_width))
    d_input = low(contract_last(d_mixed, qkv_here)).reshape(head_ways, own, width)
    qkv_part = low(contract_first(x_all, d_mixed))
    qkv_part, proj_part, small_grads, d_input = close_heads(
        qkv_part.reshape(4, 8, rows_own, 3 * head_width), proj_part, small_grads, d_input
    )
    d_input = deep_alpha * d_first + d_input
    small_grads = small_grads.ravel()[: 4 * rows_own].reshape(4, rows_own)
    qkv_grad = qkv_part.reshape(2, 4, rows_own, 3, head_width)
    qkv_grad = jnp.stack([qkv_grad[:, place] for place in (0, 2, 3, 1)])
    qkv_grad = qkv_grad.transpose(2, 3, 0, 1, 4).reshape(rows_own, 3 * width).astype(jnp.float32)
    ffn_part = ffn_part.transpose(1, 2, 0, 3).reshape(3, rows_own, unit_ways * unit_width)
    gate_grad, up_grad, down_grad = (
        ffn_part[index, :, :units].astype(jnp.float32) for index in range(3)
    )
    return (
        layer_rows.reshape(micro_count, 1, pos_count, width),
        low(d_input).reshape(micro_count, 1, pos_count, width),
        qkv_grad,
        proj_part.astype(jnp.float32),
        gate_grad,
        up_grad,
        down_grad,
        small_grads[0],
        small_grads[1],
        small_grads[2],
        small_grads[3],
    )


def body(hidden_in, token_marks, out_grad, *weights):
    joined = lax.axis_size("zo")
    if joined == 1:
        return group_body(hidden_in, token_marks, out_grad, *weights)
    rows = weights[0].shape[0]
    width = hidden_in.shape[-1]
    groups = width // (joined * rows)
    group_place = lax.axis_index(ALL[1:])

    def inward(values):
        shape = values.shape
        values = values.reshape(shape[:-1] + (joined, groups, rows))
        return jnp.swapaxes(values, -3, -2).reshape(shape)

    def outward(values):
        shape = values.shape
        values = values.reshape(shape[:-1] + (groups, joined, rows))
        return jnp.swapaxes(values, -3, -2).reshape(shape)

    proj = gather(weights[1], ALL)
    proj = inward(lax.dynamic_slice_in_dim(proj, group_place * joined * rows, joined * rows))
    weights = [gather(weight, "zo") for weight in weights]
    weights[1] = proj
    outs = list(group_body(inward(hidden_in), token_marks, inward(out_grad), *weights))
    outs[:2] = outward(outs[0]), outward(outs[1])
    proj_grad = jnp.zeros((width, width), jnp.float32)
    proj_grad = lax.dynamic_update_slice_in_dim(
        proj_grad, outward(outs[3]), group_place * joined * rows, 0
    )
    outs[2:] = [scatter_sum(grad, "zo") for grad in outs[2:]]
    outs[3] = scatter_sum(proj_grad, ALL)
    return tuple(outs)


def solution(mesh):
    seq_size, ctx_size = mesh.shape["seq"], mesh.shape["ctx"]
    cores, x_size = 2, 2
    zi_size = math.gcd(4, seq_size // x_size)
    zo_size = seq_size // (x_size * zi_size)
    devices = np.asarray(mesh.devices).reshape(
        zo_size, zi_size, x_size, ctx_size // cores, cores
    )
    inner = Mesh(devices, ALL)
    tokens = P(None, ("zo", "zi", "x"), ("y", "c"), None)
    matrix = P(ALL, None)
    vector = P(ALL)
    return jax.shard_map(
        body,
        mesh=inner,
        in_specs=(tokens,) * 3 + (matrix,) * 5 + (vector,) * 4,
        out_specs=(tokens,) * 2 + (matrix,) * 5 + (vector,) * 4,
        check_vma=False,
    )
```

```python
import math

import jax
import jax.numpy as jnp
import numpy as np
from jax import lax
from jax.experimental import pallas as pl
from jax.experimental.pallas import tpu as pltpu
from jax.sharding import Mesh
from jax.sharding import PartitionSpec as P

HEAD_DIM = 128
LANES = 128

deep_alpha = 48.0**0.25
norm_eps = 1e-05
masked_score = -1e30

ALL = ("zo", "zi", "x", "y", "c")
HEAD_AXES = ("x", "y", "c")
UNIT_AXES = ("zi", "c")
HEAD_COPIES = ("zo", "zi")
UNIT_COPIES = ("zo", "x", "y")


def contract_last(left_side, right_side):
    return lax.dot_general(
        left_side, right_side, (((1,), (1,)), ((), ())), preferred_element_type=jnp.float32
    )


def contract_first(left_side, right_side):
    return lax.dot_general(
        left_side, right_side, (((0,), (0,)), ((), ())), preferred_element_type=jnp.float32
    )


def dot(left_side, right_side):
    return jnp.dot(left_side, right_side, preferred_element_type=jnp.float32)


def low(values):
    return values.astype(jnp.bfloat16)


def norm_parts(values):
    center = values - jnp.mean(values, axis=-1, keepdims=True)
    spread = jnp.mean(center * center, axis=-1, keepdims=True)
    inverse = lax.rsqrt(spread + norm_eps)
    return center * inverse, inverse


def norm_back(cotangent, hat, inverse, gain_vec):
    scaled = cotangent * gain_vec
    return (
        scaled
        - jnp.mean(scaled, axis=-1, keepdims=True)
        - hat * jnp.mean(scaled * hat, axis=-1, keepdims=True)
    ) * inverse


def rotary_tables(positions):
    half = HEAD_DIM // 2
    exponent = jnp.arange(half, dtype=jnp.float32) * (2.0 / HEAD_DIM)
    angles = positions.astype(jnp.float32)[..., None] * jnp.exp(-math.log(10000.0) * exponent)
    return (jnp.cos(angles), jnp.sin(angles))


def rotate(values, cosine, sine):
    half = HEAD_DIM // 2
    front, back = values[..., :half], values[..., half:]
    return jnp.concatenate(
        [front * cosine - back * sine, back * cosine + front * sine], axis=-1
    )


def gather(values, axes):
    return lax.all_gather(values, axes, axis=0, tiled=True)


def scatter_sum(values, axes):
    return lax.psum_scatter(values, axes, scatter_dimension=0, tiled=True)


def gelu_parts(value):
    phi = 0.5 * lax.erfc(-value * math.sqrt(0.5))
    density = jnp.exp(-0.5 * value * value) * (1.0 / math.sqrt(2.0 * math.pi))
    return value * phi, phi + value * density


MESH = pl.DeviceIdType.MESH


class Wire:
    def __init__(self, send_sems, recv_sems):
        self.send_sems, self.recv_sems = send_sems, recv_sems
        self.keys, self.sent = {}, []

    def number(self, key, span=1):
        if key not in self.keys:
            self.keys[key] = sum(size for _, size in self.keys.values()), span
        return self.keys[key][0]

    def copy(self, key, source, target, device, slot=0, span=1, recv=None):
        send = self.number(key, span)
        receive = send if recv is None else self.number(recv)
        return pltpu.make_async_remote_copy(
            src_ref=source,
            dst_ref=target,
            send_sem=self.send_sems.at[send],
            recv_sem=self.recv_sems.at[receive + slot],
            device_id=device,
            device_id_type=MESH,
        )

    def send(self, key, source, target, device, when=None, recv=None):
        copy = self.copy(key, source, target, device, recv=recv)
        if when is None:
            copy.start()
        else:
            pl.when(when)(copy.start)
        self.sent.append((copy, when))

    def send_to_slot(self, key, source, target, device, slot, span, when):
        copy = self.copy(key, source, target, device, slot, span)
        pl.when(when)(copy.start)
        self.sent.append((copy, when))

    def arrive(self, key, target, device, when=None):
        copy = self.copy(key, target, target, device)
        if when is None:
            copy.wait_recv()
        else:
            pl.when(when)(copy.wait_recv)

    def arrive_slot(self, key, target, device, slot, span, when):
        pl.when(when)(self.copy(key, target, target, device, slot, span).wait_recv)

    def drain(self):
        for copy, when in self.sent:
            if when is None:
                copy.wait_send()
            else:
                pl.when(when)(copy.wait_send)


def flip(value, bit):
    return 1 - value if bit else value


def enter(devices):
    barrier = pltpu.get_barrier_semaphore()
    for device in devices:
        pl.semaphore_signal(barrier, inc=1, device_id=device, device_id_type=MESH)
    pl.semaphore_wait(barrier, len(devices))


class Place:
    def __init__(self):
        self.zo, self.zi, self.x, self.y, self.c = (lax.axis_index(name) for name in ALL)
        self.rank = self.x * 4 + self.y * 2 + self.c
        self.unit = self.zi * 2 + self.c

    def head_home(self):
        return self.y + self.c * (3 - 2 * self.y)

    def holder(self):
        y, c = lax.rem((self.zi + 1) // 2, 2), self.zi // 2
        return (self.zo, self.zi, self.x, y, c), self.x * 4 + y * 2 + c

    def plane(self, delta):
        dx, dy, dc = delta >> 2 & 1, delta >> 1 & 1, delta & 1
        x, y, c = flip(self.x, dx), flip(self.y, dy), flip(self.c, dc)
        return (self.zo, self.zi, x, y, c), x * 4 + y * 2 + c

    def column(self, step):
        other = lax.rem(self.unit + step + 8, 8)
        return (self.zo, other // 2, self.x, self.y, lax.rem(other, 2)), other

    def ends(self):
        return self.line(jnp.minimum(self.zi + 1, 3)), self.line(jnp.maximum(self.zi - 1, 0))

    def line(self, z):
        return (self.zo, z, self.x, self.y, self.c)

    def column_neighbours(self):
        return [self.line(z) for z in self.others()] + [self.plane(1)[0]]

    def others(self):
        return [lax.rem(self.zi + step, 4) for step in (1, 2, 3)]

    def neighbours(self):
        plane = [self.plane(delta)[0] for delta in range(1, 8)]
        column = []
        for dz in range(1, 4):
            z = lax.rem(self.zi + dz, 4)
            column += [(self.zo, z, self.x, self.y, core) for core in (0, 1)]
        return plane + column


def unit_gather_flow(at, wire, ffn_in, ffn_out, own_sem):
    x_side, y_side = at.plane(4)[0], at.plane(2)[0]
    steps = (1, 7, 2, 6, 3, 5, 4)
    mine = ffn_out.at[:, at.zi, at.x, at.y, at.c]
    own = pltpu.make_async_copy(ffn_in.at[at.unit], mine, own_sem)
    own.start()
    for step in (4, 3, 5, 2, 6, 1, 7):
        device, other = at.column(step)
        wire.send(("f", step), ffn_in.at[other], mine, device)
    own.wait()

    def slot(step, x, y):
        source = lax.rem(at.unit - step + 8, 8)
        return ffn_out.at[:, source // 2, x, y, lax.rem(source, 2)]

    def first(step):
        here = slot(step, at.x, at.y)
        if step:
            wire.arrive(("f", step), here, at.column(-step)[0])
        wire.send(("fx", step), here, here, x_side)
        wire.send(("fy", step), here, here, y_side)

    def second(step, turn):
        from_x, from_y = slot(step, 1 - at.x, at.y), slot(step, at.x, 1 - at.y)
        wire.arrive(("fx", step), from_x, x_side)
        wire.arrive(("fy", step), from_y, y_side)
        if turn % 2:
            wire.send(("fd", step), from_x, from_x, y_side)
        else:
            wire.send(("fd", step), from_y, from_y, x_side)

    yield
    first(0)
    for turn, step in enumerate(steps):
        yield
        first(step)
        if turn >= 1:
            second(((0,) + steps)[turn - 1], turn - 1)
    yield
    second(steps[5], 6)
    second(steps[6], 7)
    yield
    for step in (0,) + steps:
        wire.arrive(("fd", step), slot(step, 1 - at.x, 1 - at.y), x_side)


def open_heads_kernel(
    qkv_in,
    ffn_in,
    proj_in,
    x_in,
    small_in,
    qkv_out,
    ffn_out,
    proj_out,
    x_out,
    small_out,
    send_sems,
    recv_sems,
    own_sems,
):
    at = Place()
    wire = Wire(send_sems, recv_sems)
    enter(at.neighbours())
    up, down = at.ends()
    chunk = at.y * 2 + at.c
    holder_device, holder = at.holder()
    proj_home = at.head_home()
    own = [
        pltpu.make_async_copy(qkv_in.at[at.rank], qkv_out.at[at.zi, at.rank], own_sems.at[1]),
        pltpu.make_async_copy(small_in, small_out.at[at.zi, at.rank], own_sems.at[3]),
    ]
    for copy in own:
        copy.start()
    for delta in range(1, 8):
        device, other = at.plane(delta)
        wire.send(("q", delta), qkv_in.at[other], qkv_out.at[at.zi, at.rank], device)
    wire.send_to_slot("p", proj_in, proj_out.at[chunk], holder_device, chunk, 4, at.rank != holder)
    proj_own = pltpu.make_async_copy(proj_in, proj_out.at[chunk], own_sems.at[4])
    pl.when(at.rank == holder)(proj_own.start)
    for delta in range(1, 8):
        device, _ = at.plane(delta)
        wire.send(("s", delta), small_in, small_out.at[at.zi, at.rank], device)
    spread = plane_gather_flow(at, wire, x_in, x_out, own_sems.at[0])
    next(spread)
    for copy in own:
        copy.wait()
    pl.when(at.rank == holder)(proj_own.wait)

    def small_second():
        for delta in range(1, 8):
            device, other = at.plane(delta)
            wire.arrive(("s", delta), small_out.at[at.zi, other], device)
        for dz in range(1, 4):
            device = at.line(lax.rem(at.zi + dz, 4))
            wire.send(("t", dz), small_out.at[at.zi], small_out.at[at.zi], device)

    def small_last():
        for dz in range(1, 4):
            z = lax.rem(at.zi - dz + 4, 4)
            wire.arrive(("t", dz), small_out.at[z], at.line(z))

    def proj_start(slot):
        block = proj_out.at[slot]
        source = (at.zo, at.zi, at.x, slot // 2, slot % 2)
        home = at.zi == proj_home
        mine = home & ((chunk != slot) | (at.rank != holder))
        wire.arrive_slot("p", block, source, slot, 4, mine)
        wire.send(("pu", slot), block, block, up, home & (at.zi < 3))
        wire.send(("pd", slot), block, block, down, home & (at.zi > 0))

    def proj_relay(slot):
        block = proj_out.at[slot]
        above, below = at.zi > proj_home, at.zi < proj_home
        wire.arrive(("pu", slot), block, down, above)
        wire.arrive(("pd", slot), block, up, below)
        key = "pu", slot
        wire.send(("pu2", slot), block, block, up, above & (at.zi < 3), recv=key)
        key = "pd", slot
        wire.send(("pd2", slot), block, block, down, below & (at.zi > 0), recv=key)

    def qkv_slot(z, delta):
        return qkv_out.at[jnp.clip(z, 0, 3), at.plane(delta)[1]]

    def qkv_hop(hop, delta):
        below, above = qkv_slot(at.zi - hop, delta), qkv_slot(at.zi + hop, delta)
        if hop == 0:
            if delta:
                wire.arrive(("q", delta), below, at.plane(delta)[0])
        else:
            wire.arrive(("up", hop - 1, delta), below, down, at.zi >= hop)
            wire.arrive(("down", hop - 1, delta), above, up, at.zi <= 3 - hop)
        if hop < 3:
            wire.send(("up", hop, delta), below, below, up, (at.zi >= hop) & (at.zi < 3))
            wire.send(("down", hop, delta), above, above, down, (at.zi <= 3 - hop) & (at.zi > 0))

    for delta in range(8):
        qkv_hop(0, delta)
    units = unit_gather_flow(at, wire, ffn_in, ffn_out, own_sems.at[2])
    for slot in range(4):
        proj_start(slot)
    next(units)
    next(spread)
    small_second()
    next(units)
    for _ in spread:
        pass
    for delta in range(8):
        qkv_hop(1, delta)
        if delta % 2:
            proj_relay(delta // 2)
            next(units)
    for delta in range(8):
        qkv_hop(2, delta)
        if delta % 2:
            next(units)
    for delta in range(8):
        qkv_hop(3, delta)
    for _ in units:
        pass
    small_last()
    wire.drain()


def turned(values, cosine, sine):
    return values * cosine + pltpu.roll(values, HEAD_DIM // 2, 1) * sine


def row_place(rank, micro):
    piece = rank % 4
    return (rank // 4) * 2 + micro, piece


def open_units_kernel(
    x_all,
    qkv,
    proj,
    cosine,
    sine,
    start_query,
    start_key,
    end_key,
    x_own,
    gain,
    shift,
    ffn_in,
    queries,
    key_rows,
    value_rows,
    probs_out,
    context,
    normed,
    hat,
    inverse_out,
    normed_all,
    ffn_out,
    part,
    branch,
    *rest,
):
    at = Place()
    *scratch, send_sems, recv_sems, own_sems = rest
    wire = Wire(send_sems, recv_sems)
    enter(at.neighbours())
    own = x_own.shape[0]
    pos = own // 2
    length = 4 * pos
    heads = context.shape[-1] // HEAD_DIM
    wide = heads * HEAD_DIM

    def project():
        @pl.loop(0, 8)
        def _(rank):
            mixed = dot(x_all[rank], qkv[...])
            for micro in range(2):
                row, piece = row_place(rank, micro)
                place = pl.ds(pl.multiple_of(piece * pos, pos), pos)
                near = mixed[micro * pos : (micro + 1) * pos]
                cos, sin = cosine[row, place], sine[row, place]
                for head in range(heads):
                    cols = pl.ds(head * HEAD_DIM, HEAD_DIM)
                    for kind, target in enumerate((queries, key_rows, value_rows)):
                        first = kind * wide + head * HEAD_DIM
                        values = near[:, first : first + HEAD_DIM]
                        if kind < 2:
                            values = turned(values, cos, sin)
                        target[row, place, cols] = values.astype(jnp.bfloat16)

    def attend():
        scale = 1.0 / math.sqrt(HEAD_DIM)
        here = lax.broadcasted_iota(jnp.int32, (length, length), 0)
        there = lax.broadcasted_iota(jnp.int32, (length, length), 1)

        @pl.loop(0, 4)
        def _(row):
            bound = end_key[row].astype(jnp.int32)
            seen = (start_query[row] == start_key[row]) & ((there <= here) | (there < bound))
            for head in range(heads):
                cols = pl.ds(head * HEAD_DIM, HEAD_DIM)
                scores = contract_last(queries[row, :, cols], key_rows[row, :, cols]) * scale
                scores = jnp.where(seen, scores, masked_score)
                scores = jnp.exp(scores - jnp.max(scores, axis=-1, keepdims=True))
                probs = scores / jnp.sum(scores, axis=-1, keepdims=True)
                probs_out[row, head] = probs
                result = dot(probs.astype(jnp.bfloat16), value_rows[row, :, cols])
                result = result.astype(jnp.bfloat16)
                for piece in range(4):
                    target = pl.ds(pl.multiple_of((row % 2) * pos, pos), pos)
                    source = result[piece * pos : (piece + 1) * pos]
                    context[(row // 2) * 4 + piece, target, cols] = source

    def branch_parts():
        @pl.loop(0, 8)
        def _(rank):
            part[rank] = dot(context[rank], proj[...]).astype(jnp.bfloat16)

    pieces = 4
    height = own // pieces

    def norm_rows(start):
        count = 16

        @pl.loop(0, height // count)
        def _(index):
            rows = pl.ds(pl.multiple_of(start + index * count, count), count)
            whole = deep_alpha * x_own[rows].astype(jnp.float32) + branch[rows]
            near, inverse = norm_parts(whole)
            hat[rows] = near
            inverse_out[rows] = jnp.broadcast_to(inverse, (count, LANES))
            normed[rows] = (near * gain[...] + shift[...]).astype(jnp.bfloat16)

    core_in, core_sum, side_in, side_sum, last_in = scratch
    scatters, gathers = [], []
    for index in range(pieces):
        rows = pl.ds(index * height, height)
        views = [core_in.at[:, rows], core_sum.at[:, rows], side_in.at[:, :, rows]]
        views += [side_sum.at[:, rows], last_in.at[:, rows]]
        scatters.append(
            plane_scatter_flow(at, wire, index, part.at[:, rows], branch.at[rows], *views)
        )
        sem = own_sems.at[1 + index]
        gathers.append(
            column_gather_flow(at, wire, index, normed.at[rows], normed_all.at[:, rows], sem)
        )
    units = unit_gather_flow(at, wire, ffn_in, ffn_out, own_sems.at[0])
    next(units)
    next(units)
    project()
    next(units)
    attend()
    next(units)
    branch_parts()
    for stage in range(3):
        for flow in scatters:
            next(flow)
    for index in range(pieces + 3):
        if index < pieces:
            for _ in scatters[index]:
                pass
            norm_rows(index * height)
            next(gathers[index])
        for lag in (1, 2, 3):
            if 0 <= index - lag < pieces:
                next(gathers[index - lag], None)
        next(units, None)
    for flow in gathers + [units]:
        for _ in flow:
            pass
    wire.drain()


ANY = pl.BlockSpec(memory_space=pl.ANY)
VMEM = pl.BlockSpec(memory_space=pltpu.VMEM)


def comm_params(number):
    return pltpu.CompilerParams(
        collective_id=number, has_side_effects=True, vmem_limit_bytes=63 * 2**20
    )


def open_heads(qkv_parts, ffn_parts, proj_own, x_own, small):
    _, rows_own, qkv_width = qkv_parts.shape
    _, matrices, _, unit_width = ffn_parts.shape
    own, width = x_own.shape
    low_type = jnp.bfloat16
    return pl.pallas_call(
        open_heads_kernel,
        out_shape=(
            jax.ShapeDtypeStruct((4, 8, rows_own, qkv_width), low_type),
            jax.ShapeDtypeStruct((matrices, 4, 2, 2, 2, rows_own, unit_width), low_type),
            jax.ShapeDtypeStruct((4, rows_own, width), low_type),
            jax.ShapeDtypeStruct((8, own, width), low_type),
            jax.ShapeDtypeStruct((4, 8) + small.shape, small.dtype),
        ),
        in_specs=[VMEM] * 5,
        out_specs=(ANY,) * 5,
        scratch_shapes=[
            pltpu.SemaphoreType.DMA((136,)),
            pltpu.SemaphoreType.DMA((136,)),
            pltpu.SemaphoreType.DMA((5,)),
        ],
        compiler_params=comm_params(1),
        name="open_heads",
    )(qkv_parts, ffn_parts, proj_own, x_own, small)


def open_units(x_all, qkv, proj, tables, x_own, gain, shift, ffn_parts):
    _, matrices, rows_own, unit_width = ffn_parts.shape
    own, width = x_own.shape
    head_width = proj.shape[0]
    length = 2 * own
    low_type = jnp.bfloat16
    rows = jax.ShapeDtypeStruct((4, length, head_width), low_type)
    return pl.pallas_call(
        open_units_kernel,
        out_shape=(
            rows,
            rows,
            rows,
            jax.ShapeDtypeStruct((4, head_width // HEAD_DIM, length, length), jnp.float32),
            jax.ShapeDtypeStruct((8, own, head_width), low_type),
            jax.ShapeDtypeStruct((own, width), low_type),
            jax.ShapeDtypeStruct((own, width), jnp.float32),
            jax.ShapeDtypeStruct((own, LANES), jnp.float32),
            jax.ShapeDtypeStruct((8, own, width), low_type),
            jax.ShapeDtypeStruct((matrices, 4, 2, 2, 2, rows_own, unit_width), low_type),
        ),
        in_specs=[VMEM] * 12,
        out_specs=(VMEM,) * 8 + (ANY, ANY),
        scratch_shapes=[
            pltpu.VMEM((8, own, width), low_type),
            pltpu.VMEM((own, width), jnp.float32),
        ]
        + plane_scratch(own, width)
        + [
            pltpu.SemaphoreType.DMA((136,)),
            pltpu.SemaphoreType.DMA((136,)),
            pltpu.SemaphoreType.DMA((5,)),
        ],
        compiler_params=comm_params(4),
        name="open_units",
    )(x_all, qkv, proj, *tables, x_own, gain, shift, ffn_parts)


def add_rows(out, *terms):
    step = 32

    @pl.loop(0, out.shape[0] // step)
    def _(index):
        part = pl.ds(pl.multiple_of(index * step, step), step)
        whole = terms[0][part].astype(jnp.float32)
        for term in terms[1:]:
            whole = whole + term[part].astype(jnp.float32)
        out[part] = whole.astype(out.dtype)


def column_scatter_flow(
    at, wire, tag, part, out, core_in, core_sum, up_in, down_in, up_sum, down_sum
):
    core_side = at.plane(1)[0]
    up, down = at.ends()
    for goal in (3, 0, 2, 1):
        source = part.at[goal * 2 + 1 - at.c]
        wire.send(("rc", tag, goal), source, core_in.at[goal], core_side)
    yield
    for goal in (3, 0, 2, 1):
        wire.arrive(("rc", tag, goal), core_in.at[goal], core_side)
        add_rows(core_sum.at[goal], part.at[goal * 2 + at.c], core_in.at[goal])
        for rising in {3: (3,), 2: (2,), 1: (1,)}.get(goal, ()):
            key = "ru", tag, rising
            wire.send(key, core_sum.at[rising], up_in.at[rising], up, at.zi == 0)
        for falling in {0: (0,), 1: (1, 2)}.get(goal, ()):
            key = "rd", tag, falling
            wire.send(key, core_sum.at[falling], down_in.at[falling], down, at.zi == 3)

    def climb(goal):
        wire.arrive(("ru", tag, goal), up_in.at[goal], down)
        add_rows(up_sum.at[goal], core_sum.at[goal], up_in.at[goal])

    def descend(goal):
        wire.arrive(("rd", tag, goal), down_in.at[goal], up)
        add_rows(down_sum.at[goal], core_sum.at[goal], down_in.at[goal])

    def rise(goal, z):
        pl.when(at.zi == z)(lambda: climb(goal))
        key = "ru", tag, goal
        target = up_in.at[goal]
        wire.send(("ru2", tag, goal), up_sum.at[goal], target, up, at.zi == z, recv=key)

    def fall(goal, z):
        pl.when(at.zi == z)(lambda: descend(goal))
        key = "rd", tag, goal
        target = down_in.at[goal]
        wire.send(("rd2", tag, goal), down_sum.at[goal], target, down, at.zi == z, recv=key)

    yield
    rise(3, 1)
    fall(0, 2)
    yield
    rise(3, 2)
    fall(0, 1)
    rise(2, 1)
    fall(1, 2)
    yield
    add_rows(out, core_sum.at[at.zi])

    def last(key, source, device):
        wire.arrive(key, source, device)
        add_rows(out, out, source)

    for goal in range(4):
        if goal > 0:
            pl.when(at.zi == goal)(lambda: last(("ru", tag, goal), up_in.at[goal], down))
        if goal < 3:
            pl.when(at.zi == goal)(lambda: last(("rd", tag, goal), down_in.at[goal], up))


def column_gather_flow(at, wire, tag, own_in, out, own_sem):
    core_side = at.plane(1)[0]
    up, down = at.ends()

    def slot(z, c):
        return out.at[jnp.clip(z, 0, 3) * 2 + c]

    mine = slot(at.zi, at.c)
    wire.send(("gu", tag, 0), own_in, mine, up, at.zi < 3)
    wire.send(("gd", tag, 0), own_in, mine, down, at.zi > 0)
    wire.send(("gc", tag), own_in, mine, core_side)
    own = pltpu.make_async_copy(own_in, mine, own_sem)
    own.start()
    for hop in (1, 2, 3):
        yield
        below, above = slot(at.zi - hop, at.c), slot(at.zi + hop, at.c)
        has_below, has_above = at.zi >= hop, at.zi <= 3 - hop
        wire.arrive(("gu", tag, hop - 1), below, down, has_below)
        if hop < 3:
            wire.send(("gu", tag, hop), below, below, up, has_below & (at.zi < 3))
        wire.send(("gcu", tag, hop), below, below, core_side, has_below)
        wire.arrive(("gd", tag, hop - 1), above, up, has_above)
        if hop < 3:
            wire.send(("gd", tag, hop), above, above, down, has_above & (at.zi > 0))
        wire.send(("gcd", tag, hop), above, above, core_side, has_above)
    yield
    own.wait()
    wire.arrive(("gc", tag), slot(at.zi, 1 - at.c), core_side)
    for hop in (1, 2, 3):
        below, above = slot(at.zi - hop, 1 - at.c), slot(at.zi + hop, 1 - at.c)
        wire.arrive(("gcu", tag, hop), below, core_side, at.zi >= hop)
        wire.arrive(("gcd", tag, hop), above, core_side, at.zi <= 3 - hop)


def column_scratch(own, width):
    return [pltpu.VMEM((4, own, width), jnp.bfloat16)] * 6


def plane_scatter_flow(
    at, wire, tag, part, out, core_in, core_sum, side_in, side_sum, last_in
):
    x_side, y_side, core_side = at.plane(4)[0], at.plane(2)[0], at.plane(1)[0]
    half = out.shape[1] // 2
    halves = (pl.ds(0, half), pl.ds(half, half))
    order = ((1, 1), (1, 0), (0, 1), (0, 0))

    def place(dx, dy):
        return flip(at.x, dx), flip(at.y, dy)

    for dx, dy in order:
        x, y = place(dx, dy)
        other = x * 4 + y * 2 + 1 - at.c
        wire.send(("c", tag, dx, dy), part.at[other], core_in.at[dx * 2 + dy], core_side)
    yield
    for dx, dy in order:
        x, y = place(dx, dy)
        mine = x * 4 + y * 2 + at.c
        slot = dx * 2 + dy
        wire.arrive(("c", tag, dx, dy), core_in.at[slot], core_side)
        add_rows(core_sum.at[slot], part.at[mine], core_in.at[slot])
        if dx:
            source = core_sum.at[slot, :, halves[0]]
            wire.send(("sa", tag, dy), source, side_in.at[0, dy], x_side)
        if dy:
            source = core_sum.at[slot, :, halves[1]]
            wire.send(("sb", tag, dx), source, side_in.at[1, dx], y_side)
    yield
    wire.arrive(("sa", tag, 1), side_in.at[0, 1], x_side)
    add_rows(side_sum.at[0], core_sum.at[1, :, halves[0]], side_in.at[0, 1])
    wire.send(("sy", tag), side_sum.at[0], last_in.at[0], y_side)
    wire.arrive(("sb", tag, 1), side_in.at[1, 1], y_side)
    add_rows(side_sum.at[1], core_sum.at[2, :, halves[1]], side_in.at[1, 1])
    wire.send(("sx", tag), side_sum.at[1], last_in.at[1], x_side)
    yield
    wire.arrive(("sa", tag, 0), side_in.at[0, 0], x_side)
    wire.arrive(("sb", tag, 0), side_in.at[1, 0], y_side)
    wire.arrive(("sy", tag), last_in.at[0], y_side)
    terms = core_sum.at[0, :, halves[0]], side_in.at[0, 0], last_in.at[0]
    add_rows(out.at[:, halves[0]], *terms)
    wire.arrive(("sx", tag), last_in.at[1], x_side)
    terms = core_sum.at[0, :, halves[1]], side_in.at[1, 0], last_in.at[1]
    add_rows(out.at[:, halves[1]], *terms)


def plane_scratch(own, width):
    return [
        pltpu.VMEM((4, own, width), jnp.bfloat16),
        pltpu.VMEM((4, own, width), jnp.bfloat16),
        pltpu.VMEM((2, 2, own, width // 2), jnp.bfloat16),
        pltpu.VMEM((2, own, width // 2), jnp.bfloat16),
        pltpu.VMEM((2, own, width // 2), jnp.bfloat16),
    ]


def plane_gather_flow(at, wire, own_in, out, own_sem):
    x_side, y_side, core_side = at.plane(4)[0], at.plane(2)[0], at.plane(1)[0]
    half = own_in.shape[0] // 2
    mine = out.at[at.rank]
    wire.send("gx", own_in, mine, x_side)
    wire.send("gy", own_in, mine, y_side)
    wire.send("gc0", own_in, mine, core_side)
    own = pltpu.make_async_copy(own_in, mine, own_sem)
    own.start()
    yield
    from_x, from_y, from_xy = (at.plane(delta)[1] for delta in (4, 2, 6))
    low_half, high_half = pl.ds(0, half), pl.ds(half, half)
    wire.arrive("gx", out.at[from_x], x_side)
    wire.send("gd0", out.at[from_x, low_half], out.at[from_x, low_half], y_side)
    wire.send("gc1", out.at[from_x], out.at[from_x], core_side)
    wire.arrive("gy", out.at[from_y], y_side)
    wire.send("gd1", out.at[from_y, high_half], out.at[from_y, high_half], x_side)
    wire.send("gc2", out.at[from_y], out.at[from_y], core_side)
    yield
    wire.arrive("gd0", out.at[from_xy, low_half], y_side)
    wire.arrive("gd1", out.at[from_xy, high_half], x_side)
    wire.send("gc3", out.at[from_xy], out.at[from_xy], core_side)
    own.wait()
    for index, delta in enumerate((1, 5, 3, 7)):
        wire.arrive("gc%d" % index, out.at[at.plane(delta)[1]], core_side)


def turn_kernel(
    part,
    normed,
    out_grad,
    gain,
    shift,
    layer_out,
    d_second,
    down_out,
    norm_out,
    second,
    down_low,
    core_in,
    core_sum,
    up_in,
    down_in,
    up_sum,
    down_sum,
    send_sems,
    recv_sems,
    own_sems,
):
    at = Place()
    wire = Wire(send_sems, recv_sems)
    enter(at.column_neighbours())
    pieces = 2
    height = normed.shape[0] // pieces
    scratch = core_in, core_sum, up_in, down_in, up_sum, down_sum

    def norm_rows(start):
        count = 16

        @pl.loop(0, height // count)
        def _(index):
            rows = pl.ds(pl.multiple_of(start + index * count, count), count)
            whole = deep_alpha * normed[rows].astype(jnp.float32) + second[rows]
            near, inverse = norm_parts(whole)
            layer_out[rows] = (near * gain[...] + shift[...]).astype(jnp.bfloat16)
            cotangent = out_grad[rows].astype(jnp.float32)
            result = norm_back(cotangent, near, inverse, gain[...])
            d_second[rows] = result
            down_low[rows] = result.astype(jnp.bfloat16)
            along = cotangent * near
            norm_out[0] += along[:8] + along[8:]
            norm_out[1] += cotangent[:8] + cotangent[8:]

    scatters, gathers = [], []
    for index in range(pieces):
        rows = pl.ds(index * height, height)
        views = [ref.at[:, rows] for ref in scratch]
        scatters.append(
            column_scatter_flow(at, wire, index, part.at[:, rows], second.at[rows], *views)
        )
        gathers.append(
            column_gather_flow(
                at, wire, index, down_low.at[rows], down_out.at[:, rows], own_sems.at[index]
            )
        )
    norm_out[...] = jnp.zeros_like(norm_out)
    for flow in scatters:
        next(flow)
    for flow in scatters:
        next(flow)
    for index in range(pieces + 3):
        if index < pieces:
            for _ in scatters[index]:
                pass
            norm_rows(index * height)
            next(gathers[index])
        for lag in (1, 2, 3):
            if 0 <= index - lag < pieces:
                next(gathers[index - lag], None)
    for flow in gathers:
        for _ in flow:
            pass
    wire.drain()


def turn(part, normed, out_grad, gain, shift):
    _, own, width = part.shape
    low_type = jnp.bfloat16
    return pl.pallas_call(
        turn_kernel,
        out_shape=(
            jax.ShapeDtypeStruct((own, width), low_type),
            jax.ShapeDtypeStruct((own, width), jnp.float32),
            jax.ShapeDtypeStruct((8, own, width), low_type),
            jax.ShapeDtypeStruct((2, 8, width), jnp.float32),
        ),
        in_specs=[VMEM] * 5,
        out_specs=(VMEM, VMEM, ANY, VMEM),
        scratch_shapes=[
            pltpu.VMEM((own, width), jnp.float32),
            pltpu.VMEM((own, width), low_type),
        ]
        + column_scratch(own, width)
        + [
            pltpu.SemaphoreType.DMA((112,)),
            pltpu.SemaphoreType.DMA((112,)),
            pltpu.SemaphoreType.DMA((4,)),
        ],
        compiler_params=comm_params(5),
        name="turn",
    )(part, normed, out_grad, gain, shift)


def close_units_kernel(
    gate_in,
    raise_in,
    lower_in,
    part,
    d_second,
    hat,
    inverse,
    gain,
    ffn_out,
    branch_out,
    d_first,
    norm_out,
    first_in,
    second_sum,
    second_in,
    total,
    d_normed,
    branch_low,
    core_in,
    core_sum,
    up_in,
    down_in,
    up_sum,
    down_sum,
    send_sems,
    recv_sems,
    own_sems,
):
    at = Place()
    wire = Wire(send_sems, recv_sems)
    enter(at.neighbours())
    x_side, y_side = at.plane(4)[0], at.plane(2)[0]
    steps = (4, 3, 5, 2, 6, 1, 7, 0)
    sources = gate_in, raise_in, lower_in

    def owner(step):
        other = at.column(step)[1]
        return other // 2, lax.rem(other, 2)

    def ffn_first(turn):
        step = steps[turn]
        z, c = owner(step)
        for index, source in enumerate(sources):
            if turn % 2:
                block, device = source.at[z, 1 - at.x, :, c], x_side
            else:
                block, device = source.at[z, :, 1 - at.y, c], y_side
            wire.send(("a", step, index), block, first_in.at[step, index], device)

    def ffn_second(turn):
        step = steps[turn]
        z, c = owner(step)
        for index, source in enumerate(sources):
            if turn % 2:
                wire.arrive(("a", step, index), first_in.at[step, index], x_side)
                terms = source.at[z, at.x, 1 - at.y, c], first_in.at[step, index, 1 - at.y]
            else:
                wire.arrive(("a", step, index), first_in.at[step, index], y_side)
                terms = source.at[z, 1 - at.x, at.y, c], first_in.at[step, index, 1 - at.x]
            add_rows(second_sum.at[step, index], *terms)
        wire.send(
            ("b", step), second_sum.at[step], second_in.at[step], y_side if turn % 2 else x_side
        )

    own_total = pltpu.make_async_copy(total.at[0], ffn_out.at[at.unit], own_sems.at[0])

    def ffn_last(turn):
        step = steps[turn]
        z, c = owner(step)
        near = at.y if turn % 2 else at.x
        wire.arrive(("b", step), second_in.at[step], x_side)
        for index, source in enumerate(sources):
            add_rows(
                total.at[step, index],
                source.at[z, at.x, at.y, c],
                first_in.at[step, index, near],
                second_in.at[step, index],
            )
        if step:
            wire.send(("f", step), total.at[step], ffn_out.at[at.unit], at.column(step)[0])
        else:
            own_total.start()

    def norm_rows():
        count = 16
        norm_out[...] = jnp.zeros_like(norm_out)

        @pl.loop(0, hat.shape[0] // count)
        def _(index):
            rows = pl.ds(pl.multiple_of(index * count, count), count)
            cotangent = deep_alpha * d_second[rows] + d_normed[rows]
            near = hat[rows]
            result = norm_back(cotangent, near, inverse[rows, :1], gain[...])
            d_first[rows] = result
            branch_low[rows] = result.astype(jnp.bfloat16)
            along = cotangent * near
            norm_out[0] += along[:8] + along[8:]
            norm_out[1] += cotangent[:8] + cotangent[8:]

    scatter = column_scatter_flow(
        at, wire, 0, part, d_normed, core_in, core_sum, up_in, down_in, up_sum, down_sum
    )
    next(scatter)
    for turn in range(5):
        ffn_first(turn)
    next(scatter)
    next(scatter)
    ffn_second(0)
    ffn_first(5)
    ffn_second(1)
    ffn_first(6)
    next(scatter)
    ffn_second(2)
    ffn_first(7)
    ffn_second(3)
    for _ in scatter:
        pass
    norm_rows()
    spread = plane_gather_flow(at, wire, branch_low, branch_out, own_sems.at[1])
    next(spread)
    ffn_last(0)
    ffn_last(1)
    ffn_second(4)
    ffn_last(2)
    ffn_second(5)
    ffn_last(3)
    next(spread)
    ffn_second(6)
    ffn_second(7)
    ffn_last(4)
    for _ in spread:
        pass
    for turn in range(5, 8):
        ffn_last(turn)
    own_total.wait()
    for step in steps:
        if step:
            device, other = at.column(-step)
            wire.arrive(("f", step), ffn_out.at[other], device)
    wire.drain()


def close_units(grads, part, d_second, hat, inverse, gain):
    rows_own, unit_width = grads[0].shape[-2:]
    _, own, width = part.shape
    low_type = jnp.bfloat16
    block = (rows_own, unit_width)
    return pl.pallas_call(
        close_units_kernel,
        out_shape=(
            jax.ShapeDtypeStruct((8, 3) + block, low_type),
            jax.ShapeDtypeStruct((8, own, width), low_type),
            jax.ShapeDtypeStruct((own, width), jnp.float32),
            jax.ShapeDtypeStruct((2, 8, width), jnp.float32),
        ),
        in_specs=[VMEM] * 8,
        out_specs=(ANY, ANY, VMEM, VMEM),
        scratch_shapes=[
            pltpu.VMEM((8, 3, 2) + block, low_type),
            pltpu.VMEM((8, 3) + block, low_type),
            pltpu.VMEM((8, 3) + block, low_type),
            pltpu.VMEM((8, 3) + block, low_type),
            pltpu.VMEM((own, width), jnp.float32),
            pltpu.VMEM((own, width), low_type),
        ]
        + column_scratch(own, width)
        + [
            pltpu.SemaphoreType.DMA((80,)),
            pltpu.SemaphoreType.DMA((80,)),
            pltpu.SemaphoreType.DMA((2,)),
        ],
        compiler_params=comm_params(3),
        name="close_units",
    )(*grads, part, d_second, hat, inverse, gain)


def close_heads_kernel(
    qkv_in,
    proj_in,
    small_in,
    part,
    qkv_out,
    proj_out,
    small_out,
    d_input,
    proj_below,
    proj_above,
    proj_sum,
    small_plane,
    small_mid,
    small_line,
    up_in,
    down_in,
    up_sum,
    down_sum,
    qkv_total,
    core_in,
    core_sum,
    side_in,
    side_sum,
    last_in,
    send_sems,
    recv_sems,
    own_sems,
):
    at = Place()
    wire = Wire(send_sems, recv_sems)
    enter(at.neighbours())
    scatter = plane_scatter_flow(
        at, wire, 0, part, d_input, core_in, core_sum, side_in, side_sum, last_in
    )
    next(scatter)

    def add(*terms):
        whole = terms[0].astype(jnp.float32)
        for term in terms[1:]:
            whole = whole + term.astype(jnp.float32)
        return whole.astype(jnp.bfloat16)

    for delta in range(1, 8):
        device, other = at.plane(delta)
        wire.send(("s", delta), small_in.at[other], small_plane.at[at.rank], device)

    def small_second():
        whole = small_in[at.rank]
        for delta in range(1, 8):
            device, other = at.plane(delta)
            wire.arrive(("s", delta), small_plane.at[other], device)
            whole = whole + small_plane[other]
        small_mid[...] = whole
        for dz in range(1, 4):
            z = lax.rem(at.zi + dz, 4)
            wire.send(("t", dz), small_mid.at[z], small_line.at[at.zi], at.line(z))

    def small_last():
        whole = small_mid[at.zi]
        for dz in range(1, 4):
            z = lax.rem(at.zi - dz + 4, 4)
            wire.arrive(("t", dz), small_line.at[z], at.line(z))
            whole = whole + small_line[z]
        small_out[...] = whole

    pieces = 4
    wide = 8 // pieces
    up, down = at.line(jnp.minimum(at.zi + 1, 3)), at.line(jnp.maximum(at.zi - 1, 0))

    def qkv_rise(goal, piece, low_z, high_z):
        part = pl.ds(piece * wide, wide)
        here = (at.zi >= low_z) & (at.zi <= high_z)
        source = up_sum.at[goal, part]

        def climb():
            wire.arrive(("u", goal, piece), up_in.at[goal, part], down)
            up_sum[goal, part] = add(qkv_in[goal, part], up_in[goal, part])

        key = "u", goal, piece
        if low_z == 0:
            first = qkv_in.at[goal, part]
            wire.send(("u0", goal, piece), first, up_in.at[goal, part], up, at.zi == 0, recv=key)
        if high_z > 0:
            here = here & (at.zi > 0)
            pl.when(here)(climb)
            wire.send(key, source, up_in.at[goal, part], up, here)

    def qkv_fall(goal, piece, low_z, high_z):
        part = pl.ds(piece * wide, wide)
        here = (at.zi >= low_z) & (at.zi <= high_z)
        source = down_sum.at[goal, part]

        def descend():
            wire.arrive(("d", goal, piece), down_in.at[goal, part], up)
            down_sum[goal, part] = add(qkv_in[goal, part], down_in[goal, part])

        key = "d", goal, piece
        if high_z == 3:
            first = qkv_in.at[goal, part]
            wire.send(
                ("d0", goal, piece), first, down_in.at[goal, part], down, at.zi == 3, recv=key
            )
        if low_z < 3:
            here = here & (at.zi < 3)
            pl.when(here)(descend)
            wire.send(key, source, down_in.at[goal, part], down, here)

    proj_home = at.head_home()

    def proj_add(slot, *terms):
        add_rows(proj_sum.at[slot], *(term.at[slot] for term in terms))

    below, above = at.zi < proj_home, at.zi > proj_home
    ends = (at.zi == 0) | (at.zi == 3)

    def proj_pass(slot):
        under, over = proj_below.at[slot], proj_above.at[slot]
        wire.send(("pu", slot), proj_in.at[slot], under, up, below & ends)
        wire.send(("pd", slot), proj_in.at[slot], over, down, above & ends)

        def climb():
            wire.arrive(("pu", slot), under, down)
            proj_add(slot, proj_in, proj_below)

        def descend():
            wire.arrive(("pd", slot), over, up)
            proj_add(slot, proj_in, proj_above)

        pl.when(below & (at.zi > 0))(climb)
        pl.when(above & (at.zi < 3))(descend)
        source = proj_sum.at[slot]
        key = "pu", slot
        wire.send(("pu2", slot), source, under, up, below & (at.zi > 0), recv=key)
        key = "pd", slot
        wire.send(("pd2", slot), source, over, down, above & (at.zi < 3), recv=key)

    chunk = at.y * 2 + at.c
    holder_device, holder = at.holder()

    def proj_last():
        home = at.zi == proj_home
        for slot in range(4):
            under, over = proj_below.at[slot], proj_above.at[slot]

            def first():
                wire.arrive(("pu", slot), under, down)
                proj_add(slot, proj_in, proj_below)

            def only():
                wire.arrive(("pd", slot), over, up)
                proj_add(slot, proj_in, proj_above)

            def both():
                wire.arrive(("pd", slot), over, up)
                proj_add(slot, proj_sum, proj_above)

            pl.when(home & (at.zi > 0))(first)
            pl.when(home & (at.zi == 0))(only)
            pl.when(home & (at.zi > 0) & (at.zi < 3))(both)
            target = (at.zo, at.zi, at.x, slot // 2, slot % 2)
            other = (chunk != slot) | (at.rank != holder)
            wire.send(("o", slot), proj_sum.at[slot], proj_out, target, home & other, recv="o")
        own = pltpu.make_async_copy(proj_sum.at[chunk], proj_out, own_sems.at[2])
        pl.when(home & (at.rank == holder))(own.start)
        pl.when(home & (at.rank == holder))(own.wait)

    def qkv_last(piece):
        part = pl.ds(piece * wide, wide)
        for goal in range(4):

            @pl.when(at.zi == goal)
            def _():
                terms = [qkv_in[goal, part]]
                if goal > 0:
                    wire.arrive(("u", goal, piece), up_in.at[goal, part], down)
                    terms.append(up_in[goal, part])
                if goal < 3:
                    wire.arrive(("d", goal, piece), down_in.at[goal, part], up)
                    terms.append(down_in[goal, part])
                qkv_total[part] = add(*terms)

    for piece in range(pieces):
        qkv_rise(3, piece, 0, 1)
        qkv_fall(0, piece, 2, 3)
        if piece == 0:
            next(scatter)
    for piece in range(pieces):
        qkv_rise(3, piece, 2, 2)
        qkv_fall(0, piece, 1, 1)
    for slot in range(4):
        proj_pass(slot)
    next(scatter)
    small_second()
    for piece in range(pieces):
        qkv_rise(2, piece, 0, 1)
        qkv_fall(1, piece, 2, 3)
    for _ in scatter:
        pass
    for piece in range(pieces):
        qkv_rise(1, piece, 0, 0)
        qkv_fall(2, piece, 3, 3)
    proj_last()
    for piece in range(pieces):
        qkv_last(piece)
    own_qkv = pltpu.make_async_copy(
        qkv_total.at[at.rank], qkv_out.at[at.rank], own_sems.at[1]
    )
    own_qkv.start()
    for delta in range(1, 8):
        device, other = at.plane(delta)
        wire.send(("q", delta), qkv_total.at[other], qkv_out.at[at.rank], device)
    own_qkv.wait()
    for delta in range(1, 8):
        device, other = at.plane(delta)
        wire.arrive(("q", delta), qkv_out.at[other], device)
    small_last()
    wire.arrive("o", proj_out, holder_device, at.rank != holder)
    wire.drain()


def close_heads(qkv_part, proj_part, small_part, part):
    _, _, rows_own, qkv_width = qkv_part.shape
    _, own, width = part.shape
    low_type = jnp.bfloat16
    line = (4, 8, rows_own, qkv_width)
    small_shape = small_part.shape[1:]
    return pl.pallas_call(
        close_heads_kernel,
        out_shape=(
            jax.ShapeDtypeStruct((8, rows_own, qkv_width), low_type),
            jax.ShapeDtypeStruct((rows_own, width), low_type),
            jax.ShapeDtypeStruct(small_shape[1:], small_part.dtype),
            jax.ShapeDtypeStruct((own, width), jnp.float32),
        ),
        in_specs=[VMEM] * 4,
        out_specs=(ANY, ANY, VMEM, VMEM),
        scratch_shapes=[
            pltpu.VMEM((4, rows_own, width), low_type),
            pltpu.VMEM((4, rows_own, width), low_type),
            pltpu.VMEM((4, rows_own, width), low_type),
            pltpu.VMEM(small_part.shape, small_part.dtype),
            pltpu.VMEM(small_shape, small_part.dtype),
            pltpu.VMEM(small_shape, small_part.dtype),
            pltpu.VMEM(line, low_type),
            pltpu.VMEM(line, low_type),
            pltpu.VMEM(line, low_type),
            pltpu.VMEM(line, low_type),
            pltpu.VMEM(line[1:], low_type),
        ]
        + plane_scratch(own, width)
        + [
            pltpu.SemaphoreType.DMA((112,)),
            pltpu.SemaphoreType.DMA((112,)),
            pltpu.SemaphoreType.DMA((3,)),
        ],
        compiler_params=comm_params(2),
        name="close_heads",
    )(qkv_part, proj_part, small_part, part)


def group_body(
    hidden_in,
    token_marks,
    out_grad,
    qkv_weight,
    proj_weight,
    gate_weight,
    up_weight,
    down_weight,
    first_gain,
    first_shift,
    second_gain,
    second_shift,
):
    micro_count, _, pos_count, width = hidden_in.shape
    rows_own = qkv_weight.shape[0]
    units = gate_weight.shape[1]
    head_ways = math.prod(lax.axis_size(name) for name in HEAD_AXES)
    unit_ways = math.prod(lax.axis_size(name) for name in UNIT_AXES)
    chunk_count = lax.axis_size("y") * lax.axis_size("c")
    row_length = pos_count * chunk_count
    x_size = lax.axis_size("x")
    marks_own = token_marks.astype(jnp.float32)
    own = micro_count * pos_count
    head_width = width // head_ways
    heads_here = head_width // HEAD_DIM
    unit_width = -(-units // (unit_ways * LANES)) * LANES
    unit_pad = unit_width * unit_ways - units
    x_own = hidden_in.reshape(own, width)

    params = jnp.stack([first_gain, first_shift, second_gain, second_shift])
    small = jnp.concatenate([params.astype(jnp.float32).ravel(), marks_own.ravel()])
    small = jnp.pad(small, (0, -small.size % (8 * LANES))).reshape(-1, LANES)

    qkv_parts = qkv_weight.reshape(rows_own, 3, 4, 2, head_width)
    qkv_parts = jnp.stack([qkv_parts[:, :, home] for home in (0, 3, 1, 2)])
    qkv_parts = qkv_parts.transpose(3, 0, 1, 2, 4).reshape(head_ways, rows_own, 3 * head_width)

    def unit_parts(*matrices):
        parts = jnp.stack(matrices)
        parts = jnp.pad(parts, ((0, 0), (0, 0), (0, unit_pad)))
        parts = parts.reshape(len(matrices), rows_own, unit_ways, unit_width)
        return parts.transpose(2, 0, 1, 3)

    qkv_here, gate_here, proj_here, x_all, small = open_heads(
        qkv_parts, unit_parts(gate_weight), proj_weight, x_own, small
    )
    qkv_here = qkv_here.reshape(-1, 3 * head_width)
    gate_here = gate_here.reshape(-1, unit_width)
    x_all = x_all.reshape(-1, width)
    proj_here = proj_here.reshape(head_width, width)
    small = small.reshape(unit_ways * 4, -1)
    params = small[:, : 4 * rows_own].reshape(-1, 4, rows_own).transpose(1, 0, 2)
    gain_one, shift_one, gain_two, shift_two = params.reshape(4, 1, width)
    marks = small.reshape(4, head_ways, -1)[lax.axis_index("zi")]
    marks = marks[:, 4 * rows_own : 4 * rows_own + own * 3]

    def to_rows(values):
        inner = values.shape[1:]
        values = values.reshape((x_size, chunk_count, micro_count, pos_count) + inner)
        return jnp.swapaxes(values, 1, 2).reshape((x_size * micro_count, row_length) + inner)

    def from_rows(values):
        inner = values.shape[2:]
        values = values.reshape((x_size, micro_count, chunk_count, pos_count) + inner)
        return jnp.swapaxes(values, 1, 2).reshape((head_ways * own,) + inner)

    row_marks = to_rows(marks.reshape(head_ways * own, 3))
    cosine, sine = rotary_tables(row_marks[..., 2])
    tables = (
        jnp.concatenate([cosine, cosine], axis=-1),
        jnp.concatenate([-sine, sine], axis=-1),
        row_marks[:, :, :1],
        row_marks[:, None, :, 0],
        row_marks[:, None, :, 1],
    )
    queries, key_rows, value_rows, probs, context, normed, hat_one, inverse_one, normed_all, ffn = (
        open_units(
            x_all.reshape(head_ways, own, width),
            qkv_here,
            proj_here,
            tables,
            x_own,
            gain_one,
            shift_one,
            unit_parts(up_weight, down_weight),
        )
    )
    rows_shape = (x_size * micro_count, row_length, heads_here, HEAD_DIM)
    queries, key_rows, value_rows = (
        values.reshape(rows_shape) for values in (queries, key_rows, value_rows)
    )
    probs_low = low(probs)
    context = context.reshape(-1, head_width)
    cosine, sine = cosine[:, :, None, :], sine[:, :, None, :]
    score_scale = 1.0 / math.sqrt(HEAD_DIM)

    def pair(spec, left_side, right_side):
        return jnp.einsum(spec, left_side, right_side, preferred_element_type=jnp.float32)

    normed_all = normed_all.reshape(-1, width)
    up_here, down_here = ffn.reshape(2, -1, unit_width)

    gate_val = dot(normed_all, gate_here)
    up_val = dot(normed_all, up_here)
    gelu_val, gelu_slope = gelu_parts(gate_val)
    active = low(gelu_val * up_val)
    down_part = low(contract_last(active, down_here)).reshape(unit_ways, own, width)
    layer_rows, d_second, down_low, norm_grads = turn(
        down_part, normed, out_grad.reshape(own, width), gain_two, shift_two
    )
    gain_two_grad, shift_two_grad = jnp.sum(norm_grads, axis=1)
    down_low = down_low.reshape(-1, width)
    d_active = dot(down_low, down_here)
    gate_low = low(d_active * up_val * gelu_slope)
    up_low = low(d_active * gelu_val)
    d_normed_part = low(contract_last(gate_low, gate_here) + contract_last(up_low, up_here))

    def unit_grad(left_side, right_side):
        part = low(contract_first(left_side, right_side))
        return part.reshape(4, 2, 2, 2, rows_own, unit_width)

    ffn_grads = (
        unit_grad(normed_all, gate_low),
        unit_grad(normed_all, up_low),
        unit_grad(down_low, active),
    )
    ffn_part, branch_all, d_first, norm_grads = close_units(
        ffn_grads,
        d_normed_part.reshape(unit_ways, own, width),
        d_second,
        hat_one,
        inverse_one,
        gain_one,
    )
    gain_one_grad, shift_one_grad = jnp.sum(norm_grads, axis=1)
    branch_all = branch_all.reshape(-1, width)
    small_grads = jnp.stack([gain_one_grad, shift_one_grad, gain_two_grad, shift_two_grad])
    small_grads = small_grads.reshape(4, 4, head_ways, rows_own).transpose(2, 1, 0, 3)
    small_grads = small_grads.reshape(head_ways, 4, 4 * rows_own // LANES, LANES)
    small_grads = jnp.pad(small_grads, ((0, 0), (0, 0), (0, -small_grads.shape[2] % 8), (0, 0)))

    proj_part = low(contract_first(context, branch_all)).reshape(4, rows_own, width)
    d_context = to_rows(low(contract_last(branch_all, proj_here)))
    d_context = d_context.reshape(x_size * micro_count, row_length, heads_here, HEAD_DIM)
    d_probs = pair("rqhd,rkhd->rhqk", d_context, value_rows)
    d_scores = low(probs * (d_probs - jnp.sum(probs * d_probs, axis=-1, keepdims=True)))
    d_query = pair("rhqk,rkhd->rqhd", d_scores, key_rows) * score_scale
    d_keys = pair("rhqk,rqhd->rkhd", d_scores, queries) * score_scale
    d_values = pair("rhqk,rqhd->rkhd", probs_low, d_context)
    d_mixed = low(
        jnp.stack(
            [rotate(d_query, cosine, -sine), rotate(d_keys, cosine, -sine), d_values], axis=2
        )
    )
    d_mixed = from_rows(d_mixed.reshape(x_size * micro_count, row_length, 3 * head_width))
    d_input = low(contract_last(d_mixed, qkv_here)).reshape(head_ways, own, width)
    qkv_part = low(contract_first(x_all, d_mixed))
    qkv_part, proj_part, small_grads, d_input = close_heads(
        qkv_part.reshape(4, 8, rows_own, 3 * head_width), proj_part, small_grads, d_input
    )
    d_input = deep_alpha * d_first + d_input
    small_grads = small_grads.ravel()[: 4 * rows_own].reshape(4, rows_own)
    qkv_grad = qkv_part.reshape(2, 4, rows_own, 3, head_width)
    qkv_grad = jnp.stack([qkv_grad[:, place] for place in (0, 2, 3, 1)])
    qkv_grad = qkv_grad.transpose(2, 3, 0, 1, 4).reshape(rows_own, 3 * width).astype(jnp.float32)
    ffn_part = ffn_part.transpose(1, 2, 0, 3).reshape(3, rows_own, unit_ways * unit_width)
    gate_grad, up_grad, down_grad = (
        ffn_part[index, :, :units].astype(jnp.float32) for index in range(3)
    )
    return (
        layer_rows.reshape(micro_count, 1, pos_count, width),
        low(d_input).reshape(micro_count, 1, pos_count, width),
        qkv_grad,
        proj_part.astype(jnp.float32),
        gate_grad,
        up_grad,
        down_grad,
        small_grads[0],
        small_grads[1],
        small_grads[2],
        small_grads[3],
    )


def body(hidden_in, token_marks, out_grad, *weights):
    joined = lax.axis_size("zo")
    if joined == 1:
        return group_body(hidden_in, token_marks, out_grad, *weights)
    rows = weights[0].shape[0]
    width = hidden_in.shape[-1]
    groups = width // (joined * rows)
    group_place = lax.axis_index(ALL[1:])

    def inward(values):
        shape = values.shape
        values = values.reshape(shape[:-1] + (joined, groups, rows))
        return jnp.swapaxes(values, -3, -2).reshape(shape)

    def outward(values):
        shape = values.shape
        values = values.reshape(shape[:-1] + (groups, joined, rows))
        return jnp.swapaxes(values, -3, -2).reshape(shape)

    proj = gather(weights[1], ALL)
    proj = inward(lax.dynamic_slice_in_dim(proj, group_place * joined * rows, joined * rows))
    weights = [gather(weight, "zo") for weight in weights]
    weights[1] = proj
    outs = list(group_body(inward(hidden_in), token_marks, inward(out_grad), *weights))
    outs[:2] = outward(outs[0]), outward(outs[1])
    proj_grad = jnp.zeros((width, width), jnp.float32)
    proj_grad = lax.dynamic_update_slice_in_dim(
        proj_grad, outward(outs[3]), group_place * joined * rows, 0
    )
    outs[2:] = [scatter_sum(grad, "zo") for grad in outs[2:]]
    outs[3] = scatter_sum(proj_grad, ALL)
    return tuple(outs)


def solution(mesh):
    seq_size, ctx_size = mesh.shape["seq"], mesh.shape["ctx"]
    cores, x_size = 2, 2
    zi_size = math.gcd(4, seq_size // x_size)
    zo_size = seq_size // (x_size * zi_size)
    devices = np.asarray(mesh.devices).reshape(
        zo_size, zi_size, x_size, ctx_size // cores, cores
    )
    inner = Mesh(devices, ALL)
    tokens = P(None, ("zo", "zi", "x"), ("y", "c"), None)
    matrix = P(ALL, None)
    vector = P(ALL)
    return jax.shard_map(
        body,
        mesh=inner,
        in_specs=(tokens,) * 3 + (matrix,) * 5 + (vector,) * 4,
        out_specs=(tokens,) * 2 + (matrix,) * 5 + (vector,) * 4,
        check_vma=False,
    )
```

```python
import math

import jax
import jax.numpy as jnp
import numpy as np
from jax import lax
from jax.experimental import pallas as pl
from jax.experimental.pallas import tpu as pltpu
from jax.sharding import Mesh
from jax.sharding import PartitionSpec as P

HEAD_DIM = 128
LANES = 128

deep_alpha = 48.0**0.25
norm_eps = 1e-05
masked_score = -1e30

ALL = ("zo", "zi", "x", "y", "c")
HEAD_AXES = ("x", "y", "c")
UNIT_AXES = ("zi", "c")
HEAD_COPIES = ("zo", "zi")
UNIT_COPIES = ("zo", "x", "y")


def contract_last(left_side, right_side):
    return lax.dot_general(
        left_side, right_side, (((1,), (1,)), ((), ())), preferred_element_type=jnp.float32
    )


def contract_first(left_side, right_side):
    return lax.dot_general(
        left_side, right_side, (((0,), (0,)), ((), ())), preferred_element_type=jnp.float32
    )


def dot(left_side, right_side):
    return jnp.dot(left_side, right_side, preferred_element_type=jnp.float32)


def low(values):
    return values.astype(jnp.bfloat16)


def norm_parts(values):
    center = values - jnp.mean(values, axis=-1, keepdims=True)
    spread = jnp.mean(center * center, axis=-1, keepdims=True)
    inverse = lax.rsqrt(spread + norm_eps)
    return center * inverse, inverse


def norm_back(cotangent, hat, inverse, gain_vec):
    scaled = cotangent * gain_vec
    return (
        scaled
        - jnp.mean(scaled, axis=-1, keepdims=True)
        - hat * jnp.mean(scaled * hat, axis=-1, keepdims=True)
    ) * inverse


def rotary_tables(positions):
    half = HEAD_DIM // 2
    exponent = jnp.arange(half, dtype=jnp.float32) * (2.0 / HEAD_DIM)
    angles = positions.astype(jnp.float32)[..., None] * jnp.exp(-math.log(10000.0) * exponent)
    return (jnp.cos(angles), jnp.sin(angles))


def rotate(values, cosine, sine):
    half = HEAD_DIM // 2
    front, back = values[..., :half], values[..., half:]
    return jnp.concatenate(
        [front * cosine - back * sine, back * cosine + front * sine], axis=-1
    )


def gather(values, axes):
    return lax.all_gather(values, axes, axis=0, tiled=True)


def scatter_sum(values, axes):
    return lax.psum_scatter(values, axes, scatter_dimension=0, tiled=True)


def gelu_parts(value):
    phi = 0.5 + 0.5 * lax.erf(value * math.sqrt(0.5))
    density = jnp.exp(-0.5 * value * value) * (1.0 / math.sqrt(2.0 * math.pi))
    return value * phi, phi + value * density


MESH = pl.DeviceIdType.MESH


class Wire:
    def __init__(self, send_sems, recv_sems):
        self.send_sems, self.recv_sems = send_sems, recv_sems
        self.keys, self.sent = {}, []

    def number(self, key, span=1):
        if key not in self.keys:
            self.keys[key] = sum(size for _, size in self.keys.values()), span
        return self.keys[key][0]

    def copy(self, key, source, target, device, slot=0, span=1, recv=None):
        send = self.number(key, span)
        receive = send if recv is None else self.number(recv)
        return pltpu.make_async_remote_copy(
            src_ref=source,
            dst_ref=target,
            send_sem=self.send_sems.at[send],
            recv_sem=self.recv_sems.at[receive + slot],
            device_id=device,
            device_id_type=MESH,
        )

    def send(self, key, source, target, device, when=None, recv=None):
        copy = self.copy(key, source, target, device, recv=recv)
        if when is None:
            copy.start()
        else:
            pl.when(when)(copy.start)
        self.sent.append((copy, when))

    def send_to_slot(self, key, source, target, device, slot, span, when):
        copy = self.copy(key, source, target, device, slot, span)
        pl.when(when)(copy.start)
        self.sent.append((copy, when))

    def arrive(self, key, target, device, when=None):
        copy = self.copy(key, target, target, device)
        if when is None:
            copy.wait_recv()
        else:
            pl.when(when)(copy.wait_recv)

    def arrive_slot(self, key, target, device, slot, span, when):
        pl.when(when)(self.copy(key, target, target, device, slot, span).wait_recv)

    def drain(self):
        for copy, when in self.sent:
            if when is None:
                copy.wait_send()
            else:
                pl.when(when)(copy.wait_send)


def flip(value, bit):
    return 1 - value if bit else value


def enter(devices):
    barrier = pltpu.get_barrier_semaphore()
    for device in devices:
        pl.semaphore_signal(barrier, inc=1, device_id=device, device_id_type=MESH)
    pl.semaphore_wait(barrier, len(devices))


class Place:
    def __init__(self):
        self.zo, self.zi, self.x, self.y, self.c = (lax.axis_index(name) for name in ALL)
        self.rank = self.x * 4 + self.y * 2 + self.c
        self.unit = self.zi * 2 + self.c

    def head_home(self):
        return self.y + self.c * (3 - 2 * self.y)

    def holder(self):
        y, c = lax.rem((self.zi + 1) // 2, 2), self.zi // 2
        return (self.zo, self.zi, self.x, y, c), self.x * 4 + y * 2 + c

    def plane(self, delta):
        dx, dy, dc = delta >> 2 & 1, delta >> 1 & 1, delta & 1
        x, y, c = flip(self.x, dx), flip(self.y, dy), flip(self.c, dc)
        return (self.zo, self.zi, x, y, c), x * 4 + y * 2 + c

    def column(self, step):
        other = lax.rem(self.unit + step + 8, 8)
        return (self.zo, other // 2, self.x, self.y, lax.rem(other, 2)), other

    def ends(self):
        return self.line(jnp.minimum(self.zi + 1, 3)), self.line(jnp.maximum(self.zi - 1, 0))

    def line(self, z):
        return (self.zo, z, self.x, self.y, self.c)

    def column_neighbours(self):
        return [self.line(z) for z in self.others()] + [self.plane(1)[0]]

    def others(self):
        return [lax.rem(self.zi + step, 4) for step in (1, 2, 3)]

    def neighbours(self):
        plane = [self.plane(delta)[0] for delta in range(1, 8)]
        column = []
        for dz in range(1, 4):
            z = lax.rem(self.zi + dz, 4)
            column += [(self.zo, z, self.x, self.y, core) for core in (0, 1)]
        return plane + column


def unit_gather_flow(at, wire, ffn_in, ffn_out, own_sem):
    x_side, y_side = at.plane(4)[0], at.plane(2)[0]
    steps = (1, 7, 2, 6, 3, 5, 4)
    mine = ffn_out.at[:, at.zi, at.x, at.y, at.c]
    own = pltpu.make_async_copy(ffn_in.at[at.unit], mine, own_sem)
    own.start()
    for step in steps:
        device, other = at.column(step)
        wire.send(("f", step), ffn_in.at[other], mine, device)
    own.wait()

    def slot(step, x, y):
        source = lax.rem(at.unit - step + 8, 8)
        return ffn_out.at[:, source // 2, x, y, lax.rem(source, 2)]

    def first(step):
        here = slot(step, at.x, at.y)
        if step:
            wire.arrive(("f", step), here, at.column(-step)[0])
        wire.send(("fx", step), here, here, x_side)
        wire.send(("fy", step), here, here, y_side)

    def second(step, turn):
        from_x, from_y = slot(step, 1 - at.x, at.y), slot(step, at.x, 1 - at.y)
        wire.arrive(("fx", step), from_x, x_side)
        wire.arrive(("fy", step), from_y, y_side)
        if turn % 2:
            wire.send(("fd", step), from_x, from_x, y_side)
        else:
            wire.send(("fd", step), from_y, from_y, x_side)

    yield
    first(0)
    for turn, step in enumerate(steps):
        yield
        first(step)
        if turn >= 1:
            second(((0,) + steps)[turn - 1], turn - 1)
    yield
    second(steps[5], 6)
    second(steps[6], 7)
    yield
    for step in (0,) + steps:
        wire.arrive(("fd", step), slot(step, 1 - at.x, 1 - at.y), x_side)


def open_heads_kernel(
    qkv_in,
    ffn_in,
    proj_in,
    x_in,
    small_in,
    qkv_out,
    ffn_out,
    proj_out,
    x_out,
    small_out,
    send_sems,
    recv_sems,
    own_sems,
):
    at = Place()
    wire = Wire(send_sems, recv_sems)
    enter(at.neighbours())
    up, down = at.ends()
    chunk = at.y * 2 + at.c
    holder_device, holder = at.holder()
    proj_home = at.head_home()
    own = [
        pltpu.make_async_copy(qkv_in.at[at.rank], qkv_out.at[at.zi, at.rank], own_sems.at[1]),
        pltpu.make_async_copy(small_in, small_out.at[at.zi, at.rank], own_sems.at[3]),
    ]
    for copy in own:
        copy.start()
    for delta in range(1, 8):
        device, other = at.plane(delta)
        wire.send(("q", delta), qkv_in.at[other], qkv_out.at[at.zi, at.rank], device)
    wire.send_to_slot("p", proj_in, proj_out.at[chunk], holder_device, chunk, 4, at.rank != holder)
    proj_own = pltpu.make_async_copy(proj_in, proj_out.at[chunk], own_sems.at[4])
    pl.when(at.rank == holder)(proj_own.start)
    for delta in range(1, 8):
        device, _ = at.plane(delta)
        wire.send(("s", delta), small_in, small_out.at[at.zi, at.rank], device)
    spread = plane_gather_flow(at, wire, x_in, x_out, own_sems.at[0])
    next(spread)
    for copy in own:
        copy.wait()
    pl.when(at.rank == holder)(proj_own.wait)

    def small_second():
        for delta in range(1, 8):
            device, other = at.plane(delta)
            wire.arrive(("s", delta), small_out.at[at.zi, other], device)
        for dz in range(1, 4):
            device = at.line(lax.rem(at.zi + dz, 4))
            wire.send(("t", dz), small_out.at[at.zi], small_out.at[at.zi], device)

    def small_last():
        for dz in range(1, 4):
            z = lax.rem(at.zi - dz + 4, 4)
            wire.arrive(("t", dz), small_out.at[z], at.line(z))

    def proj_start(slot):
        block = proj_out.at[slot]
        source = (at.zo, at.zi, at.x, slot // 2, slot % 2)
        home = at.zi == proj_home
        mine = home & ((chunk != slot) | (at.rank != holder))
        wire.arrive_slot("p", block, source, slot, 4, mine)
        wire.send(("pu", slot), block, block, up, home & (at.zi < 3))
        wire.send(("pd", slot), block, block, down, home & (at.zi > 0))

    def proj_relay(slot):
        block = proj_out.at[slot]
        above, below = at.zi > proj_home, at.zi < proj_home
        wire.arrive(("pu", slot), block, down, above)
        wire.arrive(("pd", slot), block, up, below)
        key = "pu", slot
        wire.send(("pu2", slot), block, block, up, above & (at.zi < 3), recv=key)
        key = "pd", slot
        wire.send(("pd2", slot), block, block, down, below & (at.zi > 0), recv=key)

    def qkv_slot(z, delta):
        return qkv_out.at[jnp.clip(z, 0, 3), at.plane(delta)[1]]

    def qkv_hop(hop, delta):
        below, above = qkv_slot(at.zi - hop, delta), qkv_slot(at.zi + hop, delta)
        if hop == 0:
            if delta:
                wire.arrive(("q", delta), below, at.plane(delta)[0])
        else:
            wire.arrive(("up", hop - 1, delta), below, down, at.zi >= hop)
            wire.arrive(("down", hop - 1, delta), above, up, at.zi <= 3 - hop)
        if hop < 3:
            wire.send(("up", hop, delta), below, below, up, (at.zi >= hop) & (at.zi < 3))
            wire.send(("down", hop, delta), above, above, down, (at.zi <= 3 - hop) & (at.zi > 0))

    for delta in range(8):
        qkv_hop(0, delta)
    units = unit_gather_flow(at, wire, ffn_in, ffn_out, own_sems.at[2])
    for slot in range(4):
        proj_start(slot)
    next(units)
    next(spread)
    small_second()
    next(units)
    for _ in spread:
        pass
    for delta in range(8):
        qkv_hop(1, delta)
        if delta % 2:
            proj_relay(delta // 2)
            next(units)
    for delta in range(8):
        qkv_hop(2, delta)
        if delta % 2:
            next(units)
    for delta in range(8):
        qkv_hop(3, delta)
    for _ in units:
        pass
    small_last()
    wire.drain()


def turned(values, cosine, sine):
    return values * cosine + pltpu.roll(values, HEAD_DIM // 2, 1) * sine


def row_place(rank, micro):
    piece = rank % 4
    return (rank // 4) * 2 + micro, piece


def open_units_kernel(
    x_all,
    qkv,
    proj,
    cosine,
    sine,
    start_query,
    start_key,
    end_key,
    x_own,
    gain,
    shift,
    ffn_in,
    queries,
    key_rows,
    value_rows,
    probs_out,
    context,
    normed,
    hat,
    inverse_out,
    normed_all,
    ffn_out,
    part,
    branch,
    *rest,
):
    at = Place()
    *scratch, send_sems, recv_sems, own_sems = rest
    wire = Wire(send_sems, recv_sems)
    enter(at.neighbours())
    own = x_own.shape[0]
    pos = own // 2
    length = 4 * pos
    heads = context.shape[-1] // HEAD_DIM
    wide = heads * HEAD_DIM

    def project():
        @pl.loop(0, 8)
        def _(rank):
            mixed = dot(x_all[rank], qkv[...])
            for micro in range(2):
                row, piece = row_place(rank, micro)
                place = pl.ds(pl.multiple_of(piece * pos, pos), pos)
                near = mixed[micro * pos : (micro + 1) * pos]
                cos, sin = cosine[row, place], sine[row, place]
                for head in range(heads):
                    cols = pl.ds(head * HEAD_DIM, HEAD_DIM)
                    for kind, target in enumerate((queries, key_rows, value_rows)):
                        first = kind * wide + head * HEAD_DIM
                        values = near[:, first : first + HEAD_DIM]
                        if kind < 2:
                            values = turned(values, cos, sin)
                        target[row, place, cols] = values.astype(jnp.bfloat16)

    def attend():
        scale = 1.0 / math.sqrt(HEAD_DIM)
        here = lax.broadcasted_iota(jnp.int32, (length, length), 0)
        there = lax.broadcasted_iota(jnp.int32, (length, length), 1)

        @pl.loop(0, 4)
        def _(row):
            bound = end_key[row].astype(jnp.int32)
            seen = (start_query[row] == start_key[row]) & ((there <= here) | (there < bound))
            for head in range(heads):
                cols = pl.ds(head * HEAD_DIM, HEAD_DIM)
                scores = contract_last(queries[row, :, cols], key_rows[row, :, cols]) * scale
                scores = jnp.where(seen, scores, masked_score)
                scores = jnp.exp(scores - jnp.max(scores, axis=-1, keepdims=True))
                probs = scores / jnp.sum(scores, axis=-1, keepdims=True)
                probs_out[row, head] = probs
                result = dot(probs.astype(jnp.bfloat16), value_rows[row, :, cols])
                result = result.astype(jnp.bfloat16)
                for piece in range(4):
                    target = pl.ds(pl.multiple_of((row % 2) * pos, pos), pos)
                    source = result[piece * pos : (piece + 1) * pos]
                    context[(row // 2) * 4 + piece, target, cols] = source

    def branch_parts():
        @pl.loop(0, 8)
        def _(rank):
            part[rank] = dot(context[rank], proj[...]).astype(jnp.bfloat16)

    pieces = 4
    height = own // pieces

    def norm_rows(start):
        count = 16

        @pl.loop(0, height // count)
        def _(index):
            rows = pl.ds(pl.multiple_of(start + index * count, count), count)
            whole = deep_alpha * x_own[rows].astype(jnp.float32) + branch[rows]
            near, inverse = norm_parts(whole)
            hat[rows] = near
            inverse_out[rows] = jnp.broadcast_to(inverse, (count, LANES))
            normed[rows] = (near * gain[...] + shift[...]).astype(jnp.bfloat16)

    core_in, core_sum, side_in, side_sum, last_in = scratch
    scatters, gathers = [], []
    for index in range(pieces):
        rows = pl.ds(index * height, height)
        views = [core_in.at[:, rows], core_sum.at[:, rows], side_in.at[:, :, rows]]
        views += [side_sum.at[:, rows], last_in.at[:, rows]]
        scatters.append(
            plane_scatter_flow(at, wire, index, part.at[:, rows], branch.at[rows], *views)
        )
        sem = own_sems.at[1 + index]
        gathers.append(
            column_gather_flow(at, wire, index, normed.at[rows], normed_all.at[:, rows], sem)
        )
    units = unit_gather_flow(at, wire, ffn_in, ffn_out, own_sems.at[0])
    next(units)
    next(units)
    project()
    next(units)
    attend()
    next(units)
    branch_parts()
    for stage in range(3):
        for flow in scatters:
            next(flow)
    for index in range(pieces + 3):
        if index < pieces:
            for _ in scatters[index]:
                pass
            norm_rows(index * height)
            next(gathers[index])
        for lag in (1, 2, 3):
            if 0 <= index - lag < pieces:
                next(gathers[index - lag], None)
        next(units, None)
    for flow in gathers + [units]:
        for _ in flow:
            pass
    wire.drain()


ANY = pl.BlockSpec(memory_space=pl.ANY)
VMEM = pl.BlockSpec(memory_space=pltpu.VMEM)


def comm_params(number):
    return pltpu.CompilerParams(
        collective_id=number, has_side_effects=True, vmem_limit_bytes=63 * 2**20
    )


def open_heads(qkv_parts, ffn_parts, proj_own, x_own, small):
    _, rows_own, qkv_width = qkv_parts.shape
    _, matrices, _, unit_width = ffn_parts.shape
    own, width = x_own.shape
    low_type = jnp.bfloat16
    return pl.pallas_call(
        open_heads_kernel,
        out_shape=(
            jax.ShapeDtypeStruct((4, 8, rows_own, qkv_width), low_type),
            jax.ShapeDtypeStruct((matrices, 4, 2, 2, 2, rows_own, unit_width), low_type),
            jax.ShapeDtypeStruct((4, rows_own, width), low_type),
            jax.ShapeDtypeStruct((8, own, width), low_type),
            jax.ShapeDtypeStruct((4, 8) + small.shape, small.dtype),
        ),
        in_specs=[VMEM] * 5,
        out_specs=(ANY,) * 5,
        scratch_shapes=[
            pltpu.SemaphoreType.DMA((136,)),
            pltpu.SemaphoreType.DMA((136,)),
            pltpu.SemaphoreType.DMA((5,)),
        ],
        compiler_params=comm_params(1),
        name="open_heads",
    )(qkv_parts, ffn_parts, proj_own, x_own, small)


def open_units(x_all, qkv, proj, tables, x_own, gain, shift, ffn_parts):
    _, matrices, rows_own, unit_width = ffn_parts.shape
    own, width = x_own.shape
    head_width = proj.shape[0]
    length = 2 * own
    low_type = jnp.bfloat16
    rows = jax.ShapeDtypeStruct((4, length, head_width), low_type)
    return pl.pallas_call(
        open_units_kernel,
        out_shape=(
            rows,
            rows,
            rows,
            jax.ShapeDtypeStruct((4, head_width // HEAD_DIM, length, length), jnp.float32),
            jax.ShapeDtypeStruct((8, own, head_width), low_type),
            jax.ShapeDtypeStruct((own, width), low_type),
            jax.ShapeDtypeStruct((own, width), jnp.float32),
            jax.ShapeDtypeStruct((own, LANES), jnp.float32),
            jax.ShapeDtypeStruct((8, own, width), low_type),
            jax.ShapeDtypeStruct((matrices, 4, 2, 2, 2, rows_own, unit_width), low_type),
        ),
        in_specs=[VMEM] * 12,
        out_specs=(VMEM,) * 8 + (ANY, ANY),
        scratch_shapes=[
            pltpu.VMEM((8, own, width), low_type),
            pltpu.VMEM((own, width), jnp.float32),
        ]
        + plane_scratch(own, width)
        + [
            pltpu.SemaphoreType.DMA((136,)),
            pltpu.SemaphoreType.DMA((136,)),
            pltpu.SemaphoreType.DMA((5,)),
        ],
        compiler_params=comm_params(4),
        name="open_units",
    )(x_all, qkv, proj, *tables, x_own, gain, shift, ffn_parts)


def add_rows(out, *terms):
    step = 32

    @pl.loop(0, out.shape[0] // step)
    def _(index):
        part = pl.ds(pl.multiple_of(index * step, step), step)
        whole = terms[0][part].astype(jnp.float32)
        for term in terms[1:]:
            whole = whole + term[part].astype(jnp.float32)
        out[part] = whole.astype(out.dtype)


def column_scatter_flow(
    at, wire, tag, part, out, core_in, core_sum, up_in, down_in, up_sum, down_sum
):
    core_side = at.plane(1)[0]
    up, down = at.ends()
    for goal in (3, 0, 2, 1):
        source = part.at[goal * 2 + 1 - at.c]
        wire.send(("rc", tag, goal), source, core_in.at[goal], core_side)
    yield
    for goal in (3, 0, 2, 1):
        wire.arrive(("rc", tag, goal), core_in.at[goal], core_side)
        add_rows(core_sum.at[goal], part.at[goal * 2 + at.c], core_in.at[goal])
        for rising in {3: (3,), 2: (2,), 1: (1,)}.get(goal, ()):
            key = "ru", tag, rising
            wire.send(key, core_sum.at[rising], up_in.at[rising], up, at.zi == 0)
        for falling in {0: (0,), 1: (1, 2)}.get(goal, ()):
            key = "rd", tag, falling
            wire.send(key, core_sum.at[falling], down_in.at[falling], down, at.zi == 3)

    def climb(goal):
        wire.arrive(("ru", tag, goal), up_in.at[goal], down)
        add_rows(up_sum.at[goal], core_sum.at[goal], up_in.at[goal])

    def descend(goal):
        wire.arrive(("rd", tag, goal), down_in.at[goal], up)
        add_rows(down_sum.at[goal], core_sum.at[goal], down_in.at[goal])

    def rise(goal, z):
        pl.when(at.zi == z)(lambda: climb(goal))
        key = "ru", tag, goal
        target = up_in.at[goal]
        wire.send(("ru2", tag, goal), up_sum.at[goal], target, up, at.zi == z, recv=key)

    def fall(goal, z):
        pl.when(at.zi == z)(lambda: descend(goal))
        key = "rd", tag, goal
        target = down_in.at[goal]
        wire.send(("rd2", tag, goal), down_sum.at[goal], target, down, at.zi == z, recv=key)

    yield
    rise(3, 1)
    fall(0, 2)
    yield
    rise(3, 2)
    fall(0, 1)
    rise(2, 1)
    fall(1, 2)
    yield
    add_rows(out, core_sum.at[at.zi])

    def last(key, source, device):
        wire.arrive(key, source, device)
        add_rows(out, out, source)

    for goal in range(4):
        if goal > 0:
            pl.when(at.zi == goal)(lambda: last(("ru", tag, goal), up_in.at[goal], down))
        if goal < 3:
            pl.when(at.zi == goal)(lambda: last(("rd", tag, goal), down_in.at[goal], up))


def column_gather_flow(at, wire, tag, own_in, out, own_sem):
    core_side = at.plane(1)[0]
    up, down = at.ends()

    def slot(z, c):
        return out.at[jnp.clip(z, 0, 3) * 2 + c]

    mine = slot(at.zi, at.c)
    wire.send(("gu", tag, 0), own_in, mine, up, at.zi < 3)
    wire.send(("gd", tag, 0), own_in, mine, down, at.zi > 0)
    wire.send(("gc", tag), own_in, mine, core_side)
    own = pltpu.make_async_copy(own_in, mine, own_sem)
    own.start()
    for hop in (1, 2, 3):
        yield
        below, above = slot(at.zi - hop, at.c), slot(at.zi + hop, at.c)
        has_below, has_above = at.zi >= hop, at.zi <= 3 - hop
        wire.arrive(("gu", tag, hop - 1), below, down, has_below)
        if hop < 3:
            wire.send(("gu", tag, hop), below, below, up, has_below & (at.zi < 3))
        wire.send(("gcu", tag, hop), below, below, core_side, has_below)
        wire.arrive(("gd", tag, hop - 1), above, up, has_above)
        if hop < 3:
            wire.send(("gd", tag, hop), above, above, down, has_above & (at.zi > 0))
        wire.send(("gcd", tag, hop), above, above, core_side, has_above)
    yield
    own.wait()
    wire.arrive(("gc", tag), slot(at.zi, 1 - at.c), core_side)
    for hop in (1, 2, 3):
        below, above = slot(at.zi - hop, 1 - at.c), slot(at.zi + hop, 1 - at.c)
        wire.arrive(("gcu", tag, hop), below, core_side, at.zi >= hop)
        wire.arrive(("gcd", tag, hop), above, core_side, at.zi <= 3 - hop)


def column_scratch(own, width):
    return [pltpu.VMEM((4, own, width), jnp.bfloat16)] * 6


def plane_scatter_flow(
    at, wire, tag, part, out, core_in, core_sum, side_in, side_sum, last_in
):
    x_side, y_side, core_side = at.plane(4)[0], at.plane(2)[0], at.plane(1)[0]
    half = out.shape[1] // 2
    halves = (pl.ds(0, half), pl.ds(half, half))
    order = ((1, 1), (1, 0), (0, 1), (0, 0))

    def place(dx, dy):
        return flip(at.x, dx), flip(at.y, dy)

    for dx, dy in order:
        x, y = place(dx, dy)
        other = x * 4 + y * 2 + 1 - at.c
        wire.send(("c", tag, dx, dy), part.at[other], core_in.at[dx * 2 + dy], core_side)
    yield
    for dx, dy in order:
        x, y = place(dx, dy)
        mine = x * 4 + y * 2 + at.c
        slot = dx * 2 + dy
        wire.arrive(("c", tag, dx, dy), core_in.at[slot], core_side)
        add_rows(core_sum.at[slot], part.at[mine], core_in.at[slot])
        if dx:
            source = core_sum.at[slot, :, halves[0]]
            wire.send(("sa", tag, dy), source, side_in.at[0, dy], x_side)
        if dy:
            source = core_sum.at[slot, :, halves[1]]
            wire.send(("sb", tag, dx), source, side_in.at[1, dx], y_side)
    yield
    wire.arrive(("sa", tag, 1), side_in.at[0, 1], x_side)
    add_rows(side_sum.at[0], core_sum.at[1, :, halves[0]], side_in.at[0, 1])
    wire.send(("sy", tag), side_sum.at[0], last_in.at[0], y_side)
    wire.arrive(("sb", tag, 1), side_in.at[1, 1], y_side)
    add_rows(side_sum.at[1], core_sum.at[2, :, halves[1]], side_in.at[1, 1])
    wire.send(("sx", tag), side_sum.at[1], last_in.at[1], x_side)
    yield
    wire.arrive(("sa", tag, 0), side_in.at[0, 0], x_side)
    wire.arrive(("sb", tag, 0), side_in.at[1, 0], y_side)
    wire.arrive(("sy", tag), last_in.at[0], y_side)
    terms = core_sum.at[0, :, halves[0]], side_in.at[0, 0], last_in.at[0]
    add_rows(out.at[:, halves[0]], *terms)
    wire.arrive(("sx", tag), last_in.at[1], x_side)
    terms = core_sum.at[0, :, halves[1]], side_in.at[1, 0], last_in.at[1]
    add_rows(out.at[:, halves[1]], *terms)


def plane_scratch(own, width):
    return [
        pltpu.VMEM((4, own, width), jnp.bfloat16),
        pltpu.VMEM((4, own, width), jnp.bfloat16),
        pltpu.VMEM((2, 2, own, width // 2), jnp.bfloat16),
        pltpu.VMEM((2, own, width // 2), jnp.bfloat16),
        pltpu.VMEM((2, own, width // 2), jnp.bfloat16),
    ]


def plane_gather_flow(at, wire, own_in, out, own_sem):
    x_side, y_side, core_side = at.plane(4)[0], at.plane(2)[0], at.plane(1)[0]
    half = own_in.shape[0] // 2
    mine = out.at[at.rank]
    wire.send("gx", own_in, mine, x_side)
    wire.send("gy", own_in, mine, y_side)
    wire.send("gc0", own_in, mine, core_side)
    own = pltpu.make_async_copy(own_in, mine, own_sem)
    own.start()
    yield
    from_x, from_y, from_xy = (at.plane(delta)[1] for delta in (4, 2, 6))
    low_half, high_half = pl.ds(0, half), pl.ds(half, half)
    wire.arrive("gx", out.at[from_x], x_side)
    wire.send("gd0", out.at[from_x, low_half], out.at[from_x, low_half], y_side)
    wire.send("gc1", out.at[from_x], out.at[from_x], core_side)
    wire.arrive("gy", out.at[from_y], y_side)
    wire.send("gd1", out.at[from_y, high_half], out.at[from_y, high_half], x_side)
    wire.send("gc2", out.at[from_y], out.at[from_y], core_side)
    yield
    wire.arrive("gd0", out.at[from_xy, low_half], y_side)
    wire.arrive("gd1", out.at[from_xy, high_half], x_side)
    wire.send("gc3", out.at[from_xy], out.at[from_xy], core_side)
    own.wait()
    for index, delta in enumerate((1, 5, 3, 7)):
        wire.arrive("gc%d" % index, out.at[at.plane(delta)[1]], core_side)


def turn_kernel(
    part,
    normed,
    out_grad,
    gain,
    shift,
    layer_out,
    d_second,
    down_out,
    norm_out,
    second,
    down_low,
    core_in,
    core_sum,
    up_in,
    down_in,
    up_sum,
    down_sum,
    send_sems,
    recv_sems,
    own_sems,
):
    at = Place()
    wire = Wire(send_sems, recv_sems)
    enter(at.column_neighbours())
    pieces = 2
    height = normed.shape[0] // pieces
    scratch = core_in, core_sum, up_in, down_in, up_sum, down_sum

    def norm_rows(start):
        count = 16

        @pl.loop(0, height // count)
        def _(index):
            rows = pl.ds(pl.multiple_of(start + index * count, count), count)
            whole = deep_alpha * normed[rows].astype(jnp.float32) + second[rows]
            near, inverse = norm_parts(whole)
            layer_out[rows] = (near * gain[...] + shift[...]).astype(jnp.bfloat16)
            cotangent = out_grad[rows].astype(jnp.float32)
            result = norm_back(cotangent, near, inverse, gain[...])
            d_second[rows] = result
            down_low[rows] = result.astype(jnp.bfloat16)
            along = cotangent * near
            norm_out[0] += along[:8] + along[8:]
            norm_out[1] += cotangent[:8] + cotangent[8:]

    scatters, gathers = [], []
    for index in range(pieces):
        rows = pl.ds(index * height, height)
        views = [ref.at[:, rows] for ref in scratch]
        scatters.append(
            column_scatter_flow(at, wire, index, part.at[:, rows], second.at[rows], *views)
        )
        gathers.append(
            column_gather_flow(
                at, wire, index, down_low.at[rows], down_out.at[:, rows], own_sems.at[index]
            )
        )
    norm_out[...] = jnp.zeros_like(norm_out)
    for flow in scatters:
        next(flow)
    for flow in scatters:
        next(flow)
    for index in range(pieces + 3):
        if index < pieces:
            for _ in scatters[index]:
                pass
            norm_rows(index * height)
            next(gathers[index])
        for lag in (1, 2, 3):
            if 0 <= index - lag < pieces:
                next(gathers[index - lag], None)
    for flow in gathers:
        for _ in flow:
            pass
    wire.drain()


def turn(part, normed, out_grad, gain, shift):
    _, own, width = part.shape
    low_type = jnp.bfloat16
    return pl.pallas_call(
        turn_kernel,
        out_shape=(
            jax.ShapeDtypeStruct((own, width), low_type),
            jax.ShapeDtypeStruct((own, width), jnp.float32),
            jax.ShapeDtypeStruct((8, own, width), low_type),
            jax.ShapeDtypeStruct((2, 8, width), jnp.float32),
        ),
        in_specs=[VMEM] * 5,
        out_specs=(VMEM, VMEM, ANY, VMEM),
        scratch_shapes=[
            pltpu.VMEM((own, width), jnp.float32),
            pltpu.VMEM((own, width), low_type),
        ]
        + column_scratch(own, width)
        + [
            pltpu.SemaphoreType.DMA((112,)),
            pltpu.SemaphoreType.DMA((112,)),
            pltpu.SemaphoreType.DMA((4,)),
        ],
        compiler_params=comm_params(5),
        name="turn",
    )(part, normed, out_grad, gain, shift)


def close_units_kernel(
    gate_in,
    raise_in,
    lower_in,
    part,
    d_second,
    hat,
    inverse,
    gain,
    proj,
    queries,
    key_rows,
    value_rows,
    probs_in,
    cosine,
    sine,
    ffn_out,
    branch_out,
    d_mixed,
    d_first,
    norm_out,
    d_context,
    first_in,
    second_sum,
    second_in,
    total,
    d_normed,
    branch_low,
    core_in,
    core_sum,
    up_in,
    down_in,
    up_sum,
    down_sum,
    send_sems,
    recv_sems,
    own_sems,
):
    at = Place()
    wire = Wire(send_sems, recv_sems)
    enter(at.neighbours())
    x_side, y_side = at.plane(4)[0], at.plane(2)[0]
    steps = (4, 3, 5, 2, 6, 1, 7, 0)
    sources = gate_in, raise_in, lower_in

    def owner(step):
        other = at.column(step)[1]
        return other // 2, lax.rem(other, 2)

    def ffn_first(turn):
        step = steps[turn]
        z, c = owner(step)
        for index, source in enumerate(sources):
            if turn % 2:
                block, device = source.at[z, 1 - at.x, :, c], x_side
            else:
                block, device = source.at[z, :, 1 - at.y, c], y_side
            wire.send(("a", step, index), block, first_in.at[step, index], device)

    def ffn_second(turn):
        step = steps[turn]
        z, c = owner(step)
        for index, source in enumerate(sources):
            if turn % 2:
                wire.arrive(("a", step, index), first_in.at[step, index], x_side)
                terms = source.at[z, at.x, 1 - at.y, c], first_in.at[step, index, 1 - at.y]
            else:
                wire.arrive(("a", step, index), first_in.at[step, index], y_side)
                terms = source.at[z, 1 - at.x, at.y, c], first_in.at[step, index, 1 - at.x]
            add_rows(second_sum.at[step, index], *terms)
        wire.send(
            ("b", step), second_sum.at[step], second_in.at[step], y_side if turn % 2 else x_side
        )

    own_total = pltpu.make_async_copy(total.at[0], ffn_out.at[at.unit], own_sems.at[0])

    def ffn_last(turn):
        step = steps[turn]
        z, c = owner(step)
        near = at.y if turn % 2 else at.x
        wire.arrive(("b", step), second_in.at[step], x_side)
        for index, source in enumerate(sources):
            add_rows(
                total.at[step, index],
                source.at[z, at.x, at.y, c],
                first_in.at[step, index, near],
                second_in.at[step, index],
            )
        if step:
            wire.send(("f", step), total.at[step], ffn_out.at[at.unit], at.column(step)[0])
        else:
            own_total.start()

    def norm_rows():
        count = 16
        norm_out[...] = jnp.zeros_like(norm_out)

        @pl.loop(0, hat.shape[0] // count)
        def _(index):
            rows = pl.ds(pl.multiple_of(index * count, count), count)
            cotangent = deep_alpha * d_second[rows] + d_normed[rows]
            near = hat[rows]
            result = norm_back(cotangent, near, inverse[rows, :1], gain[...])
            d_first[rows] = result
            branch_low[rows] = result.astype(jnp.bfloat16)
            along = cotangent * near
            norm_out[0] += along[:8] + along[8:]
            norm_out[1] += cotangent[:8] + cotangent[8:]

    pos = hat.shape[0] // 2
    wide = proj.shape[0]
    heads = wide // HEAD_DIM
    scale = 1.0 / math.sqrt(HEAD_DIM)

    def pull():
        @pl.loop(0, 8)
        def _(rank):
            result = contract_last(branch_out[rank], proj[...]).astype(jnp.bfloat16)
            for micro in range(2):
                row, piece = row_place(rank, micro)
                place = pl.ds(pl.multiple_of(piece * pos, pos), pos)
                d_context[row, place] = result[micro * pos : (micro + 1) * pos]

    def attend_back(first, last):
        @pl.loop(first, last)
        def _(row):
            cos, sin = cosine[row], -sine[row]
            target = pl.ds(pl.multiple_of((row % 2) * pos, pos), pos)
            for head in range(heads):
                cols = pl.ds(head * HEAD_DIM, HEAD_DIM)
                probs, above = probs_in[row, head], d_context[row, :, cols]
                d_probs = contract_last(above, value_rows[row, :, cols])
                along = jnp.sum(probs * d_probs, axis=-1, keepdims=True)
                d_scores = (probs * (d_probs - along)).astype(jnp.bfloat16)
                d_query = dot(d_scores, key_rows[row, :, cols]) * scale
                d_keys = contract_first(d_scores, queries[row, :, cols]) * scale
                d_values = contract_first(probs.astype(jnp.bfloat16), above)
                results = turned(d_query, cos, sin), turned(d_keys, cos, sin), d_values
                for kind, result in enumerate(results):
                    result = result.astype(jnp.bfloat16)
                    place = pl.ds(kind * wide + head * HEAD_DIM, HEAD_DIM)
                    for piece in range(4):
                        source = result[piece * pos : (piece + 1) * pos]
                        d_mixed[(row // 2) * 4 + piece, target, place] = source

    scatter = column_scatter_flow(
        at, wire, 0, part, d_normed, core_in, core_sum, up_in, down_in, up_sum, down_sum
    )
    next(scatter)
    for turn in range(5):
        ffn_first(turn)
    next(scatter)
    next(scatter)
    ffn_second(0)
    ffn_first(5)
    ffn_second(1)
    ffn_first(6)
    next(scatter)
    ffn_second(2)
    ffn_first(7)
    ffn_second(3)
    for _ in scatter:
        pass
    norm_rows()
    spread = plane_gather_flow(at, wire, branch_low, branch_out, own_sems.at[1])
    next(spread)
    ffn_last(0)
    ffn_last(1)
    ffn_second(4)
    ffn_last(2)
    ffn_second(5)
    ffn_last(3)
    next(spread)
    ffn_second(6)
    ffn_second(7)
    ffn_last(4)
    for _ in spread:
        pass
    pull()
    ffn_last(5)
    attend_back(0, 2)
    ffn_last(6)
    attend_back(2, 4)
    ffn_last(7)
    own_total.wait()
    for step in steps:
        if step:
            device, other = at.column(-step)
            wire.arrive(("f", step), ffn_out.at[other], device)
    wire.drain()


def close_units(grads, part, d_second, hat, inverse, gain, *heads):
    rows_own, unit_width = grads[0].shape[-2:]
    _, own, width = part.shape
    low_type = jnp.bfloat16
    head_width = heads[0].shape[0]
    block = (rows_own, unit_width)
    return pl.pallas_call(
        close_units_kernel,
        out_shape=(
            jax.ShapeDtypeStruct((8, 3) + block, low_type),
            jax.ShapeDtypeStruct((8, own, width), low_type),
            jax.ShapeDtypeStruct((8, own, 3 * head_width), low_type),
            jax.ShapeDtypeStruct((own, width), jnp.float32),
            jax.ShapeDtypeStruct((2, 8, width), jnp.float32),
        ),
        in_specs=[VMEM] * 15,
        out_specs=(ANY, VMEM, VMEM, VMEM, VMEM),
        scratch_shapes=[
            pltpu.VMEM((4, 2 * own, head_width), low_type),
            pltpu.VMEM((8, 3, 2) + block, low_type),
            pltpu.VMEM((8, 3) + block, low_type),
            pltpu.VMEM((8, 3) + block, low_type),
            pltpu.VMEM((8, 3) + block, low_type),
            pltpu.VMEM((own, width), jnp.float32),
            pltpu.VMEM((own, width), low_type),
        ]
        + column_scratch(own, width)
        + [
            pltpu.SemaphoreType.DMA((80,)),
            pltpu.SemaphoreType.DMA((80,)),
            pltpu.SemaphoreType.DMA((2,)),
        ],
        compiler_params=comm_params(3),
        name="close_units",
    )(*grads, part, d_second, hat, inverse, gain, *heads)


def close_heads_kernel(
    qkv_in,
    proj_in,
    small_in,
    part,
    qkv_out,
    proj_out,
    small_out,
    d_input,
    proj_below,
    proj_above,
    proj_sum,
    small_plane,
    small_mid,
    small_line,
    up_in,
    down_in,
    up_sum,
    down_sum,
    qkv_total,
    core_in,
    core_sum,
    side_in,
    side_sum,
    last_in,
    send_sems,
    recv_sems,
    own_sems,
):
    at = Place()
    wire = Wire(send_sems, recv_sems)
    enter(at.neighbours())
    scatter = plane_scatter_flow(
        at, wire, 0, part, d_input, core_in, core_sum, side_in, side_sum, last_in
    )
    next(scatter)

    def add(*terms):
        whole = terms[0].astype(jnp.float32)
        for term in terms[1:]:
            whole = whole + term.astype(jnp.float32)
        return whole.astype(jnp.bfloat16)

    for delta in range(1, 8):
        device, other = at.plane(delta)
        wire.send(("s", delta), small_in.at[other], small_plane.at[at.rank], device)

    def small_second():
        whole = small_in[at.rank]
        for delta in range(1, 8):
            device, other = at.plane(delta)
            wire.arrive(("s", delta), small_plane.at[other], device)
            whole = whole + small_plane[other]
        small_mid[...] = whole
        for dz in range(1, 4):
            z = lax.rem(at.zi + dz, 4)
            wire.send(("t", dz), small_mid.at[z], small_line.at[at.zi], at.line(z))

    def small_last():
        whole = small_mid[at.zi]
        for dz in range(1, 4):
            z = lax.rem(at.zi - dz + 4, 4)
            wire.arrive(("t", dz), small_line.at[z], at.line(z))
            whole = whole + small_line[z]
        small_out[...] = whole

    pieces = 4
    wide = 8 // pieces
    up, down = at.line(jnp.minimum(at.zi + 1, 3)), at.line(jnp.maximum(at.zi - 1, 0))

    def qkv_rise(goal, piece, low_z, high_z):
        part = pl.ds(piece * wide, wide)
        here = (at.zi >= low_z) & (at.zi <= high_z)
        source = up_sum.at[goal, part]

        def climb():
            wire.arrive(("u", goal, piece), up_in.at[goal, part], down)
            up_sum[goal, part] = add(qkv_in[goal, part], up_in[goal, part])

        key = "u", goal, piece
        if low_z == 0:
            first = qkv_in.at[goal, part]
            wire.send(("u0", goal, piece), first, up_in.at[goal, part], up, at.zi == 0, recv=key)
        if high_z > 0:
            here = here & (at.zi > 0)
            pl.when(here)(climb)
            wire.send(key, source, up_in.at[goal, part], up, here)

    def qkv_fall(goal, piece, low_z, high_z):
        part = pl.ds(piece * wide, wide)
        here = (at.zi >= low_z) & (at.zi <= high_z)
        source = down_sum.at[goal, part]

        def descend():
            wire.arrive(("d", goal, piece), down_in.at[goal, part], up)
            down_sum[goal, part] = add(qkv_in[goal, part], down_in[goal, part])

        key = "d", goal, piece
        if high_z == 3:
            first = qkv_in.at[goal, part]
            wire.send(
                ("d0", goal, piece), first, down_in.at[goal, part], down, at.zi == 3, recv=key
            )
        if low_z < 3:
            here = here & (at.zi < 3)
            pl.when(here)(descend)
            wire.send(key, source, down_in.at[goal, part], down, here)

    proj_home = at.head_home()

    def proj_add(slot, *terms):
        add_rows(proj_sum.at[slot], *(term.at[slot] for term in terms))

    below, above = at.zi < proj_home, at.zi > proj_home
    ends = (at.zi == 0) | (at.zi == 3)

    def proj_pass(slot):
        under, over = proj_below.at[slot], proj_above.at[slot]
        wire.send(("pu", slot), proj_in.at[slot], under, up, below & ends)
        wire.send(("pd", slot), proj_in.at[slot], over, down, above & ends)

        def climb():
            wire.arrive(("pu", slot), under, down)
            proj_add(slot, proj_in, proj_below)

        def descend():
            wire.arrive(("pd", slot), over, up)
            proj_add(slot, proj_in, proj_above)

        pl.when(below & (at.zi > 0))(climb)
        pl.when(above & (at.zi < 3))(descend)
        source = proj_sum.at[slot]
        key = "pu", slot
        wire.send(("pu2", slot), source, under, up, below & (at.zi > 0), recv=key)
        key = "pd", slot
        wire.send(("pd2", slot), source, over, down, above & (at.zi < 3), recv=key)

    chunk = at.y * 2 + at.c
    holder_device, holder = at.holder()

    def proj_last():
        home = at.zi == proj_home
        for slot in range(4):
            under, over = proj_below.at[slot], proj_above.at[slot]

            def first():
                wire.arrive(("pu", slot), under, down)
                proj_add(slot, proj_in, proj_below)

            def only():
                wire.arrive(("pd", slot), over, up)
                proj_add(slot, proj_in, proj_above)

            def both():
                wire.arrive(("pd", slot), over, up)
                proj_add(slot, proj_sum, proj_above)

            pl.when(home & (at.zi > 0))(first)
            pl.when(home & (at.zi == 0))(only)
            pl.when(home & (at.zi > 0) & (at.zi < 3))(both)
            target = (at.zo, at.zi, at.x, slot // 2, slot % 2)
            other = (chunk != slot) | (at.rank != holder)
            wire.send(("o", slot), proj_sum.at[slot], proj_out, target, home & other, recv="o")
        own = pltpu.make_async_copy(proj_sum.at[chunk], proj_out, own_sems.at[2])
        pl.when(home & (at.rank == holder))(own.start)
        pl.when(home & (at.rank == holder))(own.wait)

    def qkv_last(piece):
        part = pl.ds(piece * wide, wide)
        for goal in range(4):

            @pl.when(at.zi == goal)
            def _():
                terms = [qkv_in[goal, part]]
                if goal > 0:
                    wire.arrive(("u", goal, piece), up_in.at[goal, part], down)
                    terms.append(up_in[goal, part])
                if goal < 3:
                    wire.arrive(("d", goal, piece), down_in.at[goal, part], up)
                    terms.append(down_in[goal, part])
                qkv_total[part] = add(*terms)

    for piece in range(pieces):
        qkv_rise(3, piece, 0, 1)
        qkv_fall(0, piece, 2, 3)
        if piece == 0:
            next(scatter)
    for piece in range(pieces):
        qkv_rise(3, piece, 2, 2)
        qkv_fall(0, piece, 1, 1)
    for slot in range(4):
        proj_pass(slot)
    next(scatter)
    small_second()
    for piece in range(pieces):
        qkv_rise(2, piece, 0, 1)
        qkv_fall(1, piece, 2, 3)
    for _ in scatter:
        pass
    for piece in range(pieces):
        qkv_rise(1, piece, 0, 0)
        qkv_fall(2, piece, 3, 3)
    proj_last()
    for piece in range(pieces):
        qkv_last(piece)
    own_qkv = pltpu.make_async_copy(
        qkv_total.at[at.rank], qkv_out.at[at.rank], own_sems.at[1]
    )
    own_qkv.start()
    for delta in range(1, 8):
        device, other = at.plane(delta)
        wire.send(("q", delta), qkv_total.at[other], qkv_out.at[at.rank], device)
    own_qkv.wait()
    for delta in range(1, 8):
        device, other = at.plane(delta)
        wire.arrive(("q", delta), qkv_out.at[other], device)
    small_last()
    wire.arrive("o", proj_out, holder_device, at.rank != holder)
    wire.drain()


def close_heads(qkv_part, proj_part, small_part, part):
    _, _, rows_own, qkv_width = qkv_part.shape
    _, own, width = part.shape
    low_type = jnp.bfloat16
    line = (4, 8, rows_own, qkv_width)
    small_shape = small_part.shape[1:]
    return pl.pallas_call(
        close_heads_kernel,
        out_shape=(
            jax.ShapeDtypeStruct((8, rows_own, qkv_width), low_type),
            jax.ShapeDtypeStruct((rows_own, width), low_type),
            jax.ShapeDtypeStruct(small_shape[1:], small_part.dtype),
            jax.ShapeDtypeStruct((own, width), jnp.float32),
        ),
        in_specs=[VMEM] * 4,
        out_specs=(ANY, ANY, VMEM, VMEM),
        scratch_shapes=[
            pltpu.VMEM((4, rows_own, width), low_type),
            pltpu.VMEM((4, rows_own, width), low_type),
            pltpu.VMEM((4, rows_own, width), low_type),
            pltpu.VMEM(small_part.shape, small_part.dtype),
            pltpu.VMEM(small_shape, small_part.dtype),
            pltpu.VMEM(small_shape, small_part.dtype),
            pltpu.VMEM(line, low_type),
            pltpu.VMEM(line, low_type),
            pltpu.VMEM(line, low_type),
            pltpu.VMEM(line, low_type),
            pltpu.VMEM(line[1:], low_type),
        ]
        + plane_scratch(own, width)
        + [
            pltpu.SemaphoreType.DMA((112,)),
            pltpu.SemaphoreType.DMA((112,)),
            pltpu.SemaphoreType.DMA((3,)),
        ],
        compiler_params=comm_params(2),
        name="close_heads",
    )(qkv_part, proj_part, small_part, part)


def group_body(
    hidden_in,
    token_marks,
    out_grad,
    qkv_weight,
    proj_weight,
    gate_weight,
    up_weight,
    down_weight,
    first_gain,
    first_shift,
    second_gain,
    second_shift,
):
    micro_count, _, pos_count, width = hidden_in.shape
    rows_own = qkv_weight.shape[0]
    units = gate_weight.shape[1]
    head_ways = math.prod(lax.axis_size(name) for name in HEAD_AXES)
    unit_ways = math.prod(lax.axis_size(name) for name in UNIT_AXES)
    chunk_count = lax.axis_size("y") * lax.axis_size("c")
    row_length = pos_count * chunk_count
    x_size = lax.axis_size("x")
    marks_own = token_marks.astype(jnp.float32)
    own = micro_count * pos_count
    head_width = width // head_ways
    heads_here = head_width // HEAD_DIM
    unit_width = -(-units // (unit_ways * LANES)) * LANES
    unit_pad = unit_width * unit_ways - units
    x_own = hidden_in.reshape(own, width)

    params = jnp.stack([first_gain, first_shift, second_gain, second_shift])
    small = jnp.concatenate([params.astype(jnp.float32).ravel(), marks_own.ravel()])
    small = jnp.pad(small, (0, -small.size % (8 * LANES))).reshape(-1, LANES)

    qkv_parts = qkv_weight.reshape(rows_own, 3, 4, 2, head_width)
    qkv_parts = jnp.stack([qkv_parts[:, :, home] for home in (0, 3, 1, 2)])
    qkv_parts = qkv_parts.transpose(3, 0, 1, 2, 4).reshape(head_ways, rows_own, 3 * head_width)

    def unit_parts(*matrices):
        parts = jnp.stack(matrices)
        parts = jnp.pad(parts, ((0, 0), (0, 0), (0, unit_pad)))
        parts = parts.reshape(len(matrices), rows_own, unit_ways, unit_width)
        return parts.transpose(2, 0, 1, 3)

    qkv_here, gate_here, proj_here, x_all, small = open_heads(
        qkv_parts, unit_parts(gate_weight), proj_weight, x_own, small
    )
    qkv_here = qkv_here.reshape(-1, 3 * head_width)
    gate_here = gate_here.reshape(-1, unit_width)
    x_all = x_all.reshape(-1, width)
    proj_here = proj_here.reshape(head_width, width)
    small = small.reshape(unit_ways * 4, -1)
    params = small[:, : 4 * rows_own].reshape(-1, 4, rows_own).transpose(1, 0, 2)
    gain_one, shift_one, gain_two, shift_two = params.reshape(4, 1, width)
    marks = small.reshape(4, head_ways, -1)[lax.axis_index("zi")]
    marks = marks[:, 4 * rows_own : 4 * rows_own + own * 3]

    def to_rows(values):
        inner = values.shape[1:]
        values = values.reshape((x_size, chunk_count, micro_count, pos_count) + inner)
        return jnp.swapaxes(values, 1, 2).reshape((x_size * micro_count, row_length) + inner)

    def from_rows(values):
        inner = values.shape[2:]
        values = values.reshape((x_size, micro_count, chunk_count, pos_count) + inner)
        return jnp.swapaxes(values, 1, 2).reshape((head_ways * own,) + inner)

    row_marks = to_rows(marks.reshape(head_ways * own, 3))
    cosine, sine = rotary_tables(row_marks[..., 2])
    tables = (
        jnp.concatenate([cosine, cosine], axis=-1),
        jnp.concatenate([-sine, sine], axis=-1),
        row_marks[:, :, :1],
        row_marks[:, None, :, 0],
        row_marks[:, None, :, 1],
    )
    queries, key_rows, value_rows, probs, context, normed, hat_one, inverse_one, normed_all, ffn = (
        open_units(
            x_all.reshape(head_ways, own, width),
            qkv_here,
            proj_here,
            tables,
            x_own,
            gain_one,
            shift_one,
            unit_parts(up_weight, down_weight),
        )
    )
    context = context.reshape(-1, head_width)
    normed_all = normed_all.reshape(-1, width)
    up_here, down_here = ffn.reshape(2, -1, unit_width)

    gate_val = dot(normed_all, gate_here)
    up_val = dot(normed_all, up_here)
    gelu_val, gelu_slope = gelu_parts(gate_val)
    active = low(gelu_val * up_val)
    down_part = low(contract_last(active, down_here)).reshape(unit_ways, own, width)
    layer_rows, d_second, down_low, norm_grads = turn(
        down_part, normed, out_grad.reshape(own, width), gain_two, shift_two
    )
    gain_two_grad, shift_two_grad = jnp.sum(norm_grads, axis=1)
    down_low = down_low.reshape(-1, width)
    d_active = dot(down_low, down_here)
    gate_low = low(d_active * up_val * gelu_slope)
    up_low = low(d_active * gelu_val)
    d_normed_part = low(contract_last(gate_low, gate_here) + contract_last(up_low, up_here))

    def unit_grad(left_side, right_side):
        part = low(contract_first(left_side, right_side))
        return part.reshape(4, 2, 2, 2, rows_own, unit_width)

    ffn_grads = (
        unit_grad(normed_all, gate_low),
        unit_grad(normed_all, up_low),
        unit_grad(down_low, active),
    )
    ffn_part, branch_all, d_mixed, d_first, norm_grads = close_units(
        ffn_grads,
        d_normed_part.reshape(unit_ways, own, width),
        d_second,
        hat_one,
        inverse_one,
        gain_one,
        proj_here,
        queries,
        key_rows,
        value_rows,
        probs,
        *tables[:2],
    )
    d_mixed = d_mixed.reshape(-1, 3 * head_width)
    gain_one_grad, shift_one_grad = jnp.sum(norm_grads, axis=1)
    branch_all = branch_all.reshape(-1, width)
    small_grads = jnp.stack([gain_one_grad, shift_one_grad, gain_two_grad, shift_two_grad])
    small_grads = small_grads.reshape(4, 4, head_ways, rows_own).transpose(2, 1, 0, 3)
    small_grads = small_grads.reshape(head_ways, 4, 4 * rows_own // LANES, LANES)
    small_grads = jnp.pad(small_grads, ((0, 0), (0, 0), (0, -small_grads.shape[2] % 8), (0, 0)))

    proj_part = low(contract_first(context, branch_all)).reshape(4, rows_own, width)
    d_input = low(contract_last(d_mixed, qkv_here)).reshape(head_ways, own, width)
    qkv_part = low(contract_first(x_all, d_mixed))
    qkv_part, proj_part, small_grads, d_input = close_heads(
        qkv_part.reshape(4, 8, rows_own, 3 * head_width), proj_part, small_grads, d_input
    )
    d_input = deep_alpha * d_first + d_input
    small_grads = small_grads.ravel()[: 4 * rows_own].reshape(4, rows_own)
    qkv_grad = qkv_part.reshape(2, 4, rows_own, 3, head_width)
    qkv_grad = jnp.stack([qkv_grad[:, place] for place in (0, 2, 3, 1)])
    qkv_grad = qkv_grad.transpose(2, 3, 0, 1, 4).reshape(rows_own, 3 * width).astype(jnp.float32)
    ffn_part = ffn_part.transpose(1, 2, 0, 3).reshape(3, rows_own, unit_ways * unit_width)
    gate_grad, up_grad, down_grad = (
        ffn_part[index, :, :units].astype(jnp.float32) for index in range(3)
    )
    return (
        layer_rows.reshape(micro_count, 1, pos_count, width),
        low(d_input).reshape(micro_count, 1, pos_count, width),
        qkv_grad,
        proj_part.astype(jnp.float32),
        gate_grad,
        up_grad,
        down_grad,
        small_grads[0],
        small_grads[1],
        small_grads[2],
        small_grads[3],
    )


def body(hidden_in, token_marks, out_grad, *weights):
    joined = lax.axis_size("zo")
    if joined == 1:
        return group_body(hidden_in, token_marks, out_grad, *weights)
    rows = weights[0].shape[0]
    width = hidden_in.shape[-1]
    groups = width // (joined * rows)
    group_place = lax.axis_index(ALL[1:])

    def inward(values):
        shape = values.shape
        values = values.reshape(shape[:-1] + (joined, groups, rows))
        return jnp.swapaxes(values, -3, -2).reshape(shape)

    def outward(values):
        shape = values.shape
        values = values.reshape(shape[:-1] + (groups, joined, rows))
        return jnp.swapaxes(values, -3, -2).reshape(shape)

    proj = gather(weights[1], ALL)
    proj = inward(lax.dynamic_slice_in_dim(proj, group_place * joined * rows, joined * rows))
    weights = [gather(weight, "zo") for weight in weights]
    weights[1] = proj
    outs = list(group_body(inward(hidden_in), token_marks, inward(out_grad), *weights))
    outs[:2] = outward(outs[0]), outward(outs[1])
    proj_grad = jnp.zeros((width, width), jnp.float32)
    proj_grad = lax.dynamic_update_slice_in_dim(
        proj_grad, outward(outs[3]), group_place * joined * rows, 0
    )
    outs[2:] = [scatter_sum(grad, "zo") for grad in outs[2:]]
    outs[3] = scatter_sum(proj_grad, ALL)
    return tuple(outs)


def solution(mesh):
    seq_size, ctx_size = mesh.shape["seq"], mesh.shape["ctx"]
    cores, x_size = 2, 2
    zi_size = math.gcd(4, seq_size // x_size)
    zo_size = seq_size // (x_size * zi_size)
    devices = np.asarray(mesh.devices).reshape(
        zo_size, zi_size, x_size, ctx_size // cores, cores
    )
    inner = Mesh(devices, ALL)
    tokens = P(None, ("zo", "zi", "x"), ("y", "c"), None)
    matrix = P(ALL, None)
    vector = P(ALL)
    return jax.shard_map(
        body,
        mesh=inner,
        in_specs=(tokens,) * 3 + (matrix,) * 5 + (vector,) * 4,
        out_specs=(tokens,) * 2 + (matrix,) * 5 + (vector,) * 4,
        check_vma=False,
    )
```

```python
import math

import jax
import jax.numpy as jnp
import numpy as np
from jax import lax
from jax.experimental import pallas as pl
from jax.experimental.pallas import tpu as pltpu
from jax.sharding import Mesh
from jax.sharding import PartitionSpec as P

HEAD_DIM = 128
LANES = 128

deep_alpha = 48.0**0.25
norm_eps = 1e-05
masked_score = -1e30

ALL = ("zo", "zi", "x", "y", "c")
HEAD_AXES = ("x", "y", "c")
UNIT_AXES = ("zi", "c")
HEAD_COPIES = ("zo", "zi")
UNIT_COPIES = ("zo", "x", "y")


def contract_last(left_side, right_side):
    return lax.dot_general(
        left_side, right_side, (((1,), (1,)), ((), ())), preferred_element_type=jnp.float32
    )


def contract_first(left_side, right_side):
    return lax.dot_general(
        left_side, right_side, (((0,), (0,)), ((), ())), preferred_element_type=jnp.float32
    )


def dot(left_side, right_side):
    return jnp.dot(left_side, right_side, preferred_element_type=jnp.float32)


def low(values):
    return values.astype(jnp.bfloat16)


def norm_parts(values):
    center = values - jnp.mean(values, axis=-1, keepdims=True)
    spread = jnp.mean(center * center, axis=-1, keepdims=True)
    inverse = lax.rsqrt(spread + norm_eps)
    return center * inverse, inverse


def norm_back(cotangent, hat, inverse, gain_vec):
    scaled = cotangent * gain_vec
    return (
        scaled
        - jnp.mean(scaled, axis=-1, keepdims=True)
        - hat * jnp.mean(scaled * hat, axis=-1, keepdims=True)
    ) * inverse


def rotary_tables(positions):
    half = HEAD_DIM // 2
    exponent = jnp.arange(half, dtype=jnp.float32) * (2.0 / HEAD_DIM)
    angles = positions.astype(jnp.float32)[..., None] * jnp.exp(-math.log(10000.0) * exponent)
    return (jnp.cos(angles), jnp.sin(angles))


def rotate(values, cosine, sine):
    half = HEAD_DIM // 2
    front, back = values[..., :half], values[..., half:]
    return jnp.concatenate(
        [front * cosine - back * sine, back * cosine + front * sine], axis=-1
    )


def gather(values, axes):
    return lax.all_gather(values, axes, axis=0, tiled=True)


def scatter_sum(values, axes):
    return lax.psum_scatter(values, axes, scatter_dimension=0, tiled=True)


def gelu_parts(value):
    phi = 0.5 + 0.5 * lax.erf(value * math.sqrt(0.5))
    density = jnp.exp(-0.5 * value * value) * (1.0 / math.sqrt(2.0 * math.pi))
    return value * phi, phi + value * density


MESH = pl.DeviceIdType.MESH


class Wire:
    def __init__(self, send_sems, recv_sems):
        self.send_sems, self.recv_sems = send_sems, recv_sems
        self.keys, self.sent = {}, []

    def number(self, key, span=1):
        if key not in self.keys:
            self.keys[key] = sum(size for _, size in self.keys.values()), span
        return self.keys[key][0]

    def copy(self, key, source, target, device, slot=0, span=1, recv=None):
        send = self.number(key, span)
        receive = send if recv is None else self.number(recv)
        return pltpu.make_async_remote_copy(
            src_ref=source,
            dst_ref=target,
            send_sem=self.send_sems.at[send],
            recv_sem=self.recv_sems.at[receive + slot],
            device_id=device,
            device_id_type=MESH,
        )

    def send(self, key, source, target, device, when=None, recv=None):
        copy = self.copy(key, source, target, device, recv=recv)
        if when is None:
            copy.start()
        else:
            pl.when(when)(copy.start)
        self.sent.append((copy, when))

    def send_to_slot(self, key, source, target, device, slot, span, when):
        copy = self.copy(key, source, target, device, slot, span)
        pl.when(when)(copy.start)
        self.sent.append((copy, when))

    def send_between(self, key, receive, slot, source, target, device, when):
        copy = self.copy(key, source, target, device, slot, recv=receive)
        pl.when(when)(copy.start)
        self.sent.append((copy, when))

    def arrive(self, key, target, device, when=None):
        copy = self.copy(key, target, target, device)
        if when is None:
            copy.wait_recv()
        else:
            pl.when(when)(copy.wait_recv)

    def arrive_slot(self, key, target, device, slot, span, when):
        pl.when(when)(self.copy(key, target, target, device, slot, span).wait_recv)

    def drain(self):
        for copy, when in self.sent:
            if when is None:
                copy.wait_send()
            else:
                pl.when(when)(copy.wait_send)


def flip(value, bit):
    return 1 - value if bit else value


def enter(devices):
    barrier = pltpu.get_barrier_semaphore()
    for device in devices:
        pl.semaphore_signal(barrier, inc=1, device_id=device, device_id_type=MESH)
    pl.semaphore_wait(barrier, len(devices))


class Place:
    def __init__(self):
        self.zo, self.zi, self.x, self.y, self.c = (lax.axis_index(name) for name in ALL)
        self.rank = self.x * 4 + self.y * 2 + self.c
        self.unit = self.zi * 2 + self.c

    def head_home(self):
        return self.y + self.c * (3 - 2 * self.y)

    def holder(self):
        y, c = lax.rem((self.zi + 1) // 2, 2), self.zi // 2
        return (self.zo, self.zi, self.x, y, c), self.x * 4 + y * 2 + c

    def plane(self, delta):
        dx, dy, dc = delta >> 2 & 1, delta >> 1 & 1, delta & 1
        x, y, c = flip(self.x, dx), flip(self.y, dy), flip(self.c, dc)
        return (self.zo, self.zi, x, y, c), x * 4 + y * 2 + c

    def column(self, step):
        other = lax.rem(self.unit + step + 8, 8)
        return (self.zo, other // 2, self.x, self.y, lax.rem(other, 2)), other

    def ends(self):
        return self.line(jnp.minimum(self.zi + 1, 3)), self.line(jnp.maximum(self.zi - 1, 0))

    def line(self, z):
        return (self.zo, z, self.x, self.y, self.c)

    def column_neighbours(self):
        return [self.line(z) for z in self.others()] + [self.plane(1)[0]]

    def others(self):
        return [lax.rem(self.zi + step, 4) for step in (1, 2, 3)]

    def neighbours(self):
        plane = [self.plane(delta)[0] for delta in range(1, 8)]
        column = []
        for dz in range(1, 4):
            z = lax.rem(self.zi + dz, 4)
            column += [(self.zo, z, self.x, self.y, core) for core in (0, 1)]
        return plane + column


def unit_gather_flow(at, wire, ffn_in, ffn_out, own_sem):
    x_side, y_side = at.plane(4)[0], at.plane(2)[0]
    steps = (1, 7, 2, 6, 3, 5, 4)
    mine = ffn_out.at[:, at.zi, at.x, at.y, at.c]
    own = pltpu.make_async_copy(ffn_in.at[at.unit], mine, own_sem)
    own.start()
    for step in steps:
        device, other = at.column(step)
        wire.send(("f", step), ffn_in.at[other], mine, device)
    own.wait()

    def slot(step, x, y):
        source = lax.rem(at.unit - step + 8, 8)
        return ffn_out.at[:, source // 2, x, y, lax.rem(source, 2)]

    def first(step):
        here = slot(step, at.x, at.y)
        if step:
            wire.arrive(("f", step), here, at.column(-step)[0])
        wire.send(("fx", step), here, here, x_side)
        wire.send(("fy", step), here, here, y_side)

    def second(step, turn):
        from_x, from_y = slot(step, 1 - at.x, at.y), slot(step, at.x, 1 - at.y)
        wire.arrive(("fx", step), from_x, x_side)
        wire.arrive(("fy", step), from_y, y_side)
        if turn % 2:
            wire.send(("fd", step), from_x, from_x, y_side)
        else:
            wire.send(("fd", step), from_y, from_y, x_side)

    yield
    first(0)
    for turn, step in enumerate(steps):
        yield
        first(step)
        if turn >= 1:
            second(((0,) + steps)[turn - 1], turn - 1)
    yield
    second(steps[5], 6)
    second(steps[6], 7)
    yield
    for step in (0,) + steps:
        wire.arrive(("fd", step), slot(step, 1 - at.x, 1 - at.y), x_side)


def open_heads_kernel(
    qkv_in,
    ffn_in,
    proj_in,
    x_in,
    small_in,
    qkv_out,
    ffn_out,
    proj_out,
    x_out,
    small_out,
    send_sems,
    recv_sems,
    own_sems,
):
    at = Place()
    wire = Wire(send_sems, recv_sems)
    enter(at.neighbours())
    up, down = at.ends()
    chunk = at.y * 2 + at.c
    holder_device, holder = at.holder()
    proj_home = at.head_home()
    own = [
        pltpu.make_async_copy(qkv_in.at[at.rank], qkv_out.at[at.zi, at.rank], own_sems.at[1]),
        pltpu.make_async_copy(small_in, small_out.at[at.zi, at.rank], own_sems.at[3]),
    ]
    for copy in own:
        copy.start()
    for delta in range(1, 8):
        device, other = at.plane(delta)
        wire.send(("q", delta), qkv_in.at[other], qkv_out.at[at.zi, at.rank], device)
    wire.send_to_slot("p", proj_in, proj_out.at[chunk], holder_device, chunk, 4, at.rank != holder)
    proj_own = pltpu.make_async_copy(proj_in, proj_out.at[chunk], own_sems.at[4])
    pl.when(at.rank == holder)(proj_own.start)
    for delta in range(1, 8):
        device, _ = at.plane(delta)
        wire.send(("s", delta), small_in, small_out.at[at.zi, at.rank], device)
    spread = plane_gather_flow(at, wire, x_in, x_out, own_sems.at[0])
    next(spread)
    for copy in own:
        copy.wait()
    pl.when(at.rank == holder)(proj_own.wait)

    def small_second():
        for delta in range(1, 8):
            device, other = at.plane(delta)
            wire.arrive(("s", delta), small_out.at[at.zi, other], device)
        for dz in range(1, 4):
            device = at.line(lax.rem(at.zi + dz, 4))
            wire.send(("t", dz), small_out.at[at.zi], small_out.at[at.zi], device)

    def small_last():
        for dz in range(1, 4):
            z = lax.rem(at.zi - dz + 4, 4)
            wire.arrive(("t", dz), small_out.at[z], at.line(z))

    def proj_start(slot):
        block = proj_out.at[slot]
        source = (at.zo, at.zi, at.x, slot // 2, slot % 2)
        home = at.zi == proj_home
        mine = home & ((chunk != slot) | (at.rank != holder))
        wire.arrive_slot("p", block, source, slot, 4, mine)
        wire.send(("pu", slot), block, block, up, home & (at.zi < 3))
        wire.send(("pd", slot), block, block, down, home & (at.zi > 0))

    def proj_relay(slot):
        block = proj_out.at[slot]
        above, below = at.zi > proj_home, at.zi < proj_home
        wire.arrive(("pu", slot), block, down, above)
        wire.arrive(("pd", slot), block, up, below)
        key = "pu", slot
        wire.send(("pu2", slot), block, block, up, above & (at.zi < 3), recv=key)
        key = "pd", slot
        wire.send(("pd2", slot), block, block, down, below & (at.zi > 0), recv=key)

    def qkv_slot(z, delta):
        return qkv_out.at[jnp.clip(z, 0, 3), at.plane(delta)[1]]

    def qkv_hop(hop, delta):
        below, above = qkv_slot(at.zi - hop, delta), qkv_slot(at.zi + hop, delta)
        if hop == 0:
            if delta:
                wire.arrive(("q", delta), below, at.plane(delta)[0])
        else:
            wire.arrive(("up", hop - 1, delta), below, down, at.zi >= hop)
            wire.arrive(("down", hop - 1, delta), above, up, at.zi <= 3 - hop)
        if hop < 3:
            wire.send(("up", hop, delta), below, below, up, (at.zi >= hop) & (at.zi < 3))
            wire.send(("down", hop, delta), above, above, down, (at.zi <= 3 - hop) & (at.zi > 0))

    for delta in range(8):
        qkv_hop(0, delta)
    units = unit_gather_flow(at, wire, ffn_in, ffn_out, own_sems.at[2])
    for slot in range(4):
        proj_start(slot)
    next(units)
    next(spread)
    small_second()
    next(units)
    for _ in spread:
        pass
    for delta in range(8):
        qkv_hop(1, delta)
        if delta % 2:
            proj_relay(delta // 2)
            next(units)
    for delta in range(8):
        qkv_hop(2, delta)
        if delta % 2:
            next(units)
    for delta in range(8):
        qkv_hop(3, delta)
    for _ in units:
        pass
    small_last()
    wire.drain()


def turned(values, cosine, sine):
    return values * cosine + pltpu.roll(values, HEAD_DIM // 2, 1) * sine


def row_place(rank, micro):
    piece = rank % 4
    return (rank // 4) * 2 + micro, piece


def open_units_kernel(
    x_all,
    qkv,
    proj,
    cosine,
    sine,
    start_query,
    start_key,
    end_key,
    x_own,
    gain,
    shift,
    ffn_in,
    queries,
    key_rows,
    value_rows,
    probs_out,
    context,
    normed,
    hat,
    inverse_out,
    normed_all,
    ffn_out,
    part,
    branch,
    *rest,
):
    at = Place()
    *scratch, send_sems, recv_sems, own_sems = rest
    wire = Wire(send_sems, recv_sems)
    enter(at.neighbours())
    own = x_own.shape[0]
    pos = own // 2
    length = 4 * pos
    heads = context.shape[-1] // HEAD_DIM
    wide = heads * HEAD_DIM

    def project():
        @pl.loop(0, 8)
        def _(rank):
            mixed = dot(x_all[rank], qkv[...])
            for micro in range(2):
                row, piece = row_place(rank, micro)
                place = pl.ds(pl.multiple_of(piece * pos, pos), pos)
                near = mixed[micro * pos : (micro + 1) * pos]
                cos, sin = cosine[row, place], sine[row, place]
                for head in range(heads):
                    cols = pl.ds(head * HEAD_DIM, HEAD_DIM)
                    for kind, target in enumerate((queries, key_rows, value_rows)):
                        first = kind * wide + head * HEAD_DIM
                        values = near[:, first : first + HEAD_DIM]
                        if kind < 2:
                            values = turned(values, cos, sin)
                        target[row, place, cols] = values.astype(jnp.bfloat16)

    def attend():
        scale = 1.0 / math.sqrt(HEAD_DIM)
        here = lax.broadcasted_iota(jnp.int32, (length, length), 0)
        there = lax.broadcasted_iota(jnp.int32, (length, length), 1)

        @pl.loop(0, 4)
        def _(row):
            bound = end_key[row].astype(jnp.int32)
            seen = (start_query[row] == start_key[row]) & ((there <= here) | (there < bound))
            for head in range(heads):
                cols = pl.ds(head * HEAD_DIM, HEAD_DIM)
                scores = contract_last(queries[row, :, cols], key_rows[row, :, cols]) * scale
                scores = jnp.where(seen, scores, masked_score)
                scores = jnp.exp(scores - jnp.max(scores, axis=-1, keepdims=True))
                probs = scores / jnp.sum(scores, axis=-1, keepdims=True)
                probs_out[row, head] = probs
                result = dot(probs.astype(jnp.bfloat16), value_rows[row, :, cols])
                result = result.astype(jnp.bfloat16)
                for piece in range(4):
                    target = pl.ds(pl.multiple_of((row % 2) * pos, pos), pos)
                    source = result[piece * pos : (piece + 1) * pos]
                    context[(row // 2) * 4 + piece, target, cols] = source

    def branch_parts():
        @pl.loop(0, 8)
        def _(rank):
            part[rank] = dot(context[rank], proj[...]).astype(jnp.bfloat16)

    pieces = 4
    height = own // pieces

    def norm_rows(start):
        count = 16

        @pl.loop(0, height // count)
        def _(index):
            rows = pl.ds(pl.multiple_of(start + index * count, count), count)
            whole = deep_alpha * x_own[rows].astype(jnp.float32) + branch[rows]
            near, inverse = norm_parts(whole)
            hat[rows] = near
            inverse_out[rows] = jnp.broadcast_to(inverse, (count, LANES))
            normed[rows] = (near * gain[...] + shift[...]).astype(jnp.bfloat16)

    core_in, core_sum, side_in, side_sum, last_in = scratch
    scatters, gathers = [], []
    for index in range(pieces):
        rows = pl.ds(index * height, height)
        views = [core_in.at[:, rows], core_sum.at[:, rows], side_in.at[:, :, rows]]
        views += [side_sum.at[:, rows], last_in.at[:, rows]]
        scatters.append(
            plane_scatter_flow(at, wire, index, part.at[:, rows], branch.at[rows], *views)
        )
        sem = own_sems.at[1 + index]
        gathers.append(
            column_gather_flow(at, wire, index, normed.at[rows], normed_all.at[:, rows], sem)
        )
    units = unit_gather_flow(at, wire, ffn_in, ffn_out, own_sems.at[0])
    next(units)
    next(units)
    project()
    next(units)
    attend()
    next(units)
    branch_parts()
    for stage in range(3):
        for flow in scatters:
            next(flow)
    for index in range(pieces + 3):
        if index < pieces:
            for _ in scatters[index]:
                pass
            norm_rows(index * height)
            next(gathers[index])
        for lag in (1, 2, 3):
            if 0 <= index - lag < pieces:
                next(gathers[index - lag], None)
        next(units, None)
    for flow in gathers + [units]:
        for _ in flow:
            pass
    wire.drain()


ANY = pl.BlockSpec(memory_space=pl.ANY)
VMEM = pl.BlockSpec(memory_space=pltpu.VMEM)


def comm_params(number):
    return pltpu.CompilerParams(
        collective_id=number, has_side_effects=True, vmem_limit_bytes=63 * 2**20
    )


def open_heads(qkv_parts, ffn_parts, proj_own, x_own, small):
    _, rows_own, qkv_width = qkv_parts.shape
    _, matrices, _, unit_width = ffn_parts.shape
    own, width = x_own.shape
    low_type = jnp.bfloat16
    return pl.pallas_call(
        open_heads_kernel,
        out_shape=(
            jax.ShapeDtypeStruct((4, 8, rows_own, qkv_width), low_type),
            jax.ShapeDtypeStruct((matrices, 4, 2, 2, 2, rows_own, unit_width), low_type),
            jax.ShapeDtypeStruct((4, rows_own, width), low_type),
            jax.ShapeDtypeStruct((8, own, width), low_type),
            jax.ShapeDtypeStruct((4, 8) + small.shape, small.dtype),
        ),
        in_specs=[VMEM] * 5,
        out_specs=(ANY,) * 5,
        scratch_shapes=[
            pltpu.SemaphoreType.DMA((136,)),
            pltpu.SemaphoreType.DMA((136,)),
            pltpu.SemaphoreType.DMA((5,)),
        ],
        compiler_params=comm_params(1),
        name="open_heads",
    )(qkv_parts, ffn_parts, proj_own, x_own, small)


def open_units(x_all, qkv, proj, tables, x_own, gain, shift, ffn_parts):
    _, matrices, rows_own, unit_width = ffn_parts.shape
    own, width = x_own.shape
    head_width = proj.shape[0]
    length = 2 * own
    low_type = jnp.bfloat16
    rows = jax.ShapeDtypeStruct((4, length, head_width), low_type)
    return pl.pallas_call(
        open_units_kernel,
        out_shape=(
            rows,
            rows,
            rows,
            jax.ShapeDtypeStruct((4, head_width // HEAD_DIM, length, length), jnp.float32),
            jax.ShapeDtypeStruct((8, own, head_width), low_type),
            jax.ShapeDtypeStruct((own, width), low_type),
            jax.ShapeDtypeStruct((own, width), jnp.float32),
            jax.ShapeDtypeStruct((own, LANES), jnp.float32),
            jax.ShapeDtypeStruct((8, own, width), low_type),
            jax.ShapeDtypeStruct((matrices, 4, 2, 2, 2, rows_own, unit_width), low_type),
        ),
        in_specs=[VMEM] * 12,
        out_specs=(VMEM,) * 8 + (ANY, ANY),
        scratch_shapes=[
            pltpu.VMEM((8, own, width), low_type),
            pltpu.VMEM((own, width), jnp.float32),
        ]
        + plane_scratch(own, width)
        + [
            pltpu.SemaphoreType.DMA((136,)),
            pltpu.SemaphoreType.DMA((136,)),
            pltpu.SemaphoreType.DMA((5,)),
        ],
        compiler_params=comm_params(4),
        name="open_units",
    )(x_all, qkv, proj, *tables, x_own, gain, shift, ffn_parts)


def add_rows(out, *terms):
    step = 32

    @pl.loop(0, out.shape[0] // step)
    def _(index):
        part = pl.ds(pl.multiple_of(index * step, step), step)
        whole = terms[0][part].astype(jnp.float32)
        for term in terms[1:]:
            whole = whole + term[part].astype(jnp.float32)
        out[part] = whole.astype(out.dtype)


def column_scatter_flow(
    at, wire, tag, part, out, core_in, core_sum, up_in, down_in, up_sum, down_sum
):
    core_side = at.plane(1)[0]
    up, down = at.ends()
    for goal in (3, 0, 2, 1):
        source = part.at[goal * 2 + 1 - at.c]
        wire.send(("rc", tag, goal), source, core_in.at[goal], core_side)
    yield
    for goal in (3, 0, 2, 1):
        wire.arrive(("rc", tag, goal), core_in.at[goal], core_side)
        add_rows(core_sum.at[goal], part.at[goal * 2 + at.c], core_in.at[goal])
        for rising in {3: (3,), 2: (2,), 1: (1,)}.get(goal, ()):
            key = "ru", tag, rising
            wire.send(key, core_sum.at[rising], up_in.at[rising], up, at.zi == 0)
        for falling in {0: (0,), 1: (1, 2)}.get(goal, ()):
            key = "rd", tag, falling
            wire.send(key, core_sum.at[falling], down_in.at[falling], down, at.zi == 3)

    def climb(goal):
        wire.arrive(("ru", tag, goal), up_in.at[goal], down)
        add_rows(up_sum.at[goal], core_sum.at[goal], up_in.at[goal])

    def descend(goal):
        wire.arrive(("rd", tag, goal), down_in.at[goal], up)
        add_rows(down_sum.at[goal], core_sum.at[goal], down_in.at[goal])

    def rise(goal, z):
        pl.when(at.zi == z)(lambda: climb(goal))
        key = "ru", tag, goal
        target = up_in.at[goal]
        wire.send(("ru2", tag, goal), up_sum.at[goal], target, up, at.zi == z, recv=key)

    def fall(goal, z):
        pl.when(at.zi == z)(lambda: descend(goal))
        key = "rd", tag, goal
        target = down_in.at[goal]
        wire.send(("rd2", tag, goal), down_sum.at[goal], target, down, at.zi == z, recv=key)

    yield
    rise(3, 1)
    fall(0, 2)
    yield
    rise(3, 2)
    fall(0, 1)
    rise(2, 1)
    fall(1, 2)
    yield
    add_rows(out, core_sum.at[at.zi])

    def last(key, source, device):
        wire.arrive(key, source, device)
        add_rows(out, out, source)

    for goal in range(4):
        if goal > 0:
            pl.when(at.zi == goal)(lambda: last(("ru", tag, goal), up_in.at[goal], down))
        if goal < 3:
            pl.when(at.zi == goal)(lambda: last(("rd", tag, goal), down_in.at[goal], up))


def column_gather_flow(at, wire, tag, own_in, out, own_sem):
    core_side = at.plane(1)[0]
    up, down = at.ends()

    def slot(z, c):
        return out.at[jnp.clip(z, 0, 3) * 2 + c]

    mine = slot(at.zi, at.c)
    wire.send(("gu", tag, 0), own_in, mine, up, at.zi < 3)
    wire.send(("gd", tag, 0), own_in, mine, down, at.zi > 0)
    wire.send(("gc", tag), own_in, mine, core_side)
    own = pltpu.make_async_copy(own_in, mine, own_sem)
    own.start()
    for hop in (1, 2, 3):
        yield
        below, above = slot(at.zi - hop, at.c), slot(at.zi + hop, at.c)
        has_below, has_above = at.zi >= hop, at.zi <= 3 - hop
        wire.arrive(("gu", tag, hop - 1), below, down, has_below)
        if hop < 3:
            wire.send(("gu", tag, hop), below, below, up, has_below & (at.zi < 3))
        wire.send(("gcu", tag, hop), below, below, core_side, has_below)
        wire.arrive(("gd", tag, hop - 1), above, up, has_above)
        if hop < 3:
            wire.send(("gd", tag, hop), above, above, down, has_above & (at.zi > 0))
        wire.send(("gcd", tag, hop), above, above, core_side, has_above)
    yield
    own.wait()
    wire.arrive(("gc", tag), slot(at.zi, 1 - at.c), core_side)
    for hop in (1, 2, 3):
        below, above = slot(at.zi - hop, 1 - at.c), slot(at.zi + hop, 1 - at.c)
        wire.arrive(("gcu", tag, hop), below, core_side, at.zi >= hop)
        wire.arrive(("gcd", tag, hop), above, core_side, at.zi <= 3 - hop)


def column_scratch(own, width):
    return [pltpu.VMEM((4, own, width), jnp.bfloat16)] * 6


def plane_scatter_flow(
    at, wire, tag, part, out, core_in, core_sum, side_in, side_sum, last_in
):
    x_side, y_side, core_side = at.plane(4)[0], at.plane(2)[0], at.plane(1)[0]
    half = out.shape[1] // 2
    halves = (pl.ds(0, half), pl.ds(half, half))
    order = ((1, 1), (1, 0), (0, 1), (0, 0))

    def place(dx, dy):
        return flip(at.x, dx), flip(at.y, dy)

    for dx, dy in order:
        x, y = place(dx, dy)
        other = x * 4 + y * 2 + 1 - at.c
        wire.send(("c", tag, dx, dy), part.at[other], core_in.at[dx * 2 + dy], core_side)
    yield
    for dx, dy in order:
        x, y = place(dx, dy)
        mine = x * 4 + y * 2 + at.c
        slot = dx * 2 + dy
        wire.arrive(("c", tag, dx, dy), core_in.at[slot], core_side)
        add_rows(core_sum.at[slot], part.at[mine], core_in.at[slot])
        if dx:
            source = core_sum.at[slot, :, halves[0]]
            wire.send(("sa", tag, dy), source, side_in.at[0, dy], x_side)
        if dy:
            source = core_sum.at[slot, :, halves[1]]
            wire.send(("sb", tag, dx), source, side_in.at[1, dx], y_side)
    yield
    wire.arrive(("sa", tag, 1), side_in.at[0, 1], x_side)
    add_rows(side_sum.at[0], core_sum.at[1, :, halves[0]], side_in.at[0, 1])
    wire.send(("sy", tag), side_sum.at[0], last_in.at[0], y_side)
    wire.arrive(("sb", tag, 1), side_in.at[1, 1], y_side)
    add_rows(side_sum.at[1], core_sum.at[2, :, halves[1]], side_in.at[1, 1])
    wire.send(("sx", tag), side_sum.at[1], last_in.at[1], x_side)
    yield
    wire.arrive(("sa", tag, 0), side_in.at[0, 0], x_side)
    wire.arrive(("sb", tag, 0), side_in.at[1, 0], y_side)
    wire.arrive(("sy", tag), last_in.at[0], y_side)
    terms = core_sum.at[0, :, halves[0]], side_in.at[0, 0], last_in.at[0]
    add_rows(out.at[:, halves[0]], *terms)
    wire.arrive(("sx", tag), last_in.at[1], x_side)
    terms = core_sum.at[0, :, halves[1]], side_in.at[1, 0], last_in.at[1]
    add_rows(out.at[:, halves[1]], *terms)


def plane_scratch(own, width):
    return [
        pltpu.VMEM((4, own, width), jnp.bfloat16),
        pltpu.VMEM((4, own, width), jnp.bfloat16),
        pltpu.VMEM((2, 2, own, width // 2), jnp.bfloat16),
        pltpu.VMEM((2, own, width // 2), jnp.bfloat16),
        pltpu.VMEM((2, own, width // 2), jnp.bfloat16),
    ]


def plane_gather_flow(at, wire, own_in, out, own_sem):
    x_side, y_side, core_side = at.plane(4)[0], at.plane(2)[0], at.plane(1)[0]
    half = own_in.shape[0] // 2
    mine = out.at[at.rank]
    wire.send("gx", own_in, mine, x_side)
    wire.send("gy", own_in, mine, y_side)
    wire.send("gc0", own_in, mine, core_side)
    own = pltpu.make_async_copy(own_in, mine, own_sem)
    own.start()
    yield
    from_x, from_y, from_xy = (at.plane(delta)[1] for delta in (4, 2, 6))
    low_half, high_half = pl.ds(0, half), pl.ds(half, half)
    wire.arrive("gx", out.at[from_x], x_side)
    wire.send("gd0", out.at[from_x, low_half], out.at[from_x, low_half], y_side)
    wire.send("gc1", out.at[from_x], out.at[from_x], core_side)
    wire.arrive("gy", out.at[from_y], y_side)
    wire.send("gd1", out.at[from_y, high_half], out.at[from_y, high_half], x_side)
    wire.send("gc2", out.at[from_y], out.at[from_y], core_side)
    yield
    wire.arrive("gd0", out.at[from_xy, low_half], y_side)
    wire.arrive("gd1", out.at[from_xy, high_half], x_side)
    wire.send("gc3", out.at[from_xy], out.at[from_xy], core_side)
    own.wait()
    for index, delta in enumerate((1, 5, 3, 7)):
        wire.arrive("gc%d" % index, out.at[at.plane(delta)[1]], core_side)


def turn_kernel(
    part,
    normed,
    out_grad,
    gain,
    shift,
    layer_out,
    d_second,
    down_out,
    norm_out,
    second,
    down_low,
    core_in,
    core_sum,
    up_in,
    down_in,
    up_sum,
    down_sum,
    send_sems,
    recv_sems,
    own_sems,
):
    at = Place()
    wire = Wire(send_sems, recv_sems)
    enter(at.column_neighbours())
    pieces = 2
    height = normed.shape[0] // pieces
    scratch = core_in, core_sum, up_in, down_in, up_sum, down_sum

    def norm_rows(start):
        count = 16

        @pl.loop(0, height // count)
        def _(index):
            rows = pl.ds(pl.multiple_of(start + index * count, count), count)
            whole = deep_alpha * normed[rows].astype(jnp.float32) + second[rows]
            near, inverse = norm_parts(whole)
            layer_out[rows] = (near * gain[...] + shift[...]).astype(jnp.bfloat16)
            cotangent = out_grad[rows].astype(jnp.float32)
            result = norm_back(cotangent, near, inverse, gain[...])
            d_second[rows] = result
            down_low[rows] = result.astype(jnp.bfloat16)
            along = cotangent * near
            norm_out[0] += along[:8] + along[8:]
            norm_out[1] += cotangent[:8] + cotangent[8:]

    scatters, gathers = [], []
    for index in range(pieces):
        rows = pl.ds(index * height, height)
        views = [ref.at[:, rows] for ref in scratch]
        scatters.append(
            column_scatter_flow(at, wire, index, part.at[:, rows], second.at[rows], *views)
        )
        gathers.append(
            column_gather_flow(
                at, wire, index, down_low.at[rows], down_out.at[:, rows], own_sems.at[index]
            )
        )
    norm_out[...] = jnp.zeros_like(norm_out)
    for flow in scatters:
        next(flow)
    for flow in scatters:
        next(flow)
    for index in range(pieces + 3):
        if index < pieces:
            for _ in scatters[index]:
                pass
            norm_rows(index * height)
            next(gathers[index])
        for lag in (1, 2, 3):
            if 0 <= index - lag < pieces:
                next(gathers[index - lag], None)
    for flow in gathers:
        for _ in flow:
            pass
    wire.drain()


def turn(part, normed, out_grad, gain, shift):
    _, own, width = part.shape
    low_type = jnp.bfloat16
    return pl.pallas_call(
        turn_kernel,
        out_shape=(
            jax.ShapeDtypeStruct((own, width), low_type),
            jax.ShapeDtypeStruct((own, width), jnp.float32),
            jax.ShapeDtypeStruct((8, own, width), low_type),
            jax.ShapeDtypeStruct((2, 8, width), jnp.float32),
        ),
        in_specs=[VMEM] * 5,
        out_specs=(VMEM, VMEM, ANY, VMEM),
        scratch_shapes=[
            pltpu.VMEM((own, width), jnp.float32),
            pltpu.VMEM((own, width), low_type),
        ]
        + column_scratch(own, width)
        + [
            pltpu.SemaphoreType.DMA((112,)),
            pltpu.SemaphoreType.DMA((112,)),
            pltpu.SemaphoreType.DMA((4,)),
        ],
        compiler_params=comm_params(5),
        name="turn",
    )(part, normed, out_grad, gain, shift)


def close_units_kernel(
    gate_in,
    raise_in,
    lower_in,
    part,
    d_second,
    hat,
    inverse,
    gain,
    proj,
    queries,
    key_rows,
    value_rows,
    probs_in,
    cosine,
    sine,
    ffn_out,
    branch_out,
    d_mixed,
    d_first,
    norm_out,
    d_context,
    first_in,
    second_sum,
    second_in,
    total,
    d_normed,
    branch_low,
    core_in,
    core_sum,
    up_in,
    down_in,
    up_sum,
    down_sum,
    send_sems,
    recv_sems,
    own_sems,
):
    at = Place()
    wire = Wire(send_sems, recv_sems)
    enter(at.neighbours())
    x_side, y_side = at.plane(4)[0], at.plane(2)[0]
    steps = (4, 3, 5, 2, 6, 1, 7, 0)
    sources = gate_in, raise_in, lower_in

    def owner(step):
        other = at.column(step)[1]
        return other // 2, lax.rem(other, 2)

    def ffn_first(turn):
        step = steps[turn]
        z, c = owner(step)
        for index, source in enumerate(sources):
            if turn % 2:
                block, device = source.at[z, 1 - at.x, :, c], x_side
            else:
                block, device = source.at[z, :, 1 - at.y, c], y_side
            wire.send(("a", step, index), block, first_in.at[step, index], device)

    def ffn_second(turn):
        step = steps[turn]
        z, c = owner(step)
        for index, source in enumerate(sources):
            if turn % 2:
                wire.arrive(("a", step, index), first_in.at[step, index], x_side)
                terms = source.at[z, at.x, 1 - at.y, c], first_in.at[step, index, 1 - at.y]
            else:
                wire.arrive(("a", step, index), first_in.at[step, index], y_side)
                terms = source.at[z, 1 - at.x, at.y, c], first_in.at[step, index, 1 - at.x]
            add_rows(second_sum.at[step, index], *terms)
        wire.send(
            ("b", step), second_sum.at[step], second_in.at[step], y_side if turn % 2 else x_side
        )

    own_total = pltpu.make_async_copy(total.at[0], ffn_out.at[at.unit], own_sems.at[0])

    def ffn_last(turn):
        step = steps[turn]
        z, c = owner(step)
        near = at.y if turn % 2 else at.x
        wire.arrive(("b", step), second_in.at[step], x_side)
        for index, source in enumerate(sources):
            add_rows(
                total.at[step, index],
                source.at[z, at.x, at.y, c],
                first_in.at[step, index, near],
                second_in.at[step, index],
            )
        if step:
            wire.send(("f", step), total.at[step], ffn_out.at[at.unit], at.column(step)[0])
        else:
            own_total.start()

    def norm_rows():
        count = 16
        norm_out[...] = jnp.zeros_like(norm_out)

        @pl.loop(0, hat.shape[0] // count)
        def _(index):
            rows = pl.ds(pl.multiple_of(index * count, count), count)
            cotangent = deep_alpha * d_second[rows] + d_normed[rows]
            near = hat[rows]
            result = norm_back(cotangent, near, inverse[rows, :1], gain[...])
            d_first[rows] = result
            branch_low[rows] = result.astype(jnp.bfloat16)
            along = cotangent * near
            norm_out[0] += along[:8] + along[8:]
            norm_out[1] += cotangent[:8] + cotangent[8:]

    pos = hat.shape[0] // 2
    wide = proj.shape[0]
    heads = wide // HEAD_DIM
    scale = 1.0 / math.sqrt(HEAD_DIM)

    def pull():
        @pl.loop(0, 8)
        def _(rank):
            result = contract_last(branch_out[rank], proj[...]).astype(jnp.bfloat16)
            for micro in range(2):
                row, piece = row_place(rank, micro)
                place = pl.ds(pl.multiple_of(piece * pos, pos), pos)
                d_context[row, place] = result[micro * pos : (micro + 1) * pos]

    def attend_back(first, last):
        @pl.loop(first, last)
        def _(row):
            cos, sin = cosine[row], -sine[row]
            target = pl.ds(pl.multiple_of((row % 2) * pos, pos), pos)
            for head in range(heads):
                cols = pl.ds(head * HEAD_DIM, HEAD_DIM)
                probs, above = probs_in[row, head], d_context[row, :, cols]
                d_probs = contract_last(above, value_rows[row, :, cols])
                along = jnp.sum(probs * d_probs, axis=-1, keepdims=True)
                d_scores = (probs * (d_probs - along)).astype(jnp.bfloat16)
                d_query = dot(d_scores, key_rows[row, :, cols]) * scale
                d_keys = contract_first(d_scores, queries[row, :, cols]) * scale
                d_values = contract_first(probs.astype(jnp.bfloat16), above)
                results = turned(d_query, cos, sin), turned(d_keys, cos, sin), d_values
                for kind, result in enumerate(results):
                    result = result.astype(jnp.bfloat16)
                    place = pl.ds(kind * wide + head * HEAD_DIM, HEAD_DIM)
                    for piece in range(4):
                        source = result[piece * pos : (piece + 1) * pos]
                        d_mixed[(row // 2) * 4 + piece, target, place] = source

    scatter = column_scatter_flow(
        at, wire, 0, part, d_normed, core_in, core_sum, up_in, down_in, up_sum, down_sum
    )
    next(scatter)
    for turn in range(5):
        ffn_first(turn)
    next(scatter)
    next(scatter)
    ffn_second(0)
    ffn_first(5)
    ffn_second(1)
    ffn_first(6)
    next(scatter)
    ffn_second(2)
    ffn_first(7)
    ffn_second(3)
    for _ in scatter:
        pass
    norm_rows()
    spread = plane_gather_flow(at, wire, branch_low, branch_out, own_sems.at[1])
    next(spread)
    ffn_last(0)
    ffn_last(1)
    ffn_second(4)
    ffn_last(2)
    ffn_second(5)
    ffn_last(3)
    next(spread)
    ffn_second(6)
    ffn_second(7)
    ffn_last(4)
    for _ in spread:
        pass
    ffn_last(5)
    pull()
    ffn_last(6)
    ffn_last(7)
    attend_back(0, 4)
    own_total.wait()
    for step in steps:
        if step:
            device, other = at.column(-step)
            wire.arrive(("f", step), ffn_out.at[other], device)
    wire.drain()


def close_units(grads, part, d_second, hat, inverse, gain, *heads):
    rows_own, unit_width = grads[0].shape[-2:]
    _, own, width = part.shape
    low_type = jnp.bfloat16
    head_width = heads[0].shape[0]
    block = (rows_own, unit_width)
    return pl.pallas_call(
        close_units_kernel,
        out_shape=(
            jax.ShapeDtypeStruct((8, 3) + block, low_type),
            jax.ShapeDtypeStruct((8, own, width), low_type),
            jax.ShapeDtypeStruct((8, own, 3 * head_width), low_type),
            jax.ShapeDtypeStruct((own, width), jnp.float32),
            jax.ShapeDtypeStruct((2, 8, width), jnp.float32),
        ),
        in_specs=[VMEM] * 15,
        out_specs=(ANY, VMEM, VMEM, VMEM, VMEM),
        scratch_shapes=[
            pltpu.VMEM((4, 2 * own, head_width), low_type),
            pltpu.VMEM((8, 3, 2) + block, low_type),
            pltpu.VMEM((8, 3) + block, low_type),
            pltpu.VMEM((8, 3) + block, low_type),
            pltpu.VMEM((8, 3) + block, low_type),
            pltpu.VMEM((own, width), jnp.float32),
            pltpu.VMEM((own, width), low_type),
        ]
        + column_scratch(own, width)
        + [
            pltpu.SemaphoreType.DMA((80,)),
            pltpu.SemaphoreType.DMA((80,)),
            pltpu.SemaphoreType.DMA((2,)),
        ],
        compiler_params=comm_params(3),
        name="close_units",
    )(*grads, part, d_second, hat, inverse, gain, *heads)


def close_heads_kernel(
    qkv_in,
    proj_in,
    small_in,
    part,
    qkv_out,
    proj_out,
    small_out,
    d_input,
    proj_below,
    proj_above,
    proj_sum,
    small_plane,
    small_mid,
    small_line,
    up_in,
    down_in,
    up_sum,
    down_sum,
    qkv_total,
    core_in,
    core_sum,
    side_in,
    side_sum,
    last_in,
    send_sems,
    recv_sems,
    own_sems,
):
    at = Place()
    wire = Wire(send_sems, recv_sems)
    enter(at.neighbours())
    scatter = plane_scatter_flow(
        at, wire, 0, part, d_input, core_in, core_sum, side_in, side_sum, last_in
    )
    next(scatter)

    for delta in range(1, 8):
        device, other = at.plane(delta)
        wire.send(("s", delta), small_in.at[other], small_plane.at[at.rank], device)

    def small_second():
        whole = small_in[at.rank]
        for delta in range(1, 8):
            device, other = at.plane(delta)
            wire.arrive(("s", delta), small_plane.at[other], device)
            whole = whole + small_plane[other]
        small_mid[...] = whole
        for dz in range(1, 4):
            z = lax.rem(at.zi + dz, 4)
            wire.send(("t", dz), small_mid.at[z], small_line.at[at.zi], at.line(z))

    def small_last():
        whole = small_mid[at.zi]
        for dz in range(1, 4):
            z = lax.rem(at.zi - dz + 4, 4)
            wire.arrive(("t", dz), small_line.at[z], at.line(z))
            whole = whole + small_line[z]
        small_out[...] = whole

    pieces = 4
    wide = 8 // pieces
    up, down = at.line(jnp.minimum(at.zi + 1, 3)), at.line(jnp.maximum(at.zi - 1, 0))

    def add_ranks(piece, out, *terms):
        for rank in range(piece * wide, piece * wide + wide):
            add_rows(out.at[rank], *(term.at[rank] for term in terms))

    def qkv_rise(goal, piece, low_z, high_z):
        part = pl.ds(piece * wide, wide)
        here = (at.zi >= low_z) & (at.zi <= high_z)
        source = up_sum.at[goal, part]

        def climb():
            wire.arrive(("u", goal, piece), up_in.at[goal, part], down)
            add_ranks(piece, up_sum.at[goal], qkv_in.at[goal], up_in.at[goal])

        key = "u", goal, piece
        if low_z == 0:
            first = qkv_in.at[goal, part]
            wire.send(("u0", goal, piece), first, up_in.at[goal, part], up, at.zi == 0, recv=key)
        if high_z > 0:
            here = here & (at.zi > 0)
            pl.when(here)(climb)
            wire.send(key, source, up_in.at[goal, part], up, here)

    def qkv_fall(goal, piece, low_z, high_z):
        part = pl.ds(piece * wide, wide)
        here = (at.zi >= low_z) & (at.zi <= high_z)
        source = down_sum.at[goal, part]

        def descend():
            wire.arrive(("d", goal, piece), down_in.at[goal, part], up)
            add_ranks(piece, down_sum.at[goal], qkv_in.at[goal], down_in.at[goal])

        key = "d", goal, piece
        if high_z == 3:
            first = qkv_in.at[goal, part]
            wire.send(
                ("d0", goal, piece), first, down_in.at[goal, part], down, at.zi == 3, recv=key
            )
        if low_z < 3:
            here = here & (at.zi < 3)
            pl.when(here)(descend)
            wire.send(key, source, down_in.at[goal, part], down, here)

    proj_home = at.head_home()

    def proj_add(slot, *terms):
        add_rows(proj_sum.at[slot], *(term.at[slot] for term in terms))

    below, above = at.zi < proj_home, at.zi > proj_home
    ends = (at.zi == 0) | (at.zi == 3)

    def proj_pass(slot):
        under, over = proj_below.at[slot], proj_above.at[slot]
        wire.send(("pu", slot), proj_in.at[slot], under, up, below & ends)
        wire.send(("pd", slot), proj_in.at[slot], over, down, above & ends)

        def climb():
            wire.arrive(("pu", slot), under, down)
            proj_add(slot, proj_in, proj_below)

        def descend():
            wire.arrive(("pd", slot), over, up)
            proj_add(slot, proj_in, proj_above)

        pl.when(below & (at.zi > 0))(climb)
        pl.when(above & (at.zi < 3))(descend)
        source = proj_sum.at[slot]
        key = "pu", slot
        wire.send(("pu2", slot), source, under, up, below & (at.zi > 0), recv=key)
        key = "pd", slot
        wire.send(("pd2", slot), source, over, down, above & (at.zi < 3), recv=key)

    chunk = at.y * 2 + at.c
    holder_device, holder = at.holder()

    def proj_last():
        home = at.zi == proj_home
        for slot in range(4):
            under, over = proj_below.at[slot], proj_above.at[slot]

            def first():
                wire.arrive(("pu", slot), under, down)
                proj_add(slot, proj_in, proj_below)

            def only():
                wire.arrive(("pd", slot), over, up)
                proj_add(slot, proj_in, proj_above)

            def both():
                wire.arrive(("pd", slot), over, up)
                proj_add(slot, proj_sum, proj_above)

            pl.when(home & (at.zi > 0))(first)
            pl.when(home & (at.zi == 0))(only)
            pl.when(home & (at.zi > 0) & (at.zi < 3))(both)
            target = (at.zo, at.zi, at.x, slot // 2, slot % 2)
            other = (chunk != slot) | (at.rank != holder)
            wire.send(("o", slot), proj_sum.at[slot], proj_out, target, home & other, recv="o")
        own = pltpu.make_async_copy(proj_sum.at[chunk], proj_out, own_sems.at[2])
        pl.when(home & (at.rank == holder))(own.start)
        pl.when(home & (at.rank == holder))(own.wait)

    def qkv_last(piece):
        part = pl.ds(piece * wide, wide)
        for goal in range(4):

            @pl.when(at.zi == goal)
            def _():
                terms = [qkv_in.at[goal]]
                if goal > 0:
                    wire.arrive(("u", goal, piece), up_in.at[goal, part], down)
                    terms.append(up_in.at[goal])
                if goal < 3:
                    wire.arrive(("d", goal, piece), down_in.at[goal, part], up)
                    terms.append(down_in.at[goal])
                add_ranks(piece, qkv_total, *terms)

    def qkv_owner(piece):
        for core in range(wide):
            rank = piece * wide + core
            target = (at.zo, at.zi, rank // 4, rank // 2 % 2, rank % 2)
            source, place = qkv_total.at[rank], qkv_out.at[at.rank]
            wire.number("qr", 8)
            wire.send_between(("q", rank), "qr", at.rank, source, place, target, at.rank != rank)
            own = pltpu.make_async_copy(source, place, own_sems.at[1])
            pl.when(at.rank == rank)(own.start)

    for piece in range(pieces):
        qkv_rise(3, piece, 0, 1)
        qkv_fall(0, piece, 2, 3)
        if piece == 0:
            next(scatter)
    for piece in range(pieces):
        qkv_rise(3, piece, 2, 2)
        qkv_fall(0, piece, 1, 1)
    for slot in range(4):
        proj_pass(slot)
    next(scatter)
    small_second()
    for piece in range(pieces):
        qkv_rise(2, piece, 0, 1)
        qkv_fall(1, piece, 2, 3)
    for _ in scatter:
        pass
    for piece in range(pieces):
        qkv_rise(1, piece, 0, 0)
        qkv_fall(2, piece, 3, 3)
    proj_last()
    for piece in range(pieces):
        qkv_last(piece)
        qkv_owner(piece)
    pltpu.make_async_copy(qkv_total.at[at.rank], qkv_out.at[at.rank], own_sems.at[1]).wait()
    for delta in range(1, 8):
        device, other = at.plane(delta)
        wire.arrive_slot("qr", qkv_out.at[other], device, other, 8, at.rank != other)
    small_last()
    wire.arrive("o", proj_out, holder_device, at.rank != holder)
    wire.drain()


def close_heads(qkv_part, proj_part, small_part, part):
    _, _, rows_own, qkv_width = qkv_part.shape
    _, own, width = part.shape
    low_type = jnp.bfloat16
    line = (4, 8, rows_own, qkv_width)
    small_shape = small_part.shape[1:]
    return pl.pallas_call(
        close_heads_kernel,
        out_shape=(
            jax.ShapeDtypeStruct((8, rows_own, qkv_width), low_type),
            jax.ShapeDtypeStruct((rows_own, width), low_type),
            jax.ShapeDtypeStruct(small_shape[1:], small_part.dtype),
            jax.ShapeDtypeStruct((own, width), jnp.float32),
        ),
        in_specs=[VMEM] * 4,
        out_specs=(ANY, ANY, VMEM, VMEM),
        scratch_shapes=[
            pltpu.VMEM((4, rows_own, width), low_type),
            pltpu.VMEM((4, rows_own, width), low_type),
            pltpu.VMEM((4, rows_own, width), low_type),
            pltpu.VMEM(small_part.shape, small_part.dtype),
            pltpu.VMEM(small_shape, small_part.dtype),
            pltpu.VMEM(small_shape, small_part.dtype),
            pltpu.VMEM(line, low_type),
            pltpu.VMEM(line, low_type),
            pltpu.VMEM(line, low_type),
            pltpu.VMEM(line, low_type),
            pltpu.VMEM(line[1:], low_type),
        ]
        + plane_scratch(own, width)
        + [
            pltpu.SemaphoreType.DMA((112,)),
            pltpu.SemaphoreType.DMA((112,)),
            pltpu.SemaphoreType.DMA((3,)),
        ],
        compiler_params=comm_params(2),
        name="close_heads",
    )(qkv_part, proj_part, small_part, part)


def group_body(
    hidden_in,
    token_marks,
    out_grad,
    qkv_weight,
    proj_weight,
    gate_weight,
    up_weight,
    down_weight,
    first_gain,
    first_shift,
    second_gain,
    second_shift,
):
    micro_count, _, pos_count, width = hidden_in.shape
    rows_own = qkv_weight.shape[0]
    units = gate_weight.shape[1]
    head_ways = math.prod(lax.axis_size(name) for name in HEAD_AXES)
    unit_ways = math.prod(lax.axis_size(name) for name in UNIT_AXES)
    chunk_count = lax.axis_size("y") * lax.axis_size("c")
    row_length = pos_count * chunk_count
    x_size = lax.axis_size("x")
    marks_own = token_marks.astype(jnp.float32)
    own = micro_count * pos_count
    head_width = width // head_ways
    heads_here = head_width // HEAD_DIM
    unit_width = -(-units // (unit_ways * LANES)) * LANES
    unit_pad = unit_width * unit_ways - units
    x_own = hidden_in.reshape(own, width)

    params = jnp.stack([first_gain, first_shift, second_gain, second_shift])
    small = jnp.concatenate([params.astype(jnp.float32).ravel(), marks_own.ravel()])
    small = jnp.pad(small, (0, -small.size % (8 * LANES))).reshape(-1, LANES)

    qkv_parts = qkv_weight.reshape(rows_own, 3, 4, 2, head_width)
    qkv_parts = jnp.stack([qkv_parts[:, :, home] for home in (0, 3, 1, 2)])
    qkv_parts = qkv_parts.transpose(3, 0, 1, 2, 4).reshape(head_ways, rows_own, 3 * head_width)

    def unit_parts(*matrices):
        parts = jnp.stack(matrices)
        parts = jnp.pad(parts, ((0, 0), (0, 0), (0, unit_pad)))
        parts = parts.reshape(len(matrices), rows_own, unit_ways, unit_width)
        return parts.transpose(2, 0, 1, 3)

    qkv_here, gate_here, proj_here, x_all, small = open_heads(
        qkv_parts, unit_parts(gate_weight), proj_weight, x_own, small
    )
    qkv_here = qkv_here.reshape(-1, 3 * head_width)
    gate_here = gate_here.reshape(-1, unit_width)
    x_all = x_all.reshape(-1, width)
    proj_here = proj_here.reshape(head_width, width)
    small = small.reshape(unit_ways * 4, -1)
    params = small[:, : 4 * rows_own].reshape(-1, 4, rows_own).transpose(1, 0, 2)
    gain_one, shift_one, gain_two, shift_two = params.reshape(4, 1, width)
    marks = small.reshape(4, head_ways, -1)[lax.axis_index("zi")]
    marks = marks[:, 4 * rows_own : 4 * rows_own + own * 3]

    def to_rows(values):
        inner = values.shape[1:]
        values = values.reshape((x_size, chunk_count, micro_count, pos_count) + inner)
        return jnp.swapaxes(values, 1, 2).reshape((x_size * micro_count, row_length) + inner)

    row_marks = to_rows(marks.reshape(head_ways * own, 3))
    cosine, sine = rotary_tables(row_marks[..., 2])
    tables = (
        jnp.concatenate([cosine, cosine], axis=-1),
        jnp.concatenate([-sine, sine], axis=-1),
        row_marks[:, :, :1],
        row_marks[:, None, :, 0],
        row_marks[:, None, :, 1],
    )
    queries, key_rows, value_rows, probs, context, normed, hat_one, inverse_one, normed_all, ffn = (
        open_units(
            x_all.reshape(head_ways, own, width),
            qkv_here,
            proj_here,
            tables,
            x_own,
            gain_one,
            shift_one,
            unit_parts(up_weight, down_weight),
        )
    )
    context = context.reshape(-1, head_width)
    normed_all = normed_all.reshape(-1, width)
    up_here, down_here = ffn.reshape(2, -1, unit_width)

    gate_val = dot(normed_all, gate_here)
    up_val = dot(normed_all, up_here)
    gelu_val, gelu_slope = gelu_parts(gate_val)
    active = low(gelu_val * up_val)
    down_part = low(contract_last(active, down_here)).reshape(unit_ways, own, width)
    layer_rows, d_second, down_low, norm_grads = turn(
        down_part, normed, out_grad.reshape(own, width), gain_two, shift_two
    )
    gain_two_grad, shift_two_grad = jnp.sum(norm_grads, axis=1)
    down_low = down_low.reshape(-1, width)
    d_active = dot(down_low, down_here)
    gate_low = low(d_active * up_val * gelu_slope)
    up_low = low(d_active * gelu_val)
    d_normed_part = low(contract_last(gate_low, gate_here) + contract_last(up_low, up_here))

    def unit_grad(left_side, right_side):
        part = low(contract_first(left_side, right_side))
        return part.reshape(4, 2, 2, 2, rows_own, unit_width)

    ffn_grads = (
        unit_grad(normed_all, gate_low),
        unit_grad(normed_all, up_low),
        unit_grad(down_low, active),
    )
    ffn_part, branch_all, d_mixed, d_first, norm_grads = close_units(
        ffn_grads,
        d_normed_part.reshape(unit_ways, own, width),
        d_second,
        hat_one,
        inverse_one,
        gain_one,
        proj_here,
        queries,
        key_rows,
        value_rows,
        probs,
        *tables[:2],
    )
    d_mixed = d_mixed.reshape(-1, 3 * head_width)
    gain_one_grad, shift_one_grad = jnp.sum(norm_grads, axis=1)
    branch_all = branch_all.reshape(-1, width)
    small_grads = jnp.stack([gain_one_grad, shift_one_grad, gain_two_grad, shift_two_grad])
    small_grads = small_grads.reshape(4, 4, head_ways, rows_own).transpose(2, 1, 0, 3)
    small_grads = small_grads.reshape(head_ways, 4, 4 * rows_own // LANES, LANES)
    small_grads = jnp.pad(small_grads, ((0, 0), (0, 0), (0, -small_grads.shape[2] % 8), (0, 0)))

    proj_part = low(contract_first(context, branch_all)).reshape(4, rows_own, width)
    d_input = low(contract_last(d_mixed, qkv_here)).reshape(head_ways, own, width)
    qkv_part = low(contract_first(x_all, d_mixed))
    qkv_part, proj_part, small_grads, d_input = close_heads(
        qkv_part.reshape(4, 8, rows_own, 3 * head_width), proj_part, small_grads, d_input
    )
    d_input = deep_alpha * d_first + d_input
    small_grads = small_grads.ravel()[: 4 * rows_own].reshape(4, rows_own)
    qkv_grad = qkv_part.reshape(2, 4, rows_own, 3, head_width)
    qkv_grad = jnp.stack([qkv_grad[:, place] for place in (0, 2, 3, 1)])
    qkv_grad = qkv_grad.transpose(2, 3, 0, 1, 4).reshape(rows_own, 3 * width).astype(jnp.float32)
    ffn_part = ffn_part.transpose(1, 2, 0, 3).reshape(3, rows_own, unit_ways * unit_width)
    gate_grad, up_grad, down_grad = (
        ffn_part[index, :, :units].astype(jnp.float32) for index in range(3)
    )
    return (
        layer_rows.reshape(micro_count, 1, pos_count, width),
        low(d_input).reshape(micro_count, 1, pos_count, width),
        qkv_grad,
        proj_part.astype(jnp.float32),
        gate_grad,
        up_grad,
        down_grad,
        small_grads[0],
        small_grads[1],
        small_grads[2],
        small_grads[3],
    )


def body(hidden_in, token_marks, out_grad, *weights):
    joined = lax.axis_size("zo")
    if joined == 1:
        return group_body(hidden_in, token_marks, out_grad, *weights)
    rows = weights[0].shape[0]
    width = hidden_in.shape[-1]
    groups = width // (joined * rows)
    group_place = lax.axis_index(ALL[1:])

    def inward(values):
        shape = values.shape
        values = values.reshape(shape[:-1] + (joined, groups, rows))
        return jnp.swapaxes(values, -3, -2).reshape(shape)

    def outward(values):
        shape = values.shape
        values = values.reshape(shape[:-1] + (groups, joined, rows))
        return jnp.swapaxes(values, -3, -2).reshape(shape)

    proj = gather(weights[1], ALL)
    proj = inward(lax.dynamic_slice_in_dim(proj, group_place * joined * rows, joined * rows))
    weights = [gather(weight, "zo") for weight in weights]
    weights[1] = proj
    outs = list(group_body(inward(hidden_in), token_marks, inward(out_grad), *weights))
    outs[:2] = outward(outs[0]), outward(outs[1])
    proj_grad = jnp.zeros((width, width), jnp.float32)
    proj_grad = lax.dynamic_update_slice_in_dim(
        proj_grad, outward(outs[3]), group_place * joined * rows, 0
    )
    outs[2:] = [scatter_sum(grad, "zo") for grad in outs[2:]]
    outs[3] = scatter_sum(proj_grad, ALL)
    return tuple(outs)


def solution(mesh):
    seq_size, ctx_size = mesh.shape["seq"], mesh.shape["ctx"]
    cores, x_size = 2, 2
    zi_size = math.gcd(4, seq_size // x_size)
    zo_size = seq_size // (x_size * zi_size)
    devices = np.asarray(mesh.devices).reshape(
        zo_size, zi_size, x_size, ctx_size // cores, cores
    )
    inner = Mesh(devices, ALL)
    tokens = P(None, ("zo", "zi", "x"), ("y", "c"), None)
    matrix = P(ALL, None)
    vector = P(ALL)
    return jax.shard_map(
        body,
        mesh=inner,
        in_specs=(tokens,) * 3 + (matrix,) * 5 + (vector,) * 4,
        out_specs=(tokens,) * 2 + (matrix,) * 5 + (vector,) * 4,
        check_vma=False,
    )
```

```python
import math

import jax
import jax.numpy as jnp
import numpy as np
from jax import lax
from jax.experimental import pallas as pl
from jax.experimental.pallas import tpu as pltpu
from jax.sharding import Mesh
from jax.sharding import PartitionSpec as P

HEAD_DIM = 128
LANES = 128

deep_alpha = 48.0**0.25
norm_eps = 1e-05
masked_score = -1e30

ALL = ("zo", "zi", "x", "y", "c")
HEAD_AXES = ("x", "y", "c")
UNIT_AXES = ("zi", "c")
HEAD_COPIES = ("zo", "zi")
UNIT_COPIES = ("zo", "x", "y")


def contract_last(left_side, right_side):
    return lax.dot_general(
        left_side, right_side, (((1,), (1,)), ((), ())), preferred_element_type=jnp.float32
    )


def contract_first(left_side, right_side):
    return lax.dot_general(
        left_side, right_side, (((0,), (0,)), ((), ())), preferred_element_type=jnp.float32
    )


def dot(left_side, right_side):
    return jnp.dot(left_side, right_side, preferred_element_type=jnp.float32)


def low(values):
    return values.astype(jnp.bfloat16)


def norm_parts(values):
    center = values - jnp.mean(values, axis=-1, keepdims=True)
    spread = jnp.mean(center * center, axis=-1, keepdims=True)
    inverse = lax.rsqrt(spread + norm_eps)
    return center * inverse, inverse


def norm_back(cotangent, hat, inverse, gain_vec):
    scaled = cotangent * gain_vec
    return (
        scaled
        - jnp.mean(scaled, axis=-1, keepdims=True)
        - hat * jnp.mean(scaled * hat, axis=-1, keepdims=True)
    ) * inverse


def rotary_tables(positions):
    half = HEAD_DIM // 2
    exponent = jnp.arange(half, dtype=jnp.float32) * (2.0 / HEAD_DIM)
    angles = positions.astype(jnp.float32)[..., None] * jnp.exp(-math.log(10000.0) * exponent)
    return (jnp.cos(angles), jnp.sin(angles))


def rotate(values, cosine, sine):
    half = HEAD_DIM // 2
    front, back = values[..., :half], values[..., half:]
    return jnp.concatenate(
        [front * cosine - back * sine, back * cosine + front * sine], axis=-1
    )


def gather(values, axes):
    return lax.all_gather(values, axes, axis=0, tiled=True)


def scatter_sum(values, axes):
    return lax.psum_scatter(values, axes, scatter_dimension=0, tiled=True)


def gelu_parts(value):
    phi = 0.5 + 0.5 * lax.erf(value * math.sqrt(0.5))
    density = jnp.exp(-0.5 * value * value) * (1.0 / math.sqrt(2.0 * math.pi))
    return value * phi, phi + value * density


MESH = pl.DeviceIdType.MESH


class Wire:
    def __init__(self, send_sems, recv_sems):
        self.send_sems, self.recv_sems = send_sems, recv_sems
        self.keys, self.sent = {}, []

    def number(self, key, span=1):
        if key not in self.keys:
            self.keys[key] = sum(size for _, size in self.keys.values()), span
        return self.keys[key][0]

    def copy(self, key, source, target, device, slot=0, span=1, recv=None):
        send = self.number(key, span)
        receive = send if recv is None else self.number(recv)
        return pltpu.make_async_remote_copy(
            src_ref=source,
            dst_ref=target,
            send_sem=self.send_sems.at[send],
            recv_sem=self.recv_sems.at[receive + slot],
            device_id=device,
            device_id_type=MESH,
        )

    def send(self, key, source, target, device, when=None, recv=None):
        copy = self.copy(key, source, target, device, recv=recv)
        if when is None:
            copy.start()
        else:
            pl.when(when)(copy.start)
        self.sent.append((copy, when))

    def send_to_slot(self, key, source, target, device, slot, span, when):
        copy = self.copy(key, source, target, device, slot, span)
        pl.when(when)(copy.start)
        self.sent.append((copy, when))

    def send_between(self, key, receive, slot, source, target, device, when):
        copy = self.copy(key, source, target, device, slot, recv=receive)
        pl.when(when)(copy.start)
        self.sent.append((copy, when))

    def arrive(self, key, target, device, when=None):
        copy = self.copy(key, target, target, device)
        if when is None:
            copy.wait_recv()
        else:
            pl.when(when)(copy.wait_recv)

    def arrive_slot(self, key, target, device, slot, span, when):
        pl.when(when)(self.copy(key, target, target, device, slot, span).wait_recv)

    def drain(self):
        for copy, when in self.sent:
            if when is None:
                copy.wait_send()
            else:
                pl.when(when)(copy.wait_send)


def flip(value, bit):
    return 1 - value if bit else value


def enter(devices):
    barrier = pltpu.get_barrier_semaphore()
    for device in devices:
        pl.semaphore_signal(barrier, inc=1, device_id=device, device_id_type=MESH)
    pl.semaphore_wait(barrier, len(devices))


class Place:
    def __init__(self):
        self.zo, self.zi, self.x, self.y, self.c = (lax.axis_index(name) for name in ALL)
        self.rank = self.x * 4 + self.y * 2 + self.c
        self.unit = self.zi * 2 + self.c

    def head_home(self):
        return self.y + self.c * (3 - 2 * self.y)

    def holder(self):
        y, c = lax.rem((self.zi + 1) // 2, 2), self.zi // 2
        return (self.zo, self.zi, self.x, y, c), self.x * 4 + y * 2 + c

    def plane(self, delta):
        dx, dy, dc = delta >> 2 & 1, delta >> 1 & 1, delta & 1
        x, y, c = flip(self.x, dx), flip(self.y, dy), flip(self.c, dc)
        return (self.zo, self.zi, x, y, c), x * 4 + y * 2 + c

    def column(self, step):
        other = lax.rem(self.unit + step + 8, 8)
        return (self.zo, other // 2, self.x, self.y, lax.rem(other, 2)), other

    def ends(self):
        return self.line(jnp.minimum(self.zi + 1, 3)), self.line(jnp.maximum(self.zi - 1, 0))

    def line(self, z):
        return (self.zo, z, self.x, self.y, self.c)

    def column_neighbours(self):
        return [self.line(z) for z in self.others()] + [self.plane(1)[0]]

    def others(self):
        return [lax.rem(self.zi + step, 4) for step in (1, 2, 3)]

    def neighbours(self):
        plane = [self.plane(delta)[0] for delta in range(1, 8)]
        column = []
        for dz in range(1, 4):
            z = lax.rem(self.zi + dz, 4)
            column += [(self.zo, z, self.x, self.y, core) for core in (0, 1)]
        return plane + column


def unit_gather_flow(at, wire, ffn_in, ffn_out, own_sem):
    x_side, y_side = at.plane(4)[0], at.plane(2)[0]
    steps = (1, 7, 2, 6, 3, 5, 4)
    mine = ffn_out.at[:, at.zi, at.x, at.y, at.c]
    own = pltpu.make_async_copy(ffn_in.at[at.unit], mine, own_sem)
    own.start()
    for step in steps:
        device, other = at.column(step)
        wire.send(("f", step), ffn_in.at[other], mine, device)
    own.wait()

    def slot(step, x, y):
        source = lax.rem(at.unit - step + 8, 8)
        return ffn_out.at[:, source // 2, x, y, lax.rem(source, 2)]

    def first(step):
        here = slot(step, at.x, at.y)
        if step:
            wire.arrive(("f", step), here, at.column(-step)[0])
        wire.send(("fx", step), here, here, x_side)
        wire.send(("fy", step), here, here, y_side)

    def second(step, turn):
        from_x, from_y = slot(step, 1 - at.x, at.y), slot(step, at.x, 1 - at.y)
        wire.arrive(("fx", step), from_x, x_side)
        wire.arrive(("fy", step), from_y, y_side)
        if turn % 2:
            wire.send(("fd", step), from_x, from_x, y_side)
        else:
            wire.send(("fd", step), from_y, from_y, x_side)

    yield
    first(0)
    for turn, step in enumerate(steps):
        yield
        first(step)
        if turn >= 1:
            second(((0,) + steps)[turn - 1], turn - 1)
    yield
    second(steps[5], 6)
    second(steps[6], 7)
    yield
    for step in (0,) + steps:
        wire.arrive(("fd", step), slot(step, 1 - at.x, 1 - at.y), x_side)


def open_heads_kernel(
    qkv_in,
    ffn_in,
    proj_in,
    x_in,
    small_in,
    qkv_out,
    ffn_out,
    proj_out,
    x_out,
    small_out,
    send_sems,
    recv_sems,
    own_sems,
):
    at = Place()
    wire = Wire(send_sems, recv_sems)
    enter(at.neighbours())
    up, down = at.ends()
    chunk = at.y * 2 + at.c
    holder_device, holder = at.holder()
    proj_home = at.head_home()
    own = [
        pltpu.make_async_copy(qkv_in.at[at.rank], qkv_out.at[at.zi, at.rank], own_sems.at[1]),
        pltpu.make_async_copy(small_in, small_out.at[at.zi, at.rank], own_sems.at[3]),
    ]
    for copy in own:
        copy.start()
    for delta in range(1, 8):
        device, other = at.plane(delta)
        wire.send(("q", delta), qkv_in.at[other], qkv_out.at[at.zi, at.rank], device)
    wire.send_to_slot("p", proj_in, proj_out.at[chunk], holder_device, chunk, 4, at.rank != holder)
    proj_own = pltpu.make_async_copy(proj_in, proj_out.at[chunk], own_sems.at[4])
    pl.when(at.rank == holder)(proj_own.start)
    for delta in range(1, 8):
        device, _ = at.plane(delta)
        wire.send(("s", delta), small_in, small_out.at[at.zi, at.rank], device)
    spread = plane_gather_flow(at, wire, x_in, x_out, own_sems.at[0])
    next(spread)
    for copy in own:
        copy.wait()
    pl.when(at.rank == holder)(proj_own.wait)

    def small_second():
        for delta in range(1, 8):
            device, other = at.plane(delta)
            wire.arrive(("s", delta), small_out.at[at.zi, other], device)
        for dz in range(1, 4):
            device = at.line(lax.rem(at.zi + dz, 4))
            wire.send(("t", dz), small_out.at[at.zi], small_out.at[at.zi], device)

    def small_last():
        for dz in range(1, 4):
            z = lax.rem(at.zi - dz + 4, 4)
            wire.arrive(("t", dz), small_out.at[z], at.line(z))

    def proj_start(slot):
        block = proj_out.at[slot]
        source = (at.zo, at.zi, at.x, slot // 2, slot % 2)
        home = at.zi == proj_home
        mine = home & ((chunk != slot) | (at.rank != holder))
        wire.arrive_slot("p", block, source, slot, 4, mine)
        wire.send(("pu", slot), block, block, up, home & (at.zi < 3))
        wire.send(("pd", slot), block, block, down, home & (at.zi > 0))

    def proj_relay(slot):
        block = proj_out.at[slot]
        above, below = at.zi > proj_home, at.zi < proj_home
        wire.arrive(("pu", slot), block, down, above)
        wire.arrive(("pd", slot), block, up, below)
        key = "pu", slot
        wire.send(("pu2", slot), block, block, up, above & (at.zi < 3), recv=key)
        key = "pd", slot
        wire.send(("pd2", slot), block, block, down, below & (at.zi > 0), recv=key)

    def qkv_slot(z, delta):
        return qkv_out.at[jnp.clip(z, 0, 3), at.plane(delta)[1]]

    def qkv_hop(hop, delta):
        below, above = qkv_slot(at.zi - hop, delta), qkv_slot(at.zi + hop, delta)
        if hop == 0:
            if delta:
                wire.arrive(("q", delta), below, at.plane(delta)[0])
        else:
            wire.arrive(("up", hop - 1, delta), below, down, at.zi >= hop)
            wire.arrive(("down", hop - 1, delta), above, up, at.zi <= 3 - hop)
        if hop < 3:
            wire.send(("up", hop, delta), below, below, up, (at.zi >= hop) & (at.zi < 3))
            wire.send(("down", hop, delta), above, above, down, (at.zi <= 3 - hop) & (at.zi > 0))

    for delta in range(8):
        qkv_hop(0, delta)
    units = unit_gather_flow(at, wire, ffn_in, ffn_out, own_sems.at[2])
    for slot in range(4):
        proj_start(slot)
    next(units)
    next(spread)
    small_second()
    next(units)
    for _ in spread:
        pass
    for delta in range(8):
        qkv_hop(1, delta)
        if delta % 2:
            proj_relay(delta // 2)
            next(units)
    for delta in range(8):
        qkv_hop(2, delta)
        if delta % 2:
            next(units)
    for delta in range(8):
        qkv_hop(3, delta)
    for _ in units:
        pass
    small_last()
    wire.drain()


def turned(values, cosine, sine):
    return values * cosine + pltpu.roll(values, HEAD_DIM // 2, 1) * sine


def row_place(rank, micro):
    piece = rank % 4
    return (rank // 4) * 2 + micro, piece


def open_units_kernel(
    x_all,
    qkv,
    proj,
    cosine,
    sine,
    start_query,
    start_key,
    end_key,
    x_own,
    gain,
    shift,
    ffn_in,
    queries,
    key_rows,
    value_rows,
    probs_out,
    context,
    normed,
    hat,
    inverse_out,
    normed_all,
    ffn_out,
    part,
    branch,
    *rest,
):
    at = Place()
    *scratch, send_sems, recv_sems, own_sems = rest
    wire = Wire(send_sems, recv_sems)
    enter(at.neighbours())
    own = x_own.shape[0]
    pos = own // 2
    length = 4 * pos
    heads = context.shape[-1] // HEAD_DIM
    wide = heads * HEAD_DIM

    def project():
        @pl.loop(0, 8)
        def _(rank):
            mixed = dot(x_all[rank], qkv[...])
            for micro in range(2):
                row, piece = row_place(rank, micro)
                place = pl.ds(pl.multiple_of(piece * pos, pos), pos)
                near = mixed[micro * pos : (micro + 1) * pos]
                cos, sin = cosine[row, place], sine[row, place]
                for head in range(heads):
                    cols = pl.ds(head * HEAD_DIM, HEAD_DIM)
                    for kind, target in enumerate((queries, key_rows, value_rows)):
                        first = kind * wide + head * HEAD_DIM
                        values = near[:, first : first + HEAD_DIM]
                        if kind < 2:
                            values = turned(values, cos, sin)
                        target[row, place, cols] = values.astype(jnp.bfloat16)

    def attend():
        scale = 1.0 / math.sqrt(HEAD_DIM)
        here = lax.broadcasted_iota(jnp.int32, (length, length), 0)
        there = lax.broadcasted_iota(jnp.int32, (length, length), 1)

        @pl.loop(0, 4)
        def _(row):
            bound = end_key[row].astype(jnp.int32)
            seen = (start_query[row] == start_key[row]) & ((there <= here) | (there < bound))
            for head in range(heads):
                cols = pl.ds(head * HEAD_DIM, HEAD_DIM)
                scores = contract_last(queries[row, :, cols], key_rows[row, :, cols]) * scale
                scores = jnp.where(seen, scores, masked_score)
                scores = jnp.exp(scores - jnp.max(scores, axis=-1, keepdims=True))
                probs = scores / jnp.sum(scores, axis=-1, keepdims=True)
                probs_out[row, head] = probs
                result = dot(probs.astype(jnp.bfloat16), value_rows[row, :, cols])
                result = result.astype(jnp.bfloat16)
                for piece in range(4):
                    target = pl.ds(pl.multiple_of((row % 2) * pos, pos), pos)
                    source = result[piece * pos : (piece + 1) * pos]
                    context[(row // 2) * 4 + piece, target, cols] = source

    def branch_parts():
        @pl.loop(0, 8)
        def _(rank):
            part[rank] = dot(context[rank], proj[...]).astype(jnp.bfloat16)

    pieces = 4
    height = own // pieces

    def norm_rows(start):
        count = 16

        @pl.loop(0, height // count)
        def _(index):
            rows = pl.ds(pl.multiple_of(start + index * count, count), count)
            whole = deep_alpha * x_own[rows].astype(jnp.float32) + branch[rows]
            near, inverse = norm_parts(whole)
            hat[rows] = near
            inverse_out[rows] = jnp.broadcast_to(inverse, (count, LANES))
            normed[rows] = (near * gain[...] + shift[...]).astype(jnp.bfloat16)

    core_in, core_sum, side_in, side_sum, last_in = scratch
    scatters, gathers = [], []
    for index in range(pieces):
        rows = pl.ds(index * height, height)
        views = [core_in.at[:, rows], core_sum.at[:, rows], side_in.at[:, :, rows]]
        views += [side_sum.at[:, rows], last_in.at[:, rows]]
        scatters.append(
            plane_scatter_flow(at, wire, index, part.at[:, rows], branch.at[rows], *views)
        )
        sem = own_sems.at[1 + index]
        gathers.append(
            column_gather_flow(at, wire, index, normed.at[rows], normed_all.at[:, rows], sem)
        )
    units = unit_gather_flow(at, wire, ffn_in, ffn_out, own_sems.at[0])
    next(units)
    next(units)
    project()
    next(units)
    next(units)
    attend()
    next(units)
    branch_parts()
    for stage in range(3):
        for flow in scatters:
            next(flow)
    for index in range(pieces + 3):
        if index < pieces:
            for _ in scatters[index]:
                pass
            norm_rows(index * height)
            next(gathers[index])
        for lag in (1, 2, 3):
            if 0 <= index - lag < pieces:
                next(gathers[index - lag], None)
        next(units, None)
    for flow in gathers + [units]:
        for _ in flow:
            pass
    wire.drain()


ANY = pl.BlockSpec(memory_space=pl.ANY)
VMEM = pl.BlockSpec(memory_space=pltpu.VMEM)


def comm_params(number):
    return pltpu.CompilerParams(
        collective_id=number, has_side_effects=True, vmem_limit_bytes=63 * 2**20
    )


def open_heads(qkv_parts, ffn_parts, proj_own, x_own, small):
    _, rows_own, qkv_width = qkv_parts.shape
    _, matrices, _, unit_width = ffn_parts.shape
    own, width = x_own.shape
    low_type = jnp.bfloat16
    return pl.pallas_call(
        open_heads_kernel,
        out_shape=(
            jax.ShapeDtypeStruct((4, 8, rows_own, qkv_width), low_type),
            jax.ShapeDtypeStruct((matrices, 4, 2, 2, 2, rows_own, unit_width), low_type),
            jax.ShapeDtypeStruct((4, rows_own, width), low_type),
            jax.ShapeDtypeStruct((8, own, width), low_type),
            jax.ShapeDtypeStruct((4, 8) + small.shape, small.dtype),
        ),
        in_specs=[VMEM] * 5,
        out_specs=(ANY,) * 5,
        scratch_shapes=[
            pltpu.SemaphoreType.DMA((136,)),
            pltpu.SemaphoreType.DMA((136,)),
            pltpu.SemaphoreType.DMA((5,)),
        ],
        compiler_params=comm_params(1),
        name="open_heads",
    )(qkv_parts, ffn_parts, proj_own, x_own, small)


def open_units(x_all, qkv, proj, tables, x_own, gain, shift, ffn_parts):
    _, matrices, rows_own, unit_width = ffn_parts.shape
    own, width = x_own.shape
    head_width = proj.shape[0]
    length = 2 * own
    low_type = jnp.bfloat16
    rows = jax.ShapeDtypeStruct((4, length, head_width), low_type)
    return pl.pallas_call(
        open_units_kernel,
        out_shape=(
            rows,
            rows,
            rows,
            jax.ShapeDtypeStruct((4, head_width // HEAD_DIM, length, length), jnp.float32),
            jax.ShapeDtypeStruct((8, own, head_width), low_type),
            jax.ShapeDtypeStruct((own, width), low_type),
            jax.ShapeDtypeStruct((own, width), jnp.float32),
            jax.ShapeDtypeStruct((own, LANES), jnp.float32),
            jax.ShapeDtypeStruct((8, own, width), low_type),
            jax.ShapeDtypeStruct((matrices, 4, 2, 2, 2, rows_own, unit_width), low_type),
        ),
        in_specs=[VMEM] * 12,
        out_specs=(VMEM,) * 8 + (ANY, ANY),
        scratch_shapes=[
            pltpu.VMEM((8, own, width), low_type),
            pltpu.VMEM((own, width), jnp.float32),
        ]
        + plane_scratch(own, width)
        + [
            pltpu.SemaphoreType.DMA((136,)),
            pltpu.SemaphoreType.DMA((136,)),
            pltpu.SemaphoreType.DMA((5,)),
        ],
        compiler_params=comm_params(4),
        name="open_units",
    )(x_all, qkv, proj, *tables, x_own, gain, shift, ffn_parts)


def add_rows(out, *terms):
    step = 32

    @pl.loop(0, out.shape[0] // step)
    def _(index):
        part = pl.ds(pl.multiple_of(index * step, step), step)
        whole = terms[0][part].astype(jnp.float32)
        for term in terms[1:]:
            whole = whole + term[part].astype(jnp.float32)
        out[part] = whole.astype(out.dtype)


def column_scatter_flow(
    at, wire, tag, part, out, core_in, core_sum, up_in, down_in, up_sum, down_sum
):
    core_side = at.plane(1)[0]
    up, down = at.ends()
    for goal in (3, 0, 2, 1):
        source = part.at[goal * 2 + 1 - at.c]
        wire.send(("rc", tag, goal), source, core_in.at[goal], core_side)
    yield
    for goal in (3, 0, 2, 1):
        wire.arrive(("rc", tag, goal), core_in.at[goal], core_side)
        add_rows(core_sum.at[goal], part.at[goal * 2 + at.c], core_in.at[goal])
        for rising in {3: (3,), 2: (2,), 1: (1,)}.get(goal, ()):
            key = "ru", tag, rising
            wire.send(key, core_sum.at[rising], up_in.at[rising], up, at.zi == 0)
        for falling in {0: (0,), 1: (1, 2)}.get(goal, ()):
            key = "rd", tag, falling
            wire.send(key, core_sum.at[falling], down_in.at[falling], down, at.zi == 3)

    def climb(goal):
        wire.arrive(("ru", tag, goal), up_in.at[goal], down)
        add_rows(up_sum.at[goal], core_sum.at[goal], up_in.at[goal])

    def descend(goal):
        wire.arrive(("rd", tag, goal), down_in.at[goal], up)
        add_rows(down_sum.at[goal], core_sum.at[goal], down_in.at[goal])

    def rise(goal, z):
        pl.when(at.zi == z)(lambda: climb(goal))
        key = "ru", tag, goal
        target = up_in.at[goal]
        wire.send(("ru2", tag, goal), up_sum.at[goal], target, up, at.zi == z, recv=key)

    def fall(goal, z):
        pl.when(at.zi == z)(lambda: descend(goal))
        key = "rd", tag, goal
        target = down_in.at[goal]
        wire.send(("rd2", tag, goal), down_sum.at[goal], target, down, at.zi == z, recv=key)

    yield
    rise(3, 1)
    fall(0, 2)
    yield
    rise(3, 2)
    fall(0, 1)
    rise(2, 1)
    fall(1, 2)
    yield
    add_rows(out, core_sum.at[at.zi])

    def last(key, source, device):
        wire.arrive(key, source, device)
        add_rows(out, out, source)

    for goal in range(4):
        if goal > 0:
            pl.when(at.zi == goal)(lambda: last(("ru", tag, goal), up_in.at[goal], down))
        if goal < 3:
            pl.when(at.zi == goal)(lambda: last(("rd", tag, goal), down_in.at[goal], up))


def column_gather_flow(at, wire, tag, own_in, out, own_sem):
    core_side = at.plane(1)[0]
    up, down = at.ends()

    def slot(z, c):
        return out.at[jnp.clip(z, 0, 3) * 2 + c]

    mine = slot(at.zi, at.c)
    wire.send(("gu", tag, 0), own_in, mine, up, at.zi < 3)
    wire.send(("gd", tag, 0), own_in, mine, down, at.zi > 0)
    wire.send(("gc", tag), own_in, mine, core_side)
    own = pltpu.make_async_copy(own_in, mine, own_sem)
    own.start()
    for hop in (1, 2, 3):
        yield
        below, above = slot(at.zi - hop, at.c), slot(at.zi + hop, at.c)
        has_below, has_above = at.zi >= hop, at.zi <= 3 - hop
        wire.arrive(("gu", tag, hop - 1), below, down, has_below)
        if hop < 3:
            wire.send(("gu", tag, hop), below, below, up, has_below & (at.zi < 3))
        wire.send(("gcu", tag, hop), below, below, core_side, has_below)
        wire.arrive(("gd", tag, hop - 1), above, up, has_above)
        if hop < 3:
            wire.send(("gd", tag, hop), above, above, down, has_above & (at.zi > 0))
        wire.send(("gcd", tag, hop), above, above, core_side, has_above)
    yield
    own.wait()
    wire.arrive(("gc", tag), slot(at.zi, 1 - at.c), core_side)
    for hop in (1, 2, 3):
        below, above = slot(at.zi - hop, 1 - at.c), slot(at.zi + hop, 1 - at.c)
        wire.arrive(("gcu", tag, hop), below, core_side, at.zi >= hop)
        wire.arrive(("gcd", tag, hop), above, core_side, at.zi <= 3 - hop)


def column_scratch(own, width):
    return [pltpu.VMEM((4, own, width), jnp.bfloat16)] * 6


def plane_scatter_flow(
    at, wire, tag, part, out, core_in, core_sum, side_in, side_sum, last_in
):
    x_side, y_side, core_side = at.plane(4)[0], at.plane(2)[0], at.plane(1)[0]
    half = out.shape[1] // 2
    halves = (pl.ds(0, half), pl.ds(half, half))
    order = ((1, 1), (1, 0), (0, 1), (0, 0))

    def place(dx, dy):
        return flip(at.x, dx), flip(at.y, dy)

    for dx, dy in order:
        x, y = place(dx, dy)
        other = x * 4 + y * 2 + 1 - at.c
        wire.send(("c", tag, dx, dy), part.at[other], core_in.at[dx * 2 + dy], core_side)
    yield
    for dx, dy in order:
        x, y = place(dx, dy)
        mine = x * 4 + y * 2 + at.c
        slot = dx * 2 + dy
        wire.arrive(("c", tag, dx, dy), core_in.at[slot], core_side)
        add_rows(core_sum.at[slot], part.at[mine], core_in.at[slot])
        if dx:
            source = core_sum.at[slot, :, halves[0]]
            wire.send(("sa", tag, dy), source, side_in.at[0, dy], x_side)
        if dy:
            source = core_sum.at[slot, :, halves[1]]
            wire.send(("sb", tag, dx), source, side_in.at[1, dx], y_side)
    yield
    wire.arrive(("sa", tag, 1), side_in.at[0, 1], x_side)
    add_rows(side_sum.at[0], core_sum.at[1, :, halves[0]], side_in.at[0, 1])
    wire.send(("sy", tag), side_sum.at[0], last_in.at[0], y_side)
    wire.arrive(("sb", tag, 1), side_in.at[1, 1], y_side)
    add_rows(side_sum.at[1], core_sum.at[2, :, halves[1]], side_in.at[1, 1])
    wire.send(("sx", tag), side_sum.at[1], last_in.at[1], x_side)
    yield
    wire.arrive(("sa", tag, 0), side_in.at[0, 0], x_side)
    wire.arrive(("sb", tag, 0), side_in.at[1, 0], y_side)
    wire.arrive(("sy", tag), last_in.at[0], y_side)
    terms = core_sum.at[0, :, halves[0]], side_in.at[0, 0], last_in.at[0]
    add_rows(out.at[:, halves[0]], *terms)
    wire.arrive(("sx", tag), last_in.at[1], x_side)
    terms = core_sum.at[0, :, halves[1]], side_in.at[1, 0], last_in.at[1]
    add_rows(out.at[:, halves[1]], *terms)


def plane_scratch(own, width):
    return [
        pltpu.VMEM((4, own, width), jnp.bfloat16),
        pltpu.VMEM((4, own, width), jnp.bfloat16),
        pltpu.VMEM((2, 2, own, width // 2), jnp.bfloat16),
        pltpu.VMEM((2, own, width // 2), jnp.bfloat16),
        pltpu.VMEM((2, own, width // 2), jnp.bfloat16),
    ]


def plane_gather_flow(at, wire, own_in, out, own_sem):
    x_side, y_side, core_side = at.plane(4)[0], at.plane(2)[0], at.plane(1)[0]
    half = own_in.shape[0] // 2
    mine = out.at[at.rank]
    wire.send("gx", own_in, mine, x_side)
    wire.send("gy", own_in, mine, y_side)
    wire.send("gc0", own_in, mine, core_side)
    own = pltpu.make_async_copy(own_in, mine, own_sem)
    own.start()
    yield
    from_x, from_y, from_xy = (at.plane(delta)[1] for delta in (4, 2, 6))
    low_half, high_half = pl.ds(0, half), pl.ds(half, half)
    wire.arrive("gx", out.at[from_x], x_side)
    wire.send("gd0", out.at[from_x, low_half], out.at[from_x, low_half], y_side)
    wire.send("gc1", out.at[from_x], out.at[from_x], core_side)
    wire.arrive("gy", out.at[from_y], y_side)
    wire.send("gd1", out.at[from_y, high_half], out.at[from_y, high_half], x_side)
    wire.send("gc2", out.at[from_y], out.at[from_y], core_side)
    yield
    wire.arrive("gd0", out.at[from_xy, low_half], y_side)
    wire.arrive("gd1", out.at[from_xy, high_half], x_side)
    wire.send("gc3", out.at[from_xy], out.at[from_xy], core_side)
    own.wait()
    for index, delta in enumerate((1, 5, 3, 7)):
        wire.arrive("gc%d" % index, out.at[at.plane(delta)[1]], core_side)


def turn_kernel(
    part,
    normed,
    out_grad,
    gain,
    shift,
    layer_out,
    d_second,
    down_out,
    norm_out,
    second,
    down_low,
    core_in,
    core_sum,
    up_in,
    down_in,
    up_sum,
    down_sum,
    send_sems,
    recv_sems,
    own_sems,
):
    at = Place()
    wire = Wire(send_sems, recv_sems)
    enter(at.column_neighbours())
    pieces = 2
    height = normed.shape[0] // pieces
    scratch = core_in, core_sum, up_in, down_in, up_sum, down_sum

    def norm_rows(start):
        count = 16

        @pl.loop(0, height // count)
        def _(index):
            rows = pl.ds(pl.multiple_of(start + index * count, count), count)
            whole = deep_alpha * normed[rows].astype(jnp.float32) + second[rows]
            near, inverse = norm_parts(whole)
            layer_out[rows] = (near * gain[...] + shift[...]).astype(jnp.bfloat16)
            cotangent = out_grad[rows].astype(jnp.float32)
            result = norm_back(cotangent, near, inverse, gain[...])
            d_second[rows] = result
            down_low[rows] = result.astype(jnp.bfloat16)
            along = cotangent * near
            norm_out[0] += along[:8] + along[8:]
            norm_out[1] += cotangent[:8] + cotangent[8:]

    scatters, gathers = [], []
    for index in range(pieces):
        rows = pl.ds(index * height, height)
        views = [ref.at[:, rows] for ref in scratch]
        scatters.append(
            column_scatter_flow(at, wire, index, part.at[:, rows], second.at[rows], *views)
        )
        gathers.append(
            column_gather_flow(
                at, wire, index, down_low.at[rows], down_out.at[:, rows], own_sems.at[index]
            )
        )
    norm_out[...] = jnp.zeros_like(norm_out)
    for flow in scatters:
        next(flow)
    for flow in scatters:
        next(flow)
    for index in range(pieces + 3):
        if index < pieces:
            for _ in scatters[index]:
                pass
            norm_rows(index * height)
            next(gathers[index])
        for lag in (1, 2, 3):
            if 0 <= index - lag < pieces:
                next(gathers[index - lag], None)
    for flow in gathers:
        for _ in flow:
            pass
    wire.drain()


def turn(part, normed, out_grad, gain, shift):
    _, own, width = part.shape
    low_type = jnp.bfloat16
    return pl.pallas_call(
        turn_kernel,
        out_shape=(
            jax.ShapeDtypeStruct((own, width), low_type),
            jax.ShapeDtypeStruct((own, width), jnp.float32),
            jax.ShapeDtypeStruct((8, own, width), low_type),
            jax.ShapeDtypeStruct((2, 8, width), jnp.float32),
        ),
        in_specs=[VMEM] * 5,
        out_specs=(VMEM, VMEM, ANY, VMEM),
        scratch_shapes=[
            pltpu.VMEM((own, width), jnp.float32),
            pltpu.VMEM((own, width), low_type),
        ]
        + column_scratch(own, width)
        + [
            pltpu.SemaphoreType.DMA((112,)),
            pltpu.SemaphoreType.DMA((112,)),
            pltpu.SemaphoreType.DMA((4,)),
        ],
        compiler_params=comm_params(5),
        name="turn",
    )(part, normed, out_grad, gain, shift)


def close_units_kernel(
    gate_in,
    raise_in,
    lower_in,
    part,
    d_second,
    hat,
    inverse,
    gain,
    proj,
    queries,
    key_rows,
    value_rows,
    probs_in,
    cosine,
    sine,
    ffn_out,
    branch_out,
    d_mixed,
    d_first,
    norm_out,
    d_context,
    first_in,
    second_sum,
    second_in,
    total,
    d_normed,
    branch_low,
    core_in,
    core_sum,
    up_in,
    down_in,
    up_sum,
    down_sum,
    send_sems,
    recv_sems,
    own_sems,
):
    at = Place()
    wire = Wire(send_sems, recv_sems)
    enter(at.neighbours())
    x_side, y_side = at.plane(4)[0], at.plane(2)[0]
    steps = (4, 3, 5, 2, 6, 1, 7, 0)
    sources = gate_in, raise_in, lower_in

    def owner(step):
        other = at.column(step)[1]
        return other // 2, lax.rem(other, 2)

    def ffn_first(turn):
        step = steps[turn]
        z, c = owner(step)
        for index, source in enumerate(sources):
            if turn % 2:
                block, device = source.at[z, 1 - at.x, :, c], x_side
            else:
                block, device = source.at[z, :, 1 - at.y, c], y_side
            wire.send(("a", step, index), block, first_in.at[step, index], device)

    def ffn_second(turn):
        step = steps[turn]
        z, c = owner(step)
        for index, source in enumerate(sources):
            if turn % 2:
                wire.arrive(("a", step, index), first_in.at[step, index], x_side)
                terms = source.at[z, at.x, 1 - at.y, c], first_in.at[step, index, 1 - at.y]
            else:
                wire.arrive(("a", step, index), first_in.at[step, index], y_side)
                terms = source.at[z, 1 - at.x, at.y, c], first_in.at[step, index, 1 - at.x]
            add_rows(second_sum.at[step, index], *terms)
        wire.send(
            ("b", step), second_sum.at[step], second_in.at[step], y_side if turn % 2 else x_side
        )

    own_total = pltpu.make_async_copy(total.at[0], ffn_out.at[at.unit], own_sems.at[0])

    def ffn_last(turn):
        step = steps[turn]
        z, c = owner(step)
        near = at.y if turn % 2 else at.x
        wire.arrive(("b", step), second_in.at[step], x_side)
        for index, source in enumerate(sources):
            add_rows(
                total.at[step, index],
                source.at[z, at.x, at.y, c],
                first_in.at[step, index, near],
                second_in.at[step, index],
            )
        if step:
            wire.send(("f", step), total.at[step], ffn_out.at[at.unit], at.column(step)[0])
        else:
            own_total.start()

    def norm_rows():
        count = 16
        norm_out[...] = jnp.zeros_like(norm_out)

        @pl.loop(0, hat.shape[0] // count)
        def _(index):
            rows = pl.ds(pl.multiple_of(index * count, count), count)
            cotangent = deep_alpha * d_second[rows] + d_normed[rows]
            near = hat[rows]
            result = norm_back(cotangent, near, inverse[rows, :1], gain[...])
            d_first[rows] = result
            branch_low[rows] = result.astype(jnp.bfloat16)
            along = cotangent * near
            norm_out[0] += along[:8] + along[8:]
            norm_out[1] += cotangent[:8] + cotangent[8:]

    pos = hat.shape[0] // 2
    wide = proj.shape[0]
    heads = wide // HEAD_DIM
    scale = 1.0 / math.sqrt(HEAD_DIM)

    def pull():
        @pl.loop(0, 8)
        def _(rank):
            result = contract_last(branch_out[rank], proj[...]).astype(jnp.bfloat16)
            for micro in range(2):
                row, piece = row_place(rank, micro)
                place = pl.ds(pl.multiple_of(piece * pos, pos), pos)
                d_context[row, place] = result[micro * pos : (micro + 1) * pos]

    def attend_back(first, last):
        @pl.loop(first, last)
        def _(row):
            cos, sin = cosine[row], -sine[row]
            target = pl.ds(pl.multiple_of((row % 2) * pos, pos), pos)
            for head in range(heads):
                cols = pl.ds(head * HEAD_DIM, HEAD_DIM)
                probs, above = probs_in[row, head], d_context[row, :, cols]
                d_probs = contract_last(above, value_rows[row, :, cols])
                along = jnp.sum(probs * d_probs, axis=-1, keepdims=True)
                d_scores = (probs * (d_probs - along)).astype(jnp.bfloat16)
                d_query = dot(d_scores, key_rows[row, :, cols]) * scale
                d_keys = contract_first(d_scores, queries[row, :, cols]) * scale
                d_values = contract_first(probs.astype(jnp.bfloat16), above)
                results = turned(d_query, cos, sin), turned(d_keys, cos, sin), d_values
                for kind, result in enumerate(results):
                    result = result.astype(jnp.bfloat16)
                    place = pl.ds(kind * wide + head * HEAD_DIM, HEAD_DIM)
                    for piece in range(4):
                        source = result[piece * pos : (piece + 1) * pos]
                        d_mixed[(row // 2) * 4 + piece, target, place] = source

    scatter = column_scatter_flow(
        at, wire, 0, part, d_normed, core_in, core_sum, up_in, down_in, up_sum, down_sum
    )
    next(scatter)
    for turn in range(5):
        ffn_first(turn)
    next(scatter)
    next(scatter)
    ffn_second(0)
    ffn_first(5)
    ffn_second(1)
    ffn_first(6)
    next(scatter)
    ffn_second(2)
    ffn_first(7)
    ffn_second(3)
    for _ in scatter:
        pass
    norm_rows()
    spread = plane_gather_flow(at, wire, branch_low, branch_out, own_sems.at[1])
    next(spread)
    ffn_last(0)
    ffn_last(1)
    ffn_second(4)
    ffn_last(2)
    ffn_second(5)
    ffn_last(3)
    next(spread)
    ffn_second(6)
    ffn_second(7)
    ffn_last(4)
    for _ in spread:
        pass
    ffn_last(5)
    pull()
    ffn_last(6)
    ffn_last(7)
    attend_back(0, 4)
    own_total.wait()
    for step in steps:
        if step:
            device, other = at.column(-step)
            wire.arrive(("f", step), ffn_out.at[other], device)
    wire.drain()


def close_units(grads, part, d_second, hat, inverse, gain, *heads):
    rows_own, unit_width = grads[0].shape[-2:]
    _, own, width = part.shape
    low_type = jnp.bfloat16
    head_width = heads[0].shape[0]
    block = (rows_own, unit_width)
    return pl.pallas_call(
        close_units_kernel,
        out_shape=(
            jax.ShapeDtypeStruct((8, 3) + block, low_type),
            jax.ShapeDtypeStruct((8, own, width), low_type),
            jax.ShapeDtypeStruct((8, own, 3 * head_width), low_type),
            jax.ShapeDtypeStruct((own, width), jnp.float32),
            jax.ShapeDtypeStruct((2, 8, width), jnp.float32),
        ),
        in_specs=[VMEM] * 15,
        out_specs=(ANY, VMEM, VMEM, VMEM, VMEM),
        scratch_shapes=[
            pltpu.VMEM((4, 2 * own, head_width), low_type),
            pltpu.VMEM((8, 3, 2) + block, low_type),
            pltpu.VMEM((8, 3) + block, low_type),
            pltpu.VMEM((8, 3) + block, low_type),
            pltpu.VMEM((8, 3) + block, low_type),
            pltpu.VMEM((own, width), jnp.float32),
            pltpu.VMEM((own, width), low_type),
        ]
        + column_scratch(own, width)
        + [
            pltpu.SemaphoreType.DMA((80,)),
            pltpu.SemaphoreType.DMA((80,)),
            pltpu.SemaphoreType.DMA((2,)),
        ],
        compiler_params=comm_params(3),
        name="close_units",
    )(*grads, part, d_second, hat, inverse, gain, *heads)


def close_heads_kernel(
    qkv_in,
    proj_in,
    small_in,
    part,
    qkv_out,
    proj_out,
    small_out,
    d_input,
    proj_below,
    proj_above,
    proj_sum,
    small_plane,
    small_mid,
    small_line,
    up_in,
    down_in,
    up_sum,
    down_sum,
    qkv_total,
    core_in,
    core_sum,
    side_in,
    side_sum,
    last_in,
    send_sems,
    recv_sems,
    own_sems,
):
    at = Place()
    wire = Wire(send_sems, recv_sems)
    enter(at.neighbours())
    scatter = plane_scatter_flow(
        at, wire, 0, part, d_input, core_in, core_sum, side_in, side_sum, last_in
    )
    next(scatter)

    for delta in range(1, 8):
        device, other = at.plane(delta)
        wire.send(("s", delta), small_in.at[other], small_plane.at[at.rank], device)

    def small_second():
        whole = small_in[at.rank]
        for delta in range(1, 8):
            device, other = at.plane(delta)
            wire.arrive(("s", delta), small_plane.at[other], device)
            whole = whole + small_plane[other]
        small_mid[...] = whole
        for dz in range(1, 4):
            z = lax.rem(at.zi + dz, 4)
            wire.send(("t", dz), small_mid.at[z], small_line.at[at.zi], at.line(z))

    def small_last():
        whole = small_mid[at.zi]
        for dz in range(1, 4):
            z = lax.rem(at.zi - dz + 4, 4)
            wire.arrive(("t", dz), small_line.at[z], at.line(z))
            whole = whole + small_line[z]
        small_out[...] = whole

    pieces = 4
    wide = 8 // pieces
    up, down = at.line(jnp.minimum(at.zi + 1, 3)), at.line(jnp.maximum(at.zi - 1, 0))

    def add_ranks(piece, out, *terms):
        for rank in range(piece * wide, piece * wide + wide):
            add_rows(out.at[rank], *(term.at[rank] for term in terms))

    def qkv_rise(goal, piece, low_z, high_z):
        part = pl.ds(piece * wide, wide)
        here = (at.zi >= low_z) & (at.zi <= high_z)
        source = up_sum.at[goal, part]

        def climb():
            wire.arrive(("u", goal, piece), up_in.at[goal, part], down)
            add_ranks(piece, up_sum.at[goal], qkv_in.at[goal], up_in.at[goal])

        key = "u", goal, piece
        if low_z == 0:
            first = qkv_in.at[goal, part]
            wire.send(("u0", goal, piece), first, up_in.at[goal, part], up, at.zi == 0, recv=key)
        if high_z > 0:
            here = here & (at.zi > 0)
            pl.when(here)(climb)
            wire.send(key, source, up_in.at[goal, part], up, here)

    def qkv_fall(goal, piece, low_z, high_z):
        part = pl.ds(piece * wide, wide)
        here = (at.zi >= low_z) & (at.zi <= high_z)
        source = down_sum.at[goal, part]

        def descend():
            wire.arrive(("d", goal, piece), down_in.at[goal, part], up)
            add_ranks(piece, down_sum.at[goal], qkv_in.at[goal], down_in.at[goal])

        key = "d", goal, piece
        if high_z == 3:
            first = qkv_in.at[goal, part]
            wire.send(
                ("d0", goal, piece), first, down_in.at[goal, part], down, at.zi == 3, recv=key
            )
        if low_z < 3:
            here = here & (at.zi < 3)
            pl.when(here)(descend)
            wire.send(key, source, down_in.at[goal, part], down, here)

    proj_home = at.head_home()

    def proj_add(slot, *terms):
        add_rows(proj_sum.at[slot], *(term.at[slot] for term in terms))

    below, above = at.zi < proj_home, at.zi > proj_home
    ends = (at.zi == 0) | (at.zi == 3)

    def proj_pass(slot):
        under, over = proj_below.at[slot], proj_above.at[slot]
        wire.send(("pu", slot), proj_in.at[slot], under, up, below & ends)
        wire.send(("pd", slot), proj_in.at[slot], over, down, above & ends)

        def climb():
            wire.arrive(("pu", slot), under, down)
            proj_add(slot, proj_in, proj_below)

        def descend():
            wire.arrive(("pd", slot), over, up)
            proj_add(slot, proj_in, proj_above)

        pl.when(below & (at.zi > 0))(climb)
        pl.when(above & (at.zi < 3))(descend)
        source = proj_sum.at[slot]
        key = "pu", slot
        wire.send(("pu2", slot), source, under, up, below & (at.zi > 0), recv=key)
        key = "pd", slot
        wire.send(("pd2", slot), source, over, down, above & (at.zi < 3), recv=key)

    chunk = at.y * 2 + at.c
    holder_device, holder = at.holder()

    def proj_last():
        home = at.zi == proj_home
        for slot in range(4):
            under, over = proj_below.at[slot], proj_above.at[slot]

            def first():
                wire.arrive(("pu", slot), under, down)
                proj_add(slot, proj_in, proj_below)

            def only():
                wire.arrive(("pd", slot), over, up)
                proj_add(slot, proj_in, proj_above)

            def both():
                wire.arrive(("pd", slot), over, up)
                proj_add(slot, proj_sum, proj_above)

            pl.when(home & (at.zi > 0))(first)
            pl.when(home & (at.zi == 0))(only)
            pl.when(home & (at.zi > 0) & (at.zi < 3))(both)
            target = (at.zo, at.zi, at.x, slot // 2, slot % 2)
            other = (chunk != slot) | (at.rank != holder)
            wire.send(("o", slot), proj_sum.at[slot], proj_out, target, home & other, recv="o")
        own = pltpu.make_async_copy(proj_sum.at[chunk], proj_out, own_sems.at[2])
        pl.when(home & (at.rank == holder))(own.start)
        pl.when(home & (at.rank == holder))(own.wait)

    def qkv_last(piece):
        part = pl.ds(piece * wide, wide)
        for goal in range(4):

            @pl.when(at.zi == goal)
            def _():
                terms = [qkv_in.at[goal]]
                if goal > 0:
                    wire.arrive(("u", goal, piece), up_in.at[goal, part], down)
                    terms.append(up_in.at[goal])
                if goal < 3:
                    wire.arrive(("d", goal, piece), down_in.at[goal, part], up)
                    terms.append(down_in.at[goal])
                add_ranks(piece, qkv_total, *terms)

    def qkv_owner(piece):
        for core in range(wide):
            rank = piece * wide + core
            target = (at.zo, at.zi, rank // 4, rank // 2 % 2, rank % 2)
            source, place = qkv_total.at[rank], qkv_out.at[at.rank]
            wire.number("qr", 8)
            wire.send_between(("q", rank), "qr", at.rank, source, place, target, at.rank != rank)
            own = pltpu.make_async_copy(source, place, own_sems.at[1])
            pl.when(at.rank == rank)(own.start)

    for piece in range(pieces):
        qkv_rise(3, piece, 0, 1)
        qkv_fall(0, piece, 2, 3)
        if piece == 0:
            next(scatter)
    for piece in range(pieces):
        qkv_rise(3, piece, 2, 2)
        qkv_fall(0, piece, 1, 1)
    for slot in range(4):
        proj_pass(slot)
    next(scatter)
    small_second()
    for piece in range(pieces):
        qkv_rise(2, piece, 0, 1)
        qkv_fall(1, piece, 2, 3)
    for _ in scatter:
        pass
    for piece in range(pieces):
        qkv_rise(1, piece, 0, 0)
        qkv_fall(2, piece, 3, 3)
    proj_last()
    for piece in range(pieces):
        qkv_last(piece)
        qkv_owner(piece)
    pltpu.make_async_copy(qkv_total.at[at.rank], qkv_out.at[at.rank], own_sems.at[1]).wait()
    for delta in range(1, 8):
        device, other = at.plane(delta)
        wire.arrive_slot("qr", qkv_out.at[other], device, other, 8, at.rank != other)
    small_last()
    wire.arrive("o", proj_out, holder_device, at.rank != holder)
    wire.drain()


def close_heads(qkv_part, proj_part, small_part, part):
    _, _, rows_own, qkv_width = qkv_part.shape
    _, own, width = part.shape
    low_type = jnp.bfloat16
    line = (4, 8, rows_own, qkv_width)
    small_shape = small_part.shape[1:]
    return pl.pallas_call(
        close_heads_kernel,
        out_shape=(
            jax.ShapeDtypeStruct((8, rows_own, qkv_width), low_type),
            jax.ShapeDtypeStruct((rows_own, width), low_type),
            jax.ShapeDtypeStruct(small_shape[1:], small_part.dtype),
            jax.ShapeDtypeStruct((own, width), jnp.float32),
        ),
        in_specs=[VMEM] * 4,
        out_specs=(ANY, ANY, VMEM, VMEM),
        scratch_shapes=[
            pltpu.VMEM((4, rows_own, width), low_type),
            pltpu.VMEM((4, rows_own, width), low_type),
            pltpu.VMEM((4, rows_own, width), low_type),
            pltpu.VMEM(small_part.shape, small_part.dtype),
            pltpu.VMEM(small_shape, small_part.dtype),
            pltpu.VMEM(small_shape, small_part.dtype),
            pltpu.VMEM(line, low_type),
            pltpu.VMEM(line, low_type),
            pltpu.VMEM(line, low_type),
            pltpu.VMEM(line, low_type),
            pltpu.VMEM(line[1:], low_type),
        ]
        + plane_scratch(own, width)
        + [
            pltpu.SemaphoreType.DMA((112,)),
            pltpu.SemaphoreType.DMA((112,)),
            pltpu.SemaphoreType.DMA((3,)),
        ],
        compiler_params=comm_params(2),
        name="close_heads",
    )(qkv_part, proj_part, small_part, part)


def group_body(
    hidden_in,
    token_marks,
    out_grad,
    qkv_weight,
    proj_weight,
    gate_weight,
    up_weight,
    down_weight,
    first_gain,
    first_shift,
    second_gain,
    second_shift,
):
    micro_count, _, pos_count, width = hidden_in.shape
    rows_own = qkv_weight.shape[0]
    units = gate_weight.shape[1]
    head_ways = math.prod(lax.axis_size(name) for name in HEAD_AXES)
    unit_ways = math.prod(lax.axis_size(name) for name in UNIT_AXES)
    chunk_count = lax.axis_size("y") * lax.axis_size("c")
    row_length = pos_count * chunk_count
    x_size = lax.axis_size("x")
    marks_own = token_marks.astype(jnp.float32)
    own = micro_count * pos_count
    head_width = width // head_ways
    heads_here = head_width // HEAD_DIM
    unit_width = -(-units // (unit_ways * LANES)) * LANES
    unit_pad = unit_width * unit_ways - units
    x_own = hidden_in.reshape(own, width)

    params = jnp.stack([first_gain, first_shift, second_gain, second_shift])
    small = jnp.concatenate([params.astype(jnp.float32).ravel(), marks_own.ravel()])
    small = jnp.pad(small, (0, -small.size % (8 * LANES))).reshape(-1, LANES)

    qkv_parts = qkv_weight.reshape(rows_own, 3, 4, 2, head_width)
    qkv_parts = jnp.stack([qkv_parts[:, :, home] for home in (0, 3, 1, 2)])
    qkv_parts = qkv_parts.transpose(3, 0, 1, 2, 4).reshape(head_ways, rows_own, 3 * head_width)

    def unit_parts(*matrices):
        parts = jnp.stack(matrices)
        parts = jnp.pad(parts, ((0, 0), (0, 0), (0, unit_pad)))
        parts = parts.reshape(len(matrices), rows_own, unit_ways, unit_width)
        return parts.transpose(2, 0, 1, 3)

    qkv_here, gate_here, proj_here, x_all, small = open_heads(
        qkv_parts, unit_parts(gate_weight), proj_weight, x_own, small
    )
    qkv_here = qkv_here.reshape(-1, 3 * head_width)
    gate_here = gate_here.reshape(-1, unit_width)
    x_all = x_all.reshape(-1, width)
    proj_here = proj_here.reshape(head_width, width)
    small = small.reshape(unit_ways * 4, -1)
    params = small[:, : 4 * rows_own].reshape(-1, 4, rows_own).transpose(1, 0, 2)
    gain_one, shift_one, gain_two, shift_two = params.reshape(4, 1, width)
    marks = small.reshape(4, head_ways, -1)[lax.axis_index("zi")]
    marks = marks[:, 4 * rows_own : 4 * rows_own + own * 3]

    def to_rows(values):
        inner = values.shape[1:]
        values = values.reshape((x_size, chunk_count, micro_count, pos_count) + inner)
        return jnp.swapaxes(values, 1, 2).reshape((x_size * micro_count, row_length) + inner)

    row_marks = to_rows(marks.reshape(head_ways * own, 3))
    cosine, sine = rotary_tables(row_marks[..., 2])
    tables = (
        jnp.concatenate([cosine, cosine], axis=-1),
        jnp.concatenate([-sine, sine], axis=-1),
        row_marks[:, :, :1],
        row_marks[:, None, :, 0],
        row_marks[:, None, :, 1],
    )
    queries, key_rows, value_rows, probs, context, normed, hat_one, inverse_one, normed_all, ffn = (
        open_units(
            x_all.reshape(head_ways, own, width),
            qkv_here,
            proj_here,
            tables,
            x_own,
            gain_one,
            shift_one,
            unit_parts(up_weight, down_weight),
        )
    )
    context = context.reshape(-1, head_width)
    normed_all = normed_all.reshape(-1, width)
    up_here, down_here = ffn.reshape(2, -1, unit_width)

    gate_val = dot(normed_all, gate_here)
    up_val = dot(normed_all, up_here)
    gelu_val, gelu_slope = gelu_parts(gate_val)
    active = low(gelu_val * up_val)
    down_part = low(contract_last(active, down_here)).reshape(unit_ways, own, width)
    layer_rows, d_second, down_low, norm_grads = turn(
        down_part, normed, out_grad.reshape(own, width), gain_two, shift_two
    )
    gain_two_grad, shift_two_grad = jnp.sum(norm_grads, axis=1)
    down_low = down_low.reshape(-1, width)
    d_active = dot(down_low, down_here)
    gate_low = low(d_active * up_val * gelu_slope)
    up_low = low(d_active * gelu_val)
    d_normed_part = low(contract_last(gate_low, gate_here) + contract_last(up_low, up_here))

    def unit_grad(left_side, right_side):
        part = low(contract_first(left_side, right_side))
        return part.reshape(4, 2, 2, 2, rows_own, unit_width)

    ffn_grads = (
        unit_grad(normed_all, gate_low),
        unit_grad(normed_all, up_low),
        unit_grad(down_low, active),
    )
    ffn_part, branch_all, d_mixed, d_first, norm_grads = close_units(
        ffn_grads,
        d_normed_part.reshape(unit_ways, own, width),
        d_second,
        hat_one,
        inverse_one,
        gain_one,
        proj_here,
        queries,
        key_rows,
        value_rows,
        probs,
        *tables[:2],
    )
    d_mixed = d_mixed.reshape(-1, 3 * head_width)
    gain_one_grad, shift_one_grad = jnp.sum(norm_grads, axis=1)
    branch_all = branch_all.reshape(-1, width)
    small_grads = jnp.stack([gain_one_grad, shift_one_grad, gain_two_grad, shift_two_grad])
    small_grads = small_grads.reshape(4, 4, head_ways, rows_own).transpose(2, 1, 0, 3)
    small_grads = small_grads.reshape(head_ways, 4, 4 * rows_own // LANES, LANES)
    small_grads = jnp.pad(small_grads, ((0, 0), (0, 0), (0, -small_grads.shape[2] % 8), (0, 0)))

    proj_part = low(contract_first(context, branch_all)).reshape(4, rows_own, width)
    d_input = low(contract_last(d_mixed, qkv_here)).reshape(head_ways, own, width)
    qkv_part = low(contract_first(x_all, d_mixed))
    qkv_part, proj_part, small_grads, d_input = close_heads(
        qkv_part.reshape(4, 8, rows_own, 3 * head_width), proj_part, small_grads, d_input
    )
    d_input = deep_alpha * d_first + d_input
    small_grads = small_grads.ravel()[: 4 * rows_own].reshape(4, rows_own)
    qkv_grad = qkv_part.reshape(2, 4, rows_own, 3, head_width)
    qkv_grad = jnp.stack([qkv_grad[:, place] for place in (0, 2, 3, 1)])
    qkv_grad = qkv_grad.transpose(2, 3, 0, 1, 4).reshape(rows_own, 3 * width).astype(jnp.float32)
    ffn_part = ffn_part.transpose(1, 2, 0, 3).reshape(3, rows_own, unit_ways * unit_width)
    gate_grad, up_grad, down_grad = (
        ffn_part[index, :, :units].astype(jnp.float32) for index in range(3)
    )
    return (
        layer_rows.reshape(micro_count, 1, pos_count, width),
        low(d_input).reshape(micro_count, 1, pos_count, width),
        qkv_grad,
        proj_part.astype(jnp.float32),
        gate_grad,
        up_grad,
        down_grad,
        small_grads[0],
        small_grads[1],
        small_grads[2],
        small_grads[3],
    )


def body(hidden_in, token_marks, out_grad, *weights):
    joined = lax.axis_size("zo")
    if joined == 1:
        return group_body(hidden_in, token_marks, out_grad, *weights)
    rows = weights[0].shape[0]
    width = hidden_in.shape[-1]
    groups = width // (joined * rows)
    group_place = lax.axis_index(ALL[1:])

    def inward(values):
        shape = values.shape
        values = values.reshape(shape[:-1] + (joined, groups, rows))
        return jnp.swapaxes(values, -3, -2).reshape(shape)

    def outward(values):
        shape = values.shape
        values = values.reshape(shape[:-1] + (groups, joined, rows))
        return jnp.swapaxes(values, -3, -2).reshape(shape)

    proj = gather(weights[1], ALL)
    proj = inward(lax.dynamic_slice_in_dim(proj, group_place * joined * rows, joined * rows))
    weights = [gather(weight, "zo") for weight in weights]
    weights[1] = proj
    outs = list(group_body(inward(hidden_in), token_marks, inward(out_grad), *weights))
    outs[:2] = outward(outs[0]), outward(outs[1])
    proj_grad = jnp.zeros((width, width), jnp.float32)
    proj_grad = lax.dynamic_update_slice_in_dim(
        proj_grad, outward(outs[3]), group_place * joined * rows, 0
    )
    outs[2:] = [scatter_sum(grad, "zo") for grad in outs[2:]]
    outs[3] = scatter_sum(proj_grad, ALL)
    return tuple(outs)


def solution(mesh):
    seq_size, ctx_size = mesh.shape["seq"], mesh.shape["ctx"]
    cores, x_size = 2, 2
    zi_size = math.gcd(4, seq_size // x_size)
    zo_size = seq_size // (x_size * zi_size)
    devices = np.asarray(mesh.devices).reshape(
        zo_size, zi_size, x_size, ctx_size // cores, cores
    )
    inner = Mesh(devices, ALL)
    tokens = P(None, ("zo", "zi", "x"), ("y", "c"), None)
    matrix = P(ALL, None)
    vector = P(ALL)
    return jax.shard_map(
        body,
        mesh=inner,
        in_specs=(tokens,) * 3 + (matrix,) * 5 + (vector,) * 4,
        out_specs=(tokens,) * 2 + (matrix,) * 5 + (vector,) * 4,
        check_vma=False,
    )
```
